32 devices in a mesh: rows: 16 (over z, y, x), tp: 2 (over core).
Axes of the slice: x: 2, y: 2, z: 4, core: 2. Of those that a mesh axis runs over, the one named last changes fastest.
Arguments:
- layer_input: bfloat16 [24576, 768], P('rows', 'tp'), may hold values from -6 to 6
- cotangent: bfloat16 [24576, 768], P('rows', 'tp'), may hold values from -6 to 6
- chain_lengths: int32 [48, 4], P('rows'), may hold values from 1 to 256, 486 in all within a row
- self_condition_flag: int32 [48], P('rows'), may hold values from 0 to 1
- time_embedding: bfloat16 [48, 4, 256], P('rows'), may hold values from -6 to 6
- query_key_value: bfloat16 [768, 3, 768], P(None, None, 'tp'), may hold values from -0.21875 to 0.21875
- output_projection: bfloat16 [768, 768], P('tp'), may hold values from -1.75 to 1.75
- attention_scale_weight: bfloat16 [256, 768], P(None, 'tp'), may hold values from -0.375 to 0.375
- attention_scale_bias: bfloat16 [768], P('tp'), may hold values from -4 to 4
- attention_shift_weight: bfloat16 [256, 768], P(None, 'tp'), may hold values from -0.375 to 0.375
- attention_gate_weight: bfloat16 [256, 768], P(None, 'tp'), may hold values from -0.375 to 0.375
- attention_gate_bias: bfloat16 [768], P('tp'), may hold values from -4 to 4
- transition_scale_weight: bfloat16 [256, 768], P(None, 'tp'), may hold values from -0.375 to 0.375
- transition_scale_bias: bfloat16 [768], P('tp'), may hold values from -4 to 4
- transition_shift_weight: bfloat16 [256, 768], P(None, 'tp'), may hold values from -0.375 to 0.375
- transition_gate_weight: bfloat16 [256, 768], P(None, 'tp'), may hold values from -0.375 to 0.375
- transition_gate_bias: bfloat16 [768], P('tp'), may hold values from -4 to 4
- gate_up_projection: bfloat16 [768, 2, 3072], P(None, None, 'tp'), may hold values from -0.21875 to 0.21875
- down_projection: bfloat16 [3072, 768], P('tp'), may hold values from -0.15625 to 0.15625
- pair_table: bfloat16 [65, 256], replicated, may hold values from -6 to 6
- pair_gain: bfloat16 [256], replicated, may hold values from 0.5 to 1.5
- pair_projection: bfloat16 [256, 12], P(None, 'tp'), may hold values from -0.375 to 0.375
- coordinate_head: bfloat16 [3, 768], P(None, 'tp'), may hold values from -0.21875 to 0.21875
- coordinate_embedding: bfloat16 [3, 768], P(None, 'tp'), may hold values from -3.5 to 3.5
Outputs:
- layer_output: bfloat16 [24576, 768], P('rows', 'tp')
- input_gradient: float32 [24576, 768], P('rows', 'tp')
- grad_query_key_value: float32 [768, 3, 768], P('rows', None, 'tp')
- grad_output_projection: float32 [768, 768], P('tp', 'rows')
- grad_attention_scale_weight: float32 [256, 768], P(None, 'tp')
- grad_attention_scale_bias: float32 [768], P('tp')
- grad_attention_shift_weight: float32 [256, 768], P(None, 'tp')
- grad_attention_gate_weight: float32 [256, 768], P(None, 'tp')
- grad_attention_gate_bias: float32 [768], P('tp')
- grad_transition_scale_weight: float32 [256, 768], P(None, 'tp')
- grad_transition_scale_bias: float32 [768], P('tp')
- grad_transition_shift_weight: float32 [256, 768], P(None, 'tp')
- grad_transition_gate_weight: float32 [256, 768], P(None, 'tp')
- grad_transition_gate_bias: float32 [768], P('tp')
- grad_gate_up_projection: float32 [768, 2, 3072], P('rows', None, 'tp')
- grad_down_projection: float32 [3072, 768], P('tp', 'rows')
- grad_pair_table: float32 [65, 256], replicated
- grad_pair_gain: float32 [256], replicated
- grad_pair_projection: float32 [256, 12], P(None, 'tp')
- grad_coordinate_embedding: float32 [3, 768], P(None, 'tp')
The draws below stay inside these ranges and needn't reach their ends.
Inputs may be any that keep to these rules, and one draw needn't show every extreme that they name: `chain_lengths`: the 4 chain lengths of each packed row sum to 486, and the longest chain of every row has exactly 256 residues.
All inputs are finite; a program needn't handle non-finite values.
Results may differ from the reference program's by a relative error of at most 0.018.
Values may be sent and summed in bfloat16 or wider, within the bound.
No kernel may reach another device: no remote copies, remote signals or barrier semaphores. Data moves between devices by JAX's collectives and lax.ppermute only.
A program may use at most 256 MiB of HBM per device.

```python
import math
import jax
import jax.numpy as jnp
import numpy as np
from jax import lax

D = 768
H = 12
DH = 64
FF = 3072
P_SIZE = 256
COND = 256
RADIUS = 32
ROW = 512
FILL = 486
MOST = 256
MAXCH = 4
NB = 65
HD = 768
PACKS = 48
TOKENS = 24576


def set_ends(drawn, rng, smallest, top_value):
    longest = drawn.shape.index(max(drawn.shape))
    spots = []
    for shift in (0, 1):
        where = [jax.random.randint(jax.random.fold_in(rng, axis), (), 0, length) for axis, length in enumerate(drawn.shape)]
        where[longest] = (where[longest] + shift) % drawn.shape[longest]
        spots.append(tuple(where))
    return drawn.at[spots[0]].set(smallest).at[spots[1]].set(top_value)


def block_scale(stream_key, dims, split, least, high):
    gain, own = 1.0, jax.random.fold_in(stream_key, 6)
    for position, shards_of in split:
        heights = jnp.exp(jax.random.uniform(jax.random.fold_in(own, position), (shards_of,), jnp.float32, least / len(split), high / len(split)))
        gain = gain * jnp.repeat(heights, dims[position] // shards_of).reshape([-1 if axis == position else 1 for axis in range(len(dims))])
    return gain


def split_up(count, total, limit, slope):
    portions = [(1 << 20) // math.isqrt(grade ** slope) + 1 for grade in range(2, count + 1)]
    spare, holding = total - limit - (count - 1), [1] * (count - 1)
    while spare > 0:
        movable = [i for i in range(count - 1) if holding[i] < limit]
        whole, remaining = sum([portions[i] for i in movable]), spare
        for i in movable:
            more = min(limit - holding[i], max(1, remaining * portions[i] // whole), spare)
            holding[i] = holding[i] + more
            spare = spare - more
    return np.array([limit] + holding)


def ragged(rng, amount, total, limit, skew):
    if amount == 2:
        one = jax.random.randint(rng, (), max(1, total - limit), min(limit, total - 1) + 1)
        return jnp.stack([one, total - one])
    sizes = jnp.asarray(split_up(amount, total, limit, skew), jnp.int32)
    couples = (amount - 1) // 2
    donor, taker = sizes[1:1 + 2 * couples:2], sizes[2:2 + 2 * couples:2]
    slack = jnp.minimum(donor - 1, limit - taker)
    passed = jax.random.randint(jax.random.fold_in(rng, 1), (couples,), 0, 1 << 20) % (slack + 1)
    sizes = sizes.at[1:1 + 2 * couples:2].set(donor - passed).at[2:2 + 2 * couples:2].set(taker + passed)
    return sizes[jax.random.permutation(jax.random.fold_in(rng, 2), amount)]


def bell_draw(key, extent, scale, limit, cuts=(), kind=jnp.bfloat16):
    array = jax.random.normal(key, extent, jnp.float32) * scale
    if len(cuts) > 0:
        array = block_scale(key, extent, cuts, -0.22, 0.18) * array
    return jnp.clip(array, min=-limit, max=limit).astype(kind)


def setup_inputs(seed: int = 0) -> dict:
    keys = jax.random.split(jax.random.key(seed), 25)
    return {
        "layer_input": bell_draw(keys[0], (TOKENS, D), 1.0, 6.0, ((0, 16), (1, 2))),
        "cotangent": bell_draw(keys[1], (TOKENS, D), 1.0, 6.0, ((0, 16), (1, 2))),
        "chain_lengths": jax.vmap(lambda own: ragged(own, MAXCH, FILL, MOST, 2))(jax.random.split(keys[2], PACKS)).reshape((PACKS, MAXCH)).astype(jnp.int32),
        "self_condition_flag": set_ends(jax.random.randint(keys[3], (PACKS,), 0, 2), jax.random.fold_in(keys[3], 1), 0, 1).astype(jnp.int32),
        "time_embedding": bell_draw(keys[4], (PACKS, MAXCH, COND), 1.0, 6.0, ((0, 16),)),
        "query_key_value": bell_draw(keys[5], (D, 3, HD), D ** -0.5, 0.21875, ((2, 2),)),
        "output_projection": bell_draw(keys[6], (HD, D), (HD // 64) ** -0.5, 1.75, ((0, 2),)),
        "attention_scale_weight": bell_draw(keys[7], (COND, D), COND ** -0.5, 0.375, ((1, 2),)),
        "attention_scale_bias": bell_draw(keys[8], (D,), 1.0, 4.0, ((0, 2),)),
        "attention_shift_weight": bell_draw(keys[9], (COND, D), COND ** -0.5, 0.375, ((1, 2),)),
        "attention_gate_weight": bell_draw(keys[10], (COND, D), COND ** -0.5, 0.375, ((1, 2),)),
        "attention_gate_bias": bell_draw(keys[11], (D,), 1.0, 4.0, ((0, 2),)),
        "transition_scale_weight": bell_draw(keys[12], (COND, D), COND ** -0.5, 0.375, ((1, 2),)),
        "transition_scale_bias": bell_draw(keys[13], (D,), 1.0, 4.0, ((0, 2),)),
        "transition_shift_weight": bell_draw(keys[14], (COND, D), COND ** -0.5, 0.375, ((1, 2),)),
        "transition_gate_weight": bell_draw(keys[15], (COND, D), COND ** -0.5, 0.375, ((1, 2),)),
        "transition_gate_bias": bell_draw(keys[16], (D,), 1.0, 4.0, ((0, 2),)),
        "gate_up_projection": bell_draw(keys[17], (D, 2, FF), D ** -0.5, 0.21875, ((2, 2),)),
        "down_projection": bell_draw(keys[18], (FF, D), (FF // 2) ** -0.5, 0.15625, ((0, 2),)),
        "pair_table": bell_draw(keys[19], (NB, P_SIZE), 1.0, 6.0),
        "pair_gain": jnp.clip(1.0 + 0.1 * jax.random.normal(keys[20], (P_SIZE,), jnp.float32), 0.5, 1.5).astype(jnp.bfloat16),
        "pair_projection": bell_draw(keys[21], (P_SIZE, H), P_SIZE ** -0.5, 0.375, ((1, 2),)),
        "coordinate_head": bell_draw(keys[22], (3, D), D ** -0.5, 0.21875, ((1, 2),)),
        "coordinate_embedding": bell_draw(keys[23], (3, D), 3 ** -0.5, 3.5, ((1, 2),)),
    }


@jax.custom_vjp
def low(v):
    return lax.optimization_barrier(v.astype(jnp.bfloat16)).astype(jnp.float32)

@jax.custom_vjp
def low_back(v):
    return v

def low_keep(v):
    return (low(v), None)

def low_pass(kept, grad):
    return (grad,)

def back_keep(v):
    return (v, None)

def back_low(kept, grad):
    return (low(grad),)
low.defvjp(low_keep, low_pass)
low_back.defvjp(back_keep, back_low)
EPSILON = 1e-05
MASKED = -1e+30
HIGHEST = lax.Precision.HIGHEST

def matmul_high(left, right):
    return jnp.dot(left, right, precision=HIGHEST)

def normalize(values):
    centre = lax.optimization_barrier(jnp.mean(values, axis=-1, keepdims=True))
    shifted = values - centre
    spread = lax.optimization_barrier(jnp.mean(shifted * shifted, axis=-1, keepdims=True))
    return shifted * lax.rsqrt(spread + EPSILON)

def layout(chain_lengths):
    chain_ends = jnp.cumsum(chain_lengths, axis=1).astype(jnp.int32)
    places = jnp.arange(ROW, dtype=jnp.int32)
    segment = lax.optimization_barrier(jnp.sum((places[None, :, None] >= chain_ends[:, None, :]).astype(jnp.int32), axis=2))
    starts = jnp.concatenate([jnp.zeros((chain_lengths.shape[0], 1), jnp.int32), chain_ends], axis=1)
    chain_start = jnp.take_along_axis(starts, segment, axis=1)
    return (segment, places[None, :] - chain_start)

def token_condition(segment, time_embedding):
    padded = jnp.concatenate([time_embedding, jnp.zeros((time_embedding.shape[0], 1, time_embedding.shape[2]), jnp.float32)], axis=1)
    index_rows = jnp.broadcast_to(segment[:, :, None], (segment.shape[0], segment.shape[1], time_embedding.shape[2]))
    return jnp.take_along_axis(padded, index_rows.astype(jnp.int32), axis=1)

def pair_bias(restart, bias_table):
    rel_bin = jnp.clip(restart[:, None] - restart[None, :], -RADIUS, RADIUS) + RADIUS
    return jnp.take(jnp.transpose(bias_table), rel_bin, axis=1)

def run_all(inputs, condition, segment, restart, params):
    w_qkv, w_out, w_scale_attn, b_scale_attn, w_shift_attn, w_gate_attn, b_gate_attn, w_scale_ffn, b_scale_ffn, w_shift_ffn, w_gate_ffn, b_gate_ffn, w_gate_up, w_down, pair_table, pair_gain, w_pair = params
    bias_table = matmul_high(normalize(pair_table) * pair_gain, w_pair)

    def one_pack(pieces):
        rows_in, cond_rows, seg_rows, restart_rows = pieces
        scale_attn = jax.nn.sigmoid(matmul_high(cond_rows, w_scale_attn) + b_scale_attn)
        normed_attn = low(normalize(rows_in) * scale_attn + matmul_high(cond_rows, w_shift_attn))
        qkv_rows = low(low_back(matmul_high(normed_attn, w_qkv.reshape(D, 3 * H * DH))))
        qkv_rows = qkv_rows.reshape(ROW, 3, H, DH)
        scores = jnp.einsum('ihd,jhd->hij', qkv_rows[:, 0], qkv_rows[:, 1], precision=HIGHEST) * DH ** (-0.5)
        scores = low_back(scores + pair_bias(restart_rows, bias_table))
        same_chain = seg_rows[:, None] == seg_rows[None, :]
        scores = jnp.where(same_chain[None], scores, MASKED)
        softmax_low = low(jax.nn.softmax(scores, axis=2))
        attended = jnp.einsum('hij,jhd->ihd', softmax_low, qkv_rows[:, 2], precision=HIGHEST)
        attended = low(low_back(attended)).reshape(ROW, H * DH)
        branch = low_back(matmul_high(attended, w_out))
        gate_attn = jax.nn.sigmoid(matmul_high(cond_rows, w_gate_attn) + b_gate_attn)
        middle = rows_in + gate_attn * branch
        scale_ffn = jax.nn.sigmoid(matmul_high(cond_rows, w_scale_ffn) + b_scale_ffn)
        normed_ffn = low(normalize(middle) * scale_ffn + matmul_high(cond_rows, w_shift_ffn))
        gate_up = matmul_high(normed_ffn, w_gate_up.reshape(D, 2 * FF))
        gate_pre = low_back(gate_up[:, :FF])
        up_rows = low_back(gate_up[:, FF:])
        hidden = low(jax.nn.silu(gate_pre) * up_rows)
        mixed_rows = low_back(matmul_high(hidden, w_down))
        gate_ffn = jax.nn.sigmoid(matmul_high(cond_rows, w_gate_ffn) + b_gate_ffn)
        return middle + gate_ffn * mixed_rows
    return lax.map(jax.checkpoint(one_pack), (inputs, condition, segment, restart))

def reference(layer_input, cotangent, chain_lengths, self_condition_flag, time_embedding, query_key_value, output_projection, attention_scale_weight, attention_scale_bias, attention_shift_weight, attention_gate_weight, attention_gate_bias, transition_scale_weight, transition_scale_bias, transition_shift_weight, transition_gate_weight, transition_gate_bias, gate_up_projection, down_projection, pair_table, pair_gain, pair_projection, coordinate_head, coordinate_embedding):
    segment, restart = layout(chain_lengths)
    condition = token_condition(segment, time_embedding.astype(jnp.float32))
    params = tuple((weight_arg.astype(jnp.float32) for weight_arg in (query_key_value, output_projection, attention_scale_weight, attention_scale_bias, attention_shift_weight, attention_gate_weight, attention_gate_bias, transition_scale_weight, transition_scale_bias, transition_shift_weight, transition_gate_weight, transition_gate_bias, gate_up_projection, down_projection, pair_table, pair_gain, pair_projection)))
    inputs = layer_input.astype(jnp.float32).reshape(PACKS, ROW, D)
    head_weight = coordinate_head.astype(jnp.float32)

    def first_section(layer_in):
        first_pass = run_all(layer_in, condition, segment, restart, params)
        return jnp.einsum('prd,cd->prc', first_pass, head_weight, precision=HIGHEST)
    coords, unused_pull = jax.vjp(first_section, inputs)
    lifted = coords * self_condition_flag.astype(jnp.float32)[:, None, None]

    def forward(layer_in, weights, embed_weight):
        shifted = layer_in + jnp.einsum('prc,cd->prd', lifted, embed_weight, precision=HIGHEST)
        return run_all(shifted, condition, segment, restart, weights)
    result, pull = jax.vjp(forward, inputs, params, coordinate_embedding.astype(jnp.float32))
    grad_input, grad_params, grad_embed = pull(cotangent.astype(jnp.float32).reshape(PACKS, ROW, D))
    grad_qkv, grad_out, grad_scale_attn, grad_scale_attn_bias, grad_shift_attn, grad_gate_attn, grad_gate_attn_bias, grad_scale_ffn, grad_scale_ffn_bias, grad_shift_ffn, grad_gate_ffn, grad_gate_ffn_bias, grad_gate_up, grad_down, grad_table, grad_gain, grad_pair = grad_params
    return (result.reshape(TOKENS, D).astype(jnp.bfloat16), grad_input.reshape(TOKENS, D), grad_qkv, grad_out, grad_scale_attn, grad_scale_attn_bias, grad_shift_attn, grad_gate_attn, grad_gate_attn_bias, grad_scale_ffn, grad_scale_ffn_bias, grad_shift_ffn, grad_gate_ffn, grad_gate_ffn_bias, grad_gate_up, grad_down, grad_table, grad_gain, grad_pair, grad_embed)
```

```python
import functools
import jax
import jax.numpy as jnp
from jax import lax
from jax.experimental import pallas as pl
from jax.experimental.pallas import tpu as pltpu
from jax.sharding import PartitionSpec as P

RADIUS = 32
ROW = 512
HALF = ROW // 2
SEGS = 5
EPSILON = 1e-05
MASKED = -1e30
HIGHEST = lax.Precision.HIGHEST
F32 = jnp.float32
BF16 = jnp.bfloat16
LANES = 128
FFC = 512
NT = (((1,), (1,)), ((), ()))
VMEM_LIMIT = 60 * 1024 * 1024


def mm(left, right):
    return jnp.dot(left, right, preferred_element_type=F32)


def mm_nt(left, right):
    return lax.dot_general(left, right, NT, preferred_element_type=F32)


def norm_parts(values):
    centre = jnp.mean(values, axis=1, keepdims=True)
    shifted = values - centre
    spread = jnp.mean(shifted * shifted, axis=1, keepdims=True)
    inv_std = lax.rsqrt(spread + EPSILON)
    return shifted * inv_std, inv_std


def norm_back(grad, hat, inv_std):
    first = jnp.mean(grad, axis=1, keepdims=True)
    second = jnp.mean(grad * hat, axis=1, keepdims=True)
    return inv_std * (grad - first - hat * second)


def block_loop(count, body):
    lax.fori_loop(0, count, lambda i, c: (body(i), c)[1], 0)


def call(kernel, grid, in_specs, out_specs, out_shape, scratch=(), prefetch=0, aliases=None, flops=0, moved=0):
    return pl.pallas_call(
        kernel,
        grid_spec=pltpu.PrefetchScalarGridSpec(
            num_scalar_prefetch=prefetch,
            grid=grid,
            in_specs=in_specs,
            out_specs=out_specs,
            scratch_shapes=list(scratch),
        ),
        out_shape=out_shape,
        input_output_aliases=aliases or {},
        compiler_params=pltpu.CompilerParams(
            dimension_semantics=("arbitrary",) * len(grid), vmem_limit_bytes=VMEM_LIMIT
        ),
        cost_estimate=pl.CostEstimate(flops=flops, transcendentals=0, bytes_accessed=moved),
    )


def whole(*shape):
    zeros = (0,) * len(shape)
    return pl.BlockSpec(shape, lambda *_: zeros)


def bias_kernel(base_ref, o_ref):
    for d in range(3):
        rows = jnp.broadcast_to(base_ref[0, d : d + 1, :], (HALF, 2 * HALF))
        rolled = pltpu.roll(rows, 0, axis=1, stride=1, stride_axis=0)
        o_ref[0, d] = rolled[:, :HALF]


def bias_tiles(base):
    heads = base.shape[0]
    return call(
        bias_kernel,
        (heads,),
        [pl.BlockSpec((1, 3, 2 * HALF), lambda h: (h, 0, 0))],
        pl.BlockSpec((1, 3, HALF, HALF), lambda h: (h, 0, 0, 0)),
        jax.ShapeDtypeStruct((heads, 3, HALF, HALF), F32),
        moved=heads * 3 * HALF * HALF * 4,
        flops=10**7,
    )(base)


def qkv_kernel(x_ref, oh_ref, tab_ref, own_ref, par_ref, o_ref, normed):
    width = x_ref.shape[1]
    half = own_ref.shape[1]

    @pl.when(pl.program_id(0) == 0)
    def _():
        def body(i):
            rows = pl.ds(pl.multiple_of(i * HALF, HALF), HALF)
            hat, _ = norm_parts(x_ref[rows, :].astype(F32))
            pick = oh_ref[rows, :]
            scale = mm(pick, tab_ref[:, :width])
            shift = mm(pick, tab_ref[:, width : 2 * width])
            normed[rows, :] = (hat * scale + shift).astype(BF16)

        block_loop(x_ref.shape[0] // HALF, body)

    o_ref[:, :half] = mm(normed[...], own_ref[...]).astype(BF16)
    o_ref[:, half:] = mm(normed[...], par_ref[...]).astype(BF16)


def qkv_forward(x, pick, table, w_own, w_par):
    tokens, width = x.shape
    half = w_own.shape[1] // 3
    return call(
        qkv_kernel,
        (3,),
        [
            whole(tokens, width),
            whole(*pick.shape),
            whole(*table.shape),
            pl.BlockSpec((width, half), lambda j: (0, j)),
            pl.BlockSpec((width, half), lambda j: (0, j)),
        ],
        pl.BlockSpec((tokens, 2 * half), lambda j: (0, j)),
        jax.ShapeDtypeStruct((tokens, 6 * half), BF16),
        [pltpu.VMEM((tokens, width), BF16)],
        flops=2 * tokens * width * 6 * half,
        moved=tokens * 6 * half * 2 + width * half * 12 + tokens * width * 4,
    )(x, pick, table, w_own, w_par)


def lane_masks():
    lanes = lax.broadcasted_iota(jnp.int32, (1, LANES), 1)
    first = (lanes < LANES // 2).astype(F32)
    return first.astype(BF16), (1.0 - first).astype(BF16)


def attend_forward_block(q, segq, keys, values_t, biases):
    outs, logs = [], []
    half = LANES // 2
    masks = lane_masks()
    scaled = q * jnp.asarray(half**-0.5, BF16)
    for h in range(2):
        query = jnp.concatenate([scaled * masks[h], segq], axis=1)
        scores = [mm_nt(key, query) + bias(h) for key, bias in zip(keys, biases)]
        tops = [jnp.max(s, axis=0, keepdims=True) for s in scores]
        top = functools.reduce(jnp.maximum, tops)
        weights = [jnp.exp(s - top) for s in scores]
        total = sum(jnp.sum(w, axis=0, keepdims=True) for w in weights)
        mixed = sum(
            mm(vt[h * half : (h + 1) * half, :], w.astype(BF16)) for vt, w in zip(values_t, weights)
        )
        outs.append(mixed / total)
        logs.append(top + jnp.log(total))
    attended = jnp.concatenate(outs, axis=0).T.astype(BF16)
    return attended, jnp.concatenate(logs, axis=0)


def attend_full_kernel(q_ref, k_ref, v_ref, segq_ref, segk_ref, bias_ref, o_ref, log_ref):
    keys = [
        jnp.concatenate([k_ref[pl.ds(b * HALF, HALF), :], segk_ref[pl.ds(b * HALF, HALF), :]], axis=1)
        for b in range(2)
    ]
    values_t = [v_ref[pl.ds(b * HALF, HALF), :].T for b in range(2)]
    for qb in range(2):
        rows = pl.ds(qb * HALF, HALF)
        biases = [lambda h, kb=kb: bias_ref[h, qb - kb + 1] for kb in range(2)]
        attended, logs = attend_forward_block(q_ref[rows, :], segq_ref[rows, :], keys, values_t, biases)
        o_ref[rows, :] = attended
        log_ref[0, 0:2, rows] = logs


def attend_half_kernel(
    tp_ref, q_ref, k_ref, v_ref, kp_ref, vp_ref, segq_ref, segk_ref, bias_ref, oin, login, o_ref, log_ref
):
    keys = [
        jnp.concatenate([k_ref[...], segk_ref[pl.ds(0, HALF), :]], axis=1),
        jnp.concatenate([kp_ref[...], segk_ref[pl.ds(HALF, HALF), :]], axis=1),
    ]
    values_t = [v_ref[...].T, vp_ref[...].T]
    far = 2 * tp_ref[0]
    biases = [lambda h: bias_ref[h, 1], lambda h: bias_ref[h, far]]
    attended, logs = attend_forward_block(q_ref[...], segq_ref[...], keys, values_t, biases)
    o_ref[...] = attended
    log_ref[0, 0:2, :] = logs


def attend_forward(tp, qkv, kv_par, segq, segk, bias):
    tokens = qkv.shape[0]
    width = qkv.shape[1] // 3
    pairs = width // LANES
    out_shape = (
        jax.ShapeDtypeStruct((tokens, width), BF16),
        jax.ShapeDtypeStruct((pairs, 8, tokens), F32),
    )
    bias_spec = pl.BlockSpec((2, 3, HALF, HALF), lambda p, *_: (p, 0, 0, 0))
    unit = 4 * HALF * HALF * 256 * 2
    attended, logs = call(
        attend_full_kernel,
        (pairs,),
        [
            pl.BlockSpec((ROW, LANES), lambda p: (0, p)),
            pl.BlockSpec((ROW, LANES), lambda p: (0, pairs + p)),
            pl.BlockSpec((ROW, LANES), lambda p: (0, 2 * pairs + p)),
            pl.BlockSpec((ROW, LANES), lambda p: (0, 0)),
            pl.BlockSpec((ROW, LANES), lambda p: (0, 0)),
            bias_spec,
        ],
        (
            pl.BlockSpec((ROW, LANES), lambda p: (0, p)),
            pl.BlockSpec((1, 8, ROW), lambda p: (p, 0, 0)),
        ),
        out_shape,
        flops=unit * 4 * pairs,
        moved=bias.size * 4,
    )(qkv, qkv, qkv, segq, segk, bias)
    flip = pairs // 2
    return call(
        attend_half_kernel,
        (pairs,),
        [
            pl.BlockSpec((HALF, LANES), lambda p, *_: (2, p)),
            pl.BlockSpec((HALF, LANES), lambda p, *_: (2, pairs + p)),
            pl.BlockSpec((HALF, LANES), lambda p, *_: (2, 2 * pairs + p)),
            pl.BlockSpec((HALF, LANES), lambda p, *_: (0, lax.rem(p + flip, pairs))),
            pl.BlockSpec((HALF, LANES), lambda p, *_: (0, pairs + lax.rem(p + flip, pairs))),
            pl.BlockSpec((HALF, LANES), lambda p, *_: (2, 0)),
            pl.BlockSpec((ROW, LANES), lambda p, *_: (1, 0)),
            bias_spec,
            pl.BlockSpec(memory_space=pl.ANY),
            pl.BlockSpec(memory_space=pl.ANY),
        ],
        (
            pl.BlockSpec((HALF, LANES), lambda p, *_: (2, p)),
            pl.BlockSpec((1, 8, HALF), lambda p, *_: (p, 0, 2)),
        ),
        out_shape,
        prefetch=1,
        aliases={9: 0, 10: 1},
        flops=unit * 2 * pairs,
        moved=bias.size * 4,
    )(tp, qkv, qkv, qkv, kv_par, kv_par, segq, segk, bias, attended, logs)


def ffn_kernel(
    att_ref, woo_ref, wop_ref, x_ref, oh_ref, tab_ref, guo_ref, gup_ref, wdo_ref, wdp_ref,
    head_ref, emb_ref, flag_ref, shifted_ref, lifted_ref, middle, normed, acc,
):
    step = pl.program_id(0)
    tokens, width = x_ref.shape
    half = woo_ref.shape[0]
    blocks = tokens // HALF

    @pl.when(step == 0)
    def _():
        def body(i):
            rows = pl.ds(pl.multiple_of(i * HALF, HALF), HALF)
            branch = mm(att_ref[rows, :half], woo_ref[...]) + mm(att_ref[rows, half:], wop_ref[...])
            pick = oh_ref[rows, :]
            mid = x_ref[rows, :].astype(F32) + mm(pick, tab_ref[:, 2 * width : 3 * width]) * branch
            middle[rows, :] = mid
            hat, _ = norm_parts(mid)
            scale = mm(pick, tab_ref[:, 3 * width : 4 * width])
            shift = mm(pick, tab_ref[:, 4 * width : 5 * width])
            normed[rows, :] = (hat * scale + shift).astype(BF16)
            acc[rows, :] = jnp.zeros((HALF, width), F32)

        block_loop(blocks, body)

    def body(i):
        rows = pl.ds(pl.multiple_of(i * HALF, HALF), HALF)
        total = acc[rows, :]
        for gu, wd in ((guo_ref, wdo_ref), (gup_ref, wdp_ref)):
            gate = mm(normed[rows, :], gu[0])
            up = mm(normed[rows, :], gu[1])
            hidden = (gate * jax.nn.sigmoid(gate) * up).astype(BF16)
            total = total + mm(hidden, wd[...])
        acc[rows, :] = total

    block_loop(blocks, body)

    @pl.when(step == pl.num_programs(0) - 1)
    def _():
        def body(i):
            rows = pl.ds(pl.multiple_of(i * HALF, HALF), HALF)
            gate = mm(oh_ref[rows, :], tab_ref[:, 5 * width : 6 * width])
            first = middle[rows, :] + gate * acc[rows, :]
            high = first.astype(BF16)
            rest = (first - high.astype(F32)).astype(BF16)
            coords = mm_nt(high, head_ref[...]) + mm_nt(rest, head_ref[...])
            lifted = coords * flag_ref[rows, :]
            lifted_ref[rows, :] = lifted
            high = lifted.astype(BF16)
            rest = (lifted - high.astype(F32)).astype(BF16)
            moved = mm(high, emb_ref[...]) + mm(rest, emb_ref[...])
            shifted_ref[rows, :] = x_ref[rows, :].astype(F32) + moved

        block_loop(blocks, body)


def ffn_specs(att, woo, x, pick, table):
    tokens, width = x.shape
    chunk = FFC
    return [
        whole(*att.shape),
        whole(*woo.shape),
        whole(*woo.shape),
        whole(tokens, width),
        whole(*pick.shape),
        whole(*table.shape),
        pl.BlockSpec((2, width, chunk), lambda j, *_: (0, 0, j)),
        pl.BlockSpec((2, width, chunk), lambda j, *_: (0, 0, j)),
        pl.BlockSpec((chunk, width), lambda j, *_: (j, 0)),
        pl.BlockSpec((chunk, width), lambda j, *_: (j, 0)),
    ]


def ffn_forward(att, woo, wop, x, pick, table, guo, gup, wdo, wdp, head, emb, flags):
    tokens, width = x.shape
    hidden = wdo.shape[0]
    return call(
        ffn_kernel,
        (hidden // FFC,),
        ffn_specs(att, woo, x, pick, table)
        + [whole(*head.shape), whole(*emb.shape), whole(*flags.shape)],
        (whole(tokens, width), whole(tokens, LANES)),
        (
            jax.ShapeDtypeStruct((tokens, width), F32),
            jax.ShapeDtypeStruct((tokens, LANES), F32),
        ),
        [
            pltpu.VMEM((tokens, width), F32),
            pltpu.VMEM((tokens, width), BF16),
            pltpu.VMEM((tokens, width), F32),
        ],
        flops=2 * tokens * width * (6 * hidden + width),
        moved=12 * hidden * width + 6 * tokens * width,
    )(att, woo, wop, x, pick, table, guo, gup, wdo, wdp, head, emb, flags)


def turn_kernel(
    tp_ref, att_ref, woo_ref, wop_ref, x_ref, oh_ref, tab_ref, guo_ref, gup_ref, wdo_ref, wdp_ref,
    g_ref, oht_ref,
    outo_ref, outp_ref, gmid_ref, gatt_ref, go_ref, gp_ref, goo_ref, gop_ref, sumo_ref, sump_ref,
    sums_ref, middle, hats, branches, normed, normed_t, gmixed, gmixed_t, mixed, gnormed, hid, dgate, dup,
):
    step = pl.program_id(0)
    tokens, width = x_ref.shape
    half = woo_ref.shape[0]
    blocks = tokens // HALF

    @pl.when(step == 0)
    def _():
        def body(i):
            rows = pl.ds(pl.multiple_of(i * HALF, HALF), HALF)
            branch = mm(att_ref[rows, :half], woo_ref[...]) + mm(att_ref[rows, half:], wop_ref[...])
            branches[rows, :] = branch
            pick = oh_ref[rows, :]
            mid = x_ref[rows, :] + mm(pick, tab_ref[:, 2 * width : 3 * width]) * branch
            middle[rows, :] = mid
            hat, _ = norm_parts(mid)
            scale = mm(pick, tab_ref[:, 3 * width : 4 * width])
            shift = mm(pick, tab_ref[:, 4 * width : 5 * width])
            normed[rows, :] = (hat * scale + shift).astype(BF16)
            gate = mm(pick, tab_ref[:, 5 * width : 6 * width])
            gmixed[rows, :] = (g_ref[rows, :].astype(F32) * gate).astype(BF16)
            mixed[rows, :] = jnp.zeros((HALF, width), F32)
            gnormed[rows, :] = jnp.zeros((HALF, width), F32)

        block_loop(blocks, body)
        normed_t[...] = normed[...].T
        gmixed_t[...] = gmixed[...].T

    for gu, wd, out in ((gup_ref, wdp_ref, gp_ref), (guo_ref, wdo_ref, go_ref)):

        def body(i):
            rows = pl.ds(pl.multiple_of(i * HALF, HALF), HALF)
            gate = mm(normed[rows, :], gu[0])
            up = mm(normed[rows, :], gu[1])
            ghid = mm_nt(gmixed[rows, :], wd[...])
            s = jax.nn.sigmoid(gate)
            silu = gate * s
            hidden = (silu * up).astype(BF16)
            hid[rows, :] = hidden
            mixed[rows, :] += mm(hidden, wd[...])
            dg = (ghid * up * (s + silu * (1.0 - s))).astype(BF16)
            du = (ghid * silu).astype(BF16)
            dgate[rows, :] = dg
            dup[rows, :] = du
            gnormed[rows, :] += mm_nt(dg, gu[0]) + mm_nt(du, gu[1])

        block_loop(blocks, body)
        out[0, 0] = mm(normed_t[...], dgate[...]).astype(BF16)
        out[1, 0] = mm(normed_t[...], dup[...]).astype(BF16)
        out[2, 0] = mm(gmixed_t[...], hid[...]).astype(BF16)

    @pl.when(step == pl.num_programs(0) - 1)
    def _():
        first_core = tp_ref[0] == 0
        sums_ref[...] = jnp.zeros(sums_ref.shape, F32)

        def body(i):
            rows = pl.ds(pl.multiple_of(i * HALF, HALF), HALF)
            pick = oh_ref[rows, :]
            turn = oht_ref[i]
            g = g_ref[rows, :].astype(F32)
            total = mixed[rows, :]
            gate = mm(pick, tab_ref[:, 5 * width : 6 * width])
            mid = middle[rows, :]
            result = (mid + gate * total).astype(BF16)
            low, high = result[:, : width // 2], result[:, width // 2 :]
            outo_ref[rows, :] = jnp.where(first_core, low, high)
            outp_ref[rows, :] = jnp.where(first_core, high, low)
            sums_ref[0] += mm(turn, (g * total).astype(BF16))
            hat, inv_std = norm_parts(mid)
            gn = gnormed[rows, :]
            sums_ref[1] += mm(turn, (gn * hat).astype(BF16))
            sums_ref[2] += mm(turn, gn.astype(BF16))
            scale = mm(pick, tab_ref[:, 3 * width : 4 * width])
            gmid = g + norm_back(gn * scale, hat, inv_std)
            gmid_ref[rows, :] = gmid
            sums_ref[3] += mm(turn, (gmid * branches[rows, :]).astype(BF16))
            gbranch = (gmid * mm(pick, tab_ref[:, 2 * width : 3 * width])).astype(BF16)
            gmixed[rows, :] = gbranch
            gatt_ref[rows, :half] = mm_nt(gbranch, woo_ref[...]).astype(BF16)
            gatt_ref[rows, half:] = mm_nt(gbranch, wop_ref[...]).astype(BF16)

        block_loop(blocks, body)
        gmixed_t[...] = gmixed[...].T
        goo_ref[...] = mm(gmixed_t[...], att_ref[:, :half]).astype(BF16)
        gop_ref[...] = mm(gmixed_t[...], att_ref[:, half:]).astype(BF16)
        low, high = sums_ref[:, :, : width // 2], sums_ref[:, :, width // 2 :]
        sumo_ref[...] = jnp.where(first_core, low, high)
        sump_ref[...] = jnp.where(first_core, high, low)


def ffn_turn(tp, att, woo, wop, x, pick, table, guo, gup, wdo, wdp, g, pick_t):
    tokens, width = x.shape
    half = woo.shape[0]
    hidden = wdo.shape[0]
    grads = jax.ShapeDtypeStruct((3, hidden // FFC, width, FFC), BF16)
    grads_spec = pl.BlockSpec((3, 1, width, FFC), lambda j, *_: (0, j, 0, 0))
    return call(
        turn_kernel,
        (hidden // FFC,),
        ffn_specs(att, woo, x, pick, table) + [whole(tokens, width), whole(*pick_t.shape)],
        (
            whole(tokens, width // 2),
            whole(tokens, width // 2),
            whole(tokens, width),
            whole(tokens, width),
            grads_spec,
            grads_spec,
            whole(width, half),
            whole(width, half),
            whole(4, 16, width // 2),
            whole(4, 16, width // 2),
        ),
        (
            jax.ShapeDtypeStruct((tokens, width // 2), BF16),
            jax.ShapeDtypeStruct((tokens, width // 2), BF16),
            jax.ShapeDtypeStruct((tokens, width), F32),
            jax.ShapeDtypeStruct((tokens, width), BF16),
            grads,
            grads,
            jax.ShapeDtypeStruct((width, half), BF16),
            jax.ShapeDtypeStruct((width, half), BF16),
            jax.ShapeDtypeStruct((4, 16, width // 2), F32),
            jax.ShapeDtypeStruct((4, 16, width // 2), F32),
        ),
        [
            pltpu.VMEM((4, 16, width), F32),
            pltpu.VMEM((tokens, width), F32),
            pltpu.VMEM((8, LANES), F32),
            pltpu.VMEM((tokens, width), F32),
            pltpu.VMEM((tokens, width), BF16),
            pltpu.VMEM((width, tokens), BF16),
            pltpu.VMEM((tokens, width), BF16),
            pltpu.VMEM((width, tokens), BF16),
            pltpu.VMEM((tokens, width), F32),
            pltpu.VMEM((tokens, width), F32),
            pltpu.VMEM((tokens, FFC), BF16),
            pltpu.VMEM((tokens, FFC), BF16),
            pltpu.VMEM((tokens, FFC), BF16),
        ],
        prefetch=1,
        flops=2 * tokens * width * (18 * hidden + 3 * width),
        moved=24 * hidden * width + 12 * tokens * width,
    )(tp, att, woo, wop, x, pick, table, guo, gup, wdo, wdp, g, pick_t)


def attend_back_block(q, segq, gout, logs, keys, keys_t, values, biases, bias_sums, gkeys, gvalues):
    half = LANES // 2
    masks = lane_masks()
    scale = half**-0.5
    scaled = q * jnp.asarray(scale, BF16)
    gqs = []
    for h in range(2):
        query_low = scaled * masks[h]
        query = jnp.concatenate([query_low, segq], axis=1)
        gheads = gout * masks[h]
        chances = [jnp.exp(mm_nt(key, query) + bias(h) - logs[h : h + 1, :]) for key, bias in zip(keys, biases)]
        gchances = [mm_nt(value, gheads) for value in values]
        centre = sum(jnp.sum(p * gp, axis=0, keepdims=True) for p, gp in zip(chances, gchances))
        gq = 0.0
        for b, (p, gp) in enumerate(zip(chances, gchances)):
            gs = p * (gp - centre)
            bias_sums[b](h, gs)
            low = gs.astype(BF16)
            gvalues[b] = gvalues[b] + mm(p.astype(BF16), gheads)
            gkeys[b] = gkeys[b] + mm(low, query_low)
            gq = gq + mm(keys_t[b][h * half : (h + 1) * half, :], low)
        gqs.append(gq * scale)
    return jnp.concatenate(gqs, axis=0).T.astype(BF16)


def diagonal_sums(tile):
    size = tile.shape[0]
    rows = lax.broadcasted_iota(jnp.int32, (size, size), 0)
    cols = lax.broadcasted_iota(jnp.int32, (size, size), 1)
    turn = (rows + cols == size - 1).astype(F32).astype(BF16)
    high = tile.astype(BF16)
    rest = (tile - high.astype(F32)).astype(BF16)
    flipped = mm(turn, high) + mm(turn, rest)
    padded = jnp.concatenate([flipped, jnp.zeros_like(flipped)], axis=1)
    rolled = pltpu.roll(padded, 0, axis=1, stride=1, stride_axis=0)
    return jnp.sum(rolled, axis=0, keepdims=True)


def attend_full_back_kernel(
    q_ref, k_ref, v_ref, g_ref, log_ref, segq_ref, segk_ref, bias_ref, o_ref, diag_ref, sums
):
    keys, keys_t, values = [], [], []
    for b in range(2):
        rows = pl.ds(b * HALF, HALF)
        key = k_ref[rows, :]
        keys.append(jnp.concatenate([key, segk_ref[rows, :]], axis=1))
        keys_t.append(key.T)
        values.append(v_ref[rows, :])
    gkeys, gvalues = [0.0, 0.0], [0.0, 0.0]
    sums[...] = jnp.zeros(sums.shape, F32)
    for qb in range(2):
        rows = pl.ds(qb * HALF, HALF)
        biases = [lambda h, kb=kb: bias_ref[h, qb - kb + 1] for kb in range(2)]

        def add(h, gs, d):
            sums[h, d] += gs

        adders = [functools.partial(add, d=qb - kb + 1) for kb in range(2)]
        o_ref[0, rows, :] = attend_back_block(
            q_ref[rows, :], segq_ref[rows, :], g_ref[rows, :], log_ref[0, 0:2, rows],
            keys, keys_t, values, biases, adders, gkeys, gvalues,
        )
    for b in range(2):
        rows = pl.ds(b * HALF, HALF)
        o_ref[1, rows, :] = gkeys[b].astype(BF16)
        o_ref[2, rows, :] = gvalues[b].astype(BF16)
    for h in range(2):
        for d in range(3):
            diag_ref[0, 3 * h + d : 3 * h + d + 1, :] = diagonal_sums(sums[h, d])


def attend_half_back_kernel(
    tp_ref, q_ref, k_ref, v_ref, kp_ref, vp_ref, g_ref, log_ref, segq_ref, segk_ref, bias_ref,
    o_ref, par_ref, diag_ref,
):
    keys, keys_t, values = [], [], []
    for b, (k, v) in enumerate(((k_ref, v_ref), (kp_ref, vp_ref))):
        key = k[...]
        keys.append(jnp.concatenate([key, segk_ref[pl.ds(b * HALF, HALF), :]], axis=1))
        keys_t.append(key.T)
        values.append(v[...])
    far = 2 * tp_ref[0]
    biases = [lambda h: bias_ref[h, 1], lambda h: bias_ref[h, far]]
    gkeys, gvalues = [0.0, 0.0], [0.0, 0.0]

    def put(h, gs, b):
        diag_ref[0, 2 * h + b : 2 * h + b + 1, :] = diagonal_sums(gs)

    adders = [functools.partial(put, b=b) for b in range(2)]
    o_ref[0] = attend_back_block(
        q_ref[...], segq_ref[...], g_ref[...], log_ref[0, 0:2, :],
        keys, keys_t, values, biases, adders, gkeys, gvalues,
    )
    o_ref[1] = gkeys[0].astype(BF16)
    o_ref[2] = gvalues[0].astype(BF16)
    par_ref[0] = gkeys[1].astype(BF16)
    par_ref[1] = gvalues[1].astype(BF16)


def attend_half_back(tp, qkv, kv_par, g, logs, segq, segk, bias):
    width = qkv.shape[1] // 3
    pairs = width // LANES
    flip = pairs // 2
    return call(
        attend_half_back_kernel,
        (pairs,),
        [
            pl.BlockSpec((HALF, LANES), lambda p, *_: (2, p)),
            pl.BlockSpec((HALF, LANES), lambda p, *_: (2, pairs + p)),
            pl.BlockSpec((HALF, LANES), lambda p, *_: (2, 2 * pairs + p)),
            pl.BlockSpec((HALF, LANES), lambda p, *_: (0, lax.rem(p + flip, pairs))),
            pl.BlockSpec((HALF, LANES), lambda p, *_: (0, pairs + lax.rem(p + flip, pairs))),
            pl.BlockSpec((HALF, LANES), lambda p, *_: (2, p)),
            pl.BlockSpec((1, 8, HALF), lambda p, *_: (p, 0, 2)),
            pl.BlockSpec((HALF, LANES), lambda p, *_: (2, 0)),
            pl.BlockSpec((ROW, LANES), lambda p, *_: (1, 0)),
            pl.BlockSpec((2, 3, HALF, HALF), lambda p, *_: (p, 0, 0, 0)),
        ],
        (
            pl.BlockSpec((3, HALF, LANES), lambda p, *_: (0, 0, p)),
            pl.BlockSpec((2, HALF, LANES), lambda p, *_: (0, 0, p)),
            pl.BlockSpec((1, 8, ROW), lambda p, *_: (p, 0, 0)),
        ),
        (
            jax.ShapeDtypeStruct((3, HALF, width), BF16),
            jax.ShapeDtypeStruct((2, HALF, width), BF16),
            jax.ShapeDtypeStruct((pairs, 8, ROW), F32),
        ),
        prefetch=1,
        flops=10 * HALF * HALF * 256 * 2 * pairs,
        moved=bias.size * 4,
    )(tp, qkv, qkv, qkv, kv_par, kv_par, g, logs, segq, segk, bias)


def attend_full_back(qkv, g, logs, segq, segk, bias):
    width = qkv.shape[1] // 3
    pairs = width // LANES
    return call(
        attend_full_back_kernel,
        (pairs,),
        [
            pl.BlockSpec((ROW, LANES), lambda p: (0, p)),
            pl.BlockSpec((ROW, LANES), lambda p: (0, pairs + p)),
            pl.BlockSpec((ROW, LANES), lambda p: (0, 2 * pairs + p)),
            pl.BlockSpec((ROW, LANES), lambda p: (0, p)),
            pl.BlockSpec((1, 8, ROW), lambda p: (p, 0, 0)),
            pl.BlockSpec((ROW, LANES), lambda p: (0, 0)),
            pl.BlockSpec((ROW, LANES), lambda p: (0, 0)),
            pl.BlockSpec((2, 3, HALF, HALF), lambda p: (p, 0, 0, 0)),
        ],
        (
            pl.BlockSpec((3, ROW, LANES), lambda p: (0, 0, p)),
            pl.BlockSpec((1, 8, ROW), lambda p: (p, 0, 0)),
        ),
        (
            jax.ShapeDtypeStruct((3, ROW, width), BF16),
            jax.ShapeDtypeStruct((pairs, 8, ROW), F32),
        ),
        [pltpu.VMEM((2, 3, HALF, HALF), F32)],
        flops=20 * HALF * HALF * 256 * 2 * pairs,
        moved=bias.size * 4,
    )(qkv, qkv, qkv, g, logs, segq, segk, bias)


def joined_rows(full_ref, half_ref, recv_ref, step, rows_in):
    half = recv_ref.shape[2] // 2
    rows_in[pl.ds(0, ROW), :] = full_ref[0]
    keep = (step > 0).astype(F32).astype(BF16)
    recv = jnp.concatenate([recv_ref[0, :, half:], recv_ref[0, :, :half]], axis=1)
    rows_in[pl.ds(ROW, HALF), :] = half_ref[0] + recv * keep


def qkv_weights_kernel(
    x_ref, oh_ref, tab_ref, full_ref, half_ref, recv_ref, outo_ref, outp_ref, go_ref, gp_ref, normed, normed_t, rows_in
):
    step = pl.program_id(0)
    tokens, width = x_ref.shape
    half = width // 2

    @pl.when(step == 0)
    def _():
        def body(i):
            rows = pl.ds(pl.multiple_of(i * HALF, HALF), HALF)
            hat, _ = norm_parts(x_ref[rows, :])
            pick = oh_ref[rows, :]
            scale = mm(pick, tab_ref[:, :width])
            shift = mm(pick, tab_ref[:, width : 2 * width])
            normed[rows, :] = (hat * scale + shift).astype(BF16)

        block_loop(tokens // HALF, body)
        normed_t[...] = normed[...].T

    joined_rows(full_ref, half_ref, recv_ref, step, rows_in)
    go_ref[0, :, :half] = mm(normed_t[...], rows_in[:, :half]).astype(BF16)
    gp_ref[0, :, :half] = mm(normed_t[...], rows_in[:, half:]).astype(BF16)
    go_ref[0, :, half:] = outo_ref[...]
    gp_ref[0, :, half:] = outp_ref[...]


def row_specs(width):
    return [
        pl.BlockSpec((1, ROW, width), lambda j, *_: (j, 0, 0)),
        pl.BlockSpec((1, HALF, width), lambda j, *_: (j, 0, 0)),
        pl.BlockSpec((1, HALF, width), lambda j, *_: (jnp.maximum(j - 1, 0), 0, 0)),
    ]


def qkv_weights(x, pick, table, full, half_rows, recv, out_own, out_par):
    tokens, width = x.shape
    half = width // 2
    third = half // 3
    spec = pl.BlockSpec((1, width, half + third), lambda j: (j, 0, 0))
    shape = jax.ShapeDtypeStruct((3, width, half + third), BF16)
    out_spec = pl.BlockSpec((width, third), lambda j: (0, j))
    return call(
        qkv_weights_kernel,
        (3,),
        [whole(tokens, width), whole(*pick.shape), whole(*table.shape)] + row_specs(width) + [out_spec, out_spec],
        (spec, spec),
        (shape, shape),
        [
            pltpu.VMEM((tokens, width), BF16),
            pltpu.VMEM((width, tokens), BF16),
            pltpu.VMEM((tokens, width), BF16),
        ],
        flops=2 * tokens * width * 6 * half,
        moved=16 * half * width + 12 * tokens * width,
    )(x, pick, table, full, half_rows, recv, out_own, out_par)


def qkv_back_kernel(
    tp_ref, x_ref, oh_ref, tab_ref, full_ref, half_ref, recv_ref, wo_ref, wp_ref, gmid_ref, lifted_ref, oht_ref,
    gino_ref, ginp_ref, sumo_ref, sump_ref, hats, stds, rows_in, acc, sums,
):
    step = pl.program_id(0)
    tokens, width = x_ref.shape
    half = wo_ref.shape[1]
    blocks = tokens // HALF

    @pl.when(step == 0)
    def _():
        def body(i):
            rows = pl.ds(pl.multiple_of(i * HALF, HALF), HALF)
            hat, inv_std = norm_parts(x_ref[rows, :])
            hats[rows, :] = hat
            stds[rows, :] = inv_std
            acc[rows, :] = jnp.zeros((HALF, width), F32)

        block_loop(blocks, body)

    joined_rows(full_ref, half_ref, recv_ref, step, rows_in)

    def body(i):
        rows = pl.ds(pl.multiple_of(i * HALF, HALF), HALF)
        grad = rows_in[rows, :]
        acc[rows, :] += mm_nt(grad[:, :half], wo_ref[...]) + mm_nt(grad[:, half:], wp_ref[...])

    block_loop(blocks, body)

    @pl.when(step == pl.num_programs(0) - 1)
    def _():
        first_core = tp_ref[0] == 0
        sums[...] = jnp.zeros(sums.shape, F32)

        def body(i):
            rows = pl.ds(pl.multiple_of(i * HALF, HALF), HALF)
            turn = oht_ref[i]
            gn = acc[rows, :]
            hat = hats[rows, :]
            sums[0] += mm(turn, (gn * hat).astype(BF16))
            sums[1] += mm(turn, gn.astype(BF16))
            scale = mm(oh_ref[rows, :], tab_ref[:, :width])
            grad = gmid_ref[rows, :] + norm_back(gn * scale, hat, stds[rows, :])
            low, high = grad[:, : width // 2], grad[:, width // 2 :]
            gino_ref[rows, :] = jnp.where(first_core, low, high)
            ginp_ref[rows, :] = jnp.where(first_core, high, low)
            lifted_t = lifted_ref[rows, :].astype(BF16).T
            sums[2] += mm(lifted_t[:16, :], grad.astype(BF16))

        block_loop(blocks, body)
        low, high = sums[:, :, : width // 2], sums[:, :, width // 2 :]
        sumo_ref[...] = jnp.where(first_core, low, high)
        sump_ref[...] = jnp.where(first_core, high, low)


def qkv_back(tp, x, pick, table, full, half_rows, recv, wo, wp, gmid, lifted, pick_t):
    tokens, width = x.shape
    half = wo.shape[1] // 3
    return call(
        qkv_back_kernel,
        (3,),
        [whole(tokens, width), whole(*pick.shape), whole(*table.shape)]
        + row_specs(width)
        + [
            pl.BlockSpec((width, half), lambda j, *_: (0, j)),
            pl.BlockSpec((width, half), lambda j, *_: (0, j)),
            whole(tokens, width),
            whole(tokens, LANES),
            whole(*pick_t.shape),
        ],
        (
            whole(tokens, width // 2),
            whole(tokens, width // 2),
            whole(3, 16, width // 2),
            whole(3, 16, width // 2),
        ),
        (
            jax.ShapeDtypeStruct((tokens, width // 2), F32),
            jax.ShapeDtypeStruct((tokens, width // 2), F32),
            jax.ShapeDtypeStruct((3, 16, width // 2), F32),
            jax.ShapeDtypeStruct((3, 16, width // 2), F32),
        ),
        [
            pltpu.VMEM((tokens, width), F32),
            pltpu.VMEM((tokens, 1), F32),
            pltpu.VMEM((tokens, width), BF16),
            pltpu.VMEM((tokens, width), F32),
            pltpu.VMEM((3, 16, width), F32),
        ],
        prefetch=1,
        flops=2 * tokens * width * 6 * half,
        moved=12 * half * width + 16 * tokens * width,
    )(tp, x, pick, table, full, half_rows, recv, wo, wp, gmid, lifted, pick_t)


def chain_joins(first_core):
    row = lax.broadcasted_iota(jnp.int32, (16, 16), 0)
    col = lax.broadcasted_iota(jnp.int32, (16, 16), 1)
    lower = ((row == col) & (row < 2 * SEGS)).astype(F32)
    upper = (
        ((row == col) & (row >= SEGS) & (row < 2 * SEGS)) | ((row == col + 2 * SEGS) & (row < 3 * SEGS))
    ).astype(F32)
    return jnp.where(first_core, lower, upper), jnp.where(first_core, upper, lower)


def join_chains(tp_ref, own_ref, came_ref, slope_ref, count, o_ref):
    own_join, came_join = chain_joins(tp_ref[0] == 0)
    cols = own_ref.shape[2]
    for i in range(count):
        both = jnp.dot(own_join, own_ref[i], precision=HIGHEST, preferred_element_type=F32)
        both = both + jnp.dot(came_join, came_ref[i], precision=HIGHEST, preferred_element_type=F32)
        lanes = pl.ds(i * cols, cols)
        o_ref[0:16, lanes] = (both * slope_ref[:, lanes]).astype(BF16)


def early_kernel(tp_ref, own_ref, came_ref, slope_ref, embed_ref, o_ref):
    join_chains(tp_ref, own_ref, came_ref, slope_ref, 4, o_ref)
    o_ref[:, pl.ds(4 * own_ref.shape[2], embed_ref.shape[1])] = embed_ref[...]


def late_kernel(tp_ref, own_ref, came_ref, slope_ref, bins_ref, o_ref):
    cols = own_ref.shape[2]
    join_chains(tp_ref, own_ref, came_ref, slope_ref, 2, o_ref)
    o_ref[16:32, :cols] = (own_ref[2] + came_ref[2]).astype(BF16)
    o_ref[16:32, cols:] = jnp.concatenate(
        [bins_ref[...].astype(BF16), jnp.zeros((16, cols - LANES), BF16)], axis=1
    )


def pack_rows(kernel, tp, own, came, slopes, extra, shape):
    return call(
        kernel,
        (1,),
        [whole(*own.shape), whole(*came.shape), whole(*slopes.shape), whole(*extra.shape)],
        whole(*shape),
        jax.ShapeDtypeStruct(shape, BF16),
        prefetch=1,
        flops=10**6,
        moved=10**5,
    )(tp, own, came, slopes, extra)


def closing_kernel(early_ref, late_ref, hat_ref, inv_ref, gain_ref, both_ref, *refs):
    ffn, attn, outs = refs[:2], refs[2:4], refs[4:]
    gu_ref, down_ref, qkv_ref, out_ref = outs[:4]
    w0_ref, b0_ref, w1_ref, w2_ref, b2_ref, w3_ref, b3_ref, w4_ref, w5_ref, b5_ref = outs[4:14]
    table_ref, pgain_ref, proj_ref, coord_ref = outs[14:]

    def total(pair, block):
        return pair[0][0, block].astype(F32) + pair[1][0, block].astype(F32)

    lanes = ffn[0].shape[3]
    chunks = down_ref.shape[1] // lanes
    for block in range(chunks):
        span = pl.ds(block * lanes, lanes)
        gu_ref[:, 0, span] = total(ffn, block)
        gu_ref[:, 1, span] = total(ffn, chunks + block)
        down_ref[:, span] = total(ffn, 2 * chunks + block)
    third = out_ref.shape[1] // 3
    for i in range(3):
        value = total(attn, i)
        qkv_ref[:, i, :] = value[:, : 3 * third]
        out_ref[:, i * third : (i + 1) * third] = value[:, 3 * third :]

    devices, _, wide = late_ref.shape
    cols = wide // 2
    embed_t = early_ref[:, 4 * cols :].T
    late = late_ref[:, 0:16, :].reshape(devices * 16, wide)
    parts = [late[:, :cols], late[:, cols:]] + [early_ref[:, i * cols : (i + 1) * cols] for i in range(4)]
    weights = [w0_ref, w1_ref, w5_ref, w3_ref, w4_ref, w2_ref]
    biases = [b0_ref, None, b5_ref, b3_ref, None, b2_ref]
    for part, weight, bias in zip(parts, weights, biases):
        weight[...] = mm(embed_t, part)
        if bias is not None:
            bias[...] = jnp.sum(part.astype(F32), axis=0)
    extra = jnp.sum(late_ref[:, 16:32, :].astype(F32), axis=0)
    coord_ref[...] = extra[: coord_ref.shape[0], :cols]
    bins = extra[:, cols : cols + LANES]
    hat = hat_ref[...]
    gain = gain_ref[...]
    proj = jnp.dot((hat * gain).T, bins.T, precision=HIGHEST, preferred_element_type=F32)
    proj_ref[...] = proj[:, : proj_ref.shape[1]]
    normed_grad = jnp.dot(bins.T, both_ref[...], precision=HIGHEST, preferred_element_type=F32)
    pgain_ref[...] = jnp.sum(normed_grad * hat, axis=0)
    table_ref[...] = norm_back(normed_grad * gain, hat, inv_ref[...])[: table_ref.shape[0]]


def closing(early, late, hat, inv_std, gain, both, ffn, attn, bins, heads):
    devices, _, wide = late.shape
    cols = wide // 2
    embed = early.shape[1] - 4 * cols
    features = hat.shape[1]
    height, lanes = ffn[0].shape[2:]
    weight, bias = (embed, cols), (cols,)
    hidden = lanes * (ffn[0].shape[1] // 3)
    shapes = [(height, 2, hidden), (height, hidden), (height, 3, cols), (height, cols)]
    shapes += [weight, bias, weight, weight, bias, weight, bias, weight, weight, bias]
    shapes += [(bins, features), (features,), (features, heads), (3, cols)]
    args = (early, late, hat, inv_std, gain, both, *ffn, *attn)
    return call(
        closing_kernel,
        (1,),
        [whole(*a.shape) for a in args],
        tuple(whole(*shape) for shape in shapes),
        tuple(jax.ShapeDtypeStruct(shape, F32) for shape in shapes),
        flops=10**8,
        moved=10**7,
    )(*args)


def halve_kernel(place_ref, *refs, plan, count):
    inputs, outs = refs[:count], refs[count:]
    for stream, (bit, sections) in enumerate(plan):
        sent_ref, kept_ref = outs[2 * stream], outs[2 * stream + 1]
        mine = (place_ref[0] >> bit) & 1
        done = 0
        for first, second, base, chunks, left in sections:
            spot = left.index(bit)
            shift = len(left) - 1
            half = 1 << shift

            def body(n, first=first, second=second, base=base, spot=spot, shift=shift, done=done, mine=mine):
                k = n & ((1 << shift) - 1)
                at = base + ((n >> shift) << (shift + 1)) + ((k >> spot) << (spot + 1)) + (k & ((1 << spot) - 1))
                for which, ref in ((1 - mine, sent_ref), (mine, kept_ref)):
                    block = at + (which << spot)
                    both = inputs[first][0, block].astype(F32) + inputs[second][0, block].astype(F32)
                    ref[0, done + n] = both.astype(BF16)

            block_loop(chunks * half, body)
            done += chunks * half


def halve(place, streams, bits):
    arrays, specs, plan, shapes = [], [], [], []

    def operand(array, index):
        for i, (seen, at) in enumerate(arrays):
            if seen is array and at == index:
                return i
        arrays.append((array, index))
        specs.append(pl.BlockSpec((1,) + array.shape[1:], lambda *_: (index, 0, 0, 0)))
        return len(arrays) - 1

    moved = 0
    for sections, bit in zip(streams, bits):
        entries, blocks = [], 0
        for own, i, came, k, base, chunks, left in sections:
            entries.append((operand(own, i), operand(came, k), base, chunks, left))
            blocks += chunks << (len(left) - 1)
        plan.append((bit, entries))
        shape = (1, blocks) + sections[0][0].shape[2:]
        shapes += [shape, shape]
        moved += 12 * blocks * shape[2] * shape[3]
    outs = call(
        functools.partial(halve_kernel, plan=plan, count=len(arrays)),
        (1,),
        specs,
        tuple(whole(*shape) for shape in shapes),
        tuple(jax.ShapeDtypeStruct(shape, BF16) for shape in shapes),
        prefetch=1,
        flops=10**6,
        moved=moved,
    )(place, *[array for array, _ in arrays])
    return list(outs[0::2]), list(outs[1::2])


def swap(values):
    return lax.ppermute(values, "tp", [(0, 1), (1, 0)])


def after(values, *others):
    return lax.optimization_barrier((values, *others))[0]


class Cube:
    def __init__(self, rows):
        self.bits = rows.bit_length() - 1
        assert rows == 1 << self.bits
        self.place = lax.axis_index("rows").reshape(1).astype(jnp.int32)
        self.perms = [[(i, i ^ (1 << b)) for i in range(rows)] for b in range(self.bits)]

    def turns(self):
        return [[(i + r) % 3 for i in range(3)] for r in range(3)]

    def gather(self, values, bit):
        came = lax.ppermute(values, "rows", self.perms[bit])
        return lax.optimization_barrier(jnp.concatenate([values, came], axis=0))


def next_sections(sections, kept, came, bit):
    made, base = [], 0
    for _, _, _, _, _, chunks, left in sections:
        left = [b for b in left if b != bit]
        made.append((kept, 0, came, 0, base, chunks, left))
        base += chunks << len(left)
    return made


def normalize(values):
    centre = jnp.mean(values, axis=-1, keepdims=True)
    shifted = values - centre
    spread = jnp.mean(shifted * shifted, axis=-1, keepdims=True)
    inv_std = lax.rsqrt(spread + EPSILON)
    return shifted * inv_std, inv_std


def three_parts(values):
    high = lax.reduce_precision(values, 8, 7)
    middle = lax.reduce_precision(values - high, 8, 7)
    low = values - high - middle
    return jnp.concatenate([high, middle, low], axis=0).astype(BF16)


def bias_base(heads):
    bins = heads.shape[1]
    low = lambda n: jnp.broadcast_to(heads[:, :1], (heads.shape[0], n))
    top = lambda n: jnp.broadcast_to(heads[:, bins - 1 :], (heads.shape[0], n))
    fill = HALF - RADIUS
    behind = jnp.concatenate([low(fill), heads[:, :RADIUS], low(HALF)], axis=1)
    same = jnp.concatenate([heads[:, RADIUS:], top(fill - 1), low(fill), heads[:, :RADIUS]], axis=1)
    ahead = jnp.concatenate([top(HALF), heads[:, RADIUS:], top(fill - 1)], axis=1)
    return jnp.stack([behind, same, ahead], axis=1)


def bins_of_diagonals():
    places = jnp.arange(ROW, dtype=jnp.int32)[None, :] - (HALF - 1)
    offsets = places + HALF * jnp.arange(-1, 2, dtype=jnp.int32)[:, None]
    bins = jnp.clip(offsets, -RADIUS, RADIUS) + RADIUS
    every = jnp.arange(2 * RADIUS + 1, dtype=jnp.int32)
    return (bins.reshape(-1)[:, None] == every[None, :]).astype(F32)


def per_device(
    layer_input,
    cotangent,
    chain_lengths,
    self_condition_flag,
    time_embedding,
    query_key_value,
    output_projection,
    attention_scale_weight,
    attention_scale_bias,
    attention_shift_weight,
    attention_gate_weight,
    attention_gate_bias,
    transition_scale_weight,
    transition_scale_bias,
    transition_shift_weight,
    transition_gate_weight,
    transition_gate_bias,
    gate_up_projection,
    down_projection,
    pair_table,
    pair_gain,
    pair_projection,
    coordinate_head,
    coordinate_embedding,
    rows,
):
    core = lax.axis_index("tp")
    other = 1 - core
    first_core = core == 0
    tp = core.reshape(1).astype(jnp.int32)
    cols = layer_input.shape[1]
    width = query_key_value.shape[0]
    heads_here = pair_projection.shape[1]
    bins = pair_table.shape[0]
    cube = Cube(rows)

    def side_by_side(own, came, axis):
        return jnp.where(
            first_core, jnp.concatenate([own, came], axis), jnp.concatenate([came, own], axis)
        )

    def tokens_of(values, which):
        return jnp.concatenate(
            [
                lax.dynamic_slice_in_dim(values, which * 2 * ROW, ROW, 0),
                lax.dynamic_slice_in_dim(values, ROW + which * HALF, HALF, 0),
            ],
            axis=0,
        )

    def gather_tokens(values):
        return side_by_side(tokens_of(values, core), swap(tokens_of(values, other)), 1)

    def scatter_tokens(own, sent):
        came = swap(sent)
        lower = jnp.concatenate([own[:ROW], own[ROW:], came[ROW:], came[:ROW]], axis=0)
        upper = jnp.concatenate([came[:ROW], came[ROW:], own[ROW:], own[:ROW]], axis=0)
        return jnp.where(first_core, lower, upper)

    x = gather_tokens(layer_input)
    qkv_own = query_key_value.reshape(width, -1)
    qkv_par = swap(qkv_own)

    packs = chain_lengths.shape[0]
    ends = jnp.cumsum(chain_lengths, axis=1)
    places = jnp.arange(ROW, dtype=jnp.int32)
    segment = jnp.sum((places[None, :, None] >= ends[:, None, :]).astype(jnp.int32), axis=2)
    embed = jnp.concatenate(
        [time_embedding, jnp.zeros((packs, 1, time_embedding.shape[2]), BF16)], axis=1
    )
    embed_rows = embed.reshape(packs * SEGS, -1)
    mod_weights = jnp.stack(
        [
            attention_scale_weight,
            attention_shift_weight,
            attention_gate_weight,
            transition_scale_weight,
            transition_shift_weight,
            transition_gate_weight,
        ],
        axis=1,
    ).reshape(-1, 6 * cols)
    mods = jnp.dot(embed_rows, mod_weights, preferred_element_type=F32).reshape(-1, 6, cols)
    mods = jnp.stack(
        [
            jax.nn.sigmoid(mods[:, 0] + attention_scale_bias.astype(F32)),
            mods[:, 1],
            jax.nn.sigmoid(mods[:, 2] + attention_gate_bias.astype(F32)),
            jax.nn.sigmoid(mods[:, 3] + transition_scale_bias.astype(F32)),
            mods[:, 4],
            jax.nn.sigmoid(mods[:, 5] + transition_gate_bias.astype(F32)),
        ],
        axis=1,
    )
    mods_full = side_by_side(mods, swap(mods), 2)
    mods_here = jnp.concatenate(
        [
            lax.dynamic_slice_in_dim(mods_full, 2 * SEGS * core, SEGS, 0),
            mods_full[SEGS : 2 * SEGS],
        ],
        axis=0,
    )
    table = three_parts(mods_here.reshape(2 * SEGS, 6 * width))
    table = jnp.concatenate([table, jnp.zeros((2, 6 * width), BF16)], axis=0)

    seg_full = lax.dynamic_slice_in_dim(segment, 2 * core, 1, 0)[0]
    seg_half = lax.dynamic_slice_in_dim(segment[1], HALF * core, HALF, 0)
    seg_far = lax.dynamic_slice_in_dim(segment[1], HALF * other, HALF, 0)
    seg_q = jnp.concatenate([seg_full, seg_half])
    seg_k = jnp.concatenate([seg_full, seg_half, seg_far])
    lanes = jnp.arange(LANES, dtype=jnp.int32)
    mask_k = (seg_k[:, None] == lanes[None, :]).astype(BF16)
    mask_q = jnp.where(
        (seg_q[:, None] != lanes[None, :]) & (lanes[None, :] < SEGS), MASKED, 0.0
    ).astype(BF16)
    row_of = jnp.concatenate([seg_full, seg_half + SEGS])
    spots = jnp.arange(32, dtype=jnp.int32)
    pick = (
        (row_of[:, None] == lax.rem(spots, 2 * SEGS)[None, :]) & (spots[None, :] < 6 * SEGS)
    ).astype(BF16)
    pick_t = (row_of.reshape(-1, 1, HALF) == jnp.arange(16, dtype=jnp.int32)[None, :, None]).astype(BF16)
    flag_full = lax.dynamic_slice_in_dim(self_condition_flag, 2 * core, 1, 0)
    flags = jnp.concatenate(
        [jnp.broadcast_to(flag_full, (ROW,)), jnp.broadcast_to(self_condition_flag[1:2], (HALF,))]
    ).astype(F32)[:, None]

    pair_hat, pair_inv = normalize(pair_table.astype(F32))
    gain = pair_gain.astype(F32)
    pair_normed = pair_hat * gain
    pair_both = jnp.concatenate([pair_projection, swap(pair_projection)], axis=1).astype(F32)
    bias_heads = jnp.transpose(jnp.dot(pair_normed, pair_both, precision=HIGHEST))
    bias_source = jnp.transpose(pair_both)
    bias = bias_tiles(bias_base(bias_heads))

    out_own = output_projection
    out_par = swap(output_projection)
    gu_own = jnp.transpose(gate_up_projection, (1, 0, 2))
    gu_par = swap(gu_own)
    down_own = down_projection
    down_par = swap(down_projection)
    coord = jnp.concatenate([coordinate_head, coordinate_embedding], axis=0)
    coord = side_by_side(coord, swap(coord), 1)
    fill = jnp.zeros((LANES - 3, width), BF16)
    head = jnp.concatenate([coord[:3], fill], axis=0)
    emb = jnp.concatenate([coord[3:], fill], axis=0)
    cot = gather_tokens(cotangent)

    def attention(values):
        qkv = qkv_forward(values, pick, table, qkv_own, qkv_par)
        kv_par = swap(qkv[ROW:, width:])
        attended, logs = attend_forward(tp, qkv, kv_par, mask_q, mask_k, bias)
        return qkv, kv_par, attended, logs

    _, _, attended, _ = attention(x)
    shifted, lifted = ffn_forward(
        attended, out_own, out_par, x, pick, table, gu_own, gu_par, down_own, down_par, head, emb, flags
    )
    qkv, kv_par, attended, logs = attention(shifted)
    (
        result_own,
        result_sent,
        grad_middle,
        grad_attended,
        grads_own,
        grads_sent,
        grad_out_own,
        grad_out_sent,
        early_own,
        early_sent,
    ) = ffn_turn(
        tp, attended, out_own, out_par, shifted, pick, table, gu_own, gu_par, down_own, down_par, cot, pick_t
    )

    slopes = mods * (1.0 - mods)
    ones = jnp.ones_like(slopes[:, 0])
    row_fill = lambda values: jnp.pad(values, ((0, 16 - values.shape[0]), (0, 0)))
    early_slopes = row_fill(jnp.concatenate([slopes[:, 5], slopes[:, 3], ones, slopes[:, 2]], axis=1))
    late_slopes = row_fill(jnp.concatenate([slopes[:, 0], ones], axis=1))
    embed_fill = row_fill(embed_rows)
    early = pack_rows(
        early_kernel, tp, early_own, swap(early_sent), early_slopes, embed_fill,
        (16, 4 * cols + embed_rows.shape[1]),
    )

    came_ffn = swap(grads_sent)
    mask_half = after(mask_q, early)
    half_grads, far_grads, diag_half = attend_half_back(
        tp, qkv, kv_par, grad_attended, logs, mask_half, mask_k, bias
    )
    came_grads = swap(far_grads)

    turns = cube.turns()
    every = list(range(cube.bits))
    height = width // rows
    slots = lambda values: values.reshape(3, -1, height, values.shape[-1])
    chunks = grads_own.shape[1]
    own_slots, came_slots = slots(grads_own), slots(came_ffn)
    ffn = [[(own_slots, i, came_slots, i, 0, chunks, every)] for i in range(3)]

    def one_round(streams, bits, *others):
        sent, kept = halve(cube.place, streams, bits)
        held = lax.optimization_barrier((*sent, *others))
        came = [lax.ppermute(v, "rows", cube.perms[bit]) for v, bit in zip(held, bits)]
        made = [next_sections(*parts) for parts in zip(streams, kept, came, bits)]
        return made, came, held[len(sent) :]

    early = cube.gather(early, 0)
    ffn, came, (mask_full, early, _) = one_round(ffn, turns[0], mask_half, early, diag_half)
    full_grads, diag_full = attend_full_back(qkv, grad_attended, logs, mask_full, mask_k, bias)
    early = cube.gather(early, 1)
    ffn, came, (pick_weights, early, _) = one_round(ffn, turns[1], pick, early, diag_full)
    gqkv_own, gqkv_sent = qkv_weights(
        shifted, pick_weights, table, full_grads, half_grads, came_grads, grad_out_own, grad_out_sent
    )
    early = cube.gather(early, 2)
    gqkv_sent, early, *_ = lax.optimization_barrier((gqkv_sent, early, *came))
    own_slots, came_slots = slots(gqkv_own), slots(swap(gqkv_sent))
    streams = [ffn[i] + [(own_slots, i, came_slots, i, 0, 1, every)] for i in range(3)]
    streams, came, (pick_back, early) = one_round(streams, turns[2], pick_weights, early)
    gin_own, gin_sent, late_own, late_sent = qkv_back(
        tp, shifted, pick_back, table, full_grads, half_grads, came_grads, qkv_own, qkv_par, grad_middle, lifted, pick_t
    )
    for step in range(3, cube.bits):
        early = cube.gather(early, step)
    late_sent, early, *_ = lax.optimization_barrier((late_sent, early, *came))

    diag_half = diag_half[:, :4].reshape(-1, 2, ROW)
    quiet = jnp.zeros_like(diag_half[:, 0])
    diag_far = diag_half[:, 1]
    diag = diag_full[:, :6].reshape(-1, 3, ROW) + jnp.stack(
        [
            jnp.where(first_core, diag_far, quiet),
            diag_half[:, 0],
            jnp.where(first_core, quiet, diag_far),
        ],
        axis=1,
    )
    grad_bins = jnp.dot(diag.reshape(-1, 3 * ROW), bins_of_diagonals(), precision=HIGHEST)
    came_bins = swap(grad_bins)
    grad_bins = grad_bins + jnp.concatenate([came_bins[heads_here:], came_bins[:heads_here]], axis=0)
    bins_fill = jnp.pad(grad_bins, ((0, 16 - 2 * heads_here), (0, LANES - bins)))

    late_came = swap(late_sent)
    late = pack_rows(late_kernel, tp, late_own, late_came, late_slopes, bins_fill, (32, 2 * cols))
    ffn = [[stream[0] for stream in streams]]
    attn = [stream[1:] for stream in streams]
    rest = list(range(3, cube.bits))
    waited = []
    for step in range(max(len(rest), 2)):
        now, bits = [], []
        if step < len(rest):
            now, bits = ffn, rest[step : step + 1]
        count = len(now)
        if step < 2:
            now, bits = now + attn, bits + turns[step]
        now, came, (late, *_) = one_round(now, bits, late, *waited)
        waited = came[:count]
        if count:
            ffn = now[:count]
        if step < 2:
            attn = now[count:]
        late = cube.gather(late, step)
    done = max(len(rest), 2)
    attn = [[section for stream in attn for section in stream]]
    for bit in rest:
        attn, came, (late,) = one_round(attn, [bit], late)
        if done < cube.bits:
            late = cube.gather(late, done)
            done += 1
    for step in range(done, cube.bits):
        late = cube.gather(late, step)
    ffn_last = (ffn[0][0][0], ffn[0][0][2])
    attn_last = (attn[0][0][0], attn[0][0][2])

    layer_output = scatter_tokens(result_own, result_sent)
    input_gradient = scatter_tokens(gin_own, gin_sent)

    bins_pad = ((0, LANES - bins), (0, 0))
    grad_gu, grad_down, grad_qkv, grad_out, *conditioning = closing(
        early,
        late.reshape(rows, 32, 2 * cols),
        jnp.pad(pair_hat, bins_pad),
        jnp.pad(pair_inv, bins_pad),
        gain[None, :],
        jnp.pad(bias_source, ((0, 16 - 2 * heads_here), (0, 0))),
        ffn_last,
        attn_last,
        bins,
        heads_here,
    )
    *conditioning, grad_table, grad_gain, grad_pair, coord_grad = conditioning
    return (
        layer_output,
        input_gradient,
        grad_qkv,
        grad_out.T,
        *conditioning,
        grad_gu,
        grad_down.T,
        grad_table,
        grad_gain,
        grad_pair,
        coord_grad,
    )


def solution(mesh):
    in_specs = (
        P("rows", "tp"),
        P("rows", "tp"),
        P("rows", None),
        P("rows"),
        P("rows", None, None),
        P(None, None, "tp"),
        P("tp", None),
        P(None, "tp"),
        P("tp"),
        P(None, "tp"),
        P(None, "tp"),
        P("tp"),
        P(None, "tp"),
        P("tp"),
        P(None, "tp"),
        P(None, "tp"),
        P("tp"),
        P(None, None, "tp"),
        P("tp", None),
        P(),
        P(),
        P(None, "tp"),
        P(None, "tp"),
        P(None, "tp"),
    )
    out_specs = (
        P("rows", "tp"),
        P("rows", "tp"),
        P("rows", None, "tp"),
        P("tp", "rows"),
        P(None, "tp"),
        P("tp"),
        P(None, "tp"),
        P(None, "tp"),
        P("tp"),
        P(None, "tp"),
        P("tp"),
        P(None, "tp"),
        P(None, "tp"),
        P("tp"),
        P("rows", None, "tp"),
        P("tp", "rows"),
        P(),
        P(),
        P(None, "tp"),
        P(None, "tp"),
    )
    return jax.shard_map(
        functools.partial(per_device, rows=mesh.shape["rows"]),
        mesh=mesh,
        in_specs=in_specs,
        out_specs=out_specs,
        check_vma=False,
    )
```

```python
import functools
import jax
import jax.numpy as jnp
from jax import lax
from jax.experimental import pallas as pl
from jax.experimental.pallas import tpu as pltpu
from jax.sharding import PartitionSpec as P

RADIUS = 32
ROW = 512
HALF = ROW // 2
SEGS = 5
EPSILON = 1e-05
MASKED = -1e30
HIGHEST = lax.Precision.HIGHEST
F32 = jnp.float32
BF16 = jnp.bfloat16
LANES = 128
FFC = 512
NT = (((1,), (1,)), ((), ()))
VMEM_LIMIT = 60 * 1024 * 1024


def mm(left, right):
    return jnp.dot(left, right, preferred_element_type=F32)


def mm_nt(left, right):
    return lax.dot_general(left, right, NT, preferred_element_type=F32)


def norm_parts(values):
    centre = jnp.mean(values, axis=1, keepdims=True)
    shifted = values - centre
    spread = jnp.mean(shifted * shifted, axis=1, keepdims=True)
    inv_std = lax.rsqrt(spread + EPSILON)
    return shifted * inv_std, inv_std


def norm_back(grad, hat, inv_std):
    first = jnp.mean(grad, axis=1, keepdims=True)
    second = jnp.mean(grad * hat, axis=1, keepdims=True)
    return inv_std * (grad - first - hat * second)


def block_loop(count, body):
    lax.fori_loop(0, count, lambda i, c: (body(i), c)[1], 0)


def call(kernel, grid, in_specs, out_specs, out_shape, scratch=(), prefetch=0, aliases=None, flops=0, moved=0):
    return pl.pallas_call(
        kernel,
        grid_spec=pltpu.PrefetchScalarGridSpec(
            num_scalar_prefetch=prefetch,
            grid=grid,
            in_specs=in_specs,
            out_specs=out_specs,
            scratch_shapes=list(scratch),
        ),
        out_shape=out_shape,
        input_output_aliases=aliases or {},
        compiler_params=pltpu.CompilerParams(
            dimension_semantics=("arbitrary",) * len(grid), vmem_limit_bytes=VMEM_LIMIT
        ),
        cost_estimate=pl.CostEstimate(flops=flops, transcendentals=0, bytes_accessed=moved),
    )


def whole(*shape):
    zeros = (0,) * len(shape)
    return pl.BlockSpec(shape, lambda *_: zeros)


def bias_kernel(base_ref, near_ref, far_ref):
    for d, height, start, out in (
        (1, HALF, 0, near_ref.at[0]),
        (0, RADIUS, 0, far_ref.at[0, 0]),
        (2, RADIUS, HALF - RADIUS, far_ref.at[0, 1]),
    ):
        rows = jnp.broadcast_to(base_ref[0, d : d + 1, :], (height, 2 * HALF))
        rolled = pltpu.roll(rows, start, axis=1, stride=1, stride_axis=0)
        out[...] = rolled[:, :HALF]


def bias_tiles(base):
    heads = base.shape[0]
    near, far = (heads, HALF, HALF), (heads, 2, RADIUS, HALF)
    return call(
        bias_kernel,
        (heads,),
        [pl.BlockSpec((1, 3, 2 * HALF), lambda h: (h, 0, 0))],
        (
            pl.BlockSpec((1,) + near[1:], lambda h: (h, 0, 0)),
            pl.BlockSpec((1,) + far[1:], lambda h: (h, 0, 0, 0)),
        ),
        (jax.ShapeDtypeStruct(near, F32), jax.ShapeDtypeStruct(far, F32)),
        moved=heads * HALF * HALF * 4,
        flops=10**7,
    )(base)


def bias_specs():
    return [
        pl.BlockSpec((2, HALF, HALF), lambda p, *_: (p, 0, 0)),
        pl.BlockSpec((2, 2, RADIUS, HALF), lambda p, *_: (p, 0, 0, 0)),
    ]


def add_near(near_ref, far_ref, h, scores):
    return scores + near_ref[h]


def add_later(near_ref, far_ref, h, scores):
    edge = far_ref[h, 0]
    return jnp.concatenate([scores[:RADIUS] + edge, scores[RADIUS:] + edge[RADIUS - 1 :, :1]], axis=0)


def add_earlier(near_ref, far_ref, h, scores):
    edge = far_ref[h, 1]
    return jnp.concatenate(
        [scores[: HALF - RADIUS] + edge[:1, HALF - 1 :], scores[HALF - RADIUS :] + edge], axis=0
    )


def add_either(first, near_ref, far_ref, h, scores):
    later, earlier = far_ref[h, 0], far_ref[h, 1]
    rest = jnp.where(first, later[RADIUS - 1 :, :1], earlier[:1, HALF - 1 :])
    return jnp.concatenate(
        [
            scores[:RADIUS] + jnp.where(first, later, rest),
            scores[RADIUS : HALF - RADIUS] + rest,
            scores[HALF - RADIUS :] + jnp.where(first, rest, earlier),
        ],
        axis=0,
    )


def full_biases(near_ref, far_ref, qb):
    kinds = (add_near, add_later) if qb == 0 else (add_earlier, add_near)
    return [functools.partial(kind, near_ref, far_ref) for kind in kinds]


def half_biases(near_ref, far_ref, first):
    return [
        functools.partial(add_near, near_ref, far_ref),
        functools.partial(add_either, first, near_ref, far_ref),
    ]


def qkv_kernel(x_ref, oh_ref, tab_ref, own_ref, par_ref, o_ref, normed):
    width = x_ref.shape[1]
    half = own_ref.shape[1]

    @pl.when(pl.program_id(0) == 0)
    def _():
        def body(i):
            rows = pl.ds(pl.multiple_of(i * HALF, HALF), HALF)
            hat, _ = norm_parts(x_ref[rows, :].astype(F32))
            pick = oh_ref[rows, :]
            scale = mm(pick, tab_ref[:, :width])
            shift = mm(pick, tab_ref[:, width : 2 * width])
            normed[rows, :] = (hat * scale + shift).astype(BF16)

        block_loop(x_ref.shape[0] // HALF, body)

    o_ref[:, :half] = mm(normed[...], own_ref[...]).astype(BF16)
    o_ref[:, half:] = mm(normed[...], par_ref[...]).astype(BF16)


def qkv_forward(x, pick, table, w_own, w_par):
    tokens, width = x.shape
    half = w_own.shape[1] // 3
    return call(
        qkv_kernel,
        (3,),
        [
            whole(tokens, width),
            whole(*pick.shape),
            whole(*table.shape),
            pl.BlockSpec((width, half), lambda j: (0, j)),
            pl.BlockSpec((width, half), lambda j: (0, j)),
        ],
        pl.BlockSpec((tokens, 2 * half), lambda j: (0, j)),
        jax.ShapeDtypeStruct((tokens, 6 * half), BF16),
        [pltpu.VMEM((tokens, width), BF16)],
        flops=2 * tokens * width * 6 * half,
        moved=tokens * 6 * half * 2 + width * half * 12 + tokens * width * 4,
    )(x, pick, table, w_own, w_par)


def lane_masks():
    lanes = lax.broadcasted_iota(jnp.int32, (1, LANES), 1)
    first = (lanes < LANES // 2).astype(F32)
    return first.astype(BF16), (1.0 - first).astype(BF16)


def attend_forward_block(q, segq, keys, values_t, biases):
    outs, logs = [], []
    half = LANES // 2
    masks = lane_masks()
    scaled = q * jnp.asarray(half**-0.5, BF16)
    for h in range(2):
        query = jnp.concatenate([scaled * masks[h], segq], axis=1)
        scores = [bias(h, mm_nt(key, query)) for key, bias in zip(keys, biases)]
        tops = [jnp.max(s, axis=0, keepdims=True) for s in scores]
        top = functools.reduce(jnp.maximum, tops)
        weights = [jnp.exp(s - top) for s in scores]
        total = sum(jnp.sum(w, axis=0, keepdims=True) for w in weights)
        mixed = sum(
            mm(vt[h * half : (h + 1) * half, :], w.astype(BF16)) for vt, w in zip(values_t, weights)
        )
        outs.append(mixed / total)
        logs.append(top + jnp.log(total))
    attended = jnp.concatenate(outs, axis=0).T.astype(BF16)
    return attended, jnp.concatenate(logs, axis=0)


def attend_full_kernel(q_ref, k_ref, v_ref, segq_ref, segk_ref, near_ref, far_ref, o_ref, log_ref):
    keys = [
        jnp.concatenate([k_ref[pl.ds(b * HALF, HALF), :], segk_ref[pl.ds(b * HALF, HALF), :]], axis=1)
        for b in range(2)
    ]
    values_t = [v_ref[pl.ds(b * HALF, HALF), :].T for b in range(2)]
    for qb in range(2):
        rows = pl.ds(qb * HALF, HALF)
        biases = full_biases(near_ref, far_ref, qb)
        attended, logs = attend_forward_block(q_ref[rows, :], segq_ref[rows, :], keys, values_t, biases)
        o_ref[rows, :] = attended
        log_ref[0, 0:2, rows] = logs


def attend_half_kernel(
    tp_ref, q_ref, k_ref, v_ref, kp_ref, vp_ref, segq_ref, segk_ref, near_ref, far_ref, oin, login, o_ref, log_ref
):
    keys = [
        jnp.concatenate([k_ref[...], segk_ref[pl.ds(0, HALF), :]], axis=1),
        jnp.concatenate([kp_ref[...], segk_ref[pl.ds(HALF, HALF), :]], axis=1),
    ]
    values_t = [v_ref[...].T, vp_ref[...].T]
    biases = half_biases(near_ref, far_ref, tp_ref[0] == 0)
    attended, logs = attend_forward_block(q_ref[...], segq_ref[...], keys, values_t, biases)
    o_ref[...] = attended
    log_ref[0, 0:2, :] = logs


def attend_forward(tp, qkv, kv_par, segq, segk, bias):
    tokens = qkv.shape[0]
    width = qkv.shape[1] // 3
    pairs = width // LANES
    out_shape = (
        jax.ShapeDtypeStruct((tokens, width), BF16),
        jax.ShapeDtypeStruct((pairs, 8, tokens), F32),
    )
    unit = 4 * HALF * HALF * 256 * 2
    attended, logs = call(
        attend_full_kernel,
        (pairs,),
        [
            pl.BlockSpec((ROW, LANES), lambda p: (0, p)),
            pl.BlockSpec((ROW, LANES), lambda p: (0, pairs + p)),
            pl.BlockSpec((ROW, LANES), lambda p: (0, 2 * pairs + p)),
            pl.BlockSpec((ROW, LANES), lambda p: (0, 0)),
            pl.BlockSpec((ROW, LANES), lambda p: (0, 0)),
        ]
        + bias_specs(),
        (
            pl.BlockSpec((ROW, LANES), lambda p: (0, p)),
            pl.BlockSpec((1, 8, ROW), lambda p: (p, 0, 0)),
        ),
        out_shape,
        flops=unit * 4 * pairs,
        moved=bias[0].size * 4,
    )(qkv, qkv, qkv, segq, segk, *bias)
    flip = pairs // 2
    return call(
        attend_half_kernel,
        (pairs,),
        [
            pl.BlockSpec((HALF, LANES), lambda p, *_: (2, p)),
            pl.BlockSpec((HALF, LANES), lambda p, *_: (2, pairs + p)),
            pl.BlockSpec((HALF, LANES), lambda p, *_: (2, 2 * pairs + p)),
            pl.BlockSpec((HALF, LANES), lambda p, *_: (0, lax.rem(p + flip, pairs))),
            pl.BlockSpec((HALF, LANES), lambda p, *_: (0, pairs + lax.rem(p + flip, pairs))),
            pl.BlockSpec((HALF, LANES), lambda p, *_: (2, 0)),
            pl.BlockSpec((ROW, LANES), lambda p, *_: (1, 0)),
        ]
        + bias_specs()
        + [pl.BlockSpec(memory_space=pl.ANY), pl.BlockSpec(memory_space=pl.ANY)],
        (
            pl.BlockSpec((HALF, LANES), lambda p, *_: (2, p)),
            pl.BlockSpec((1, 8, HALF), lambda p, *_: (p, 0, 2)),
        ),
        out_shape,
        prefetch=1,
        aliases={10: 0, 11: 1},
        flops=unit * 2 * pairs,
        moved=bias[0].size * 4,
    )(tp, qkv, qkv, qkv, kv_par, kv_par, segq, segk, *bias, attended, logs)


def ffn_kernel(
    att_ref, woo_ref, wop_ref, x_ref, oh_ref, tab_ref, guo_ref, gup_ref, wdo_ref, wdp_ref,
    head_ref, emb_ref, flag_ref, shifted_ref, lifted_ref, middle, normed, acc,
):
    step = pl.program_id(0)
    tokens, width = x_ref.shape
    half = woo_ref.shape[0]
    blocks = tokens // HALF

    @pl.when(step == 0)
    def _():
        def body(i):
            rows = pl.ds(pl.multiple_of(i * HALF, HALF), HALF)
            branch = mm(att_ref[rows, :half], woo_ref[...]) + mm(att_ref[rows, half:], wop_ref[...])
            pick = oh_ref[rows, :]
            mid = x_ref[rows, :].astype(F32) + mm(pick, tab_ref[:, 2 * width : 3 * width]) * branch
            middle[rows, :] = mid
            hat, _ = norm_parts(mid)
            scale = mm(pick, tab_ref[:, 3 * width : 4 * width])
            shift = mm(pick, tab_ref[:, 4 * width : 5 * width])
            normed[rows, :] = (hat * scale + shift).astype(BF16)
            acc[rows, :] = jnp.zeros((HALF, width), F32)

        block_loop(blocks, body)

    def body(i):
        rows = pl.ds(pl.multiple_of(i * HALF, HALF), HALF)
        total = acc[rows, :]
        for gu, wd in ((guo_ref, wdo_ref), (gup_ref, wdp_ref)):
            gate = mm(normed[rows, :], gu[0])
            up = mm(normed[rows, :], gu[1])
            hidden = (gate * jax.nn.sigmoid(gate) * up).astype(BF16)
            total = total + mm(hidden, wd[...])
        acc[rows, :] = total

    block_loop(blocks, body)

    @pl.when(step == pl.num_programs(0) - 1)
    def _():
        def body(i):
            rows = pl.ds(pl.multiple_of(i * HALF, HALF), HALF)
            gate = mm(oh_ref[rows, :], tab_ref[:, 5 * width : 6 * width])
            first = middle[rows, :] + gate * acc[rows, :]
            high = first.astype(BF16)
            rest = (first - high.astype(F32)).astype(BF16)
            coords = mm_nt(high, head_ref[...]) + mm_nt(rest, head_ref[...])
            lifted = coords * flag_ref[rows, :]
            lifted_ref[rows, :] = lifted
            high = lifted.astype(BF16)
            rest = (lifted - high.astype(F32)).astype(BF16)
            moved = mm(high, emb_ref[...]) + mm(rest, emb_ref[...])
            shifted_ref[rows, :] = x_ref[rows, :].astype(F32) + moved

        block_loop(blocks, body)


def ffn_specs(att, woo, x, pick, table):
    tokens, width = x.shape
    chunk = FFC
    return [
        whole(*att.shape),
        whole(*woo.shape),
        whole(*woo.shape),
        whole(tokens, width),
        whole(*pick.shape),
        whole(*table.shape),
        pl.BlockSpec((2, width, chunk), lambda j, *_: (0, 0, j)),
        pl.BlockSpec((2, width, chunk), lambda j, *_: (0, 0, j)),
        pl.BlockSpec((chunk, width), lambda j, *_: (j, 0)),
        pl.BlockSpec((chunk, width), lambda j, *_: (j, 0)),
    ]


def ffn_forward(att, woo, wop, x, pick, table, guo, gup, wdo, wdp, head, emb, flags):
    tokens, width = x.shape
    hidden = wdo.shape[0]
    return call(
        ffn_kernel,
        (hidden // FFC,),
        ffn_specs(att, woo, x, pick, table)
        + [whole(*head.shape), whole(*emb.shape), whole(*flags.shape)],
        (whole(tokens, width), whole(tokens, LANES)),
        (
            jax.ShapeDtypeStruct((tokens, width), F32),
            jax.ShapeDtypeStruct((tokens, LANES), F32),
        ),
        [
            pltpu.VMEM((tokens, width), F32),
            pltpu.VMEM((tokens, width), BF16),
            pltpu.VMEM((tokens, width), F32),
        ],
        flops=2 * tokens * width * (6 * hidden + width),
        moved=12 * hidden * width + 6 * tokens * width,
    )(att, woo, wop, x, pick, table, guo, gup, wdo, wdp, head, emb, flags)


def turn_kernel(
    tp_ref, att_ref, woo_ref, wop_ref, x_ref, oh_ref, tab_ref, guo_ref, gup_ref, wdo_ref, wdp_ref,
    g_ref, oht_ref,
    outo_ref, outp_ref, gmid_ref, gatt_ref, go_ref, gp_ref, goo_ref, gop_ref, sumo_ref, sump_ref,
    sums_ref, middle, hats, branches, normed, normed_t, gmixed, gmixed_t, mixed, gnormed, hid, dgate, dup,
):
    step = pl.program_id(0)
    tokens, width = x_ref.shape
    half = woo_ref.shape[0]
    blocks = tokens // HALF

    @pl.when(step == 0)
    def _():
        def body(i):
            rows = pl.ds(pl.multiple_of(i * HALF, HALF), HALF)
            branch = mm(att_ref[rows, :half], woo_ref[...]) + mm(att_ref[rows, half:], wop_ref[...])
            branches[rows, :] = branch
            pick = oh_ref[rows, :]
            mid = x_ref[rows, :] + mm(pick, tab_ref[:, 2 * width : 3 * width]) * branch
            middle[rows, :] = mid
            hat, _ = norm_parts(mid)
            scale = mm(pick, tab_ref[:, 3 * width : 4 * width])
            shift = mm(pick, tab_ref[:, 4 * width : 5 * width])
            normed[rows, :] = (hat * scale + shift).astype(BF16)
            gate = mm(pick, tab_ref[:, 5 * width : 6 * width])
            gmixed[rows, :] = (g_ref[rows, :].astype(F32) * gate).astype(BF16)
            mixed[rows, :] = jnp.zeros((HALF, width), F32)
            gnormed[rows, :] = jnp.zeros((HALF, width), F32)

        block_loop(blocks, body)
        normed_t[...] = normed[...].T
        gmixed_t[...] = gmixed[...].T

    for gu, wd, out in ((gup_ref, wdp_ref, gp_ref), (guo_ref, wdo_ref, go_ref)):

        def body(i):
            rows = pl.ds(pl.multiple_of(i * HALF, HALF), HALF)
            gate = mm(normed[rows, :], gu[0])
            up = mm(normed[rows, :], gu[1])
            ghid = mm_nt(gmixed[rows, :], wd[...])
            s = jax.nn.sigmoid(gate)
            silu = gate * s
            hidden = (silu * up).astype(BF16)
            hid[rows, :] = hidden
            mixed[rows, :] += mm(hidden, wd[...])
            dg = (ghid * up * (s + silu * (1.0 - s))).astype(BF16)
            du = (ghid * silu).astype(BF16)
            dgate[rows, :] = dg
            dup[rows, :] = du
            gnormed[rows, :] += mm_nt(dg, gu[0]) + mm_nt(du, gu[1])

        block_loop(blocks, body)
        out[0, 0] = mm(normed_t[...], dgate[...]).astype(BF16)
        out[1, 0] = mm(normed_t[...], dup[...]).astype(BF16)
        out[2, 0] = mm(gmixed_t[...], hid[...]).astype(BF16)

    @pl.when(step == pl.num_programs(0) - 1)
    def _():
        first_core = tp_ref[0] == 0
        sums_ref[...] = jnp.zeros(sums_ref.shape, F32)

        def body(i):
            rows = pl.ds(pl.multiple_of(i * HALF, HALF), HALF)
            pick = oh_ref[rows, :]
            turn = oht_ref[i]
            g = g_ref[rows, :].astype(F32)
            total = mixed[rows, :]
            gate = mm(pick, tab_ref[:, 5 * width : 6 * width])
            mid = middle[rows, :]
            result = (mid + gate * total).astype(BF16)
            low, high = result[:, : width // 2], result[:, width // 2 :]
            outo_ref[rows, :] = jnp.where(first_core, low, high)
            outp_ref[rows, :] = jnp.where(first_core, high, low)
            sums_ref[0] += mm(turn, (g * total).astype(BF16))
            hat, inv_std = norm_parts(mid)
            gn = gnormed[rows, :]
            sums_ref[1] += mm(turn, (gn * hat).astype(BF16))
            sums_ref[2] += mm(turn, gn.astype(BF16))
            scale = mm(pick, tab_ref[:, 3 * width : 4 * width])
            gmid = g + norm_back(gn * scale, hat, inv_std)
            gmid_ref[rows, :] = gmid
            sums_ref[3] += mm(turn, (gmid * branches[rows, :]).astype(BF16))
            gbranch = (gmid * mm(pick, tab_ref[:, 2 * width : 3 * width])).astype(BF16)
            gmixed[rows, :] = gbranch
            gatt_ref[rows, :half] = mm_nt(gbranch, woo_ref[...]).astype(BF16)
            gatt_ref[rows, half:] = mm_nt(gbranch, wop_ref[...]).astype(BF16)

        block_loop(blocks, body)
        gmixed_t[...] = gmixed[...].T
        goo_ref[...] = mm(gmixed_t[...], att_ref[:, :half]).astype(BF16)
        gop_ref[...] = mm(gmixed_t[...], att_ref[:, half:]).astype(BF16)
        low, high = sums_ref[:, :, : width // 2], sums_ref[:, :, width // 2 :]
        sumo_ref[...] = jnp.where(first_core, low, high)
        sump_ref[...] = jnp.where(first_core, high, low)


def ffn_turn(tp, att, woo, wop, x, pick, table, guo, gup, wdo, wdp, g, pick_t):
    tokens, width = x.shape
    half = woo.shape[0]
    hidden = wdo.shape[0]
    grads = jax.ShapeDtypeStruct((3, hidden // FFC, width, FFC), BF16)
    grads_spec = pl.BlockSpec((3, 1, width, FFC), lambda j, *_: (0, j, 0, 0))
    return call(
        turn_kernel,
        (hidden // FFC,),
        ffn_specs(att, woo, x, pick, table) + [whole(tokens, width), whole(*pick_t.shape)],
        (
            whole(tokens, width // 2),
            whole(tokens, width // 2),
            whole(tokens, width),
            whole(tokens, width),
            grads_spec,
            grads_spec,
            whole(width, half),
            whole(width, half),
            whole(4, 16, width // 2),
            whole(4, 16, width // 2),
        ),
        (
            jax.ShapeDtypeStruct((tokens, width // 2), BF16),
            jax.ShapeDtypeStruct((tokens, width // 2), BF16),
            jax.ShapeDtypeStruct((tokens, width), F32),
            jax.ShapeDtypeStruct((tokens, width), BF16),
            grads,
            grads,
            jax.ShapeDtypeStruct((width, half), BF16),
            jax.ShapeDtypeStruct((width, half), BF16),
            jax.ShapeDtypeStruct((4, 16, width // 2), F32),
            jax.ShapeDtypeStruct((4, 16, width // 2), F32),
        ),
        [
            pltpu.VMEM((4, 16, width), F32),
            pltpu.VMEM((tokens, width), F32),
            pltpu.VMEM((8, LANES), F32),
            pltpu.VMEM((tokens, width), F32),
            pltpu.VMEM((tokens, width), BF16),
            pltpu.VMEM((width, tokens), BF16),
            pltpu.VMEM((tokens, width), BF16),
            pltpu.VMEM((width, tokens), BF16),
            pltpu.VMEM((tokens, width), F32),
            pltpu.VMEM((tokens, width), F32),
            pltpu.VMEM((tokens, FFC), BF16),
            pltpu.VMEM((tokens, FFC), BF16),
            pltpu.VMEM((tokens, FFC), BF16),
        ],
        prefetch=1,
        flops=2 * tokens * width * (18 * hidden + 3 * width),
        moved=24 * hidden * width + 12 * tokens * width,
    )(tp, att, woo, wop, x, pick, table, guo, gup, wdo, wdp, g, pick_t)


def attend_back_block(q, segq, gout, logs, keys, keys_t, values, biases, bias_sums, gkeys, gvalues):
    half = LANES // 2
    masks = lane_masks()
    scale = half**-0.5
    scaled = q * jnp.asarray(scale, BF16)
    gqs = []
    for h in range(2):
        query_low = scaled * masks[h]
        query = jnp.concatenate([query_low, segq], axis=1)
        gheads = gout * masks[h]
        chances = [jnp.exp(bias(h, mm_nt(key, query)) - logs[h : h + 1, :]) for key, bias in zip(keys, biases)]
        gchances = [mm_nt(value, gheads) for value in values]
        centre = sum(jnp.sum(p * gp, axis=0, keepdims=True) for p, gp in zip(chances, gchances))
        gq = 0.0
        for b, (p, gp) in enumerate(zip(chances, gchances)):
            gs = p * (gp - centre)
            bias_sums[b](h, gs)
            low = gs.astype(BF16)
            gvalues[b] = gvalues[b] + mm(p.astype(BF16), gheads)
            gkeys[b] = gkeys[b] + mm(low, query_low)
            gq = gq + mm(keys_t[b][h * half : (h + 1) * half, :], low)
        gqs.append(gq * scale)
    return jnp.concatenate(gqs, axis=0).T.astype(BF16)


def diagonal_sums(tile):
    size, wide = tile.shape
    rows = lax.broadcasted_iota(jnp.int32, (size, size), 0)
    cols = lax.broadcasted_iota(jnp.int32, (size, size), 1)
    turn = (rows + cols == size - 1).astype(F32).astype(BF16)
    high = tile.astype(BF16)
    rest = (tile - high.astype(F32)).astype(BF16)
    flipped = mm(turn, high) + mm(turn, rest)
    padded = jnp.concatenate([flipped, jnp.zeros((size, wide), F32)], axis=1)
    rolled = pltpu.roll(padded, 0, axis=1, stride=1, stride_axis=0)
    return jnp.sum(rolled, axis=0, keepdims=True)


def far_sums(tile, later):
    whole_sum = jnp.sum(jnp.sum(tile, axis=0, keepdims=True), axis=1, keepdims=True)
    edge = tile[:RADIUS, LANES:] if later else tile[HALF - RADIUS :, :LANES]
    sums = diagonal_sums(edge)
    rest = whole_sum - jnp.sum(sums, axis=1, keepdims=True)
    row = jnp.concatenate([sums, jnp.zeros((1, 2 * HALF - sums.shape[1]), F32)], axis=1)
    row = jnp.broadcast_to(row, (8, 2 * HALF))
    if later:
        row = pltpu.roll(row, 2 * HALF - LANES - RADIUS, axis=1)
    lanes = lax.broadcasted_iota(jnp.int32, (1, 2 * HALF), 1)
    return row[:1] + jnp.where(lanes == (0 if later else 2 * HALF - 2), rest, 0.0)


def attend_full_back_kernel(
    q_ref, k_ref, v_ref, g_ref, log_ref, segq_ref, segk_ref, near_ref, far_ref, o_ref, diag_ref, sums
):
    keys, keys_t, values = [], [], []
    for b in range(2):
        rows = pl.ds(b * HALF, HALF)
        key = k_ref[rows, :]
        keys.append(jnp.concatenate([key, segk_ref[rows, :]], axis=1))
        keys_t.append(key.T)
        values.append(v_ref[rows, :])
    gkeys, gvalues = [0.0, 0.0], [0.0, 0.0]
    sums[...] = jnp.zeros(sums.shape, F32)
    for qb in range(2):
        rows = pl.ds(qb * HALF, HALF)
        biases = full_biases(near_ref, far_ref, qb)

        def add(h, gs):
            sums[h] += gs

        def put(h, gs, later):
            row = 3 * h + (0 if later else 2)
            diag_ref[0, row : row + 1, :] = far_sums(gs, later)

        adders = [add, functools.partial(put, later=True)] if qb == 0 else [functools.partial(put, later=False), add]
        o_ref[0, rows, :] = attend_back_block(
            q_ref[rows, :], segq_ref[rows, :], g_ref[rows, :], log_ref[0, 0:2, rows],
            keys, keys_t, values, biases, adders, gkeys, gvalues,
        )
    for b in range(2):
        rows = pl.ds(b * HALF, HALF)
        o_ref[1, rows, :] = gkeys[b].astype(BF16)
        o_ref[2, rows, :] = gvalues[b].astype(BF16)
    for h in range(2):
        diag_ref[0, 3 * h + 1 : 3 * h + 2, :] = diagonal_sums(sums[h])


def attend_half_back_kernel(
    tp_ref, q_ref, k_ref, v_ref, kp_ref, vp_ref, g_ref, log_ref, segq_ref, segk_ref, near_ref, far_ref,
    o_ref, par_ref, diag_ref,
):
    keys, keys_t, values = [], [], []
    for b, (k, v) in enumerate(((k_ref, v_ref), (kp_ref, vp_ref))):
        key = k[...]
        keys.append(jnp.concatenate([key, segk_ref[pl.ds(b * HALF, HALF), :]], axis=1))
        keys_t.append(key.T)
        values.append(v[...])
    first = tp_ref[0] == 0
    biases = half_biases(near_ref, far_ref, first)
    gkeys, gvalues = [0.0, 0.0], [0.0, 0.0]

    def put(h, gs, b):
        sums = jnp.where(first, far_sums(gs, True), far_sums(gs, False)) if b else diagonal_sums(gs)
        diag_ref[0, 2 * h + b : 2 * h + b + 1, :] = sums

    adders = [functools.partial(put, b=b) for b in range(2)]
    o_ref[0] = attend_back_block(
        q_ref[...], segq_ref[...], g_ref[...], log_ref[0, 0:2, :],
        keys, keys_t, values, biases, adders, gkeys, gvalues,
    )
    o_ref[1] = gkeys[0].astype(BF16)
    o_ref[2] = gvalues[0].astype(BF16)
    par_ref[0] = gkeys[1].astype(BF16)
    par_ref[1] = gvalues[1].astype(BF16)


def attend_half_back(tp, qkv, kv_par, g, logs, segq, segk, bias):
    width = qkv.shape[1] // 3
    pairs = width // LANES
    flip = pairs // 2
    return call(
        attend_half_back_kernel,
        (pairs,),
        [
            pl.BlockSpec((HALF, LANES), lambda p, *_: (2, p)),
            pl.BlockSpec((HALF, LANES), lambda p, *_: (2, pairs + p)),
            pl.BlockSpec((HALF, LANES), lambda p, *_: (2, 2 * pairs + p)),
            pl.BlockSpec((HALF, LANES), lambda p, *_: (0, lax.rem(p + flip, pairs))),
            pl.BlockSpec((HALF, LANES), lambda p, *_: (0, pairs + lax.rem(p + flip, pairs))),
            pl.BlockSpec((HALF, LANES), lambda p, *_: (2, p)),
            pl.BlockSpec((1, 8, HALF), lambda p, *_: (p, 0, 2)),
            pl.BlockSpec((HALF, LANES), lambda p, *_: (2, 0)),
            pl.BlockSpec((ROW, LANES), lambda p, *_: (1, 0)),
        ]
        + bias_specs(),
        (
            pl.BlockSpec((3, HALF, LANES), lambda p, *_: (0, 0, p)),
            pl.BlockSpec((2, HALF, LANES), lambda p, *_: (0, 0, p)),
            pl.BlockSpec((1, 8, ROW), lambda p, *_: (p, 0, 0)),
        ),
        (
            jax.ShapeDtypeStruct((3, HALF, width), BF16),
            jax.ShapeDtypeStruct((2, HALF, width), BF16),
            jax.ShapeDtypeStruct((pairs, 8, ROW), F32),
        ),
        prefetch=1,
        flops=10 * HALF * HALF * 256 * 2 * pairs,
        moved=bias[0].size * 4,
    )(tp, qkv, qkv, qkv, kv_par, kv_par, g, logs, segq, segk, *bias)


def attend_full_back(qkv, g, logs, segq, segk, bias):
    width = qkv.shape[1] // 3
    pairs = width // LANES
    return call(
        attend_full_back_kernel,
        (pairs,),
        [
            pl.BlockSpec((ROW, LANES), lambda p: (0, p)),
            pl.BlockSpec((ROW, LANES), lambda p: (0, pairs + p)),
            pl.BlockSpec((ROW, LANES), lambda p: (0, 2 * pairs + p)),
            pl.BlockSpec((ROW, LANES), lambda p: (0, p)),
            pl.BlockSpec((1, 8, ROW), lambda p: (p, 0, 0)),
            pl.BlockSpec((ROW, LANES), lambda p: (0, 0)),
            pl.BlockSpec((ROW, LANES), lambda p: (0, 0)),
        ]
        + bias_specs(),
        (
            pl.BlockSpec((3, ROW, LANES), lambda p: (0, 0, p)),
            pl.BlockSpec((1, 8, ROW), lambda p: (p, 0, 0)),
        ),
        (
            jax.ShapeDtypeStruct((3, ROW, width), BF16),
            jax.ShapeDtypeStruct((pairs, 8, ROW), F32),
        ),
        [pltpu.VMEM((2, HALF, HALF), F32)],
        flops=20 * HALF * HALF * 256 * 2 * pairs,
        moved=bias[0].size * 4,
    )(qkv, qkv, qkv, g, logs, segq, segk, *bias)


def joined_rows(full_ref, half_ref, recv_ref, step, rows_in):
    half = recv_ref.shape[2] // 2
    rows_in[pl.ds(0, ROW), :] = full_ref[0]
    keep = (step > 0).astype(F32).astype(BF16)
    recv = jnp.concatenate([recv_ref[0, :, half:], recv_ref[0, :, :half]], axis=1)
    rows_in[pl.ds(ROW, HALF), :] = half_ref[0] + recv * keep


def qkv_weights_kernel(
    x_ref, oh_ref, tab_ref, full_ref, half_ref, recv_ref, outo_ref, outp_ref, go_ref, gp_ref, normed, normed_t, rows_in
):
    step = pl.program_id(0)
    tokens, width = x_ref.shape
    half = width // 2

    @pl.when(step == 0)
    def _():
        def body(i):
            rows = pl.ds(pl.multiple_of(i * HALF, HALF), HALF)
            hat, _ = norm_parts(x_ref[rows, :])
            pick = oh_ref[rows, :]
            scale = mm(pick, tab_ref[:, :width])
            shift = mm(pick, tab_ref[:, width : 2 * width])
            normed[rows, :] = (hat * scale + shift).astype(BF16)

        block_loop(tokens // HALF, body)
        normed_t[...] = normed[...].T

    joined_rows(full_ref, half_ref, recv_ref, step, rows_in)
    go_ref[0, :, :half] = mm(normed_t[...], rows_in[:, :half]).astype(BF16)
    gp_ref[0, :, :half] = mm(normed_t[...], rows_in[:, half:]).astype(BF16)
    go_ref[0, :, half:] = outo_ref[...]
    gp_ref[0, :, half:] = outp_ref[...]


def row_specs(width):
    return [
        pl.BlockSpec((1, ROW, width), lambda j, *_: (j, 0, 0)),
        pl.BlockSpec((1, HALF, width), lambda j, *_: (j, 0, 0)),
        pl.BlockSpec((1, HALF, width), lambda j, *_: (jnp.maximum(j - 1, 0), 0, 0)),
    ]


def qkv_weights(x, pick, table, full, half_rows, recv, out_own, out_par):
    tokens, width = x.shape
    half = width // 2
    third = half // 3
    spec = pl.BlockSpec((1, width, half + third), lambda j: (j, 0, 0))
    shape = jax.ShapeDtypeStruct((3, width, half + third), BF16)
    out_spec = pl.BlockSpec((width, third), lambda j: (0, j))
    return call(
        qkv_weights_kernel,
        (3,),
        [whole(tokens, width), whole(*pick.shape), whole(*table.shape)] + row_specs(width) + [out_spec, out_spec],
        (spec, spec),
        (shape, shape),
        [
            pltpu.VMEM((tokens, width), BF16),
            pltpu.VMEM((width, tokens), BF16),
            pltpu.VMEM((tokens, width), BF16),
        ],
        flops=2 * tokens * width * 6 * half,
        moved=16 * half * width + 12 * tokens * width,
    )(x, pick, table, full, half_rows, recv, out_own, out_par)


def qkv_back_kernel(
    tp_ref, x_ref, oh_ref, tab_ref, full_ref, half_ref, recv_ref, wo_ref, wp_ref, gmid_ref, lifted_ref, oht_ref,
    gino_ref, ginp_ref, sumo_ref, sump_ref, hats, stds, rows_in, acc, sums,
):
    step = pl.program_id(0)
    tokens, width = x_ref.shape
    half = wo_ref.shape[1]
    blocks = tokens // HALF

    @pl.when(step == 0)
    def _():
        def body(i):
            rows = pl.ds(pl.multiple_of(i * HALF, HALF), HALF)
            hat, inv_std = norm_parts(x_ref[rows, :])
            hats[rows, :] = hat
            stds[rows, :] = inv_std
            acc[rows, :] = jnp.zeros((HALF, width), F32)

        block_loop(blocks, body)

    joined_rows(full_ref, half_ref, recv_ref, step, rows_in)

    def body(i):
        rows = pl.ds(pl.multiple_of(i * HALF, HALF), HALF)
        grad = rows_in[rows, :]
        acc[rows, :] += mm_nt(grad[:, :half], wo_ref[...]) + mm_nt(grad[:, half:], wp_ref[...])

    block_loop(blocks, body)

    @pl.when(step == pl.num_programs(0) - 1)
    def _():
        first_core = tp_ref[0] == 0
        sums[...] = jnp.zeros(sums.shape, F32)

        def body(i):
            rows = pl.ds(pl.multiple_of(i * HALF, HALF), HALF)
            turn = oht_ref[i]
            gn = acc[rows, :]
            hat = hats[rows, :]
            sums[0] += mm(turn, (gn * hat).astype(BF16))
            sums[1] += mm(turn, gn.astype(BF16))
            scale = mm(oh_ref[rows, :], tab_ref[:, :width])
            grad = gmid_ref[rows, :] + norm_back(gn * scale, hat, stds[rows, :])
            low, high = grad[:, : width // 2], grad[:, width // 2 :]
            gino_ref[rows, :] = jnp.where(first_core, low, high)
            ginp_ref[rows, :] = jnp.where(first_core, high, low)
            lifted_t = lifted_ref[rows, :].astype(BF16).T
            sums[2] += mm(lifted_t[:16, :], grad.astype(BF16))

        block_loop(blocks, body)
        low, high = sums[:, :, : width // 2], sums[:, :, width // 2 :]
        sumo_ref[...] = jnp.where(first_core, low, high)
        sump_ref[...] = jnp.where(first_core, high, low)


def qkv_back(tp, x, pick, table, full, half_rows, recv, wo, wp, gmid, lifted, pick_t):
    tokens, width = x.shape
    half = wo.shape[1] // 3
    return call(
        qkv_back_kernel,
        (3,),
        [whole(tokens, width), whole(*pick.shape), whole(*table.shape)]
        + row_specs(width)
        + [
            pl.BlockSpec((width, half), lambda j, *_: (0, j)),
            pl.BlockSpec((width, half), lambda j, *_: (0, j)),
            whole(tokens, width),
            whole(tokens, LANES),
            whole(*pick_t.shape),
        ],
        (
            whole(tokens, width // 2),
            whole(tokens, width // 2),
            whole(3, 16, width // 2),
            whole(3, 16, width // 2),
        ),
        (
            jax.ShapeDtypeStruct((tokens, width // 2), F32),
            jax.ShapeDtypeStruct((tokens, width // 2), F32),
            jax.ShapeDtypeStruct((3, 16, width // 2), F32),
            jax.ShapeDtypeStruct((3, 16, width // 2), F32),
        ),
        [
            pltpu.VMEM((tokens, width), F32),
            pltpu.VMEM((tokens, 1), F32),
            pltpu.VMEM((tokens, width), BF16),
            pltpu.VMEM((tokens, width), F32),
            pltpu.VMEM((3, 16, width), F32),
        ],
        prefetch=1,
        flops=2 * tokens * width * 6 * half,
        moved=12 * half * width + 16 * tokens * width,
    )(tp, x, pick, table, full, half_rows, recv, wo, wp, gmid, lifted, pick_t)


def chain_joins(first_core):
    row = lax.broadcasted_iota(jnp.int32, (16, 16), 0)
    col = lax.broadcasted_iota(jnp.int32, (16, 16), 1)
    lower = ((row == col) & (row < 2 * SEGS)).astype(F32)
    upper = (
        ((row == col) & (row >= SEGS) & (row < 2 * SEGS)) | ((row == col + 2 * SEGS) & (row < 3 * SEGS))
    ).astype(F32)
    return jnp.where(first_core, lower, upper), jnp.where(first_core, upper, lower)


def join_chains(tp_ref, own_ref, came_ref, slope_ref, count, o_ref):
    own_join, came_join = chain_joins(tp_ref[0] == 0)
    cols = own_ref.shape[2]
    for i in range(count):
        both = jnp.dot(own_join, own_ref[i], precision=HIGHEST, preferred_element_type=F32)
        both = both + jnp.dot(came_join, came_ref[i], precision=HIGHEST, preferred_element_type=F32)
        lanes = pl.ds(i * cols, cols)
        o_ref[0:16, lanes] = (both * slope_ref[:, lanes]).astype(BF16)


def early_kernel(tp_ref, own_ref, came_ref, slope_ref, embed_ref, o_ref):
    join_chains(tp_ref, own_ref, came_ref, slope_ref, 4, o_ref)
    o_ref[:, pl.ds(4 * own_ref.shape[2], embed_ref.shape[1])] = embed_ref[...]


def late_kernel(tp_ref, own_ref, came_ref, slope_ref, bins_ref, o_ref):
    cols = own_ref.shape[2]
    join_chains(tp_ref, own_ref, came_ref, slope_ref, 2, o_ref)
    o_ref[16:32, :cols] = (own_ref[2] + came_ref[2]).astype(BF16)
    o_ref[16:32, cols:] = jnp.concatenate(
        [bins_ref[...].astype(BF16), jnp.zeros((16, cols - LANES), BF16)], axis=1
    )


def pack_rows(kernel, tp, own, came, slopes, extra, shape):
    return call(
        kernel,
        (1,),
        [whole(*own.shape), whole(*came.shape), whole(*slopes.shape), whole(*extra.shape)],
        whole(*shape),
        jax.ShapeDtypeStruct(shape, BF16),
        prefetch=1,
        flops=10**6,
        moved=10**5,
    )(tp, own, came, slopes, extra)


def closing_kernel(early_ref, late_ref, hat_ref, inv_ref, gain_ref, both_ref, *refs):
    ffn, attn, outs = refs[:2], refs[2:4], refs[4:]
    gu_ref, down_ref, qkv_ref, out_ref = outs[:4]
    w0_ref, b0_ref, w1_ref, w2_ref, b2_ref, w3_ref, b3_ref, w4_ref, w5_ref, b5_ref = outs[4:14]
    table_ref, pgain_ref, proj_ref, coord_ref = outs[14:]

    def total(pair, block):
        return pair[0][0, block].astype(F32) + pair[1][0, block].astype(F32)

    lanes = ffn[0].shape[3]
    chunks = down_ref.shape[1] // lanes
    for block in range(chunks):
        span = pl.ds(block * lanes, lanes)
        gu_ref[:, 0, span] = total(ffn, block)
        gu_ref[:, 1, span] = total(ffn, chunks + block)
        down_ref[:, span] = total(ffn, 2 * chunks + block)
    third = out_ref.shape[1] // 3
    for i in range(3):
        value = total(attn, i)
        qkv_ref[:, i, :] = value[:, : 3 * third]
        out_ref[:, i * third : (i + 1) * third] = value[:, 3 * third :]

    devices, _, wide = late_ref.shape
    cols = wide // 2
    embed_t = early_ref[:, 4 * cols :].T
    late = late_ref[:, 0:16, :].reshape(devices * 16, wide)
    parts = [late[:, :cols], late[:, cols:]] + [early_ref[:, i * cols : (i + 1) * cols] for i in range(4)]
    weights = [w0_ref, w1_ref, w5_ref, w3_ref, w4_ref, w2_ref]
    biases = [b0_ref, None, b5_ref, b3_ref, None, b2_ref]
    for part, weight, bias in zip(parts, weights, biases):
        weight[...] = mm(embed_t, part)
        if bias is not None:
            bias[...] = jnp.sum(part.astype(F32), axis=0)
    extra = jnp.sum(late_ref[:, 16:32, :].astype(F32), axis=0)
    coord_ref[...] = extra[: coord_ref.shape[0], :cols]
    bins = extra[:, cols : cols + LANES]
    hat = hat_ref[...]
    gain = gain_ref[...]
    proj = jnp.dot((hat * gain).T, bins.T, precision=HIGHEST, preferred_element_type=F32)
    proj_ref[...] = proj[:, : proj_ref.shape[1]]
    normed_grad = jnp.dot(bins.T, both_ref[...], precision=HIGHEST, preferred_element_type=F32)
    pgain_ref[...] = jnp.sum(normed_grad * hat, axis=0)
    table_ref[...] = norm_back(normed_grad * gain, hat, inv_ref[...])[: table_ref.shape[0]]


def closing(early, late, hat, inv_std, gain, both, ffn, attn, bins, heads):
    devices, _, wide = late.shape
    cols = wide // 2
    embed = early.shape[1] - 4 * cols
    features = hat.shape[1]
    height, lanes = ffn[0].shape[2:]
    weight, bias = (embed, cols), (cols,)
    hidden = lanes * (ffn[0].shape[1] // 3)
    shapes = [(height, 2, hidden), (height, hidden), (height, 3, cols), (height, cols)]
    shapes += [weight, bias, weight, weight, bias, weight, bias, weight, weight, bias]
    shapes += [(bins, features), (features,), (features, heads), (3, cols)]
    args = (early, late, hat, inv_std, gain, both, *ffn, *attn)
    return call(
        closing_kernel,
        (1,),
        [whole(*a.shape) for a in args],
        tuple(whole(*shape) for shape in shapes),
        tuple(jax.ShapeDtypeStruct(shape, F32) for shape in shapes),
        flops=10**8,
        moved=10**7,
    )(*args)


def halve_kernel(place_ref, *refs, plan, count):
    inputs, outs = refs[:count], refs[count:]
    for stream, (bit, sections) in enumerate(plan):
        sent_ref, kept_ref = outs[2 * stream], outs[2 * stream + 1]
        mine = (place_ref[0] >> bit) & 1
        done = 0
        for first, second, base, chunks, left in sections:
            spot = left.index(bit)
            shift = len(left) - 1
            half = 1 << shift

            def body(n, first=first, second=second, base=base, spot=spot, shift=shift, done=done, mine=mine):
                k = n & ((1 << shift) - 1)
                at = base + ((n >> shift) << (shift + 1)) + ((k >> spot) << (spot + 1)) + (k & ((1 << spot) - 1))
                for which, ref in ((1 - mine, sent_ref), (mine, kept_ref)):
                    block = at + (which << spot)
                    both = inputs[first][0, block].astype(F32) + inputs[second][0, block].astype(F32)
                    ref[0, done + n] = both.astype(BF16)

            block_loop(chunks * half, body)
            done += chunks * half


def halve(place, streams, bits):
    arrays, specs, plan, shapes = [], [], [], []

    def operand(array, index):
        for i, (seen, at) in enumerate(arrays):
            if seen is array and at == index:
                return i
        arrays.append((array, index))
        specs.append(pl.BlockSpec((1,) + array.shape[1:], lambda *_: (index, 0, 0, 0)))
        return len(arrays) - 1

    moved = 0
    for sections, bit in zip(streams, bits):
        entries, blocks = [], 0
        for own, i, came, k, base, chunks, left in sections:
            entries.append((operand(own, i), operand(came, k), base, chunks, left))
            blocks += chunks << (len(left) - 1)
        plan.append((bit, entries))
        shape = (1, blocks) + sections[0][0].shape[2:]
        shapes += [shape, shape]
        moved += 12 * blocks * shape[2] * shape[3]
    outs = call(
        functools.partial(halve_kernel, plan=plan, count=len(arrays)),
        (1,),
        specs,
        tuple(whole(*shape) for shape in shapes),
        tuple(jax.ShapeDtypeStruct(shape, BF16) for shape in shapes),
        prefetch=1,
        flops=10**6,
        moved=moved,
    )(place, *[array for array, _ in arrays])
    return list(outs[0::2]), list(outs[1::2])


def swap(values):
    return lax.ppermute(values, "tp", [(0, 1), (1, 0)])


def after(values, *others):
    return lax.optimization_barrier((values, *others))[0]


class Cube:
    def __init__(self, rows):
        self.bits = rows.bit_length() - 1
        assert rows == 1 << self.bits
        self.place = lax.axis_index("rows").reshape(1).astype(jnp.int32)
        self.perms = [[(i, i ^ (1 << b)) for i in range(rows)] for b in range(self.bits)]

    def turns(self):
        return [[(i + r) % 3 for i in range(3)] for r in range(3)]

    def gather(self, values, bit):
        came = lax.ppermute(values, "rows", self.perms[bit])
        return lax.optimization_barrier(jnp.concatenate([values, came], axis=0))


def next_sections(sections, kept, came, bit):
    made, base = [], 0
    for _, _, _, _, _, chunks, left in sections:
        left = [b for b in left if b != bit]
        made.append((kept, 0, came, 0, base, chunks, left))
        base += chunks << len(left)
    return made


def normalize(values):
    centre = jnp.mean(values, axis=-1, keepdims=True)
    shifted = values - centre
    spread = jnp.mean(shifted * shifted, axis=-1, keepdims=True)
    inv_std = lax.rsqrt(spread + EPSILON)
    return shifted * inv_std, inv_std


def three_parts(values):
    high = lax.reduce_precision(values, 8, 7)
    middle = lax.reduce_precision(values - high, 8, 7)
    low = values - high - middle
    return jnp.concatenate([high, middle, low], axis=0).astype(BF16)


def bias_base(heads):
    bins = heads.shape[1]
    low = lambda n: jnp.broadcast_to(heads[:, :1], (heads.shape[0], n))
    top = lambda n: jnp.broadcast_to(heads[:, bins - 1 :], (heads.shape[0], n))
    fill = HALF - RADIUS
    behind = jnp.concatenate([low(fill), heads[:, :RADIUS], low(HALF)], axis=1)
    same = jnp.concatenate([heads[:, RADIUS:], top(fill - 1), low(fill), heads[:, :RADIUS]], axis=1)
    ahead = jnp.concatenate([top(HALF), heads[:, RADIUS:], top(fill - 1)], axis=1)
    return jnp.stack([behind, same, ahead], axis=1)


def bins_of_diagonals():
    places = jnp.arange(ROW, dtype=jnp.int32)[None, :] - (HALF - 1)
    offsets = places + HALF * jnp.arange(-1, 2, dtype=jnp.int32)[:, None]
    bins = jnp.clip(offsets, -RADIUS, RADIUS) + RADIUS
    every = jnp.arange(2 * RADIUS + 1, dtype=jnp.int32)
    return (bins.reshape(-1)[:, None] == every[None, :]).astype(F32)


def per_device(
    layer_input,
    cotangent,
    chain_lengths,
    self_condition_flag,
    time_embedding,
    query_key_value,
    output_projection,
    attention_scale_weight,
    attention_scale_bias,
    attention_shift_weight,
    attention_gate_weight,
    attention_gate_bias,
    transition_scale_weight,
    transition_scale_bias,
    transition_shift_weight,
    transition_gate_weight,
    transition_gate_bias,
    gate_up_projection,
    down_projection,
    pair_table,
    pair_gain,
    pair_projection,
    coordinate_head,
    coordinate_embedding,
    rows,
):
    core = lax.axis_index("tp")
    other = 1 - core
    first_core = core == 0
    tp = core.reshape(1).astype(jnp.int32)
    cols = layer_input.shape[1]
    width = query_key_value.shape[0]
    heads_here = pair_projection.shape[1]
    bins = pair_table.shape[0]
    cube = Cube(rows)

    def side_by_side(own, came, axis):
        return jnp.where(
            first_core, jnp.concatenate([own, came], axis), jnp.concatenate([came, own], axis)
        )

    def tokens_of(values, which):
        return jnp.concatenate(
            [
                lax.dynamic_slice_in_dim(values, which * 2 * ROW, ROW, 0),
                lax.dynamic_slice_in_dim(values, ROW + which * HALF, HALF, 0),
            ],
            axis=0,
        )

    def gather_tokens(values):
        return side_by_side(tokens_of(values, core), swap(tokens_of(values, other)), 1)

    def scatter_tokens(own, sent):
        came = swap(sent)
        lower = jnp.concatenate([own[:ROW], own[ROW:], came[ROW:], came[:ROW]], axis=0)
        upper = jnp.concatenate([came[:ROW], came[ROW:], own[ROW:], own[:ROW]], axis=0)
        return jnp.where(first_core, lower, upper)

    x = gather_tokens(layer_input)
    qkv_own = query_key_value.reshape(width, -1)
    qkv_par = swap(qkv_own)

    packs = chain_lengths.shape[0]
    ends = jnp.cumsum(chain_lengths, axis=1)
    places = jnp.arange(ROW, dtype=jnp.int32)
    segment = jnp.sum((places[None, :, None] >= ends[:, None, :]).astype(jnp.int32), axis=2)
    embed = jnp.concatenate(
        [time_embedding, jnp.zeros((packs, 1, time_embedding.shape[2]), BF16)], axis=1
    )
    embed_rows = embed.reshape(packs * SEGS, -1)
    mod_weights = jnp.stack(
        [
            attention_scale_weight,
            attention_shift_weight,
            attention_gate_weight,
            transition_scale_weight,
            transition_shift_weight,
            transition_gate_weight,
        ],
        axis=1,
    ).reshape(-1, 6 * cols)
    mods = jnp.dot(embed_rows, mod_weights, preferred_element_type=F32).reshape(-1, 6, cols)
    mods = jnp.stack(
        [
            jax.nn.sigmoid(mods[:, 0] + attention_scale_bias.astype(F32)),
            mods[:, 1],
            jax.nn.sigmoid(mods[:, 2] + attention_gate_bias.astype(F32)),
            jax.nn.sigmoid(mods[:, 3] + transition_scale_bias.astype(F32)),
            mods[:, 4],
            jax.nn.sigmoid(mods[:, 5] + transition_gate_bias.astype(F32)),
        ],
        axis=1,
    )
    mods_full = side_by_side(mods, swap(mods), 2)
    mods_here = jnp.concatenate(
        [
            lax.dynamic_slice_in_dim(mods_full, 2 * SEGS * core, SEGS, 0),
            mods_full[SEGS : 2 * SEGS],
        ],
        axis=0,
    )
    table = three_parts(mods_here.reshape(2 * SEGS, 6 * width))
    table = jnp.concatenate([table, jnp.zeros((2, 6 * width), BF16)], axis=0)

    seg_full = lax.dynamic_slice_in_dim(segment, 2 * core, 1, 0)[0]
    seg_half = lax.dynamic_slice_in_dim(segment[1], HALF * core, HALF, 0)
    seg_far = lax.dynamic_slice_in_dim(segment[1], HALF * other, HALF, 0)
    seg_q = jnp.concatenate([seg_full, seg_half])
    seg_k = jnp.concatenate([seg_full, seg_half, seg_far])
    lanes = jnp.arange(LANES, dtype=jnp.int32)
    mask_k = (seg_k[:, None] == lanes[None, :]).astype(BF16)
    mask_q = jnp.where(
        (seg_q[:, None] != lanes[None, :]) & (lanes[None, :] < SEGS), MASKED, 0.0
    ).astype(BF16)
    row_of = jnp.concatenate([seg_full, seg_half + SEGS])
    spots = jnp.arange(32, dtype=jnp.int32)
    pick = (
        (row_of[:, None] == lax.rem(spots, 2 * SEGS)[None, :]) & (spots[None, :] < 6 * SEGS)
    ).astype(BF16)
    pick_t = (row_of.reshape(-1, 1, HALF) == jnp.arange(16, dtype=jnp.int32)[None, :, None]).astype(BF16)
    flag_full = lax.dynamic_slice_in_dim(self_condition_flag, 2 * core, 1, 0)
    flags = jnp.concatenate(
        [jnp.broadcast_to(flag_full, (ROW,)), jnp.broadcast_to(self_condition_flag[1:2], (HALF,))]
    ).astype(F32)[:, None]

    pair_hat, pair_inv = normalize(pair_table.astype(F32))
    gain = pair_gain.astype(F32)
    pair_normed = pair_hat * gain
    pair_both = jnp.concatenate([pair_projection, swap(pair_projection)], axis=1).astype(F32)
    bias_heads = jnp.transpose(jnp.dot(pair_normed, pair_both, precision=HIGHEST))
    bias_source = jnp.transpose(pair_both)
    bias = bias_tiles(bias_base(bias_heads))

    out_own = output_projection
    out_par = swap(output_projection)
    gu_own = jnp.transpose(gate_up_projection, (1, 0, 2))
    gu_par = swap(gu_own)
    down_own = down_projection
    down_par = swap(down_projection)
    coord = jnp.concatenate([coordinate_head, coordinate_embedding], axis=0)
    coord = side_by_side(coord, swap(coord), 1)
    fill = jnp.zeros((LANES - 3, width), BF16)
    head = jnp.concatenate([coord[:3], fill], axis=0)
    emb = jnp.concatenate([coord[3:], fill], axis=0)
    cot = gather_tokens(cotangent)

    def attention(values):
        qkv = qkv_forward(values, pick, table, qkv_own, qkv_par)
        kv_par = swap(qkv[ROW:, width:])
        attended, logs = attend_forward(tp, qkv, kv_par, mask_q, mask_k, bias)
        return qkv, kv_par, attended, logs

    _, _, attended, _ = attention(x)
    shifted, lifted = ffn_forward(
        attended, out_own, out_par, x, pick, table, gu_own, gu_par, down_own, down_par, head, emb, flags
    )
    qkv, kv_par, attended, logs = attention(shifted)
    (
        result_own,
        result_sent,
        grad_middle,
        grad_attended,
        grads_own,
        grads_sent,
        grad_out_own,
        grad_out_sent,
        early_own,
        early_sent,
    ) = ffn_turn(
        tp, attended, out_own, out_par, shifted, pick, table, gu_own, gu_par, down_own, down_par, cot, pick_t
    )

    slopes = mods * (1.0 - mods)
    ones = jnp.ones_like(slopes[:, 0])
    row_fill = lambda values: jnp.pad(values, ((0, 16 - values.shape[0]), (0, 0)))
    early_slopes = row_fill(jnp.concatenate([slopes[:, 5], slopes[:, 3], ones, slopes[:, 2]], axis=1))
    late_slopes = row_fill(jnp.concatenate([slopes[:, 0], ones], axis=1))
    embed_fill = row_fill(embed_rows)
    early_came = swap(early_sent)

    came_ffn = swap(grads_sent)
    half_grads, far_grads, diag_half = attend_half_back(
        tp, qkv, kv_par, grad_attended, logs, mask_q, mask_k, bias
    )
    came_grads = swap(far_grads)

    turns = cube.turns()
    every = list(range(cube.bits))
    height = width // rows
    slots = lambda values: values.reshape(3, -1, height, values.shape[-1])
    chunks = grads_own.shape[1]
    own_slots, came_slots = slots(grads_own), slots(came_ffn)
    ffn = [[(own_slots, i, came_slots, i, 0, chunks, every)] for i in range(3)]

    def one_round(streams, bits, *others):
        sent, kept = halve(cube.place, streams, bits)
        held = lax.optimization_barrier((*sent, *others))
        came = [lax.ppermute(v, "rows", cube.perms[bit]) for v, bit in zip(held, bits)]
        made = [next_sections(*parts) for parts in zip(streams, kept, came, bits)]
        return made, came, held[len(sent) :]

    early_came, _ = lax.optimization_barrier((early_came, diag_half))
    early = pack_rows(
        early_kernel, tp, early_own, early_came, early_slopes, embed_fill, (16, 4 * cols + embed_rows.shape[1])
    )
    ffn, came, (mask_full, early, _) = one_round(ffn, turns[0], mask_q, early, diag_half)
    full_grads, diag_full = attend_full_back(qkv, grad_attended, logs, mask_full, mask_k, bias)
    early = cube.gather(early, 0)
    ffn, came, (pick_weights, early, _) = one_round(ffn, turns[1], pick, early, diag_full)
    gqkv_own, gqkv_sent = qkv_weights(
        shifted, pick_weights, table, full_grads, half_grads, came_grads, grad_out_own, grad_out_sent
    )
    early = cube.gather(early, 1)
    gqkv_sent, early, *_ = lax.optimization_barrier((gqkv_sent, early, *came))
    own_slots, came_slots = slots(gqkv_own), slots(swap(gqkv_sent))
    streams = [ffn[i] + [(own_slots, i, came_slots, i, 0, 1, every)] for i in range(3)]
    streams, came, (pick_back, early) = one_round(streams, turns[2], pick_weights, early)
    gin_own, gin_sent, late_own, late_sent = qkv_back(
        tp, shifted, pick_back, table, full_grads, half_grads, came_grads, qkv_own, qkv_par, grad_middle, lifted, pick_t
    )
    early = cube.gather(early, 2)
    late_sent, early, *_ = lax.optimization_barrier((late_sent, early, *came))

    diag_half = diag_half[:, :4].reshape(-1, 2, ROW)
    quiet = jnp.zeros_like(diag_half[:, 0])
    diag_far = diag_half[:, 1]
    diag = diag_full[:, :6].reshape(-1, 3, ROW) + jnp.stack(
        [
            jnp.where(first_core, diag_far, quiet),
            diag_half[:, 0],
            jnp.where(first_core, quiet, diag_far),
        ],
        axis=1,
    )
    grad_bins = jnp.dot(diag.reshape(-1, 3 * ROW), bins_of_diagonals(), precision=HIGHEST)
    came_bins = swap(grad_bins)
    grad_bins = grad_bins + jnp.concatenate([came_bins[heads_here:], came_bins[:heads_here]], axis=0)
    bins_fill = jnp.pad(grad_bins, ((0, 16 - 2 * heads_here), (0, LANES - bins)))

    late_came = swap(late_sent)
    late = pack_rows(late_kernel, tp, late_own, late_came, late_slopes, bins_fill, (32, 2 * cols))
    ffn = [[stream[0] for stream in streams]]
    attn = [stream[1:] for stream in streams]
    rest = list(range(3, cube.bits))
    waited = []
    for step in range(max(len(rest), 2)):
        now, bits = [], []
        if step < len(rest):
            now, bits = ffn, rest[step : step + 1]
        count = len(now)
        if step < 2:
            now, bits = now + attn, bits + turns[step]
        now, came, (late, *_) = one_round(now, bits, late, *waited)
        waited = came[:count]
        if count:
            ffn = now[:count]
        if step < 2:
            attn = now[count:]
        late = cube.gather(late, step)
    done = max(len(rest), 2)
    attn = [[section for stream in attn for section in stream]]
    for bit in rest:
        attn, came, (late,) = one_round(attn, [bit], late)
        if done < cube.bits:
            late = cube.gather(late, done)
            done += 1
    for step in range(done, cube.bits):
        late = cube.gather(late, step)
    for step in range(3, cube.bits):
        early = cube.gather(early, step)
    ffn_last = (ffn[0][0][0], ffn[0][0][2])
    attn_last = (attn[0][0][0], attn[0][0][2])

    layer_output = scatter_tokens(result_own, result_sent)
    input_gradient = scatter_tokens(gin_own, gin_sent)

    bins_pad = ((0, LANES - bins), (0, 0))
    grad_gu, grad_down, grad_qkv, grad_out, *conditioning = closing(
        early,
        late.reshape(rows, 32, 2 * cols),
        jnp.pad(pair_hat, bins_pad),
        jnp.pad(pair_inv, bins_pad),
        gain[None, :],
        jnp.pad(bias_source, ((0, 16 - 2 * heads_here), (0, 0))),
        ffn_last,
        attn_last,
        bins,
        heads_here,
    )
    *conditioning, grad_table, grad_gain, grad_pair, coord_grad = conditioning
    return (
        layer_output,
        input_gradient,
        grad_qkv,
        grad_out.T,
        *conditioning,
        grad_gu,
        grad_down.T,
        grad_table,
        grad_gain,
        grad_pair,
        coord_grad,
    )


def solution(mesh):
    in_specs = (
        P("rows", "tp"),
        P("rows", "tp"),
        P("rows", None),
        P("rows"),
        P("rows", None, None),
        P(None, None, "tp"),
        P("tp", None),
        P(None, "tp"),
        P("tp"),
        P(None, "tp"),
        P(None, "tp"),
        P("tp"),
        P(None, "tp"),
        P("tp"),
        P(None, "tp"),
        P(None, "tp"),
        P("tp"),
        P(None, None, "tp"),
        P("tp", None),
        P(),
        P(),
        P(None, "tp"),
        P(None, "tp"),
        P(None, "tp"),
    )
    out_specs = (
        P("rows", "tp"),
        P("rows", "tp"),
        P("rows", None, "tp"),
        P("tp", "rows"),
        P(None, "tp"),
        P("tp"),
        P(None, "tp"),
        P(None, "tp"),
        P("tp"),
        P(None, "tp"),
        P("tp"),
        P(None, "tp"),
        P(None, "tp"),
        P("tp"),
        P("rows", None, "tp"),
        P("tp", "rows"),
        P(),
        P(),
        P(None, "tp"),
        P(None, "tp"),
    )
    return jax.shard_map(
        functools.partial(per_device, rows=mesh.shape["rows"]),
        mesh=mesh,
        in_specs=in_specs,
        out_specs=out_specs,
        check_vma=False,
    )
```

```python
import functools
import jax
import jax.numpy as jnp
from jax import lax
from jax.experimental import pallas as pl
from jax.experimental.pallas import tpu as pltpu
from jax.sharding import PartitionSpec as P

RADIUS = 32
ROW = 512
HALF = ROW // 2
SEGS = 5
EPSILON = 1e-05
MASKED = -1e30
HIGHEST = lax.Precision.HIGHEST
F32 = jnp.float32
BF16 = jnp.bfloat16
LANES = 128
FFC = 512
NT = (((1,), (1,)), ((), ()))
VMEM_LIMIT = 60 * 1024 * 1024


def mm(left, right):
    return jnp.dot(left, right, preferred_element_type=F32)


def mm_nt(left, right):
    return lax.dot_general(left, right, NT, preferred_element_type=F32)


def norm_parts(values):
    centre = jnp.mean(values, axis=1, keepdims=True)
    shifted = values - centre
    spread = jnp.mean(shifted * shifted, axis=1, keepdims=True)
    inv_std = lax.rsqrt(spread + EPSILON)
    return shifted * inv_std, inv_std


def norm_back(grad, hat, inv_std):
    first = jnp.mean(grad, axis=1, keepdims=True)
    second = jnp.mean(grad * hat, axis=1, keepdims=True)
    return inv_std * (grad - first - hat * second)


def block_loop(count, body):
    lax.fori_loop(0, count, lambda i, c: (body(i), c)[1], 0)


def call(kernel, grid, in_specs, out_specs, out_shape, scratch=(), prefetch=0, aliases=None, flops=0, moved=0):
    return pl.pallas_call(
        kernel,
        grid_spec=pltpu.PrefetchScalarGridSpec(
            num_scalar_prefetch=prefetch,
            grid=grid,
            in_specs=in_specs,
            out_specs=out_specs,
            scratch_shapes=list(scratch),
        ),
        out_shape=out_shape,
        input_output_aliases=aliases or {},
        compiler_params=pltpu.CompilerParams(
            dimension_semantics=("arbitrary",) * len(grid), vmem_limit_bytes=VMEM_LIMIT
        ),
        cost_estimate=pl.CostEstimate(flops=flops, transcendentals=0, bytes_accessed=moved),
    )


def whole(*shape):
    zeros = (0,) * len(shape)
    return pl.BlockSpec(shape, lambda *_: zeros)


def bias_kernel(base_ref, near_ref, far_ref):
    for d, height, start, out in (
        (1, HALF, 0, near_ref.at[0]),
        (0, RADIUS, 0, far_ref.at[0, 0]),
        (2, RADIUS, HALF - RADIUS, far_ref.at[0, 1]),
    ):
        rows = jnp.broadcast_to(base_ref[0, d : d + 1, :], (height, 2 * HALF))
        rolled = pltpu.roll(rows, start, axis=1, stride=1, stride_axis=0)
        out[...] = rolled[:, :HALF]


def bias_tiles(base):
    heads = base.shape[0]
    near, far = (heads, HALF, HALF), (heads, 2, RADIUS, HALF)
    return call(
        bias_kernel,
        (heads,),
        [pl.BlockSpec((1, 3, 2 * HALF), lambda h: (h, 0, 0))],
        (
            pl.BlockSpec((1,) + near[1:], lambda h: (h, 0, 0)),
            pl.BlockSpec((1,) + far[1:], lambda h: (h, 0, 0, 0)),
        ),
        (jax.ShapeDtypeStruct(near, F32), jax.ShapeDtypeStruct(far, F32)),
        moved=heads * HALF * HALF * 4,
        flops=10**7,
    )(base)


def bias_specs():
    return [
        pl.BlockSpec((2, HALF, HALF), lambda p, *_: (p, 0, 0)),
        pl.BlockSpec((2, 2, RADIUS, HALF), lambda p, *_: (p, 0, 0, 0)),
    ]


def add_near(near_ref, far_ref, h, scores):
    return scores + near_ref[h]


def add_later(near_ref, far_ref, h, scores):
    edge = far_ref[h, 0]
    return jnp.concatenate([scores[:RADIUS] + edge, scores[RADIUS:] + edge[RADIUS - 1 :, :1]], axis=0)


def add_earlier(near_ref, far_ref, h, scores):
    edge = far_ref[h, 1]
    return jnp.concatenate(
        [scores[: HALF - RADIUS] + edge[:1, HALF - 1 :], scores[HALF - RADIUS :] + edge], axis=0
    )


def add_either(first, near_ref, far_ref, h, scores):
    later, earlier = far_ref[h, 0], far_ref[h, 1]
    rest = jnp.where(first, later[RADIUS - 1 :, :1], earlier[:1, HALF - 1 :])
    return jnp.concatenate(
        [
            scores[:RADIUS] + jnp.where(first, later, rest),
            scores[RADIUS : HALF - RADIUS] + rest,
            scores[HALF - RADIUS :] + jnp.where(first, rest, earlier),
        ],
        axis=0,
    )


def full_biases(near_ref, far_ref, qb):
    kinds = (add_near, add_later) if qb == 0 else (add_earlier, add_near)
    return [functools.partial(kind, near_ref, far_ref) for kind in kinds]


def half_biases(near_ref, far_ref, first):
    return [
        functools.partial(add_near, near_ref, far_ref),
        functools.partial(add_either, first, near_ref, far_ref),
    ]


def mods_kernel(embed_ref, *refs):
    weights, biases = refs[:6], {0: refs[6], 2: refs[7], 3: refs[8], 5: refs[9]}
    mods_ref, early_ref, late_ref = refs[10:]
    cols = early_ref.shape[1] // 4
    homes = {0: (late_ref, 0), 1: (late_ref, 1), 5: (early_ref, 0), 3: (early_ref, 1), 4: (early_ref, 2), 2: (early_ref, 3)}
    for i in range(6):
        value = mm(embed_ref[...], weights[i][...])
        slope = jnp.ones_like(value)
        if i in biases:
            value = jax.nn.sigmoid(value + biases[i][...].astype(F32))
            slope = value * (1.0 - value)
        mods_ref[i] = value
        home, place = homes[i]
        home[:, pl.ds(place * cols, cols)] = slope


def modulations(embed, weights, biases):
    cols = weights[0].shape[1]
    args = (embed, *weights, *biases)
    shapes = [(6, 16, cols), (16, 4 * cols), (16, 2 * cols)]
    return call(
        mods_kernel,
        (1,),
        [whole(*a.shape) for a in args],
        tuple(whole(*shape) for shape in shapes),
        tuple(jax.ShapeDtypeStruct(shape, F32) for shape in shapes),
        flops=10**8,
        moved=2 * 10**6,
    )(*args)


def table_kernel(tp_ref, own_ref, came_ref, o_ref):
    first = tp_ref[0] == 0
    row = lax.broadcasted_iota(jnp.int32, (32, 16), 0)
    col = lax.broadcasted_iota(jnp.int32, (32, 16), 1)
    part = (row >= 2 * SEGS).astype(jnp.int32) + (row >= 4 * SEGS).astype(jnp.int32)
    chain = row - 2 * SEGS * part
    chain = chain + jnp.where((chain < SEGS) & jnp.logical_not(first), 2 * SEGS, 0)
    take = ((col == chain) & (row < 6 * SEGS)).astype(F32)
    rows = lax.broadcasted_iota(jnp.int32, (32, 1), 0)
    width = 2 * own_ref.shape[2]
    for i in range(6):
        own, came = own_ref[i], came_ref[i]
        low, high = jnp.where(first, own, came), jnp.where(first, came, own)
        value = jnp.dot(take, jnp.concatenate([low, high], axis=1), precision=HIGHEST, preferred_element_type=F32)
        top = value.astype(BF16).astype(F32)
        middle = (value - top).astype(BF16).astype(F32)
        parts = jnp.where(rows < 2 * SEGS, top, jnp.where(rows < 4 * SEGS, middle, value - top - middle))
        o_ref[:, pl.ds(i * width, width)] = parts.astype(BF16)


def chain_table(tp, own, came):
    shape = (32, 12 * own.shape[2])
    return call(
        table_kernel,
        (1,),
        [whole(*own.shape), whole(*came.shape)],
        whole(*shape),
        jax.ShapeDtypeStruct(shape, BF16),
        prefetch=1,
        flops=10**7,
        moved=10**6,
    )(tp, own, came)


def masks_kernel(tp_ref, length_ref, flag_ref, q_ref, k_ref, pick_ref, turn_ref, marks_ref):
    core = tp_ref[0]

    def segments(pack, shape, axis, start):
        spot = lax.broadcasted_iota(jnp.int32, shape, axis) + start
        segment = jnp.zeros(shape, jnp.int32)
        end = 0
        for i in range(SEGS - 1):
            end = end + length_ref[pack * (SEGS - 1) + i]
            segment = segment + (spot >= end).astype(jnp.int32)
        return segment

    runs = [(2 * core, 0, 0), (2 * core, HALF, 0), (1, HALF * core, SEGS), (1, HALF * (1 - core), SEGS)]
    for i, (pack, start, shift) in enumerate(runs):
        rows = pl.ds(i * HALF, HALF)
        segment = segments(pack, (HALF, LANES), 0, start)
        lanes = lax.broadcasted_iota(jnp.int32, (HALF, LANES), 1)
        k_ref[rows, :] = (segment == lanes).astype(F32).astype(BF16)
        if i == 3:
            break
        q_ref[rows, :] = jnp.where((segment != lanes) & (lanes < SEGS), MASKED, 0.0).astype(BF16)
        chain = (segment + shift)[:, :32]
        lanes = lanes[:, :32]
        spot = lanes - 2 * SEGS * (
            (lanes >= 2 * SEGS).astype(jnp.int32) + (lanes >= 4 * SEGS).astype(jnp.int32)
        )
        pick_ref[rows, :] = ((chain == spot) & (lanes < 6 * SEGS)).astype(F32).astype(BF16)
        marks_ref[rows, :] = jnp.full((HALF, 1), flag_ref[pack].astype(F32))
        across = segments(pack, (16, HALF), 1, start) + shift
        turn_ref[i] = (across == lax.broadcasted_iota(jnp.int32, (16, HALF), 0)).astype(F32).astype(BF16)


def masks(tp, lengths, flags):
    shapes = [(3 * HALF, LANES), (4 * HALF, LANES), (3 * HALF, 32), (3, 16, HALF)]
    return call(
        masks_kernel,
        (1,),
        [],
        tuple(whole(*shape) for shape in shapes) + (whole(3 * HALF, 1),),
        tuple(jax.ShapeDtypeStruct(shape, BF16) for shape in shapes)
        + (jax.ShapeDtypeStruct((3 * HALF, 1), F32),),
        prefetch=3,
        flops=10**6,
        moved=10**6,
    )(tp, lengths, flags)


def halves_kernel(tp_ref, *refs):
    for source, target in zip(refs[:4], refs[4:]):
        target[...] = source[...]


def token_halves(tp, first, second):
    cols = first.shape[1]

    def mine(j, tp_ref):
        return jnp.where(j < 2, 4 * tp_ref[0] + j, 2 + tp_ref[0]), 0

    def others(j, tp_ref):
        return jnp.where(j < 2, 4 * (1 - tp_ref[0]) + j, 3 - tp_ref[0]), 0

    spec = pl.BlockSpec((HALF, cols), lambda j, _: (j, 0))
    shape = jax.ShapeDtypeStruct((3 * HALF, cols), BF16)
    places = [pl.BlockSpec((HALF, cols), place) for place in (mine, others)]
    return call(
        halves_kernel, (3,), places + places, (spec,) * 4, (shape,) * 4, prefetch=1, flops=10, moved=24 * HALF * cols
    )(tp, first, first, second, second)


def qkv_kernel(x_ref, oh_ref, tab_ref, own_ref, par_ref, o_ref, normed):
    width = x_ref.shape[1]
    half = own_ref.shape[1]

    @pl.when(pl.program_id(0) == 0)
    def _():
        def body(i):
            rows = pl.ds(pl.multiple_of(i * HALF, HALF), HALF)
            hat, _ = norm_parts(x_ref[rows, :].astype(F32))
            pick = oh_ref[rows, :]
            scale = mm(pick, tab_ref[:, :width])
            shift = mm(pick, tab_ref[:, width : 2 * width])
            normed[rows, :] = (hat * scale + shift).astype(BF16)

        block_loop(x_ref.shape[0] // HALF, body)

    o_ref[:, :half] = mm(normed[...], own_ref[...]).astype(BF16)
    o_ref[:, half:] = mm(normed[...], par_ref[...]).astype(BF16)


def qkv_forward(x, pick, table, w_own, w_par):
    tokens, width = x.shape
    half = w_own.shape[1] // 3
    return call(
        qkv_kernel,
        (3,),
        [
            whole(tokens, width),
            whole(*pick.shape),
            whole(*table.shape),
            pl.BlockSpec((width, half), lambda j: (0, j)),
            pl.BlockSpec((width, half), lambda j: (0, j)),
        ],
        pl.BlockSpec((tokens, 2 * half), lambda j: (0, j)),
        jax.ShapeDtypeStruct((tokens, 6 * half), BF16),
        [pltpu.VMEM((tokens, width), BF16)],
        flops=2 * tokens * width * 6 * half,
        moved=tokens * 6 * half * 2 + width * half * 12 + tokens * width * 4,
    )(x, pick, table, w_own, w_par)


def lane_masks():
    lanes = lax.broadcasted_iota(jnp.int32, (1, LANES), 1)
    first = (lanes < LANES // 2).astype(F32)
    return first.astype(BF16), (1.0 - first).astype(BF16)


def attend_forward_block(q, segq, keys, values_t, biases):
    outs, logs = [], []
    half = LANES // 2
    masks = lane_masks()
    scaled = q * jnp.asarray(half**-0.5, BF16)
    for h in range(2):
        query = jnp.concatenate([scaled * masks[h], segq], axis=1)
        scores = [bias(h, mm_nt(key, query)) for key, bias in zip(keys, biases)]
        tops = [jnp.max(s, axis=0, keepdims=True) for s in scores]
        top = functools.reduce(jnp.maximum, tops)
        weights = [jnp.exp(s - top) for s in scores]
        total = sum(jnp.sum(w, axis=0, keepdims=True) for w in weights)
        mixed = sum(
            mm(vt[h * half : (h + 1) * half, :], w.astype(BF16)) for vt, w in zip(values_t, weights)
        )
        outs.append(mixed / total)
        logs.append(top + jnp.log(total))
    attended = jnp.concatenate(outs, axis=0).T.astype(BF16)
    return attended, jnp.concatenate(logs, axis=0)


def attend_full_kernel(q_ref, k_ref, v_ref, segq_ref, segk_ref, near_ref, far_ref, o_ref, log_ref):
    keys = [
        jnp.concatenate([k_ref[pl.ds(b * HALF, HALF), :], segk_ref[pl.ds(b * HALF, HALF), :]], axis=1)
        for b in range(2)
    ]
    values_t = [v_ref[pl.ds(b * HALF, HALF), :].T for b in range(2)]
    for qb in range(2):
        rows = pl.ds(qb * HALF, HALF)
        biases = full_biases(near_ref, far_ref, qb)
        attended, logs = attend_forward_block(q_ref[rows, :], segq_ref[rows, :], keys, values_t, biases)
        o_ref[rows, :] = attended
        log_ref[0, 0:2, rows] = logs


def attend_half_kernel(
    tp_ref, q_ref, k_ref, v_ref, kp_ref, vp_ref, segq_ref, segk_ref, near_ref, far_ref, oin, login, o_ref, log_ref
):
    keys = [
        jnp.concatenate([k_ref[...], segk_ref[pl.ds(0, HALF), :]], axis=1),
        jnp.concatenate([kp_ref[...], segk_ref[pl.ds(HALF, HALF), :]], axis=1),
    ]
    values_t = [v_ref[...].T, vp_ref[...].T]
    biases = half_biases(near_ref, far_ref, tp_ref[0] == 0)
    attended, logs = attend_forward_block(q_ref[...], segq_ref[...], keys, values_t, biases)
    o_ref[...] = attended
    log_ref[0, 0:2, :] = logs


def attend_forward(tp, qkv, kv_par, segq, segk, bias):
    tokens = qkv.shape[0]
    width = qkv.shape[1] // 3
    pairs = width // LANES
    out_shape = (
        jax.ShapeDtypeStruct((tokens, width), BF16),
        jax.ShapeDtypeStruct((pairs, 8, tokens), F32),
    )
    unit = 4 * HALF * HALF * 256 * 2
    attended, logs = call(
        attend_full_kernel,
        (pairs,),
        [
            pl.BlockSpec((ROW, LANES), lambda p: (0, p)),
            pl.BlockSpec((ROW, LANES), lambda p: (0, pairs + p)),
            pl.BlockSpec((ROW, LANES), lambda p: (0, 2 * pairs + p)),
            pl.BlockSpec((ROW, LANES), lambda p: (0, 0)),
            pl.BlockSpec((ROW, LANES), lambda p: (0, 0)),
        ]
        + bias_specs(),
        (
            pl.BlockSpec((ROW, LANES), lambda p: (0, p)),
            pl.BlockSpec((1, 8, ROW), lambda p: (p, 0, 0)),
        ),
        out_shape,
        flops=unit * 4 * pairs,
        moved=bias[0].size * 4,
    )(qkv, qkv, qkv, segq, segk, *bias)
    flip = pairs // 2
    return call(
        attend_half_kernel,
        (pairs,),
        [
            pl.BlockSpec((HALF, LANES), lambda p, *_: (2, p)),
            pl.BlockSpec((HALF, LANES), lambda p, *_: (2, pairs + p)),
            pl.BlockSpec((HALF, LANES), lambda p, *_: (2, 2 * pairs + p)),
            pl.BlockSpec((HALF, LANES), lambda p, *_: (0, lax.rem(p + flip, pairs))),
            pl.BlockSpec((HALF, LANES), lambda p, *_: (0, pairs + lax.rem(p + flip, pairs))),
            pl.BlockSpec((HALF, LANES), lambda p, *_: (2, 0)),
            pl.BlockSpec((ROW, LANES), lambda p, *_: (1, 0)),
        ]
        + bias_specs()
        + [pl.BlockSpec(memory_space=pl.ANY), pl.BlockSpec(memory_space=pl.ANY)],
        (
            pl.BlockSpec((HALF, LANES), lambda p, *_: (2, p)),
            pl.BlockSpec((1, 8, HALF), lambda p, *_: (p, 0, 2)),
        ),
        out_shape,
        prefetch=1,
        aliases={10: 0, 11: 1},
        flops=unit * 2 * pairs,
        moved=bias[0].size * 4,
    )(tp, qkv, qkv, qkv, kv_par, kv_par, segq, segk, *bias, attended, logs)


def ffn_kernel(
    att_ref, woo_ref, wop_ref, x_ref, oh_ref, tab_ref, guo_ref, gup_ref, wdo_ref, wdp_ref,
    head_ref, emb_ref, flag_ref, shifted_ref, lifted_ref, middle, normed, acc,
):
    step = pl.program_id(0)
    tokens, width = x_ref.shape
    half = woo_ref.shape[0]
    blocks = tokens // HALF

    @pl.when(step == 0)
    def _():
        def body(i):
            rows = pl.ds(pl.multiple_of(i * HALF, HALF), HALF)
            branch = mm(att_ref[rows, :half], woo_ref[...]) + mm(att_ref[rows, half:], wop_ref[...])
            pick = oh_ref[rows, :]
            mid = x_ref[rows, :].astype(F32) + mm(pick, tab_ref[:, 2 * width : 3 * width]) * branch
            middle[rows, :] = mid
            hat, _ = norm_parts(mid)
            scale = mm(pick, tab_ref[:, 3 * width : 4 * width])
            shift = mm(pick, tab_ref[:, 4 * width : 5 * width])
            normed[rows, :] = (hat * scale + shift).astype(BF16)
            acc[rows, :] = jnp.zeros((HALF, width), F32)

        block_loop(blocks, body)

    def body(i):
        rows = pl.ds(pl.multiple_of(i * HALF, HALF), HALF)
        total = acc[rows, :]
        for gu, wd in ((guo_ref, wdo_ref), (gup_ref, wdp_ref)):
            gate = mm(normed[rows, :], gu[0])
            up = mm(normed[rows, :], gu[1])
            hidden = (gate * jax.nn.sigmoid(gate) * up).astype(BF16)
            total = total + mm(hidden, wd[...])
        acc[rows, :] = total

    block_loop(blocks, body)

    @pl.when(step == pl.num_programs(0) - 1)
    def _():
        def body(i):
            rows = pl.ds(pl.multiple_of(i * HALF, HALF), HALF)
            gate = mm(oh_ref[rows, :], tab_ref[:, 5 * width : 6 * width])
            first = middle[rows, :] + gate * acc[rows, :]
            high = first.astype(BF16)
            rest = (first - high.astype(F32)).astype(BF16)
            coords = mm_nt(high, head_ref[...]) + mm_nt(rest, head_ref[...])
            lifted = coords * flag_ref[rows, :]
            lifted_ref[rows, :] = lifted
            high = lifted.astype(BF16)
            rest = (lifted - high.astype(F32)).astype(BF16)
            moved = mm(high, emb_ref[...]) + mm(rest, emb_ref[...])
            shifted_ref[rows, :] = x_ref[rows, :].astype(F32) + moved

        block_loop(blocks, body)


def ffn_specs(att, woo, x, pick, table):
    tokens, width = x.shape
    chunk = FFC
    return [
        whole(*att.shape),
        whole(*woo.shape),
        whole(*woo.shape),
        whole(tokens, width),
        whole(*pick.shape),
        whole(*table.shape),
        pl.BlockSpec((2, width, chunk), lambda j, *_: (0, 0, j)),
        pl.BlockSpec((2, width, chunk), lambda j, *_: (0, 0, j)),
        pl.BlockSpec((chunk, width), lambda j, *_: (j, 0)),
        pl.BlockSpec((chunk, width), lambda j, *_: (j, 0)),
    ]


def ffn_forward(att, woo, wop, x, pick, table, guo, gup, wdo, wdp, head, emb, flags):
    tokens, width = x.shape
    hidden = wdo.shape[0]
    return call(
        ffn_kernel,
        (hidden // FFC,),
        ffn_specs(att, woo, x, pick, table)
        + [whole(*head.shape), whole(*emb.shape), whole(*flags.shape)],
        (whole(tokens, width), whole(tokens, LANES)),
        (
            jax.ShapeDtypeStruct((tokens, width), F32),
            jax.ShapeDtypeStruct((tokens, LANES), F32),
        ),
        [
            pltpu.VMEM((tokens, width), F32),
            pltpu.VMEM((tokens, width), BF16),
            pltpu.VMEM((tokens, width), F32),
        ],
        flops=2 * tokens * width * (6 * hidden + width),
        moved=12 * hidden * width + 6 * tokens * width,
    )(att, woo, wop, x, pick, table, guo, gup, wdo, wdp, head, emb, flags)


def turn_kernel(
    tp_ref, att_ref, woo_ref, wop_ref, x_ref, oh_ref, tab_ref, guo_ref, gup_ref, wdo_ref, wdp_ref,
    g_ref, oht_ref,
    outo_ref, outp_ref, gmid_ref, gatt_ref, go_ref, gp_ref, goo_ref, gop_ref, sumo_ref, sump_ref,
    sums_ref, middle, hats, branches, normed, normed_t, gmixed, gmixed_t, mixed, gnormed, hid, dgate, dup,
):
    step = pl.program_id(0)
    tokens, width = x_ref.shape
    half = woo_ref.shape[0]
    blocks = tokens // HALF

    @pl.when(step == 0)
    def _():
        def body(i):
            rows = pl.ds(pl.multiple_of(i * HALF, HALF), HALF)
            branch = mm(att_ref[rows, :half], woo_ref[...]) + mm(att_ref[rows, half:], wop_ref[...])
            branches[rows, :] = branch
            pick = oh_ref[rows, :]
            mid = x_ref[rows, :] + mm(pick, tab_ref[:, 2 * width : 3 * width]) * branch
            middle[rows, :] = mid
            hat, _ = norm_parts(mid)
            scale = mm(pick, tab_ref[:, 3 * width : 4 * width])
            shift = mm(pick, tab_ref[:, 4 * width : 5 * width])
            normed[rows, :] = (hat * scale + shift).astype(BF16)
            gate = mm(pick, tab_ref[:, 5 * width : 6 * width])
            gmixed[rows, :] = (g_ref[rows, :].astype(F32) * gate).astype(BF16)
            mixed[rows, :] = jnp.zeros((HALF, width), F32)
            gnormed[rows, :] = jnp.zeros((HALF, width), F32)

        block_loop(blocks, body)
        normed_t[...] = normed[...].T
        gmixed_t[...] = gmixed[...].T

    for gu, wd, out in ((gup_ref, wdp_ref, gp_ref), (guo_ref, wdo_ref, go_ref)):

        def body(i):
            rows = pl.ds(pl.multiple_of(i * HALF, HALF), HALF)
            gate = mm(normed[rows, :], gu[0])
            up = mm(normed[rows, :], gu[1])
            ghid = mm_nt(gmixed[rows, :], wd[...])
            s = jax.nn.sigmoid(gate)
            silu = gate * s
            hidden = (silu * up).astype(BF16)
            hid[rows, :] = hidden
            mixed[rows, :] += mm(hidden, wd[...])
            dg = (ghid * up * (s + silu * (1.0 - s))).astype(BF16)
            du = (ghid * silu).astype(BF16)
            dgate[rows, :] = dg
            dup[rows, :] = du
            gnormed[rows, :] += mm_nt(dg, gu[0]) + mm_nt(du, gu[1])

        block_loop(blocks, body)
        out[0, 0] = mm(normed_t[...], dgate[...]).astype(BF16)
        out[1, 0] = mm(normed_t[...], dup[...]).astype(BF16)
        out[2, 0] = mm(gmixed_t[...], hid[...]).astype(BF16)

    @pl.when(step == pl.num_programs(0) - 1)
    def _():
        first_core = tp_ref[0] == 0
        sums_ref[...] = jnp.zeros(sums_ref.shape, F32)

        def body(i):
            rows = pl.ds(pl.multiple_of(i * HALF, HALF), HALF)
            pick = oh_ref[rows, :]
            turn = oht_ref[i]
            g = g_ref[rows, :].astype(F32)
            total = mixed[rows, :]
            gate = mm(pick, tab_ref[:, 5 * width : 6 * width])
            mid = middle[rows, :]
            result = (mid + gate * total).astype(BF16)
            low, high = result[:, : width // 2], result[:, width // 2 :]
            outo_ref[rows, :] = jnp.where(first_core, low, high)
            outp_ref[rows, :] = jnp.where(first_core, high, low)
            sums_ref[0] += mm(turn, (g * total).astype(BF16))
            hat, inv_std = norm_parts(mid)
            gn = gnormed[rows, :]
            sums_ref[1] += mm(turn, (gn * hat).astype(BF16))
            sums_ref[2] += mm(turn, gn.astype(BF16))
            scale = mm(pick, tab_ref[:, 3 * width : 4 * width])
            gmid = g + norm_back(gn * scale, hat, inv_std)
            gmid_ref[rows, :] = gmid
            sums_ref[3] += mm(turn, (gmid * branches[rows, :]).astype(BF16))
            gbranch = (gmid * mm(pick, tab_ref[:, 2 * width : 3 * width])).astype(BF16)
            gmixed[rows, :] = gbranch
            gatt_ref[rows, :half] = mm_nt(gbranch, woo_ref[...]).astype(BF16)
            gatt_ref[rows, half:] = mm_nt(gbranch, wop_ref[...]).astype(BF16)

        block_loop(blocks, body)
        gmixed_t[...] = gmixed[...].T
        goo_ref[...] = mm(gmixed_t[...], att_ref[:, :half]).astype(BF16)
        gop_ref[...] = mm(gmixed_t[...], att_ref[:, half:]).astype(BF16)
        low, high = sums_ref[:, :, : width // 2], sums_ref[:, :, width // 2 :]
        sumo_ref[...] = jnp.where(first_core, low, high)
        sump_ref[...] = jnp.where(first_core, high, low)


def ffn_turn(tp, att, woo, wop, x, pick, table, guo, gup, wdo, wdp, g, pick_t):
    tokens, width = x.shape
    half = woo.shape[0]
    hidden = wdo.shape[0]
    grads = jax.ShapeDtypeStruct((3, hidden // FFC, width, FFC), BF16)
    grads_spec = pl.BlockSpec((3, 1, width, FFC), lambda j, *_: (0, j, 0, 0))
    return call(
        turn_kernel,
        (hidden // FFC,),
        ffn_specs(att, woo, x, pick, table) + [whole(tokens, width), whole(*pick_t.shape)],
        (
            whole(tokens, width // 2),
            whole(tokens, width // 2),
            whole(tokens, width),
            whole(tokens, width),
            grads_spec,
            grads_spec,
            whole(width, half),
            whole(width, half),
            whole(4, 16, width // 2),
            whole(4, 16, width // 2),
        ),
        (
            jax.ShapeDtypeStruct((tokens, width // 2), BF16),
            jax.ShapeDtypeStruct((tokens, width // 2), BF16),
            jax.ShapeDtypeStruct((tokens, width), F32),
            jax.ShapeDtypeStruct((tokens, width), BF16),
            grads,
            grads,
            jax.ShapeDtypeStruct((width, half), BF16),
            jax.ShapeDtypeStruct((width, half), BF16),
            jax.ShapeDtypeStruct((4, 16, width // 2), F32),
            jax.ShapeDtypeStruct((4, 16, width // 2), F32),
        ),
        [
            pltpu.VMEM((4, 16, width), F32),
            pltpu.VMEM((tokens, width), F32),
            pltpu.VMEM((8, LANES), F32),
            pltpu.VMEM((tokens, width), F32),
            pltpu.VMEM((tokens, width), BF16),
            pltpu.VMEM((width, tokens), BF16),
            pltpu.VMEM((tokens, width), BF16),
            pltpu.VMEM((width, tokens), BF16),
            pltpu.VMEM((tokens, width), F32),
            pltpu.VMEM((tokens, width), F32),
            pltpu.VMEM((tokens, FFC), BF16),
            pltpu.VMEM((tokens, FFC), BF16),
            pltpu.VMEM((tokens, FFC), BF16),
        ],
        prefetch=1,
        flops=2 * tokens * width * (18 * hidden + 3 * width),
        moved=24 * hidden * width + 12 * tokens * width,
    )(tp, att, woo, wop, x, pick, table, guo, gup, wdo, wdp, g, pick_t)


def attend_back_block(q, segq, gout, logs, keys, keys_t, values, biases, bias_sums, gkeys, gvalues):
    half = LANES // 2
    masks = lane_masks()
    scale = half**-0.5
    scaled = q * jnp.asarray(scale, BF16)
    gqs = []
    for h in range(2):
        query_low = scaled * masks[h]
        query = jnp.concatenate([query_low, segq], axis=1)
        gheads = gout * masks[h]
        chances = [jnp.exp(bias(h, mm_nt(key, query)) - logs[h : h + 1, :]) for key, bias in zip(keys, biases)]
        gchances = [mm_nt(value, gheads) for value in values]
        centre = sum(jnp.sum(p * gp, axis=0, keepdims=True) for p, gp in zip(chances, gchances))
        gq = 0.0
        for b, (p, gp) in enumerate(zip(chances, gchances)):
            gs = p * (gp - centre)
            bias_sums[b](h, gs)
            low = gs.astype(BF16)
            gvalues[b] = gvalues[b] + mm(p.astype(BF16), gheads)
            gkeys[b] = gkeys[b] + mm(low, query_low)
            gq = gq + mm(keys_t[b][h * half : (h + 1) * half, :], low)
        gqs.append(gq * scale)
    return jnp.concatenate(gqs, axis=0).T.astype(BF16)


def diagonal_sums(tile):
    size, wide = tile.shape
    rows = lax.broadcasted_iota(jnp.int32, (size, size), 0)
    cols = lax.broadcasted_iota(jnp.int32, (size, size), 1)
    turn = (rows + cols == size - 1).astype(F32).astype(BF16)
    high = tile.astype(BF16)
    rest = (tile - high.astype(F32)).astype(BF16)
    flipped = mm(turn, high) + mm(turn, rest)
    padded = jnp.concatenate([flipped, jnp.zeros((size, wide), F32)], axis=1)
    rolled = pltpu.roll(padded, 0, axis=1, stride=1, stride_axis=0)
    return jnp.sum(rolled, axis=0, keepdims=True)


def far_sums(tile, later):
    whole_sum = jnp.sum(jnp.sum(tile, axis=0, keepdims=True), axis=1, keepdims=True)
    edge = tile[:RADIUS, LANES:] if later else tile[HALF - RADIUS :, :LANES]
    sums = diagonal_sums(edge)
    rest = whole_sum - jnp.sum(sums, axis=1, keepdims=True)
    row = jnp.concatenate([sums, jnp.zeros((1, 2 * HALF - sums.shape[1]), F32)], axis=1)
    row = jnp.broadcast_to(row, (8, 2 * HALF))
    if later:
        row = pltpu.roll(row, 2 * HALF - LANES - RADIUS, axis=1)
    lanes = lax.broadcasted_iota(jnp.int32, (1, 2 * HALF), 1)
    return row[:1] + jnp.where(lanes == (0 if later else 2 * HALF - 2), rest, 0.0)


def attend_full_back_kernel(
    q_ref, k_ref, v_ref, g_ref, log_ref, segq_ref, segk_ref, near_ref, far_ref, o_ref, diag_ref, sums
):
    keys, keys_t, values = [], [], []
    for b in range(2):
        rows = pl.ds(b * HALF, HALF)
        key = k_ref[rows, :]
        keys.append(jnp.concatenate([key, segk_ref[rows, :]], axis=1))
        keys_t.append(key.T)
        values.append(v_ref[rows, :])
    gkeys, gvalues = [0.0, 0.0], [0.0, 0.0]
    sums[...] = jnp.zeros(sums.shape, F32)
    for qb in range(2):
        rows = pl.ds(qb * HALF, HALF)
        biases = full_biases(near_ref, far_ref, qb)

        def add(h, gs):
            sums[h] += gs

        def put(h, gs, later):
            row = 3 * h + (0 if later else 2)
            diag_ref[0, row : row + 1, :] = far_sums(gs, later)

        adders = [add, functools.partial(put, later=True)] if qb == 0 else [functools.partial(put, later=False), add]
        o_ref[0, rows, :] = attend_back_block(
            q_ref[rows, :], segq_ref[rows, :], g_ref[rows, :], log_ref[0, 0:2, rows],
            keys, keys_t, values, biases, adders, gkeys, gvalues,
        )
    for b in range(2):
        rows = pl.ds(b * HALF, HALF)
        o_ref[1, rows, :] = gkeys[b].astype(BF16)
        o_ref[2, rows, :] = gvalues[b].astype(BF16)
    for h in range(2):
        diag_ref[0, 3 * h + 1 : 3 * h + 2, :] = diagonal_sums(sums[h])


def attend_half_back_kernel(
    tp_ref, q_ref, k_ref, v_ref, kp_ref, vp_ref, g_ref, log_ref, segq_ref, segk_ref, near_ref, far_ref,
    o_ref, par_ref, diag_ref,
):
    keys, keys_t, values = [], [], []
    for b, (k, v) in enumerate(((k_ref, v_ref), (kp_ref, vp_ref))):
        key = k[...]
        keys.append(jnp.concatenate([key, segk_ref[pl.ds(b * HALF, HALF), :]], axis=1))
        keys_t.append(key.T)
        values.append(v[...])
    first = tp_ref[0] == 0
    biases = half_biases(near_ref, far_ref, first)
    gkeys, gvalues = [0.0, 0.0], [0.0, 0.0]

    def put(h, gs, b):
        sums = jnp.where(first, far_sums(gs, True), far_sums(gs, False)) if b else diagonal_sums(gs)
        diag_ref[0, 2 * h + b : 2 * h + b + 1, :] = sums

    adders = [functools.partial(put, b=b) for b in range(2)]
    o_ref[0] = attend_back_block(
        q_ref[...], segq_ref[...], g_ref[...], log_ref[0, 0:2, :],
        keys, keys_t, values, biases, adders, gkeys, gvalues,
    )
    o_ref[1] = gkeys[0].astype(BF16)
    o_ref[2] = gvalues[0].astype(BF16)
    par_ref[0] = gkeys[1].astype(BF16)
    par_ref[1] = gvalues[1].astype(BF16)


def attend_half_back(tp, qkv, kv_par, g, logs, segq, segk, bias):
    width = qkv.shape[1] // 3
    pairs = width // LANES
    flip = pairs // 2
    return call(
        attend_half_back_kernel,
        (pairs,),
        [
            pl.BlockSpec((HALF, LANES), lambda p, *_: (2, p)),
            pl.BlockSpec((HALF, LANES), lambda p, *_: (2, pairs + p)),
            pl.BlockSpec((HALF, LANES), lambda p, *_: (2, 2 * pairs + p)),
            pl.BlockSpec((HALF, LANES), lambda p, *_: (0, lax.rem(p + flip, pairs))),
            pl.BlockSpec((HALF, LANES), lambda p, *_: (0, pairs + lax.rem(p + flip, pairs))),
            pl.BlockSpec((HALF, LANES), lambda p, *_: (2, p)),
            pl.BlockSpec((1, 8, HALF), lambda p, *_: (p, 0, 2)),
            pl.BlockSpec((HALF, LANES), lambda p, *_: (2, 0)),
            pl.BlockSpec((ROW, LANES), lambda p, *_: (1, 0)),
        ]
        + bias_specs(),
        (
            pl.BlockSpec((3, HALF, LANES), lambda p, *_: (0, 0, p)),
            pl.BlockSpec((2, HALF, LANES), lambda p, *_: (0, 0, p)),
            pl.BlockSpec((1, 8, ROW), lambda p, *_: (p, 0, 0)),
        ),
        (
            jax.ShapeDtypeStruct((3, HALF, width), BF16),
            jax.ShapeDtypeStruct((2, HALF, width), BF16),
            jax.ShapeDtypeStruct((pairs, 8, ROW), F32),
        ),
        prefetch=1,
        flops=10 * HALF * HALF * 256 * 2 * pairs,
        moved=bias[0].size * 4,
    )(tp, qkv, qkv, qkv, kv_par, kv_par, g, logs, segq, segk, *bias)


def attend_full_back(qkv, g, logs, segq, segk, bias):
    width = qkv.shape[1] // 3
    pairs = width // LANES
    return call(
        attend_full_back_kernel,
        (pairs,),
        [
            pl.BlockSpec((ROW, LANES), lambda p: (0, p)),
            pl.BlockSpec((ROW, LANES), lambda p: (0, pairs + p)),
            pl.BlockSpec((ROW, LANES), lambda p: (0, 2 * pairs + p)),
            pl.BlockSpec((ROW, LANES), lambda p: (0, p)),
            pl.BlockSpec((1, 8, ROW), lambda p: (p, 0, 0)),
            pl.BlockSpec((ROW, LANES), lambda p: (0, 0)),
            pl.BlockSpec((ROW, LANES), lambda p: (0, 0)),
        ]
        + bias_specs(),
        (
            pl.BlockSpec((3, ROW, LANES), lambda p: (0, 0, p)),
            pl.BlockSpec((1, 8, ROW), lambda p: (p, 0, 0)),
        ),
        (
            jax.ShapeDtypeStruct((3, ROW, width), BF16),
            jax.ShapeDtypeStruct((pairs, 8, ROW), F32),
        ),
        [pltpu.VMEM((2, HALF, HALF), F32)],
        flops=20 * HALF * HALF * 256 * 2 * pairs,
        moved=bias[0].size * 4,
    )(qkv, qkv, qkv, g, logs, segq, segk, *bias)


def joined_rows(full_ref, half_ref, recv_ref, step, rows_in):
    half = recv_ref.shape[2] // 2
    rows_in[pl.ds(0, ROW), :] = full_ref[0]
    keep = (step > 0).astype(F32).astype(BF16)
    recv = jnp.concatenate([recv_ref[0, :, half:], recv_ref[0, :, :half]], axis=1)
    rows_in[pl.ds(ROW, HALF), :] = half_ref[0] + recv * keep


def qkv_weights_kernel(
    x_ref, oh_ref, tab_ref, full_ref, half_ref, recv_ref, outo_ref, outp_ref, go_ref, gp_ref, normed, normed_t, rows_in
):
    step = pl.program_id(0)
    tokens, width = x_ref.shape
    half = width // 2

    @pl.when(step == 0)
    def _():
        def body(i):
            rows = pl.ds(pl.multiple_of(i * HALF, HALF), HALF)
            hat, _ = norm_parts(x_ref[rows, :])
            pick = oh_ref[rows, :]
            scale = mm(pick, tab_ref[:, :width])
            shift = mm(pick, tab_ref[:, width : 2 * width])
            normed[rows, :] = (hat * scale + shift).astype(BF16)

        block_loop(tokens // HALF, body)
        normed_t[...] = normed[...].T

    joined_rows(full_ref, half_ref, recv_ref, step, rows_in)
    go_ref[0, :, :half] = mm(normed_t[...], rows_in[:, :half]).astype(BF16)
    gp_ref[0, :, :half] = mm(normed_t[...], rows_in[:, half:]).astype(BF16)
    go_ref[0, :, half:] = outo_ref[...]
    gp_ref[0, :, half:] = outp_ref[...]


def row_specs(width):
    return [
        pl.BlockSpec((1, ROW, width), lambda j, *_: (j, 0, 0)),
        pl.BlockSpec((1, HALF, width), lambda j, *_: (j, 0, 0)),
        pl.BlockSpec((1, HALF, width), lambda j, *_: (jnp.maximum(j - 1, 0), 0, 0)),
    ]


def qkv_weights(x, pick, table, full, half_rows, recv, out_own, out_par):
    tokens, width = x.shape
    half = width // 2
    third = half // 3
    spec = pl.BlockSpec((1, width, half + third), lambda j: (j, 0, 0))
    shape = jax.ShapeDtypeStruct((3, width, half + third), BF16)
    out_spec = pl.BlockSpec((width, third), lambda j: (0, j))
    return call(
        qkv_weights_kernel,
        (3,),
        [whole(tokens, width), whole(*pick.shape), whole(*table.shape)] + row_specs(width) + [out_spec, out_spec],
        (spec, spec),
        (shape, shape),
        [
            pltpu.VMEM((tokens, width), BF16),
            pltpu.VMEM((width, tokens), BF16),
            pltpu.VMEM((tokens, width), BF16),
        ],
        flops=2 * tokens * width * 6 * half,
        moved=16 * half * width + 12 * tokens * width,
    )(x, pick, table, full, half_rows, recv, out_own, out_par)


def qkv_back_kernel(
    tp_ref, x_ref, oh_ref, tab_ref, full_ref, half_ref, recv_ref, wo_ref, wp_ref, gmid_ref, lifted_ref, oht_ref,
    gino_ref, ginp_ref, sumo_ref, sump_ref, hats, stds, rows_in, acc, sums,
):
    step = pl.program_id(0)
    tokens, width = x_ref.shape
    half = wo_ref.shape[1]
    blocks = tokens // HALF

    @pl.when(step == 0)
    def _():
        def body(i):
            rows = pl.ds(pl.multiple_of(i * HALF, HALF), HALF)
            hat, inv_std = norm_parts(x_ref[rows, :])
            hats[rows, :] = hat
            stds[rows, :] = inv_std
            acc[rows, :] = jnp.zeros((HALF, width), F32)

        block_loop(blocks, body)

    joined_rows(full_ref, half_ref, recv_ref, step, rows_in)

    def body(i):
        rows = pl.ds(pl.multiple_of(i * HALF, HALF), HALF)
        grad = rows_in[rows, :]
        acc[rows, :] += mm_nt(grad[:, :half], wo_ref[...]) + mm_nt(grad[:, half:], wp_ref[...])

    block_loop(blocks, body)

    @pl.when(step == pl.num_programs(0) - 1)
    def _():
        first_core = tp_ref[0] == 0
        sums[...] = jnp.zeros(sums.shape, F32)

        def body(i):
            rows = pl.ds(pl.multiple_of(i * HALF, HALF), HALF)
            turn = oht_ref[i]
            gn = acc[rows, :]
            hat = hats[rows, :]
            sums[0] += mm(turn, (gn * hat).astype(BF16))
            sums[1] += mm(turn, gn.astype(BF16))
            scale = mm(oh_ref[rows, :], tab_ref[:, :width])
            grad = gmid_ref[rows, :] + norm_back(gn * scale, hat, stds[rows, :])
            low, high = grad[:, : width // 2], grad[:, width // 2 :]
            gino_ref[rows, :] = jnp.where(first_core, low, high)
            ginp_ref[rows, :] = jnp.where(first_core, high, low)
            lifted_t = lifted_ref[rows, :].astype(BF16).T
            sums[2] += mm(lifted_t[:16, :], grad.astype(BF16))

        block_loop(blocks, body)
        low, high = sums[:, :, : width // 2], sums[:, :, width // 2 :]
        sumo_ref[...] = jnp.where(first_core, low, high)
        sump_ref[...] = jnp.where(first_core, high, low)


def qkv_back(tp, x, pick, table, full, half_rows, recv, wo, wp, gmid, lifted, pick_t):
    tokens, width = x.shape
    half = wo.shape[1] // 3
    return call(
        qkv_back_kernel,
        (3,),
        [whole(tokens, width), whole(*pick.shape), whole(*table.shape)]
        + row_specs(width)
        + [
            pl.BlockSpec((width, half), lambda j, *_: (0, j)),
            pl.BlockSpec((width, half), lambda j, *_: (0, j)),
            whole(tokens, width),
            whole(tokens, LANES),
            whole(*pick_t.shape),
        ],
        (
            whole(tokens, width // 2),
            whole(tokens, width // 2),
            whole(3, 16, width // 2),
            whole(3, 16, width // 2),
        ),
        (
            jax.ShapeDtypeStruct((tokens, width // 2), F32),
            jax.ShapeDtypeStruct((tokens, width // 2), F32),
            jax.ShapeDtypeStruct((3, 16, width // 2), F32),
            jax.ShapeDtypeStruct((3, 16, width // 2), F32),
        ),
        [
            pltpu.VMEM((tokens, width), F32),
            pltpu.VMEM((tokens, 1), F32),
            pltpu.VMEM((tokens, width), BF16),
            pltpu.VMEM((tokens, width), F32),
            pltpu.VMEM((3, 16, width), F32),
        ],
        prefetch=1,
        flops=2 * tokens * width * 6 * half,
        moved=12 * half * width + 16 * tokens * width,
    )(tp, x, pick, table, full, half_rows, recv, wo, wp, gmid, lifted, pick_t)


def chain_joins(first_core):
    row = lax.broadcasted_iota(jnp.int32, (16, 16), 0)
    col = lax.broadcasted_iota(jnp.int32, (16, 16), 1)
    lower = ((row == col) & (row < 2 * SEGS)).astype(F32)
    upper = (
        ((row == col) & (row >= SEGS) & (row < 2 * SEGS)) | ((row == col + 2 * SEGS) & (row < 3 * SEGS))
    ).astype(F32)
    return jnp.where(first_core, lower, upper), jnp.where(first_core, upper, lower)


def join_chains(tp_ref, own_ref, came_ref, slope_ref, count, o_ref):
    own_join, came_join = chain_joins(tp_ref[0] == 0)
    cols = own_ref.shape[2]
    for i in range(count):
        both = jnp.dot(own_join, own_ref[i], precision=HIGHEST, preferred_element_type=F32)
        both = both + jnp.dot(came_join, came_ref[i], precision=HIGHEST, preferred_element_type=F32)
        lanes = pl.ds(i * cols, cols)
        o_ref[0:16, lanes] = (both * slope_ref[:, lanes]).astype(BF16)


def early_kernel(tp_ref, own_ref, came_ref, slope_ref, embed_ref, o_ref):
    join_chains(tp_ref, own_ref, came_ref, slope_ref, 4, o_ref)
    o_ref[:, pl.ds(4 * own_ref.shape[2], embed_ref.shape[1])] = embed_ref[...]


def late_kernel(tp_ref, own_ref, came_ref, slope_ref, bins_ref, o_ref):
    cols = own_ref.shape[2]
    join_chains(tp_ref, own_ref, came_ref, slope_ref, 2, o_ref)
    o_ref[:, pl.ds(2 * cols, LANES)] = bins_ref[...].astype(BF16)
    coords = own_ref[2] + came_ref[2]
    parts = [coords[i : i + 1, j : j + LANES] for j in range(0, cols, LANES) for i in range(3)]
    parts.append(jnp.zeros((16 - len(parts), LANES), F32))
    o_ref[:, pl.ds(2 * cols + LANES, LANES)] = jnp.concatenate(parts, axis=0).astype(BF16)


def pack_rows(kernel, tp, own, came, slopes, extra, shape):
    return call(
        kernel,
        (1,),
        [whole(*own.shape), whole(*came.shape), whole(*slopes.shape), whole(*extra.shape)],
        whole(*shape),
        jax.ShapeDtypeStruct(shape, BF16),
        prefetch=1,
        flops=10**6,
        moved=10**5,
    )(tp, own, came, slopes, extra)


def closing_kernel(early_ref, late_ref, hat_ref, inv_ref, gain_ref, both_ref, *refs):
    ffn, attn, outs = refs[:2], refs[2:4], refs[4:]
    gu_ref, down_ref, qkv_ref, out_ref = outs[:4]
    w0_ref, b0_ref, w1_ref, w2_ref, b2_ref, w3_ref, b3_ref, w4_ref, w5_ref, b5_ref = outs[4:14]
    table_ref, pgain_ref, proj_ref, coord_ref = outs[14:]

    def total(pair, block):
        return pair[0][0, block].astype(F32) + pair[1][0, block].astype(F32)

    lanes = ffn[0].shape[3]
    chunks = down_ref.shape[1] // lanes
    for block in range(chunks):
        span = pl.ds(block * lanes, lanes)
        gu_ref[:, 0, span] = total(ffn, block)
        gu_ref[:, 1, span] = total(ffn, chunks + block)
        down_ref[:, span] = total(ffn, 2 * chunks + block)
    third = out_ref.shape[1] // 3
    for i in range(3):
        value = total(attn, i)
        qkv_ref[i] = value[:, : 3 * third]
        out_ref[:, i * third : (i + 1) * third] = value[:, 3 * third :]

    cols = coord_ref.shape[1]
    embed_t = early_ref[:, 4 * cols :].T
    parts = [late_ref[:, :cols], late_ref[:, cols : 2 * cols]] + [early_ref[:, i * cols : (i + 1) * cols] for i in range(4)]
    weights = [w0_ref, w1_ref, w5_ref, w3_ref, w4_ref, w2_ref]
    biases = [b0_ref, None, b5_ref, b3_ref, None, b2_ref]
    for part, weight, bias in zip(parts, weights, biases):
        weight[...] = mm(embed_t, part)
        if bias is not None:
            bias[...] = jnp.sum(part.astype(F32), axis=0)
    extra = late_ref[:, 2 * cols :].reshape(-1, 16, 2 * LANES)
    extra = jnp.sum(extra.astype(F32), axis=0)
    for i in range(cols // LANES):
        coord_ref[:, pl.ds(i * LANES, LANES)] = extra[3 * i : 3 * i + 3, LANES:]
    bins = extra[:, :LANES]
    hat = hat_ref[...]
    gain = gain_ref[...]
    proj = jnp.dot(bins, hat * gain, precision=HIGHEST, preferred_element_type=F32)
    proj_ref[...] = proj[: proj_ref.shape[0]]
    normed_grad = jnp.dot(bins.T, both_ref[...], precision=HIGHEST, preferred_element_type=F32)
    pgain_ref[...] = jnp.sum(normed_grad * hat, axis=0)
    table_ref[...] = norm_back(normed_grad * gain, hat, inv_ref[...])[: table_ref.shape[0]]


def closing(early, late, hat, inv_std, gain, both, ffn, attn, bins, heads):
    cols = (late.shape[1] - 2 * LANES) // 2
    embed = early.shape[1] - 4 * cols
    features = hat.shape[1]
    height, lanes = ffn[0].shape[2:]
    weight, bias = (embed, cols), (cols,)
    hidden = lanes * (ffn[0].shape[1] // 3)
    shapes = [(height, 2, hidden), (height, hidden), (3, height, cols), (height, cols)]
    shapes += [weight, bias, weight, weight, bias, weight, bias, weight, weight, bias]
    shapes += [(bins, features), (features,), (heads, features), (3, cols)]
    args = (early, late, hat, inv_std, gain, both, *ffn, *attn)
    return call(
        closing_kernel,
        (1,),
        [whole(*a.shape) for a in args],
        tuple(whole(*shape) for shape in shapes),
        tuple(jax.ShapeDtypeStruct(shape, F32) for shape in shapes),
        flops=10**8,
        moved=10**7,
    )(*args)


def halve_kernel(place_ref, *refs, plan, count):
    inputs, outs = refs[:count], refs[count:]
    for stream, (bit, sections) in enumerate(plan):
        sent_ref, kept_ref = outs[2 * stream], outs[2 * stream + 1]
        mine = (place_ref[0] >> bit) & 1
        done = 0
        for first, second, base, chunks, left in sections:
            spot = left.index(bit)
            shift = len(left) - 1
            half = 1 << shift

            def body(n, first=first, second=second, base=base, spot=spot, shift=shift, done=done, mine=mine):
                k = n & ((1 << shift) - 1)
                at = base + ((n >> shift) << (shift + 1)) + ((k >> spot) << (spot + 1)) + (k & ((1 << spot) - 1))
                for which, ref in ((1 - mine, sent_ref), (mine, kept_ref)):
                    block = at + (which << spot)
                    both = inputs[first][0, block].astype(F32) + inputs[second][0, block].astype(F32)
                    ref[0, done + n] = both.astype(BF16)

            block_loop(chunks * half, body)
            done += chunks * half


def halve(place, streams, bits):
    arrays, specs, plan, shapes = [], [], [], []

    def operand(array, index):
        for i, (seen, at) in enumerate(arrays):
            if seen is array and at == index:
                return i
        arrays.append((array, index))
        specs.append(pl.BlockSpec((1,) + array.shape[1:], lambda *_: (index, 0, 0, 0)))
        return len(arrays) - 1

    moved = 0
    for sections, bit in zip(streams, bits):
        entries, blocks = [], 0
        for own, i, came, k, base, chunks, left in sections:
            entries.append((operand(own, i), operand(came, k), base, chunks, left))
            blocks += chunks << (len(left) - 1)
        plan.append((bit, entries))
        shape = (1, blocks) + sections[0][0].shape[2:]
        shapes += [shape, shape]
        moved += 12 * blocks * shape[2] * shape[3]
    outs = call(
        functools.partial(halve_kernel, plan=plan, count=len(arrays)),
        (1,),
        specs,
        tuple(whole(*shape) for shape in shapes),
        tuple(jax.ShapeDtypeStruct(shape, BF16) for shape in shapes),
        prefetch=1,
        flops=10**6,
        moved=moved,
    )(place, *[array for array, _ in arrays])
    return list(outs[0::2]), list(outs[1::2])


def swap(values):
    return lax.ppermute(values, "tp", [(0, 1), (1, 0)])


def after(values, *others):
    return lax.optimization_barrier((values, *others))[0]


class Cube:
    def __init__(self, rows):
        self.bits = rows.bit_length() - 1
        assert rows == 1 << self.bits
        self.place = lax.axis_index("rows").reshape(1).astype(jnp.int32)
        self.perms = [[(i, i ^ (1 << b)) for i in range(rows)] for b in range(self.bits)]

    def turns(self):
        return [[(i + r) % 3 for i in range(3)] for r in range(3)]

    def gather(self, values, step):
        bit = (list(range(self.bits - 1, 1, -1)) + list(range(min(2, self.bits))))[step]
        came = lax.ppermute(values, "rows", self.perms[bit])
        return lax.optimization_barrier(jnp.concatenate([values, came], axis=0))


def next_sections(sections, kept, came, bit):
    made, base = [], 0
    for _, _, _, _, _, chunks, left in sections:
        left = [b for b in left if b != bit]
        made.append((kept, 0, came, 0, base, chunks, left))
        base += chunks << len(left)
    return made


def normalize(values):
    centre = jnp.mean(values, axis=-1, keepdims=True)
    shifted = values - centre
    spread = jnp.mean(shifted * shifted, axis=-1, keepdims=True)
    inv_std = lax.rsqrt(spread + EPSILON)
    return shifted * inv_std, inv_std


def three_parts(values):
    high = lax.reduce_precision(values, 8, 7)
    middle = lax.reduce_precision(values - high, 8, 7)
    low = values - high - middle
    return jnp.concatenate([high, middle, low], axis=0).astype(BF16)


def bias_base(heads):
    bins = heads.shape[1]
    low = lambda n: jnp.broadcast_to(heads[:, :1], (heads.shape[0], n))
    top = lambda n: jnp.broadcast_to(heads[:, bins - 1 :], (heads.shape[0], n))
    fill = HALF - RADIUS
    behind = jnp.concatenate([low(fill), heads[:, :RADIUS], low(HALF)], axis=1)
    same = jnp.concatenate([heads[:, RADIUS:], top(fill - 1), low(fill), heads[:, :RADIUS]], axis=1)
    ahead = jnp.concatenate([top(HALF), heads[:, RADIUS:], top(fill - 1)], axis=1)
    return jnp.stack([behind, same, ahead], axis=1)


def bins_of_diagonals():
    places = jnp.arange(ROW, dtype=jnp.int32)[None, :] - (HALF - 1)
    offsets = places + HALF * jnp.arange(-1, 2, dtype=jnp.int32)[:, None]
    bins = jnp.clip(offsets, -RADIUS, RADIUS) + RADIUS
    every = jnp.arange(2 * RADIUS + 1, dtype=jnp.int32)
    return (bins.reshape(-1)[:, None] == every[None, :]).astype(F32)


def per_device(
    layer_input,
    cotangent,
    chain_lengths,
    self_condition_flag,
    time_embedding,
    query_key_value,
    output_projection,
    attention_scale_weight,
    attention_scale_bias,
    attention_shift_weight,
    attention_gate_weight,
    attention_gate_bias,
    transition_scale_weight,
    transition_scale_bias,
    transition_shift_weight,
    transition_gate_weight,
    transition_gate_bias,
    gate_up_projection,
    down_projection,
    pair_table,
    pair_gain,
    pair_projection,
    coordinate_head,
    coordinate_embedding,
    rows,
):
    core = lax.axis_index("tp")
    first_core = core == 0
    tp = core.reshape(1).astype(jnp.int32)
    cols = layer_input.shape[1]
    width = query_key_value.shape[0]
    heads_here = pair_projection.shape[1]
    bins = pair_table.shape[0]
    cube = Cube(rows)

    def side_by_side(own, came, axis):
        return jnp.where(
            first_core, jnp.concatenate([own, came], axis), jnp.concatenate([came, own], axis)
        )

    def scatter_tokens(own, sent):
        came = swap(sent)
        lower = jnp.concatenate([own[:ROW], own[ROW:], came[ROW:], came[:ROW]], axis=0)
        upper = jnp.concatenate([came[:ROW], came[ROW:], own[ROW:], own[:ROW]], axis=0)
        return jnp.where(first_core, lower, upper)

    x_own, x_sent, cot_own, cot_sent = token_halves(tp, layer_input, cotangent)
    x = side_by_side(x_own, swap(x_sent), 1)
    qkv_own = query_key_value.reshape(width, -1)
    qkv_par = swap(qkv_own)

    packs = chain_lengths.shape[0]
    embed = jnp.pad(time_embedding, ((0, 0), (0, 1), (0, 0))).reshape(packs * SEGS, -1)
    embed_fill = jnp.pad(embed, ((0, 16 - packs * SEGS), (0, 0)))
    mods, early_slopes, late_slopes = modulations(
        embed_fill,
        [
            attention_scale_weight,
            attention_shift_weight,
            attention_gate_weight,
            transition_scale_weight,
            transition_shift_weight,
            transition_gate_weight,
        ],
        [
            b[None, :]
            for b in (attention_scale_bias, attention_gate_bias, transition_scale_bias, transition_gate_bias)
        ],
    )
    table = chain_table(tp, mods, swap(mods))
    mask_q, mask_k, pick, pick_t, flags = masks(tp, chain_lengths.reshape(-1), self_condition_flag)

    pair_hat, pair_inv = normalize(pair_table.astype(F32))
    gain = pair_gain.astype(F32)
    pair_normed = pair_hat * gain
    pair_both = jnp.concatenate([pair_projection, swap(pair_projection)], axis=1).astype(F32)
    bias_heads = jnp.transpose(jnp.dot(pair_normed, pair_both, precision=HIGHEST))
    bias_source = jnp.transpose(pair_both)
    bias = bias_tiles(bias_base(bias_heads))

    out_own = output_projection
    out_par = swap(output_projection)
    gu_own = jnp.transpose(gate_up_projection, (1, 0, 2))
    gu_par = swap(gu_own)
    down_own = down_projection
    down_par = swap(down_projection)
    coord = jnp.concatenate([coordinate_head, coordinate_embedding], axis=0)
    coord = side_by_side(coord, swap(coord), 1)
    fill = jnp.zeros((LANES - 3, width), BF16)
    head = jnp.concatenate([coord[:3], fill], axis=0)
    emb = jnp.concatenate([coord[3:], fill], axis=0)
    cot = side_by_side(cot_own, swap(cot_sent), 1)

    def attention(values):
        qkv = qkv_forward(values, pick, table, qkv_own, qkv_par)
        kv_par = swap(qkv[ROW:, width:])
        attended, logs = attend_forward(tp, qkv, kv_par, mask_q, mask_k, bias)
        return qkv, kv_par, attended, logs

    _, _, attended, _ = attention(x)
    shifted, lifted = ffn_forward(
        attended, out_own, out_par, x, pick, table, gu_own, gu_par, down_own, down_par, head, emb, flags
    )
    qkv, kv_par, attended, logs = attention(shifted)
    (
        result_own,
        result_sent,
        grad_middle,
        grad_attended,
        grads_own,
        grads_sent,
        grad_out_own,
        grad_out_sent,
        early_own,
        early_sent,
    ) = ffn_turn(
        tp, attended, out_own, out_par, shifted, pick, table, gu_own, gu_par, down_own, down_par, cot, pick_t
    )

    early_came = swap(early_sent)

    came_ffn = swap(grads_sent)
    half_grads, far_grads, diag_half = attend_half_back(
        tp, qkv, kv_par, grad_attended, logs, mask_q, mask_k, bias
    )
    came_grads = swap(far_grads)

    turns = cube.turns()
    every = list(range(cube.bits))
    height = width // rows
    slots = lambda values: values.reshape(3, -1, height, values.shape[-1])
    chunks = grads_own.shape[1]
    own_slots, came_slots = slots(grads_own), slots(came_ffn)
    ffn = [[(own_slots, i, came_slots, i, 0, chunks, every)] for i in range(3)]

    def one_round(streams, bits, *others):
        sent, kept = halve(cube.place, streams, bits)
        held = lax.optimization_barrier((*sent, *others))
        came = [lax.ppermute(v, "rows", cube.perms[bit]) for v, bit in zip(held, bits)]
        made = [next_sections(*parts) for parts in zip(streams, kept, came, bits)]
        return made, came, held[len(sent) :]

    early_came, _ = lax.optimization_barrier((early_came, diag_half))
    early = pack_rows(
        early_kernel, tp, early_own, early_came, early_slopes, embed_fill, (16, 4 * cols + embed.shape[1])
    )
    ffn, came, (mask_full, early, _) = one_round(ffn, turns[0], mask_q, early, diag_half)
    full_grads, diag_full = attend_full_back(qkv, grad_attended, logs, mask_full, mask_k, bias)
    early = cube.gather(early, 0)
    ffn, came, (pick_weights, early, _) = one_round(ffn, turns[1], pick, early, diag_full)
    gqkv_own, gqkv_sent = qkv_weights(
        shifted, pick_weights, table, full_grads, half_grads, came_grads, grad_out_own, grad_out_sent
    )
    early = cube.gather(early, 1)
    gqkv_sent, early, *_ = lax.optimization_barrier((gqkv_sent, early, *came))
    own_slots, came_slots = slots(gqkv_own), slots(swap(gqkv_sent))
    streams = [ffn[i] + [(own_slots, i, came_slots, i, 0, 1, every)] for i in range(3)]
    streams, came, (pick_back, early) = one_round(streams, turns[2], pick_weights, early)
    gin_own, gin_sent, late_own, late_sent = qkv_back(
        tp, shifted, pick_back, table, full_grads, half_grads, came_grads, qkv_own, qkv_par, grad_middle, lifted, pick_t
    )
    early = cube.gather(early, 2)
    late_sent, early, *_ = lax.optimization_barrier((late_sent, early, *came))

    diag_half = diag_half[:, :4].reshape(-1, 2, ROW)
    quiet = jnp.zeros_like(diag_half[:, 0])
    diag_far = diag_half[:, 1]
    diag = diag_full[:, :6].reshape(-1, 3, ROW) + jnp.stack(
        [
            jnp.where(first_core, diag_far, quiet),
            diag_half[:, 0],
            jnp.where(first_core, quiet, diag_far),
        ],
        axis=1,
    )
    grad_bins = jnp.dot(diag.reshape(-1, 3 * ROW), bins_of_diagonals(), precision=HIGHEST)
    came_bins = swap(grad_bins)
    grad_bins = grad_bins + jnp.concatenate([came_bins[heads_here:], came_bins[:heads_here]], axis=0)
    bins_fill = jnp.pad(grad_bins, ((0, 16 - 2 * heads_here), (0, LANES - bins)))

    late_came = swap(late_sent)
    late = pack_rows(late_kernel, tp, late_own, late_came, late_slopes, bins_fill, (16, 2 * cols + 2 * LANES))
    ffn = [[stream[0] for stream in streams]]
    attn = [stream[1:] for stream in streams]
    rest = list(range(3, cube.bits))
    waited = []
    for step in range(max(len(rest), 2)):
        now, bits = [], []
        if step < len(rest):
            now, bits = ffn, rest[step : step + 1]
        count = len(now)
        if step < 2:
            now, bits = now + attn, bits + turns[step]
        now, came, (late, *_) = one_round(now, bits, late, *waited)
        waited = came[:count]
        if count:
            ffn = now[:count]
        if step < 2:
            attn = now[count:]
        late = cube.gather(late, step)
    done = max(len(rest), 2)
    attn = [[section for stream in attn for section in stream]]
    for bit in rest:
        attn, came, (late,) = one_round(attn, [bit], late)
        if done < cube.bits:
            late = cube.gather(late, done)
            done += 1
    for step in range(done, cube.bits):
        late = cube.gather(late, step)
    for step in range(3, cube.bits):
        early = cube.gather(early, step)
    ffn_last = (ffn[0][0][0], ffn[0][0][2])
    attn_last = (attn[0][0][0], attn[0][0][2])

    layer_output = scatter_tokens(result_own, result_sent)
    input_gradient = scatter_tokens(gin_own, gin_sent)

    bins_pad = ((0, LANES - bins), (0, 0))
    grad_gu, grad_down, grad_qkv, grad_out, *conditioning = closing(
        early,
        late,
        jnp.pad(pair_hat, bins_pad),
        jnp.pad(pair_inv, bins_pad),
        gain[None, :],
        jnp.pad(bias_source, ((0, 16 - 2 * heads_here), (0, 0))),
        ffn_last,
        attn_last,
        bins,
        heads_here,
    )
    *conditioning, grad_table, grad_gain, grad_pair, coord_grad = conditioning
    return (
        layer_output,
        input_gradient,
        jnp.transpose(grad_qkv, (1, 0, 2)),
        grad_out.T,
        *conditioning,
        grad_gu,
        grad_down.T,
        grad_table,
        grad_gain,
        grad_pair.T,
        coord_grad,
    )


def solution(mesh):
    in_specs = (
        P("rows", "tp"),
        P("rows", "tp"),
        P("rows", None),
        P("rows"),
        P("rows", None, None),
        P(None, None, "tp"),
        P("tp", None),
        P(None, "tp"),
        P("tp"),
        P(None, "tp"),
        P(None, "tp"),
        P("tp"),
        P(None, "tp"),
        P("tp"),
        P(None, "tp"),
        P(None, "tp"),
        P("tp"),
        P(None, None, "tp"),
        P("tp", None),
        P(),
        P(),
        P(None, "tp"),
        P(None, "tp"),
        P(None, "tp"),
    )
    out_specs = (
        P("rows", "tp"),
        P("rows", "tp"),
        P("rows", None, "tp"),
        P("tp", "rows"),
        P(None, "tp"),
        P("tp"),
        P(None, "tp"),
        P(None, "tp"),
        P("tp"),
        P(None, "tp"),
        P("tp"),
        P(None, "tp"),
        P(None, "tp"),
        P("tp"),
        P("rows", None, "tp"),
        P("tp", "rows"),
        P(),
        P(),
        P(None, "tp"),
        P(None, "tp"),
    )
    return jax.shard_map(
        functools.partial(per_device, rows=mesh.shape["rows"]),
        mesh=mesh,
        in_specs=in_specs,
        out_specs=out_specs,
        check_vma=False,
    )
```

```python
import functools
import jax
import jax.numpy as jnp
from jax import lax
from jax.experimental import pallas as pl
from jax.experimental.pallas import tpu as pltpu
from jax.sharding import PartitionSpec as P

RADIUS = 32
ROW = 512
HALF = ROW // 2
SEGS = 5
EPSILON = 1e-05
MASKED = -1e30
HIGHEST = lax.Precision.HIGHEST
F32 = jnp.float32
BF16 = jnp.bfloat16
LANES = 128
FFC = 512
NT = (((1,), (1,)), ((), ()))
VMEM_LIMIT = 60 * 1024 * 1024


def mm(left, right):
    return jnp.dot(left, right, preferred_element_type=F32)


def mm_nt(left, right):
    return lax.dot_general(left, right, NT, preferred_element_type=F32)


def norm_parts(values):
    centre = jnp.mean(values, axis=1, keepdims=True)
    shifted = values - centre
    spread = jnp.mean(shifted * shifted, axis=1, keepdims=True)
    inv_std = lax.rsqrt(spread + EPSILON)
    return shifted * inv_std, inv_std


def norm_back(grad, hat, inv_std):
    first = jnp.mean(grad, axis=1, keepdims=True)
    second = jnp.mean(grad * hat, axis=1, keepdims=True)
    return inv_std * (grad - first - hat * second)


def block_loop(count, body):
    lax.fori_loop(0, count, lambda i, c: (body(i), c)[1], 0)


def call(kernel, grid, in_specs, out_specs, out_shape, scratch=(), prefetch=0, aliases=None, flops=0, moved=0):
    return pl.pallas_call(
        kernel,
        grid_spec=pltpu.PrefetchScalarGridSpec(
            num_scalar_prefetch=prefetch,
            grid=grid,
            in_specs=in_specs,
            out_specs=out_specs,
            scratch_shapes=list(scratch),
        ),
        out_shape=out_shape,
        input_output_aliases=aliases or {},
        compiler_params=pltpu.CompilerParams(
            dimension_semantics=("arbitrary",) * len(grid), vmem_limit_bytes=VMEM_LIMIT
        ),
        cost_estimate=pl.CostEstimate(flops=flops, transcendentals=0, bytes_accessed=moved),
    )


def whole(*shape):
    zeros = (0,) * len(shape)
    return pl.BlockSpec(shape, lambda *_: zeros)


def bias_kernel(base_ref, near_ref, far_ref):
    for d, height, start, out in (
        (1, HALF, 0, near_ref.at[0]),
        (0, RADIUS, 0, far_ref.at[0, 0]),
        (2, RADIUS, HALF - RADIUS, far_ref.at[0, 1]),
    ):
        rows = jnp.broadcast_to(base_ref[0, d : d + 1, :], (height, 2 * HALF))
        rolled = pltpu.roll(rows, start, axis=1, stride=1, stride_axis=0)
        out[...] = rolled[:, :HALF]


def bias_tiles(base):
    heads = base.shape[0]
    near, far = (heads, HALF, HALF), (heads, 2, RADIUS, HALF)
    return call(
        bias_kernel,
        (heads,),
        [pl.BlockSpec((1, 3, 2 * HALF), lambda h: (h, 0, 0))],
        (
            pl.BlockSpec((1,) + near[1:], lambda h: (h, 0, 0)),
            pl.BlockSpec((1,) + far[1:], lambda h: (h, 0, 0, 0)),
        ),
        (jax.ShapeDtypeStruct(near, F32), jax.ShapeDtypeStruct(far, F32)),
        moved=heads * HALF * HALF * 4,
        flops=10**7,
    )(base)


def bias_specs():
    return [
        pl.BlockSpec((2, HALF, HALF), lambda p, *_: (p, 0, 0)),
        pl.BlockSpec((2, 2, RADIUS, HALF), lambda p, *_: (p, 0, 0, 0)),
    ]


def add_near(near_ref, far_ref, h, scores):
    return scores + near_ref[h]


def add_later(near_ref, far_ref, h, scores):
    edge = far_ref[h, 0]
    return jnp.concatenate([scores[:RADIUS] + edge, scores[RADIUS:] + edge[RADIUS - 1 :, :1]], axis=0)


def add_earlier(near_ref, far_ref, h, scores):
    edge = far_ref[h, 1]
    return jnp.concatenate(
        [scores[: HALF - RADIUS] + edge[:1, HALF - 1 :], scores[HALF - RADIUS :] + edge], axis=0
    )


def add_either(first, near_ref, far_ref, h, scores):
    later, earlier = far_ref[h, 0], far_ref[h, 1]
    rest = jnp.where(first, later[RADIUS - 1 :, :1], earlier[:1, HALF - 1 :])
    return jnp.concatenate(
        [
            scores[:RADIUS] + jnp.where(first, later, rest),
            scores[RADIUS : HALF - RADIUS] + rest,
            scores[HALF - RADIUS :] + jnp.where(first, rest, earlier),
        ],
        axis=0,
    )


def full_biases(near_ref, far_ref, qb):
    kinds = (add_near, add_later) if qb == 0 else (add_earlier, add_near)
    return [functools.partial(kind, near_ref, far_ref) for kind in kinds]


def half_biases(near_ref, far_ref, first):
    return [
        functools.partial(add_near, near_ref, far_ref),
        functools.partial(add_either, first, near_ref, far_ref),
    ]


def mods_kernel(time_ref, *refs):
    weights, biases = refs[:6], {0: refs[6], 2: refs[7], 3: refs[8], 5: refs[9]}
    mods_ref, early_ref, late_ref, embed_ref = refs[10:]
    rows = []
    blank = jnp.zeros((1, time_ref.shape[2]), F32)
    for i in range(time_ref.shape[0]):
        rows += [time_ref[i].astype(F32), blank]
    embed_ref[...] = jnp.concatenate(rows + [blank] * (16 - SEGS * time_ref.shape[0]), axis=0).astype(BF16)
    cols = early_ref.shape[1] // 4
    homes = {0: (late_ref, 0), 1: (late_ref, 1), 5: (early_ref, 0), 3: (early_ref, 1), 4: (early_ref, 2), 2: (early_ref, 3)}
    for i in range(6):
        value = mm(embed_ref[...], weights[i][...])
        slope = jnp.ones_like(value)
        if i in biases:
            value = jax.nn.sigmoid(value + biases[i][...].astype(F32).reshape(1, cols))
            slope = value * (1.0 - value)
        mods_ref[i] = value
        home, place = homes[i]
        home[:, pl.ds(place * cols, cols)] = slope


def modulations(embed, weights, biases):
    cols = weights[0].shape[1]
    args = (embed, *weights, *biases)
    shapes = [(6, 16, cols), (16, 4 * cols), (16, 2 * cols), (16, embed.shape[2])]
    return call(
        mods_kernel,
        (1,),
        [whole(*a.shape) for a in args],
        tuple(whole(*shape) for shape in shapes),
        tuple(jax.ShapeDtypeStruct(shape, dtype) for shape, dtype in zip(shapes, (F32, F32, F32, BF16))),
        flops=10**8,
        moved=2 * 10**6,
    )(*args)


def table_kernel(tp_ref, own_ref, came_ref, o_ref):
    first = tp_ref[0] == 0
    row = lax.broadcasted_iota(jnp.int32, (32, 16), 0)
    col = lax.broadcasted_iota(jnp.int32, (32, 16), 1)
    part = (row >= 2 * SEGS).astype(jnp.int32) + (row >= 4 * SEGS).astype(jnp.int32)
    chain = row - 2 * SEGS * part
    chain = chain + jnp.where((chain < SEGS) & jnp.logical_not(first), 2 * SEGS, 0)
    take = ((col == chain) & (row < 6 * SEGS)).astype(F32)
    rows = lax.broadcasted_iota(jnp.int32, (32, 1), 0)
    width = 2 * own_ref.shape[2]
    for i in range(6):
        own, came = own_ref[i], came_ref[i]
        low, high = jnp.where(first, own, came), jnp.where(first, came, own)
        value = jnp.dot(take, jnp.concatenate([low, high], axis=1), precision=HIGHEST, preferred_element_type=F32)
        top = value.astype(BF16).astype(F32)
        middle = (value - top).astype(BF16).astype(F32)
        parts = jnp.where(rows < 2 * SEGS, top, jnp.where(rows < 4 * SEGS, middle, value - top - middle))
        o_ref[:, pl.ds(i * width, width)] = parts.astype(BF16)


def chain_table(tp, own, came):
    shape = (32, 12 * own.shape[2])
    return call(
        table_kernel,
        (1,),
        [whole(*own.shape), whole(*came.shape)],
        whole(*shape),
        jax.ShapeDtypeStruct(shape, BF16),
        prefetch=1,
        flops=10**7,
        moved=10**6,
    )(tp, own, came)


def masks_kernel(tp_ref, length_ref, flag_ref, q_ref, k_ref, pick_ref, turn_ref, marks_ref):
    core = tp_ref[0]

    def segments(pack, shape, axis, start):
        spot = lax.broadcasted_iota(jnp.int32, shape, axis) + start
        segment = jnp.zeros(shape, jnp.int32)
        end = 0
        for i in range(SEGS - 1):
            end = end + length_ref[pack, i]
            segment = segment + (spot >= end).astype(jnp.int32)
        return segment

    runs = [(2 * core, 0, 0), (2 * core, HALF, 0), (1, HALF * core, SEGS), (1, HALF * (1 - core), SEGS)]
    for i, (pack, start, shift) in enumerate(runs):
        rows = pl.ds(i * HALF, HALF)
        segment = segments(pack, (HALF, LANES), 0, start)
        lanes = lax.broadcasted_iota(jnp.int32, (HALF, LANES), 1)
        k_ref[rows, :] = (segment == lanes).astype(F32).astype(BF16)
        if i == 3:
            break
        q_ref[rows, :] = jnp.where((segment != lanes) & (lanes < SEGS), MASKED, 0.0).astype(BF16)
        chain = (segment + shift)[:, :32]
        lanes = lanes[:, :32]
        spot = lanes - 2 * SEGS * (
            (lanes >= 2 * SEGS).astype(jnp.int32) + (lanes >= 4 * SEGS).astype(jnp.int32)
        )
        pick_ref[rows, :] = ((chain == spot) & (lanes < 6 * SEGS)).astype(F32).astype(BF16)
        marks_ref[rows, :] = jnp.full((HALF, 1), flag_ref[pack].astype(F32))
        across = segments(pack, (16, HALF), 1, start) + shift
        turn_ref[i] = (across == lax.broadcasted_iota(jnp.int32, (16, HALF), 0)).astype(F32).astype(BF16)


def masks(tp, lengths, flags):
    shapes = [(3 * HALF, LANES), (4 * HALF, LANES), (3 * HALF, 32), (3, 16, HALF)]
    return call(
        masks_kernel,
        (1,),
        [],
        tuple(whole(*shape) for shape in shapes) + (whole(3 * HALF, 1),),
        tuple(jax.ShapeDtypeStruct(shape, BF16) for shape in shapes)
        + (jax.ShapeDtypeStruct((3 * HALF, 1), F32),),
        prefetch=3,
        flops=10**6,
        moved=10**6,
    )(tp, lengths, flags)


def halves_kernel(tp_ref, *refs):
    for source, target in zip(refs[:4], refs[4:]):
        target[...] = source[...]


def token_halves(tp, first, second):
    cols = first.shape[1]

    def mine(j, tp_ref):
        return jnp.where(j < 2, 4 * tp_ref[0] + j, 2 + tp_ref[0]), 0

    def others(j, tp_ref):
        return jnp.where(j < 2, 4 * (1 - tp_ref[0]) + j, 3 - tp_ref[0]), 0

    spec = pl.BlockSpec((HALF, cols), lambda j, _: (j, 0))
    shape = jax.ShapeDtypeStruct((3 * HALF, cols), BF16)
    places = [pl.BlockSpec((HALF, cols), place) for place in (mine, others)]
    return call(
        halves_kernel, (3,), places + places, (spec,) * 4, (shape,) * 4, prefetch=1, flops=10, moved=24 * HALF * cols
    )(tp, first, first, second, second)


def put_together(first_core, own, came):
    return jnp.concatenate([jnp.where(first_core, own, came), jnp.where(first_core, came, own)], axis=1)


def qkv_first_kernel(tp_ref, xo_ref, xp_ref, oh_ref, tab_ref, own_ref, par_ref, o_ref, x_ref, normed):
    @pl.when(pl.program_id(0) == 0)
    def _():
        x_ref[...] = put_together(tp_ref[0] == 0, xo_ref[...], xp_ref[...])

    qkv_kernel(x_ref, oh_ref, tab_ref, own_ref, par_ref, o_ref, normed)


def qkv_kernel(x_ref, oh_ref, tab_ref, own_ref, par_ref, o_ref, normed):
    width = x_ref.shape[1]
    half = own_ref.shape[1]

    @pl.when(pl.program_id(0) == 0)
    def _():
        def body(i):
            rows = pl.ds(pl.multiple_of(i * HALF, HALF), HALF)
            hat, _ = norm_parts(x_ref[rows, :].astype(F32))
            pick = oh_ref[rows, :]
            scale = mm(pick, tab_ref[:, :width])
            shift = mm(pick, tab_ref[:, width : 2 * width])
            normed[rows, :] = (hat * scale + shift).astype(BF16)

        block_loop(x_ref.shape[0] // HALF, body)

    o_ref[:, :half] = mm(normed[...], own_ref[...]).astype(BF16)
    o_ref[:, half:] = mm(normed[...], par_ref[...]).astype(BF16)


def qkv_first(tp, x_own, x_came, pick, table, w_own, w_par):
    tokens, cols = x_own.shape
    width = 2 * cols
    half = w_own.shape[1] // 3
    return call(
        qkv_first_kernel,
        (3,),
        [
            whole(tokens, cols),
            whole(tokens, cols),
            whole(*pick.shape),
            whole(*table.shape),
            pl.BlockSpec((width, half), lambda j, *_: (0, j)),
            pl.BlockSpec((width, half), lambda j, *_: (0, j)),
        ],
        (pl.BlockSpec((tokens, 2 * half), lambda j, *_: (0, j)), whole(tokens, width)),
        (jax.ShapeDtypeStruct((tokens, 6 * half), BF16), jax.ShapeDtypeStruct((tokens, width), BF16)),
        [pltpu.VMEM((tokens, width), BF16)],
        prefetch=1,
        flops=2 * tokens * width * 6 * half,
        moved=tokens * 6 * half * 2 + width * half * 12 + tokens * width * 4,
    )(tp, x_own, x_came, pick, table, w_own, w_par)


def qkv_forward(x, pick, table, w_own, w_par):
    tokens, width = x.shape
    half = w_own.shape[1] // 3
    return call(
        qkv_kernel,
        (3,),
        [
            whole(tokens, width),
            whole(*pick.shape),
            whole(*table.shape),
            pl.BlockSpec((width, half), lambda j: (0, j)),
            pl.BlockSpec((width, half), lambda j: (0, j)),
        ],
        pl.BlockSpec((tokens, 2 * half), lambda j: (0, j)),
        jax.ShapeDtypeStruct((tokens, 6 * half), BF16),
        [pltpu.VMEM((tokens, width), BF16)],
        flops=2 * tokens * width * 6 * half,
        moved=tokens * 6 * half * 2 + width * half * 12 + tokens * width * 4,
    )(x, pick, table, w_own, w_par)


def lane_masks():
    lanes = lax.broadcasted_iota(jnp.int32, (1, LANES), 1)
    first = (lanes < LANES // 2).astype(F32)
    return first.astype(BF16), (1.0 - first).astype(BF16)


def attend_forward_block(q, segq, keys, values_t, biases):
    outs, logs = [], []
    half = LANES // 2
    masks = lane_masks()
    scaled = q * jnp.asarray(half**-0.5, BF16)
    for h in range(2):
        query = jnp.concatenate([scaled * masks[h], segq], axis=1)
        scores = [bias(h, mm_nt(key, query)) for key, bias in zip(keys, biases)]
        tops = [jnp.max(s, axis=0, keepdims=True) for s in scores]
        top = functools.reduce(jnp.maximum, tops)
        weights = [jnp.exp(s - top) for s in scores]
        total = sum(jnp.sum(w, axis=0, keepdims=True) for w in weights)
        mixed = sum(
            mm(vt[h * half : (h + 1) * half, :], w.astype(BF16)) for vt, w in zip(values_t, weights)
        )
        outs.append(mixed / total)
        logs.append(top + jnp.log(total))
    attended = jnp.concatenate(outs, axis=0).T.astype(BF16)
    return attended, jnp.concatenate(logs, axis=0)


def attend_full_kernel(q_ref, k_ref, v_ref, segq_ref, segk_ref, near_ref, far_ref, o_ref, log_ref):
    keys = [
        jnp.concatenate([k_ref[pl.ds(b * HALF, HALF), :], segk_ref[pl.ds(b * HALF, HALF), :]], axis=1)
        for b in range(2)
    ]
    values_t = [v_ref[pl.ds(b * HALF, HALF), :].T for b in range(2)]
    for qb in range(2):
        rows = pl.ds(qb * HALF, HALF)
        biases = full_biases(near_ref, far_ref, qb)
        attended, logs = attend_forward_block(q_ref[rows, :], segq_ref[rows, :], keys, values_t, biases)
        o_ref[rows, :] = attended
        log_ref[0, 0:2, rows] = logs


def attend_half_kernel(
    tp_ref, q_ref, k_ref, v_ref, kp_ref, vp_ref, segq_ref, segk_ref, near_ref, far_ref, oin, login, o_ref, log_ref
):
    keys = [
        jnp.concatenate([k_ref[...], segk_ref[pl.ds(0, HALF), :]], axis=1),
        jnp.concatenate([kp_ref[...], segk_ref[pl.ds(HALF, HALF), :]], axis=1),
    ]
    values_t = [v_ref[...].T, vp_ref[...].T]
    biases = half_biases(near_ref, far_ref, tp_ref[0] == 0)
    attended, logs = attend_forward_block(q_ref[...], segq_ref[...], keys, values_t, biases)
    o_ref[...] = attended
    log_ref[0, 0:2, :] = logs


def attend_forward(tp, qkv, kv_par, segq, segk, bias):
    tokens = qkv.shape[0]
    width = qkv.shape[1] // 3
    pairs = width // LANES
    out_shape = (
        jax.ShapeDtypeStruct((tokens, width), BF16),
        jax.ShapeDtypeStruct((pairs, 8, tokens), F32),
    )
    unit = 4 * HALF * HALF * 256 * 2
    attended, logs = call(
        attend_full_kernel,
        (pairs,),
        [
            pl.BlockSpec((ROW, LANES), lambda p: (0, p)),
            pl.BlockSpec((ROW, LANES), lambda p: (0, pairs + p)),
            pl.BlockSpec((ROW, LANES), lambda p: (0, 2 * pairs + p)),
            pl.BlockSpec((ROW, LANES), lambda p: (0, 0)),
            pl.BlockSpec((ROW, LANES), lambda p: (0, 0)),
        ]
        + bias_specs(),
        (
            pl.BlockSpec((ROW, LANES), lambda p: (0, p)),
            pl.BlockSpec((1, 8, ROW), lambda p: (p, 0, 0)),
        ),
        out_shape,
        flops=unit * 4 * pairs,
        moved=bias[0].size * 4,
    )(qkv, qkv, qkv, segq, segk, *bias)
    flip = pairs // 2
    return call(
        attend_half_kernel,
        (pairs,),
        [
            pl.BlockSpec((HALF, LANES), lambda p, *_: (2, p)),
            pl.BlockSpec((HALF, LANES), lambda p, *_: (2, pairs + p)),
            pl.BlockSpec((HALF, LANES), lambda p, *_: (2, 2 * pairs + p)),
            pl.BlockSpec((HALF, LANES), lambda p, *_: (0, lax.rem(p + flip, pairs))),
            pl.BlockSpec((HALF, LANES), lambda p, *_: (0, pairs + lax.rem(p + flip, pairs))),
            pl.BlockSpec((HALF, LANES), lambda p, *_: (2, 0)),
            pl.BlockSpec((ROW, LANES), lambda p, *_: (1, 0)),
        ]
        + bias_specs()
        + [pl.BlockSpec(memory_space=pl.ANY), pl.BlockSpec(memory_space=pl.ANY)],
        (
            pl.BlockSpec((HALF, LANES), lambda p, *_: (2, p)),
            pl.BlockSpec((1, 8, HALF), lambda p, *_: (p, 0, 2)),
        ),
        out_shape,
        prefetch=1,
        aliases={10: 0, 11: 1},
        flops=unit * 2 * pairs,
        moved=bias[0].size * 4,
    )(tp, qkv, qkv, qkv, kv_par, kv_par, segq, segk, *bias, attended, logs)


def ffn_kernel(
    att_ref, woo_ref, wop_ref, x_ref, oh_ref, tab_ref, guo_ref, gup_ref, wdo_ref, wdp_ref,
    head_ref, emb_ref, flag_ref, shifted_ref, lifted_ref, middle, normed, acc,
):
    step = pl.program_id(0)
    tokens, width = x_ref.shape
    half = woo_ref.shape[0]
    blocks = tokens // HALF

    @pl.when(step == 0)
    def _():
        def body(i):
            rows = pl.ds(pl.multiple_of(i * HALF, HALF), HALF)
            branch = mm(att_ref[rows, :half], woo_ref[...]) + mm(att_ref[rows, half:], wop_ref[...])
            pick = oh_ref[rows, :]
            mid = x_ref[rows, :].astype(F32) + mm(pick, tab_ref[:, 2 * width : 3 * width]) * branch
            middle[rows, :] = mid
            hat, _ = norm_parts(mid)
            scale = mm(pick, tab_ref[:, 3 * width : 4 * width])
            shift = mm(pick, tab_ref[:, 4 * width : 5 * width])
            normed[rows, :] = (hat * scale + shift).astype(BF16)
            acc[rows, :] = jnp.zeros((HALF, width), F32)

        block_loop(blocks, body)

    def body(i):
        rows = pl.ds(pl.multiple_of(i * HALF, HALF), HALF)
        total = acc[rows, :]
        for gu, wd in ((guo_ref, wdo_ref), (gup_ref, wdp_ref)):
            gate = mm(normed[rows, :], gu[0])
            up = mm(normed[rows, :], gu[1])
            hidden = (gate * jax.nn.sigmoid(gate) * up).astype(BF16)
            total = total + mm(hidden, wd[...])
        acc[rows, :] = total

    block_loop(blocks, body)

    @pl.when(step == pl.num_programs(0) - 1)
    def _():
        def body(i):
            rows = pl.ds(pl.multiple_of(i * HALF, HALF), HALF)
            gate = mm(oh_ref[rows, :], tab_ref[:, 5 * width : 6 * width])
            first = middle[rows, :] + gate * acc[rows, :]
            high = first.astype(BF16)
            rest = (first - high.astype(F32)).astype(BF16)
            coords = mm_nt(high, head_ref[...]) + mm_nt(rest, head_ref[...])
            lifted = coords * flag_ref[rows, :]
            lifted_ref[rows, :] = lifted
            high = lifted.astype(BF16)
            rest = (lifted - high.astype(F32)).astype(BF16)
            moved = mm(high, emb_ref[...]) + mm(rest, emb_ref[...])
            shifted_ref[rows, :] = x_ref[rows, :].astype(F32) + moved

        block_loop(blocks, body)


def ffn_specs(att, woo, x, pick, table):
    tokens, width = x.shape
    chunk = FFC
    return [
        whole(*att.shape),
        whole(*woo.shape),
        whole(*woo.shape),
        whole(tokens, width),
        whole(*pick.shape),
        whole(*table.shape),
        pl.BlockSpec((2, width, chunk), lambda j, *_: (0, 0, j)),
        pl.BlockSpec((2, width, chunk), lambda j, *_: (0, 0, j)),
        pl.BlockSpec((chunk, width), lambda j, *_: (j, 0)),
        pl.BlockSpec((chunk, width), lambda j, *_: (j, 0)),
    ]


def ffn_forward(att, woo, wop, x, pick, table, guo, gup, wdo, wdp, head, emb, flags):
    tokens, width = x.shape
    hidden = wdo.shape[0]
    return call(
        ffn_kernel,
        (hidden // FFC,),
        ffn_specs(att, woo, x, pick, table)
        + [whole(*head.shape), whole(*emb.shape), whole(*flags.shape)],
        (whole(tokens, width), whole(tokens, LANES)),
        (
            jax.ShapeDtypeStruct((tokens, width), F32),
            jax.ShapeDtypeStruct((tokens, LANES), F32),
        ),
        [
            pltpu.VMEM((tokens, width), F32),
            pltpu.VMEM((tokens, width), BF16),
            pltpu.VMEM((tokens, width), F32),
        ],
        flops=2 * tokens * width * (6 * hidden + width),
        moved=12 * hidden * width + 6 * tokens * width,
    )(att, woo, wop, x, pick, table, guo, gup, wdo, wdp, head, emb, flags)


def turn_kernel(
    tp_ref, att_ref, woo_ref, wop_ref, x_ref, oh_ref, tab_ref, guo_ref, gup_ref, wdo_ref, wdp_ref,
    gown_ref, gcame_ref, oht_ref,
    outo_ref, outp_ref, gmid_ref, gatt_ref, go_ref, gp_ref, goo_ref, gop_ref, sumo_ref, sump_ref,
    sums_ref, middle, hats, branches, normed, normed_t, gmixed, gmixed_t, mixed, gnormed, hid, dgate, dup,
):
    step = pl.program_id(0)
    tokens, width = x_ref.shape
    half = woo_ref.shape[0]
    blocks = tokens // HALF

    @pl.when(step == 0)
    def _():
        def body(i):
            rows = pl.ds(pl.multiple_of(i * HALF, HALF), HALF)
            branch = mm(att_ref[rows, :half], woo_ref[...]) + mm(att_ref[rows, half:], wop_ref[...])
            branches[rows, :] = branch
            pick = oh_ref[rows, :]
            mid = x_ref[rows, :] + mm(pick, tab_ref[:, 2 * width : 3 * width]) * branch
            middle[rows, :] = mid
            hat, _ = norm_parts(mid)
            scale = mm(pick, tab_ref[:, 3 * width : 4 * width])
            shift = mm(pick, tab_ref[:, 4 * width : 5 * width])
            normed[rows, :] = (hat * scale + shift).astype(BF16)
            gate = mm(pick, tab_ref[:, 5 * width : 6 * width])
            g = put_together(tp_ref[0] == 0, gown_ref[rows, :], gcame_ref[rows, :])
            gmixed[rows, :] = (g.astype(F32) * gate).astype(BF16)
            mixed[rows, :] = jnp.zeros((HALF, width), F32)
            gnormed[rows, :] = jnp.zeros((HALF, width), F32)

        block_loop(blocks, body)
        normed_t[...] = normed[...].T
        gmixed_t[...] = gmixed[...].T

    for gu, wd, out in ((gup_ref, wdp_ref, gp_ref), (guo_ref, wdo_ref, go_ref)):

        def body(i):
            rows = pl.ds(pl.multiple_of(i * HALF, HALF), HALF)
            gate = mm(normed[rows, :], gu[0])
            up = mm(normed[rows, :], gu[1])
            ghid = mm_nt(gmixed[rows, :], wd[...])
            s = jax.nn.sigmoid(gate)
            silu = gate * s
            hidden = (silu * up).astype(BF16)
            hid[rows, :] = hidden
            mixed[rows, :] += mm(hidden, wd[...])
            dg = (ghid * up * (s + silu * (1.0 - s))).astype(BF16)
            du = (ghid * silu).astype(BF16)
            dgate[rows, :] = dg
            dup[rows, :] = du
            gnormed[rows, :] += mm_nt(dg, gu[0]) + mm_nt(du, gu[1])

        block_loop(blocks, body)
        out[0, 0] = mm(normed_t[...], dgate[...]).astype(BF16)
        out[1, 0] = mm(normed_t[...], dup[...]).astype(BF16)
        out[2, 0] = mm(gmixed_t[...], hid[...]).astype(BF16)

    @pl.when(step == pl.num_programs(0) - 1)
    def _():
        first_core = tp_ref[0] == 0
        sums_ref[...] = jnp.zeros(sums_ref.shape, F32)

        def body(i):
            rows = pl.ds(pl.multiple_of(i * HALF, HALF), HALF)
            pick = oh_ref[rows, :]
            turn = oht_ref[i]
            g = put_together(first_core, gown_ref[rows, :], gcame_ref[rows, :]).astype(F32)
            total = mixed[rows, :]
            gate = mm(pick, tab_ref[:, 5 * width : 6 * width])
            mid = middle[rows, :]
            result = (mid + gate * total).astype(BF16)
            low, high = result[:, : width // 2], result[:, width // 2 :]
            outo_ref[rows, :] = jnp.where(first_core, low, high)
            outp_ref[rows, :] = jnp.where(first_core, high, low)
            sums_ref[0] += mm(turn, (g * total).astype(BF16))
            hat, inv_std = norm_parts(mid)
            gn = gnormed[rows, :]
            sums_ref[1] += mm(turn, (gn * hat).astype(BF16))
            sums_ref[2] += mm(turn, gn.astype(BF16))
            scale = mm(pick, tab_ref[:, 3 * width : 4 * width])
            gmid = g + norm_back(gn * scale, hat, inv_std)
            gmid_ref[rows, :] = gmid
            sums_ref[3] += mm(turn, (gmid * branches[rows, :]).astype(BF16))
            gbranch = (gmid * mm(pick, tab_ref[:, 2 * width : 3 * width])).astype(BF16)
            gmixed[rows, :] = gbranch
            gatt_ref[rows, :half] = mm_nt(gbranch, woo_ref[...]).astype(BF16)
            gatt_ref[rows, half:] = mm_nt(gbranch, wop_ref[...]).astype(BF16)

        block_loop(blocks, body)
        gmixed_t[...] = gmixed[...].T
        goo_ref[...] = mm(gmixed_t[...], att_ref[:, :half]).astype(BF16)
        gop_ref[...] = mm(gmixed_t[...], att_ref[:, half:]).astype(BF16)
        low, high = sums_ref[:, :, : width // 2], sums_ref[:, :, width // 2 :]
        sumo_ref[...] = jnp.where(first_core, low, high)
        sump_ref[...] = jnp.where(first_core, high, low)


def ffn_turn(tp, att, woo, wop, x, pick, table, guo, gup, wdo, wdp, g_own, g_came, pick_t):
    tokens, width = x.shape
    half = woo.shape[0]
    hidden = wdo.shape[0]
    grads = jax.ShapeDtypeStruct((3, hidden // FFC, width, FFC), BF16)
    grads_spec = pl.BlockSpec((3, 1, width, FFC), lambda j, *_: (0, j, 0, 0))
    return call(
        turn_kernel,
        (hidden // FFC,),
        ffn_specs(att, woo, x, pick, table) + [whole(tokens, width // 2), whole(tokens, width // 2), whole(*pick_t.shape)],
        (
            whole(tokens, width // 2),
            whole(tokens, width // 2),
            whole(tokens, width),
            whole(tokens, width),
            grads_spec,
            grads_spec,
            whole(width, half),
            whole(width, half),
            whole(4, 16, width // 2),
            whole(4, 16, width // 2),
        ),
        (
            jax.ShapeDtypeStruct((tokens, width // 2), BF16),
            jax.ShapeDtypeStruct((tokens, width // 2), BF16),
            jax.ShapeDtypeStruct((tokens, width), F32),
            jax.ShapeDtypeStruct((tokens, width), BF16),
            grads,
            grads,
            jax.ShapeDtypeStruct((width, half), BF16),
            jax.ShapeDtypeStruct((width, half), BF16),
            jax.ShapeDtypeStruct((4, 16, width // 2), F32),
            jax.ShapeDtypeStruct((4, 16, width // 2), F32),
        ),
        [
            pltpu.VMEM((4, 16, width), F32),
            pltpu.VMEM((tokens, width), F32),
            pltpu.VMEM((8, LANES), F32),
            pltpu.VMEM((tokens, width), F32),
            pltpu.VMEM((tokens, width), BF16),
            pltpu.VMEM((width, tokens), BF16),
            pltpu.VMEM((tokens, width), BF16),
            pltpu.VMEM((width, tokens), BF16),
            pltpu.VMEM((tokens, width), F32),
            pltpu.VMEM((tokens, width), F32),
            pltpu.VMEM((tokens, FFC), BF16),
            pltpu.VMEM((tokens, FFC), BF16),
            pltpu.VMEM((tokens, FFC), BF16),
        ],
        prefetch=1,
        flops=2 * tokens * width * (18 * hidden + 3 * width),
        moved=24 * hidden * width + 12 * tokens * width,
    )(tp, att, woo, wop, x, pick, table, guo, gup, wdo, wdp, g_own, g_came, pick_t)


def attend_back_block(q, segq, gout, logs, keys, keys_t, values, biases, bias_sums, gkeys, gvalues):
    half = LANES // 2
    masks = lane_masks()
    scale = half**-0.5
    scaled = q * jnp.asarray(scale, BF16)
    gqs = []
    for h in range(2):
        query_low = scaled * masks[h]
        query = jnp.concatenate([query_low, segq], axis=1)
        gheads = gout * masks[h]
        chances = [jnp.exp(bias(h, mm_nt(key, query)) - logs[h : h + 1, :]) for key, bias in zip(keys, biases)]
        gchances = [mm_nt(value, gheads) for value in values]
        centre = sum(jnp.sum(p * gp, axis=0, keepdims=True) for p, gp in zip(chances, gchances))
        gq = 0.0
        for b, (p, gp) in enumerate(zip(chances, gchances)):
            gs = p * (gp - centre)
            bias_sums[b](h, gs)
            low = gs.astype(BF16)
            gvalues[b] = gvalues[b] + mm(p.astype(BF16), gheads)
            gkeys[b] = gkeys[b] + mm(low, query_low)
            gq = gq + mm(keys_t[b][h * half : (h + 1) * half, :], low)
        gqs.append(gq * scale)
    return jnp.concatenate(gqs, axis=0).T.astype(BF16)


def diagonal_sums(tile):
    size, wide = tile.shape
    rows = lax.broadcasted_iota(jnp.int32, (size, size), 0)
    cols = lax.broadcasted_iota(jnp.int32, (size, size), 1)
    turn = (rows + cols == size - 1).astype(F32).astype(BF16)
    high = tile.astype(BF16)
    rest = (tile - high.astype(F32)).astype(BF16)
    flipped = mm(turn, high) + mm(turn, rest)
    padded = jnp.concatenate([flipped, jnp.zeros((size, wide), F32)], axis=1)
    rolled = pltpu.roll(padded, 0, axis=1, stride=1, stride_axis=0)
    return jnp.sum(rolled, axis=0, keepdims=True)


def far_sums(tile, later):
    whole_sum = jnp.sum(jnp.sum(tile, axis=0, keepdims=True), axis=1, keepdims=True)
    edge = tile[:RADIUS, LANES:] if later else tile[HALF - RADIUS :, :LANES]
    sums = diagonal_sums(edge)
    rest = whole_sum - jnp.sum(sums, axis=1, keepdims=True)
    row = jnp.concatenate([sums, jnp.zeros((1, 2 * HALF - sums.shape[1]), F32)], axis=1)
    row = jnp.broadcast_to(row, (8, 2 * HALF))
    if later:
        row = pltpu.roll(row, 2 * HALF - LANES - RADIUS, axis=1)
    lanes = lax.broadcasted_iota(jnp.int32, (1, 2 * HALF), 1)
    return row[:1] + jnp.where(lanes == (0 if later else 2 * HALF - 2), rest, 0.0)


def attend_full_back_kernel(
    q_ref, k_ref, v_ref, g_ref, log_ref, segq_ref, segk_ref, near_ref, far_ref, o_ref, diag_ref, sums
):
    keys, keys_t, values = [], [], []
    for b in range(2):
        rows = pl.ds(b * HALF, HALF)
        key = k_ref[rows, :]
        keys.append(jnp.concatenate([key, segk_ref[rows, :]], axis=1))
        keys_t.append(key.T)
        values.append(v_ref[rows, :])
    gkeys, gvalues = [0.0, 0.0], [0.0, 0.0]
    sums[...] = jnp.zeros(sums.shape, F32)
    for qb in range(2):
        rows = pl.ds(qb * HALF, HALF)
        biases = full_biases(near_ref, far_ref, qb)

        def add(h, gs):
            sums[h] += gs

        def put(h, gs, later):
            row = 3 * h + (0 if later else 2)
            diag_ref[0, row : row + 1, :] = far_sums(gs, later)

        adders = [add, functools.partial(put, later=True)] if qb == 0 else [functools.partial(put, later=False), add]
        o_ref[0, rows, :] = attend_back_block(
            q_ref[rows, :], segq_ref[rows, :], g_ref[rows, :], log_ref[0, 0:2, rows],
            keys, keys_t, values, biases, adders, gkeys, gvalues,
        )
    for b in range(2):
        rows = pl.ds(b * HALF, HALF)
        o_ref[1, rows, :] = gkeys[b].astype(BF16)
        o_ref[2, rows, :] = gvalues[b].astype(BF16)
    for h in range(2):
        diag_ref[0, 3 * h + 1 : 3 * h + 2, :] = diagonal_sums(sums[h])


def attend_half_back_kernel(
    tp_ref, q_ref, k_ref, v_ref, kp_ref, vp_ref, g_ref, log_ref, segq_ref, segk_ref, near_ref, far_ref,
    o_ref, par_ref, diag_ref,
):
    keys, keys_t, values = [], [], []
    for b, (k, v) in enumerate(((k_ref, v_ref), (kp_ref, vp_ref))):
        key = k[...]
        keys.append(jnp.concatenate([key, segk_ref[pl.ds(b * HALF, HALF), :]], axis=1))
        keys_t.append(key.T)
        values.append(v[...])
    first = tp_ref[0] == 0
    biases = half_biases(near_ref, far_ref, first)
    gkeys, gvalues = [0.0, 0.0], [0.0, 0.0]

    def put(h, gs, b):
        sums = jnp.where(first, far_sums(gs, True), far_sums(gs, False)) if b else diagonal_sums(gs)
        diag_ref[0, 2 * h + b : 2 * h + b + 1, :] = sums

    adders = [functools.partial(put, b=b) for b in range(2)]
    o_ref[0] = attend_back_block(
        q_ref[...], segq_ref[...], g_ref[...], log_ref[0, 0:2, :],
        keys, keys_t, values, biases, adders, gkeys, gvalues,
    )
    o_ref[1] = gkeys[0].astype(BF16)
    o_ref[2] = gvalues[0].astype(BF16)
    par_ref[0] = gkeys[1].astype(BF16)
    par_ref[1] = gvalues[1].astype(BF16)


def attend_half_back(tp, qkv, kv_par, g, logs, segq, segk, bias):
    width = qkv.shape[1] // 3
    pairs = width // LANES
    flip = pairs // 2
    return call(
        attend_half_back_kernel,
        (pairs,),
        [
            pl.BlockSpec((HALF, LANES), lambda p, *_: (2, p)),
            pl.BlockSpec((HALF, LANES), lambda p, *_: (2, pairs + p)),
            pl.BlockSpec((HALF, LANES), lambda p, *_: (2, 2 * pairs + p)),
            pl.BlockSpec((HALF, LANES), lambda p, *_: (0, lax.rem(p + flip, pairs))),
            pl.BlockSpec((HALF, LANES), lambda p, *_: (0, pairs + lax.rem(p + flip, pairs))),
            pl.BlockSpec((HALF, LANES), lambda p, *_: (2, p)),
            pl.BlockSpec((1, 8, HALF), lambda p, *_: (p, 0, 2)),
            pl.BlockSpec((HALF, LANES), lambda p, *_: (2, 0)),
            pl.BlockSpec((ROW, LANES), lambda p, *_: (1, 0)),
        ]
        + bias_specs(),
        (
            pl.BlockSpec((3, HALF, LANES), lambda p, *_: (0, 0, p)),
            pl.BlockSpec((2, HALF, LANES), lambda p, *_: (0, 0, p)),
            pl.BlockSpec((1, 8, ROW), lambda p, *_: (p, 0, 0)),
        ),
        (
            jax.ShapeDtypeStruct((3, HALF, width), BF16),
            jax.ShapeDtypeStruct((2, HALF, width), BF16),
            jax.ShapeDtypeStruct((pairs, 8, ROW), F32),
        ),
        prefetch=1,
        flops=10 * HALF * HALF * 256 * 2 * pairs,
        moved=bias[0].size * 4,
    )(tp, qkv, qkv, qkv, kv_par, kv_par, g, logs, segq, segk, *bias)


def attend_full_back(qkv, g, logs, segq, segk, bias):
    width = qkv.shape[1] // 3
    pairs = width // LANES
    return call(
        attend_full_back_kernel,
        (pairs,),
        [
            pl.BlockSpec((ROW, LANES), lambda p: (0, p)),
            pl.BlockSpec((ROW, LANES), lambda p: (0, pairs + p)),
            pl.BlockSpec((ROW, LANES), lambda p: (0, 2 * pairs + p)),
            pl.BlockSpec((ROW, LANES), lambda p: (0, p)),
            pl.BlockSpec((1, 8, ROW), lambda p: (p, 0, 0)),
            pl.BlockSpec((ROW, LANES), lambda p: (0, 0)),
            pl.BlockSpec((ROW, LANES), lambda p: (0, 0)),
        ]
        + bias_specs(),
        (
            pl.BlockSpec((3, ROW, LANES), lambda p: (0, 0, p)),
            pl.BlockSpec((1, 8, ROW), lambda p: (p, 0, 0)),
        ),
        (
            jax.ShapeDtypeStruct((3, ROW, width), BF16),
            jax.ShapeDtypeStruct((pairs, 8, ROW), F32),
        ),
        [pltpu.VMEM((2, HALF, HALF), F32)],
        flops=20 * HALF * HALF * 256 * 2 * pairs,
        moved=bias[0].size * 4,
    )(qkv, qkv, qkv, g, logs, segq, segk, *bias)


def joined_rows(full_ref, half_ref, recv_ref, step, rows_in):
    half = recv_ref.shape[2] // 2
    rows_in[pl.ds(0, ROW), :] = full_ref[0]
    keep = (step > 0).astype(F32).astype(BF16)
    recv = jnp.concatenate([recv_ref[0, :, half:], recv_ref[0, :, :half]], axis=1)
    rows_in[pl.ds(ROW, HALF), :] = half_ref[0] + recv * keep


def qkv_weights_kernel(
    x_ref, oh_ref, tab_ref, full_ref, half_ref, recv_ref, outo_ref, outp_ref, go_ref, gp_ref, normed, normed_t, rows_in
):
    step = pl.program_id(0)
    tokens, width = x_ref.shape
    half = width // 2

    @pl.when(step == 0)
    def _():
        def body(i):
            rows = pl.ds(pl.multiple_of(i * HALF, HALF), HALF)
            hat, _ = norm_parts(x_ref[rows, :])
            pick = oh_ref[rows, :]
            scale = mm(pick, tab_ref[:, :width])
            shift = mm(pick, tab_ref[:, width : 2 * width])
            normed[rows, :] = (hat * scale + shift).astype(BF16)

        block_loop(tokens // HALF, body)
        normed_t[...] = normed[...].T

    joined_rows(full_ref, half_ref, recv_ref, step, rows_in)
    go_ref[0, :, :half] = mm(normed_t[...], rows_in[:, :half]).astype(BF16)
    gp_ref[0, :, :half] = mm(normed_t[...], rows_in[:, half:]).astype(BF16)
    go_ref[0, :, half:] = outo_ref[...]
    gp_ref[0, :, half:] = outp_ref[...]


def row_specs(width):
    return [
        pl.BlockSpec((1, ROW, width), lambda j, *_: (j, 0, 0)),
        pl.BlockSpec((1, HALF, width), lambda j, *_: (j, 0, 0)),
        pl.BlockSpec((1, HALF, width), lambda j, *_: (jnp.maximum(j - 1, 0), 0, 0)),
    ]


def qkv_weights(x, pick, table, full, half_rows, recv, out_own, out_par):
    tokens, width = x.shape
    half = width // 2
    third = half // 3
    spec = pl.BlockSpec((1, width, half + third), lambda j: (j, 0, 0))
    shape = jax.ShapeDtypeStruct((3, width, half + third), BF16)
    out_spec = pl.BlockSpec((width, third), lambda j: (0, j))
    return call(
        qkv_weights_kernel,
        (3,),
        [whole(tokens, width), whole(*pick.shape), whole(*table.shape)] + row_specs(width) + [out_spec, out_spec],
        (spec, spec),
        (shape, shape),
        [
            pltpu.VMEM((tokens, width), BF16),
            pltpu.VMEM((width, tokens), BF16),
            pltpu.VMEM((tokens, width), BF16),
        ],
        flops=2 * tokens * width * 6 * half,
        moved=16 * half * width + 12 * tokens * width,
    )(x, pick, table, full, half_rows, recv, out_own, out_par)


def qkv_back_kernel(
    tp_ref, x_ref, oh_ref, tab_ref, full_ref, half_ref, recv_ref, wo_ref, wp_ref, gmid_ref, lifted_ref, oht_ref,
    gino_ref, ginp_ref, sumo_ref, sump_ref, hats, stds, rows_in, acc, sums,
):
    step = pl.program_id(0)
    tokens, width = x_ref.shape
    half = wo_ref.shape[1]
    blocks = tokens // HALF

    @pl.when(step == 0)
    def _():
        def body(i):
            rows = pl.ds(pl.multiple_of(i * HALF, HALF), HALF)
            hat, inv_std = norm_parts(x_ref[rows, :])
            hats[rows, :] = hat
            stds[rows, :] = inv_std
            acc[rows, :] = jnp.zeros((HALF, width), F32)

        block_loop(blocks, body)

    joined_rows(full_ref, half_ref, recv_ref, step, rows_in)

    def body(i):
        rows = pl.ds(pl.multiple_of(i * HALF, HALF), HALF)
        grad = rows_in[rows, :]
        acc[rows, :] += mm_nt(grad[:, :half], wo_ref[...]) + mm_nt(grad[:, half:], wp_ref[...])

    block_loop(blocks, body)

    @pl.when(step == pl.num_programs(0) - 1)
    def _():
        first_core = tp_ref[0] == 0
        sums[...] = jnp.zeros(sums.shape, F32)

        def body(i):
            rows = pl.ds(pl.multiple_of(i * HALF, HALF), HALF)
            turn = oht_ref[i]
            gn = acc[rows, :]
            hat = hats[rows, :]
            sums[0] += mm(turn, (gn * hat).astype(BF16))
            sums[1] += mm(turn, gn.astype(BF16))
            scale = mm(oh_ref[rows, :], tab_ref[:, :width])
            grad = gmid_ref[rows, :] + norm_back(gn * scale, hat, stds[rows, :])
            low, high = grad[:, : width // 2], grad[:, width // 2 :]
            gino_ref[rows, :] = jnp.where(first_core, low, high)
            ginp_ref[rows, :] = jnp.where(first_core, high, low)
            lifted_t = lifted_ref[rows, :].astype(BF16).T
            sums[2] += mm(lifted_t[:16, :], grad.astype(BF16))

        block_loop(blocks, body)
        low, high = sums[:, :, : width // 2], sums[:, :, width // 2 :]
        sumo_ref[...] = jnp.where(first_core, low, high)
        sump_ref[...] = jnp.where(first_core, high, low)


def qkv_back(tp, x, pick, table, full, half_rows, recv, wo, wp, gmid, lifted, pick_t):
    tokens, width = x.shape
    half = wo.shape[1] // 3
    return call(
        qkv_back_kernel,
        (3,),
        [whole(tokens, width), whole(*pick.shape), whole(*table.shape)]
        + row_specs(width)
        + [
            pl.BlockSpec((width, half), lambda j, *_: (0, j)),
            pl.BlockSpec((width, half), lambda j, *_: (0, j)),
            whole(tokens, width),
            whole(tokens, LANES),
            whole(*pick_t.shape),
        ],
        (
            whole(tokens, width // 2),
            whole(tokens, width // 2),
            whole(3, 16, width // 2),
            whole(3, 16, width // 2),
        ),
        (
            jax.ShapeDtypeStruct((tokens, width // 2), F32),
            jax.ShapeDtypeStruct((tokens, width // 2), F32),
            jax.ShapeDtypeStruct((3, 16, width // 2), F32),
            jax.ShapeDtypeStruct((3, 16, width // 2), F32),
        ),
        [
            pltpu.VMEM((tokens, width), F32),
            pltpu.VMEM((tokens, 1), F32),
            pltpu.VMEM((tokens, width), BF16),
            pltpu.VMEM((tokens, width), F32),
            pltpu.VMEM((3, 16, width), F32),
        ],
        prefetch=1,
        flops=2 * tokens * width * 6 * half,
        moved=12 * half * width + 16 * tokens * width,
    )(tp, x, pick, table, full, half_rows, recv, wo, wp, gmid, lifted, pick_t)


def chain_joins(first_core):
    row = lax.broadcasted_iota(jnp.int32, (16, 16), 0)
    col = lax.broadcasted_iota(jnp.int32, (16, 16), 1)
    lower = ((row == col) & (row < 2 * SEGS)).astype(F32)
    upper = (
        ((row == col) & (row >= SEGS) & (row < 2 * SEGS)) | ((row == col + 2 * SEGS) & (row < 3 * SEGS))
    ).astype(F32)
    return jnp.where(first_core, lower, upper), jnp.where(first_core, upper, lower)


def join_chains(tp_ref, own_ref, came_ref, slope_ref, count, o_ref):
    own_join, came_join = chain_joins(tp_ref[0] == 0)
    cols = own_ref.shape[2]
    for i in range(count):
        both = jnp.dot(own_join, own_ref[i], precision=HIGHEST, preferred_element_type=F32)
        both = both + jnp.dot(came_join, came_ref[i], precision=HIGHEST, preferred_element_type=F32)
        lanes = pl.ds(i * cols, cols)
        o_ref[0:16, lanes] = (both * slope_ref[:, lanes]).astype(BF16)


def early_kernel(tp_ref, own_ref, came_ref, slope_ref, embed_ref, o_ref):
    join_chains(tp_ref, own_ref, came_ref, slope_ref, 4, o_ref)
    o_ref[:, pl.ds(4 * own_ref.shape[2], embed_ref.shape[1])] = embed_ref[...]


def late_kernel(tp_ref, own_ref, came_ref, slope_ref, bins_ref, o_ref):
    cols = own_ref.shape[2]
    join_chains(tp_ref, own_ref, came_ref, slope_ref, 2, o_ref)
    o_ref[:, pl.ds(2 * cols, LANES)] = bins_ref[...].astype(BF16)
    coords = own_ref[2] + came_ref[2]
    parts = [coords[i : i + 1, j : j + LANES] for j in range(0, cols, LANES) for i in range(3)]
    parts.append(jnp.zeros((16 - len(parts), LANES), F32))
    o_ref[:, pl.ds(2 * cols + LANES, LANES)] = jnp.concatenate(parts, axis=0).astype(BF16)


def pack_rows(kernel, tp, own, came, slopes, extra, shape):
    return call(
        kernel,
        (1,),
        [whole(*own.shape), whole(*came.shape), whole(*slopes.shape), whole(*extra.shape)],
        whole(*shape),
        jax.ShapeDtypeStruct(shape, BF16),
        prefetch=1,
        flops=10**6,
        moved=10**5,
    )(tp, own, came, slopes, extra)


def closing_kernel(early_ref, late_ref, hat_ref, inv_ref, gain_ref, both_ref, *refs):
    ffn, attn, outs = refs[:2], refs[2:4], refs[4:]
    gu_ref, down_ref, qkv_ref, out_ref = outs[:4]
    w0_ref, b0_ref, w1_ref, w2_ref, b2_ref, w3_ref, b3_ref, w4_ref, w5_ref, b5_ref = outs[4:14]
    table_ref, pgain_ref, proj_ref, coord_ref = outs[14:]

    def total(pair, block):
        return pair[0][0, block].astype(F32) + pair[1][0, block].astype(F32)

    lanes = ffn[0].shape[3]
    chunks = down_ref.shape[1] // lanes
    for block in range(chunks):
        span = pl.ds(block * lanes, lanes)
        gu_ref[:, 0, span] = total(ffn, block)
        gu_ref[:, 1, span] = total(ffn, chunks + block)
        down_ref[:, span] = total(ffn, 2 * chunks + block)
    third = out_ref.shape[1] // 3
    for i in range(3):
        value = total(attn, i)
        qkv_ref[i] = value[:, : 3 * third]
        out_ref[:, i * third : (i + 1) * third] = value[:, 3 * third :]

    cols = coord_ref.shape[1]
    embed_t = early_ref[:, 4 * cols :].T
    parts = [late_ref[:, :cols], late_ref[:, cols : 2 * cols]] + [early_ref[:, i * cols : (i + 1) * cols] for i in range(4)]
    weights = [w0_ref, w1_ref, w5_ref, w3_ref, w4_ref, w2_ref]
    biases = [b0_ref, None, b5_ref, b3_ref, None, b2_ref]
    for part, weight, bias in zip(parts, weights, biases):
        weight[...] = mm(embed_t, part)
        if bias is not None:
            bias[...] = jnp.sum(part.astype(F32), axis=0)
    extra = late_ref[:, 2 * cols :].reshape(-1, 16, 2 * LANES)
    extra = jnp.sum(extra.astype(F32), axis=0)
    for i in range(cols // LANES):
        coord_ref[:, pl.ds(i * LANES, LANES)] = extra[3 * i : 3 * i + 3, LANES:]
    bins = extra[:, :LANES]
    hat = hat_ref[...]
    gain = gain_ref[...]
    proj = jnp.dot(bins, hat * gain, precision=HIGHEST, preferred_element_type=F32)
    proj_ref[...] = proj[: proj_ref.shape[0]]
    normed_grad = jnp.dot(bins.T, both_ref[...], precision=HIGHEST, preferred_element_type=F32)
    pgain_ref[...] = jnp.sum(normed_grad * hat, axis=0)
    table_ref[...] = norm_back(normed_grad * gain, hat, inv_ref[...])[: table_ref.shape[0]]


def closing(early, late, hat, inv_std, gain, both, ffn, attn, bins, heads):
    cols = (late.shape[1] - 2 * LANES) // 2
    embed = early.shape[1] - 4 * cols
    features = hat.shape[1]
    height, lanes = ffn[0].shape[2:]
    weight, bias = (embed, cols), (cols,)
    hidden = lanes * (ffn[0].shape[1] // 3)
    shapes = [(height, 2, hidden), (height, hidden), (3, height, cols), (height, cols)]
    shapes += [weight, bias, weight, weight, bias, weight, bias, weight, weight, bias]
    shapes += [(bins, features), (features,), (heads, features), (3, cols)]
    args = (early, late, hat, inv_std, gain, both, *ffn, *attn)
    return call(
        closing_kernel,
        (1,),
        [whole(*a.shape) for a in args],
        tuple(whole(*shape) for shape in shapes),
        tuple(jax.ShapeDtypeStruct(shape, F32) for shape in shapes),
        flops=10**8,
        moved=10**7,
    )(*args)


def halve_kernel(place_ref, *refs, plan, count):
    inputs, outs = refs[:count], refs[count:]
    for stream, (bit, sections) in enumerate(plan):
        sent_ref, kept_ref = outs[2 * stream], outs[2 * stream + 1]
        mine = (place_ref[0] >> bit) & 1
        done = 0
        for first, second, base, chunks, left in sections:
            spot = left.index(bit)
            shift = len(left) - 1
            half = 1 << shift

            def body(n, first=first, second=second, base=base, spot=spot, shift=shift, done=done, mine=mine):
                k = n & ((1 << shift) - 1)
                at = base + ((n >> shift) << (shift + 1)) + ((k >> spot) << (spot + 1)) + (k & ((1 << spot) - 1))
                for which, ref in ((1 - mine, sent_ref), (mine, kept_ref)):
                    block = at + (which << spot)
                    ref[0, done + n] = inputs[first][0, block] + inputs[second][0, block]

            block_loop(chunks * half, body)
            done += chunks * half


def halve(place, streams, bits):
    arrays, specs, plan, shapes = [], [], [], []
    steps = streams[0][0][5]
    if any(len(sections) > 1 or sections[0][5] != steps for sections in streams):
        steps = 1

    def operand(array, index):
        for i, (seen, at) in enumerate(arrays):
            if seen is array and at == index:
                return i
        arrays.append((array, index))
        block = (1, array.shape[1] // steps) + array.shape[2:]
        specs.append(pl.BlockSpec(block, lambda j, *_: (index, j, 0, 0)))
        return len(arrays) - 1

    moved = 0
    for sections, bit in zip(streams, bits):
        entries, blocks = [], 0
        for own, i, came, k, base, chunks, left in sections:
            entries.append((operand(own, i), operand(came, k), base, chunks // steps, left))
            blocks += chunks << (len(left) - 1)
        plan.append((bit, entries))
        shape = (1, blocks) + sections[0][0].shape[2:]
        shapes += [shape, shape]
        moved += 12 * blocks * shape[2] * shape[3]
    outs = call(
        functools.partial(halve_kernel, plan=plan, count=len(arrays)),
        (steps,),
        specs,
        tuple(pl.BlockSpec((1, n // steps, h, c), lambda j, *_: (0, j, 0, 0)) for _, n, h, c in shapes),
        tuple(jax.ShapeDtypeStruct(shape, BF16) for shape in shapes),
        prefetch=1,
        flops=10**6,
        moved=moved,
    )(place, *[array for array, _ in arrays])
    return list(outs[0::2]), list(outs[1::2])


def swap(values):
    return lax.ppermute(values, "tp", [(0, 1), (1, 0)])


def after(values, *others):
    return lax.optimization_barrier((values, *others))[0]


class Cube:
    def __init__(self, rows):
        self.bits = rows.bit_length() - 1
        assert rows == 1 << self.bits
        self.place = lax.axis_index("rows").reshape(1).astype(jnp.int32)
        self.perms = [[(i, i ^ (1 << b)) for i in range(rows)] for b in range(self.bits)]

    def turns(self):
        return [[(i + r) % 3 for i in range(3)] for r in range(3)]

    def gather(self, values, step):
        bit = (list(range(self.bits - 1, 1, -1)) + list(range(min(2, self.bits))))[step]
        came = lax.ppermute(values, "rows", self.perms[bit])
        return lax.optimization_barrier(jnp.concatenate([values, came], axis=0))


def next_sections(sections, kept, came, bit):
    made, base = [], 0
    for _, _, _, _, _, chunks, left in sections:
        left = [b for b in left if b != bit]
        made.append((kept, 0, came, 0, base, chunks, left))
        base += chunks << len(left)
    return made


def normalize(values):
    centre = jnp.mean(values, axis=-1, keepdims=True)
    shifted = values - centre
    spread = jnp.mean(shifted * shifted, axis=-1, keepdims=True)
    inv_std = lax.rsqrt(spread + EPSILON)
    return shifted * inv_std, inv_std


def three_parts(values):
    high = lax.reduce_precision(values, 8, 7)
    middle = lax.reduce_precision(values - high, 8, 7)
    low = values - high - middle
    return jnp.concatenate([high, middle, low], axis=0).astype(BF16)


def bias_base(heads):
    bins = heads.shape[1]
    low = lambda n: jnp.broadcast_to(heads[:, :1], (heads.shape[0], n))
    top = lambda n: jnp.broadcast_to(heads[:, bins - 1 :], (heads.shape[0], n))
    fill = HALF - RADIUS
    behind = jnp.concatenate([low(fill), heads[:, :RADIUS], low(HALF)], axis=1)
    same = jnp.concatenate([heads[:, RADIUS:], top(fill - 1), low(fill), heads[:, :RADIUS]], axis=1)
    ahead = jnp.concatenate([top(HALF), heads[:, RADIUS:], top(fill - 1)], axis=1)
    return jnp.stack([behind, same, ahead], axis=1)


def bins_of_diagonals():
    places = jnp.arange(ROW, dtype=jnp.int32)[None, :] - (HALF - 1)
    offsets = places + HALF * jnp.arange(-1, 2, dtype=jnp.int32)[:, None]
    bins = jnp.clip(offsets, -RADIUS, RADIUS) + RADIUS
    every = jnp.arange(2 * RADIUS + 1, dtype=jnp.int32)
    return (bins.reshape(-1)[:, None] == every[None, :]).astype(F32)


def per_device(
    layer_input,
    cotangent,
    chain_lengths,
    self_condition_flag,
    time_embedding,
    query_key_value,
    output_projection,
    attention_scale_weight,
    attention_scale_bias,
    attention_shift_weight,
    attention_gate_weight,
    attention_gate_bias,
    transition_scale_weight,
    transition_scale_bias,
    transition_shift_weight,
    transition_gate_weight,
    transition_gate_bias,
    gate_up_projection,
    down_projection,
    pair_table,
    pair_gain,
    pair_projection,
    coordinate_head,
    coordinate_embedding,
    rows,
):
    core = lax.axis_index("tp")
    first_core = core == 0
    tp = core.reshape(1).astype(jnp.int32)
    cols = layer_input.shape[1]
    width = query_key_value.shape[0]
    heads_here = pair_projection.shape[1]
    bins = pair_table.shape[0]
    cube = Cube(rows)

    def side_by_side(own, came, axis):
        return jnp.where(
            first_core, jnp.concatenate([own, came], axis), jnp.concatenate([came, own], axis)
        )

    def scatter_tokens(own, sent):
        came = swap(sent)
        lower = jnp.concatenate([own[:ROW], own[ROW:], came[ROW:], came[:ROW]], axis=0)
        upper = jnp.concatenate([came[:ROW], came[ROW:], own[ROW:], own[:ROW]], axis=0)
        return jnp.where(first_core, lower, upper)

    x_own, x_sent, cot_own, cot_sent = token_halves(tp, layer_input, cotangent)
    x_came = swap(x_sent)
    qkv_own = query_key_value.reshape(width, -1)
    qkv_par = swap(qkv_own)

    mods, early_slopes, late_slopes, embed = modulations(
        time_embedding,
        [
            attention_scale_weight,
            attention_shift_weight,
            attention_gate_weight,
            transition_scale_weight,
            transition_shift_weight,
            transition_gate_weight,
        ],
        [attention_scale_bias, attention_gate_bias, transition_scale_bias, transition_gate_bias],
    )
    table = chain_table(tp, mods, swap(mods))
    mask_q, mask_k, pick, pick_t, flags = masks(tp, chain_lengths, self_condition_flag)

    pair_hat, pair_inv = normalize(pair_table.astype(F32))
    gain = pair_gain.astype(F32)
    pair_normed = pair_hat * gain
    pair_both = jnp.concatenate([pair_projection, swap(pair_projection)], axis=1).astype(F32)
    bias_heads = jnp.transpose(jnp.dot(pair_normed, pair_both, precision=HIGHEST))
    bias_source = jnp.transpose(pair_both)
    bias = bias_tiles(bias_base(bias_heads))

    out_own = output_projection
    out_par = swap(output_projection)
    gu_own = jnp.transpose(gate_up_projection, (1, 0, 2))
    gu_par = swap(gu_own)
    down_own = down_projection
    down_par = swap(down_projection)
    coord = jnp.concatenate([coordinate_head, coordinate_embedding], axis=0)
    coord = side_by_side(coord, swap(coord), 1)
    fill = jnp.zeros((LANES - 3, width), BF16)
    head = jnp.concatenate([coord[:3], fill], axis=0)
    emb = jnp.concatenate([coord[3:], fill], axis=0)
    cot_came = swap(cot_sent)

    def attention(qkv):
        kv_par = swap(qkv[ROW:, width:])
        attended, logs = attend_forward(tp, qkv, kv_par, mask_q, mask_k, bias)
        return qkv, kv_par, attended, logs

    qkv, x = qkv_first(tp, x_own, x_came, pick, table, qkv_own, qkv_par)
    _, _, attended, _ = attention(qkv)
    shifted, lifted = ffn_forward(
        attended, out_own, out_par, x, pick, table, gu_own, gu_par, down_own, down_par, head, emb, flags
    )
    qkv, kv_par, attended, logs = attention(qkv_forward(shifted, pick, table, qkv_own, qkv_par))
    (
        result_own,
        result_sent,
        grad_middle,
        grad_attended,
        grads_own,
        grads_sent,
        grad_out_own,
        grad_out_sent,
        early_own,
        early_sent,
    ) = ffn_turn(
        tp, attended, out_own, out_par, shifted, pick, table, gu_own, gu_par, down_own, down_par, cot_own, cot_came, pick_t
    )

    early_came = swap(early_sent)

    came_ffn = swap(grads_sent)
    half_grads, far_grads, diag_half = attend_half_back(
        tp, qkv, kv_par, grad_attended, logs, mask_q, mask_k, bias
    )
    came_grads = swap(far_grads)

    turns = cube.turns()
    every = list(range(cube.bits))
    height = width // rows
    slots = lambda values: values.reshape(3, -1, height, values.shape[-1])
    chunks = grads_own.shape[1]
    own_slots, came_slots = slots(grads_own), slots(came_ffn)
    ffn = [[(own_slots, i, came_slots, i, 0, chunks, every)] for i in range(3)]

    def one_round(streams, bits, *others):
        sent, kept = halve(cube.place, streams, bits)
        held = lax.optimization_barrier((*sent, *others))
        came = [lax.ppermute(v, "rows", cube.perms[bit]) for v, bit in zip(held, bits)]
        made = [next_sections(*parts) for parts in zip(streams, kept, came, bits)]
        return made, came, held[len(sent) :]

    early_came, _ = lax.optimization_barrier((early_came, diag_half))
    early = pack_rows(
        early_kernel, tp, early_own, early_came, early_slopes, embed, (16, 4 * cols + embed.shape[1])
    )
    ffn, came, (mask_full, early, _) = one_round(ffn, turns[0], mask_q, early, diag_half)
    full_grads, diag_full = attend_full_back(qkv, grad_attended, logs, mask_full, mask_k, bias)
    early = cube.gather(early, 0)
    ffn, came, (pick_weights, early, _) = one_round(ffn, turns[1], pick, early, diag_full)
    gqkv_own, gqkv_sent = qkv_weights(
        shifted, pick_weights, table, full_grads, half_grads, came_grads, grad_out_own, grad_out_sent
    )
    early = cube.gather(early, 1)
    gqkv_sent, early, *_ = lax.optimization_barrier((gqkv_sent, early, *came))
    own_slots, came_slots = slots(gqkv_own), slots(swap(gqkv_sent))
    streams = [ffn[i] + [(own_slots, i, came_slots, i, 0, 1, every)] for i in range(3)]
    streams, came, (pick_back, early) = one_round(streams, turns[2], pick_weights, early)
    gin_own, gin_sent, late_own, late_sent = qkv_back(
        tp, shifted, pick_back, table, full_grads, half_grads, came_grads, qkv_own, qkv_par, grad_middle, lifted, pick_t
    )
    early = cube.gather(early, 2)
    late_sent, early, *_ = lax.optimization_barrier((late_sent, early, *came))

    diag_half = diag_half[:, :4].reshape(-1, 2, ROW)
    quiet = jnp.zeros_like(diag_half[:, 0])
    diag_far = diag_half[:, 1]
    diag = diag_full[:, :6].reshape(-1, 3, ROW) + jnp.stack(
        [
            jnp.where(first_core, diag_far, quiet),
            diag_half[:, 0],
            jnp.where(first_core, quiet, diag_far),
        ],
        axis=1,
    )
    grad_bins = jnp.dot(diag.reshape(-1, 3 * ROW), bins_of_diagonals(), precision=HIGHEST)
    came_bins = swap(grad_bins)
    grad_bins = grad_bins + jnp.concatenate([came_bins[heads_here:], came_bins[:heads_here]], axis=0)
    bins_fill = jnp.pad(grad_bins, ((0, 16 - 2 * heads_here), (0, LANES - bins)))

    late_came = swap(late_sent)
    late = pack_rows(late_kernel, tp, late_own, late_came, late_slopes, bins_fill, (16, 2 * cols + 2 * LANES))
    ffn = [[stream[0] for stream in streams]]
    attn = [stream[1:] for stream in streams]
    rest = list(range(3, cube.bits))
    waited = []
    for step in range(max(len(rest), 2)):
        now, bits = [], []
        if step < len(rest):
            now, bits = ffn, rest[step : step + 1]
        count = len(now)
        if step < 2:
            attn, came, _ = one_round(attn, turns[step], *waited)
        late = cube.gather(late, step)
        if count:
            ffn, waited, (late,) = one_round(now, bits, late)
    done = max(len(rest), 2)
    attn = [[section for stream in attn for section in stream]]
    for bit in rest:
        attn, came, _ = one_round(attn, [bit])
        if done < cube.bits:
            late = cube.gather(late, done)
            done += 1
    for step in range(done, cube.bits):
        late = cube.gather(late, step)
    for step in range(3, cube.bits):
        early = cube.gather(early, step)
    ffn_last = (ffn[0][0][0], ffn[0][0][2])
    attn_last = (attn[0][0][0], attn[0][0][2])

    layer_output = scatter_tokens(result_own, result_sent)
    input_gradient = scatter_tokens(gin_own, gin_sent)

    bins_pad = ((0, LANES - bins), (0, 0))
    grad_gu, grad_down, grad_qkv, grad_out, *conditioning = closing(
        early,
        late,
        jnp.pad(pair_hat, bins_pad),
        jnp.pad(pair_inv, bins_pad),
        gain[None, :],
        jnp.pad(bias_source, ((0, 16 - 2 * heads_here), (0, 0))),
        ffn_last,
        attn_last,
        bins,
        heads_here,
    )
    *conditioning, grad_table, grad_gain, grad_pair, coord_grad = conditioning
    return (
        layer_output,
        input_gradient,
        jnp.transpose(grad_qkv, (1, 0, 2)),
        grad_out.T,
        *conditioning,
        grad_gu,
        grad_down.T,
        grad_table,
        grad_gain,
        grad_pair.T,
        coord_grad,
    )


def solution(mesh):
    in_specs = (
        P("rows", "tp"),
        P("rows", "tp"),
        P("rows", None),
        P("rows"),
        P("rows", None, None),
        P(None, None, "tp"),
        P("tp", None),
        P(None, "tp"),
        P("tp"),
        P(None, "tp"),
        P(None, "tp"),
        P("tp"),
        P(None, "tp"),
        P("tp"),
        P(None, "tp"),
        P(None, "tp"),
        P("tp"),
        P(None, None, "tp"),
        P("tp", None),
        P(),
        P(),
        P(None, "tp"),
        P(None, "tp"),
        P(None, "tp"),
    )
    out_specs = (
        P("rows", "tp"),
        P("rows", "tp"),
        P("rows", None, "tp"),
        P("tp", "rows"),
        P(None, "tp"),
        P("tp"),
        P(None, "tp"),
        P(None, "tp"),
        P("tp"),
        P(None, "tp"),
        P("tp"),
        P(None, "tp"),
        P(None, "tp"),
        P("tp"),
        P("rows", None, "tp"),
        P("tp", "rows"),
        P(),
        P(),
        P(None, "tp"),
        P(None, "tp"),
    )
    return jax.shard_map(
        functools.partial(per_device, rows=mesh.shape["rows"]),
        mesh=mesh,
        in_specs=in_specs,
        out_specs=out_specs,
        check_vma=False,
    )
```

```python
import functools
import jax
import jax.numpy as jnp
from jax import lax
from jax.experimental import pallas as pl
from jax.experimental.pallas import tpu as pltpu
from jax.sharding import PartitionSpec as P

RADIUS = 32
ROW = 512
HALF = ROW // 2
SEGS = 5
EPSILON = 1e-05
MASKED = -1e30
HIGHEST = lax.Precision.HIGHEST
F32 = jnp.float32
BF16 = jnp.bfloat16
LANES = 128
FFC = 512
BLOCK = 384
SUB = 8
NT = (((1,), (1,)), ((), ()))
VMEM_LIMIT = 60 * 1024 * 1024


def mm(left, right):
    return jnp.dot(left, right, preferred_element_type=F32)


def mm_nt(left, right):
    return lax.dot_general(left, right, NT, preferred_element_type=F32)


def norm_parts(values):
    centre = jnp.mean(values, axis=1, keepdims=True)
    shifted = values - centre
    spread = jnp.mean(shifted * shifted, axis=1, keepdims=True)
    inv_std = lax.rsqrt(spread + EPSILON)
    return shifted * inv_std, inv_std


def norm_back(grad, hat, inv_std):
    first = jnp.mean(grad, axis=1, keepdims=True)
    second = jnp.mean(grad * hat, axis=1, keepdims=True)
    return inv_std * (grad - first - hat * second)


def block_loop(count, body):
    lax.fori_loop(0, count, lambda i, c: (body(i), c)[1], 0)


def call(kernel, grid, in_specs, out_specs, out_shape, scratch=(), prefetch=0, aliases=None, flops=0, moved=0):
    return pl.pallas_call(
        kernel,
        grid_spec=pltpu.PrefetchScalarGridSpec(
            num_scalar_prefetch=prefetch,
            grid=grid,
            in_specs=in_specs,
            out_specs=out_specs,
            scratch_shapes=list(scratch),
        ),
        out_shape=out_shape,
        input_output_aliases=aliases or {},
        compiler_params=pltpu.CompilerParams(
            dimension_semantics=("arbitrary",) * len(grid), vmem_limit_bytes=VMEM_LIMIT
        ),
        cost_estimate=pl.CostEstimate(flops=flops, transcendentals=0, bytes_accessed=moved),
    )


def whole(*shape):
    zeros = (0,) * len(shape)
    return pl.BlockSpec(shape, lambda *_: zeros)


def bias_kernel(base_ref, near_ref, far_ref):
    for d, height, start, out in (
        (1, HALF, 0, near_ref.at[0]),
        (0, RADIUS, 0, far_ref.at[0, 0]),
        (2, RADIUS, HALF - RADIUS, far_ref.at[0, 1]),
    ):
        rows = jnp.broadcast_to(base_ref[0, d : d + 1, :], (SUB, 2 * HALF))
        rows = pltpu.roll(rows, 0, axis=1, stride=1, stride_axis=0)
        for a in range(0, height, SUB):
            out[a : a + SUB, :] = pltpu.roll(rows, start + a, axis=1)[:, :HALF]


def bias_tiles(base):
    heads = base.shape[0]
    near, far = (heads, HALF, HALF), (heads, 2, RADIUS, HALF)
    return call(
        bias_kernel,
        (heads,),
        [pl.BlockSpec((1, 3, 2 * HALF), lambda h: (h, 0, 0))],
        (
            pl.BlockSpec((1,) + near[1:], lambda h: (h, 0, 0)),
            pl.BlockSpec((1,) + far[1:], lambda h: (h, 0, 0, 0)),
        ),
        (jax.ShapeDtypeStruct(near, F32), jax.ShapeDtypeStruct(far, F32)),
        moved=heads * HALF * HALF * 4,
        flops=10**7,
    )(base)


def bias_specs():
    return [
        pl.BlockSpec((2, HALF, HALF), lambda p, *_: (p, 0, 0)),
        pl.BlockSpec((2, 2, RADIUS, HALF), lambda p, *_: (p, 0, 0, 0)),
    ]


def add_near(near_ref, far_ref, h, scores):
    return scores + near_ref[h]


def add_later(near_ref, far_ref, h, scores):
    edge = far_ref[h, 0]
    return jnp.concatenate([scores[:RADIUS] + edge, scores[RADIUS:] + edge[RADIUS - 1 :, :1]], axis=0)


def add_earlier(near_ref, far_ref, h, scores):
    edge = far_ref[h, 1]
    return jnp.concatenate(
        [scores[: HALF - RADIUS] + edge[:1, HALF - 1 :], scores[HALF - RADIUS :] + edge], axis=0
    )


def add_either(first, near_ref, far_ref, h, scores):
    later, earlier = far_ref[h, 0], far_ref[h, 1]
    rest = jnp.where(first, later[RADIUS - 1 :, :1], earlier[:1, HALF - 1 :])
    return jnp.concatenate(
        [
            scores[:RADIUS] + jnp.where(first, later, rest),
            scores[RADIUS : HALF - RADIUS] + rest,
            scores[HALF - RADIUS :] + jnp.where(first, rest, earlier),
        ],
        axis=0,
    )


def full_biases(near_ref, far_ref, qb):
    kinds = (add_near, add_later) if qb == 0 else (add_earlier, add_near)
    return [functools.partial(kind, near_ref, far_ref) for kind in kinds]


def half_biases(near_ref, far_ref, first):
    return [
        functools.partial(add_near, near_ref, far_ref),
        functools.partial(add_either, first, near_ref, far_ref),
    ]


def mods_kernel(time_ref, *refs):
    weights, biases = refs[:6], {0: refs[6], 2: refs[7], 3: refs[8], 5: refs[9]}
    mods_ref, early_ref, late_ref, embed_ref = refs[10:]
    rows = []
    blank = jnp.zeros((1, time_ref.shape[2]), F32)
    for i in range(time_ref.shape[0]):
        rows += [time_ref[i].astype(F32), blank]
    embed_ref[...] = jnp.concatenate(rows + [blank] * (16 - SEGS * time_ref.shape[0]), axis=0).astype(BF16)
    cols = early_ref.shape[1] // 4
    homes = {0: (late_ref, 0), 1: (late_ref, 1), 5: (early_ref, 0), 3: (early_ref, 1), 4: (early_ref, 2), 2: (early_ref, 3)}
    for i in range(6):
        value = mm(embed_ref[...], weights[i][...])
        slope = jnp.ones_like(value)
        if i in biases:
            value = jax.nn.sigmoid(value + biases[i][...].astype(F32).reshape(1, cols))
            slope = value * (1.0 - value)
        mods_ref[i] = value
        home, place = homes[i]
        home[:, pl.ds(place * cols, cols)] = slope


def modulations(embed, weights, biases):
    cols = weights[0].shape[1]
    args = (embed, *weights, *biases)
    shapes = [(6, 16, cols), (16, 4 * cols), (16, 2 * cols), (16, embed.shape[2])]
    return call(
        mods_kernel,
        (1,),
        [whole(*a.shape) for a in args],
        tuple(whole(*shape) for shape in shapes),
        tuple(jax.ShapeDtypeStruct(shape, dtype) for shape, dtype in zip(shapes, (F32, F32, F32, BF16))),
        flops=10**8,
        moved=2 * 10**6,
    )(*args)


def table_kernel(tp_ref, own_ref, came_ref, o_ref):
    first = tp_ref[0] == 0
    row = lax.broadcasted_iota(jnp.int32, (32, 16), 0)
    col = lax.broadcasted_iota(jnp.int32, (32, 16), 1)
    part = (row >= 2 * SEGS).astype(jnp.int32) + (row >= 4 * SEGS).astype(jnp.int32)
    chain = row - 2 * SEGS * part
    chain = chain + jnp.where((chain < SEGS) & jnp.logical_not(first), 2 * SEGS, 0)
    take = ((col == chain) & (row < 6 * SEGS)).astype(F32)
    rows = lax.broadcasted_iota(jnp.int32, (32, 1), 0)
    width = 2 * own_ref.shape[2]
    for i in range(6):
        own, came = own_ref[i], came_ref[i]
        low, high = jnp.where(first, own, came), jnp.where(first, came, own)
        value = jnp.dot(take, jnp.concatenate([low, high], axis=1), precision=HIGHEST, preferred_element_type=F32)
        top = value.astype(BF16).astype(F32)
        middle = (value - top).astype(BF16).astype(F32)
        parts = jnp.where(rows < 2 * SEGS, top, jnp.where(rows < 4 * SEGS, middle, value - top - middle))
        o_ref[:, pl.ds(i * width, width)] = parts.astype(BF16)


def chain_table(tp, own, came):
    shape = (32, 12 * own.shape[2])
    return call(
        table_kernel,
        (1,),
        [whole(*own.shape), whole(*came.shape)],
        whole(*shape),
        jax.ShapeDtypeStruct(shape, BF16),
        prefetch=1,
        flops=10**7,
        moved=10**6,
    )(tp, own, came)


def masks_kernel(tp_ref, length_ref, flag_ref, q_ref, k_ref, pick_ref, turn_ref, marks_ref):
    core = tp_ref[0]

    def segments(pack, shape, axis, start):
        spot = lax.broadcasted_iota(jnp.int32, shape, axis) + start
        segment = jnp.zeros(shape, jnp.int32)
        end = 0
        for i in range(SEGS - 1):
            end = end + length_ref[pack, i]
            segment = segment + (spot >= end).astype(jnp.int32)
        return segment

    runs = [(2 * core, 0, 0), (2 * core, HALF, 0), (1, HALF * core, SEGS), (1, HALF * (1 - core), SEGS)]
    for i, (pack, start, shift) in enumerate(runs):
        rows = pl.ds(i * HALF, HALF)
        segment = segments(pack, (HALF, LANES), 0, start)
        lanes = lax.broadcasted_iota(jnp.int32, (HALF, LANES), 1)
        k_ref[rows, :] = (segment == lanes).astype(F32).astype(BF16)
        if i == 3:
            break
        q_ref[rows, :] = jnp.where((segment != lanes) & (lanes < SEGS), MASKED, 0.0).astype(BF16)
        chain = (segment + shift)[:, :32]
        lanes = lanes[:, :32]
        spot = lanes - 2 * SEGS * (
            (lanes >= 2 * SEGS).astype(jnp.int32) + (lanes >= 4 * SEGS).astype(jnp.int32)
        )
        pick_ref[rows, :] = ((chain == spot) & (lanes < 6 * SEGS)).astype(F32).astype(BF16)
        marks_ref[rows, :] = jnp.full((HALF, 1), flag_ref[pack].astype(F32))
        across = segments(pack, (16, HALF), 1, start) + shift
        turn_ref[i] = (across == lax.broadcasted_iota(jnp.int32, (16, HALF), 0)).astype(F32).astype(BF16)


def masks(tp, lengths, flags):
    shapes = [(3 * HALF, LANES), (4 * HALF, LANES), (3 * HALF, 32), (3, 16, HALF)]
    return call(
        masks_kernel,
        (1,),
        [],
        tuple(whole(*shape) for shape in shapes) + (whole(3 * HALF, 1),),
        tuple(jax.ShapeDtypeStruct(shape, BF16) for shape in shapes)
        + (jax.ShapeDtypeStruct((3 * HALF, 1), F32),),
        prefetch=3,
        flops=10**6,
        moved=10**6,
    )(tp, lengths, flags)


def halves_kernel(tp_ref, *refs):
    for source, target in zip(refs[:4], refs[4:]):
        target[...] = source[...]


def token_halves(tp, first, second):
    cols = first.shape[1]

    def mine(j, tp_ref):
        return jnp.where(j < 2, 4 * tp_ref[0] + j, 2 + tp_ref[0]), 0

    def others(j, tp_ref):
        return jnp.where(j < 2, 4 * (1 - tp_ref[0]) + j, 3 - tp_ref[0]), 0

    spec = pl.BlockSpec((HALF, cols), lambda j, _: (j, 0))
    shape = jax.ShapeDtypeStruct((3 * HALF, cols), BF16)
    places = [pl.BlockSpec((HALF, cols), place) for place in (mine, others)]
    return call(
        halves_kernel, (3,), places + places, (spec,) * 4, (shape,) * 4, prefetch=1, flops=10, moved=24 * HALF * cols
    )(tp, first, first, second, second)


def put_together(first_core, own, came):
    return jnp.concatenate([jnp.where(first_core, own, came), jnp.where(first_core, came, own)], axis=1)


def qkv_first_kernel(tp_ref, xo_ref, xp_ref, oh_ref, tab_ref, own_ref, par_ref, o_ref, kv_ref, x_ref, normed):
    @pl.when(pl.program_id(0) == 0)
    def _():
        x_ref[...] = put_together(tp_ref[0] == 0, xo_ref[...], xp_ref[...])

    qkv_kernel(x_ref, oh_ref, tab_ref, own_ref, par_ref, o_ref, kv_ref, normed)


def qkv_kernel(x_ref, oh_ref, tab_ref, own_ref, par_ref, o_ref, kv_ref, normed):
    width = x_ref.shape[1]
    half = own_ref.shape[1]

    @pl.when(pl.program_id(0) == 0)
    def _():
        def body(i):
            rows = pl.ds(pl.multiple_of(i * HALF, HALF), HALF)
            hat, _ = norm_parts(x_ref[rows, :].astype(F32))
            pick = oh_ref[rows, :]
            scale = mm(pick, tab_ref[:, :width])
            shift = mm(pick, tab_ref[:, width : 2 * width])
            normed[rows, :] = (hat * scale + shift).astype(BF16)

        block_loop(x_ref.shape[0] // HALF, body)

    o_ref[:, :half] = mm(normed[...], own_ref[...]).astype(BF16)
    o_ref[:, half:] = mm(normed[...], par_ref[...]).astype(BF16)
    kv_ref[...] = o_ref[pl.ds(ROW, HALF), :]


def qkv_outs(tokens, half):
    specs = (
        pl.BlockSpec((tokens, 2 * half), lambda j, *_: (0, j)),
        pl.BlockSpec((HALF, 2 * half), lambda j, *_: (0, jnp.maximum(j - 1, 0))),
    )
    return specs, (jax.ShapeDtypeStruct((tokens, 6 * half), BF16), jax.ShapeDtypeStruct((HALF, 4 * half), BF16))


def qkv_first(tp, x_own, x_came, pick, table, w_own, w_par):
    tokens, cols = x_own.shape
    width = 2 * cols
    half = w_own.shape[1] // 3
    return call(
        qkv_first_kernel,
        (3,),
        [
            whole(tokens, cols),
            whole(tokens, cols),
            whole(*pick.shape),
            whole(*table.shape),
            pl.BlockSpec((width, half), lambda j, *_: (0, j)),
            pl.BlockSpec((width, half), lambda j, *_: (0, j)),
        ],
        (*qkv_outs(tokens, half)[0], whole(tokens, width)),
        (*qkv_outs(tokens, half)[1], jax.ShapeDtypeStruct((tokens, width), BF16)),
        [pltpu.VMEM((tokens, width), BF16)],
        prefetch=1,
        flops=2 * tokens * width * 6 * half,
        moved=tokens * 6 * half * 2 + width * half * 12 + tokens * width * 4,
    )(tp, x_own, x_came, pick, table, w_own, w_par)


def qkv_forward(x, pick, table, w_own, w_par):
    tokens, width = x.shape
    half = w_own.shape[1] // 3
    return call(
        qkv_kernel,
        (3,),
        [
            whole(tokens, width),
            whole(*pick.shape),
            whole(*table.shape),
            pl.BlockSpec((width, half), lambda j: (0, j)),
            pl.BlockSpec((width, half), lambda j: (0, j)),
        ],
        *qkv_outs(tokens, half),
        [pltpu.VMEM((tokens, width), BF16)],
        flops=2 * tokens * width * 6 * half,
        moved=tokens * 6 * half * 2 + width * half * 12 + tokens * width * 4,
    )(x, pick, table, w_own, w_par)


def lane_masks():
    lanes = lax.broadcasted_iota(jnp.int32, (1, LANES), 1)
    first = (lanes < LANES // 2).astype(F32)
    return first.astype(BF16), (1.0 - first).astype(BF16)


def attend_forward_block(q, segq, keys, values_t, biases):
    outs, logs = [], []
    half = LANES // 2
    masks = lane_masks()
    scaled = q * jnp.asarray(half**-0.5, BF16)
    for h in range(2):
        query = jnp.concatenate([scaled * masks[h], segq], axis=1)
        scores = [bias(h, mm_nt(key, query)) for key, bias in zip(keys, biases)]
        tops = [jnp.max(s, axis=0, keepdims=True) for s in scores]
        top = functools.reduce(jnp.maximum, tops)
        weights = [jnp.exp(s - top) for s in scores]
        total = sum(jnp.sum(w, axis=0, keepdims=True) for w in weights)
        mixed = sum(
            mm(vt[h * half : (h + 1) * half, :], w.astype(BF16)) for vt, w in zip(values_t, weights)
        )
        outs.append(mixed / total)
        logs.append(top + jnp.log(total))
    attended = jnp.concatenate(outs, axis=0).T.astype(BF16)
    return attended, jnp.concatenate(logs, axis=0)


def attend_full_kernel(q_ref, k_ref, v_ref, segq_ref, segk_ref, near_ref, far_ref, o_ref, log_ref):
    keys = [
        jnp.concatenate([k_ref[pl.ds(b * HALF, HALF), :], segk_ref[pl.ds(b * HALF, HALF), :]], axis=1)
        for b in range(2)
    ]
    values_t = [v_ref[pl.ds(b * HALF, HALF), :].T for b in range(2)]
    for qb in range(2):
        rows = pl.ds(qb * HALF, HALF)
        biases = full_biases(near_ref, far_ref, qb)
        attended, logs = attend_forward_block(q_ref[rows, :], segq_ref[rows, :], keys, values_t, biases)
        o_ref[rows, :] = attended
        log_ref[0, 0:2, rows] = logs


def attend_half_kernel(
    tp_ref, q_ref, k_ref, v_ref, kp_ref, vp_ref, segq_ref, segk_ref, near_ref, far_ref, oin, login, o_ref, log_ref
):
    keys = [
        jnp.concatenate([k_ref[...], segk_ref[pl.ds(0, HALF), :]], axis=1),
        jnp.concatenate([kp_ref[...], segk_ref[pl.ds(HALF, HALF), :]], axis=1),
    ]
    values_t = [v_ref[...].T, vp_ref[...].T]
    biases = half_biases(near_ref, far_ref, tp_ref[0] == 0)
    attended, logs = attend_forward_block(q_ref[...], segq_ref[...], keys, values_t, biases)
    o_ref[...] = attended
    log_ref[0, 0:2, :] = logs


def attend_forward(tp, qkv, kv_par, segq, segk, bias):
    tokens = qkv.shape[0]
    width = qkv.shape[1] // 3
    pairs = width // LANES
    out_shape = (
        jax.ShapeDtypeStruct((tokens, width), BF16),
        jax.ShapeDtypeStruct((pairs, 8, tokens), F32),
    )
    unit = 4 * HALF * HALF * 256 * 2
    attended, logs = call(
        attend_full_kernel,
        (pairs,),
        [
            pl.BlockSpec((ROW, LANES), lambda p: (0, p)),
            pl.BlockSpec((ROW, LANES), lambda p: (0, pairs + p)),
            pl.BlockSpec((ROW, LANES), lambda p: (0, 2 * pairs + p)),
            pl.BlockSpec((ROW, LANES), lambda p: (0, 0)),
            pl.BlockSpec((ROW, LANES), lambda p: (0, 0)),
        ]
        + bias_specs(),
        (
            pl.BlockSpec((ROW, LANES), lambda p: (0, p)),
            pl.BlockSpec((1, 8, ROW), lambda p: (p, 0, 0)),
        ),
        out_shape,
        flops=unit * 4 * pairs,
        moved=bias[0].size * 4,
    )(qkv, qkv, qkv, segq, segk, *bias)
    flip = pairs // 2
    return call(
        attend_half_kernel,
        (pairs,),
        [
            pl.BlockSpec((HALF, LANES), lambda p, *_: (2, p)),
            pl.BlockSpec((HALF, LANES), lambda p, *_: (2, pairs + p)),
            pl.BlockSpec((HALF, LANES), lambda p, *_: (2, 2 * pairs + p)),
            pl.BlockSpec((HALF, LANES), lambda p, *_: (0, lax.rem(p + flip, pairs))),
            pl.BlockSpec((HALF, LANES), lambda p, *_: (0, pairs + lax.rem(p + flip, pairs))),
            pl.BlockSpec((HALF, LANES), lambda p, *_: (2, 0)),
            pl.BlockSpec((ROW, LANES), lambda p, *_: (1, 0)),
        ]
        + bias_specs()
        + [pl.BlockSpec(memory_space=pl.ANY), pl.BlockSpec(memory_space=pl.ANY)],
        (
            pl.BlockSpec((HALF, LANES), lambda p, *_: (2, p)),
            pl.BlockSpec((1, 8, HALF), lambda p, *_: (p, 0, 2)),
        ),
        out_shape,
        prefetch=1,
        aliases={10: 0, 11: 1},
        flops=unit * 2 * pairs,
        moved=bias[0].size * 4,
    )(tp, qkv, qkv, qkv, kv_par, kv_par, segq, segk, *bias, attended, logs)


def ffn_kernel(
    att_ref, woo_ref, wop_ref, x_ref, oh_ref, tab_ref, guo_ref, gup_ref, wdo_ref, wdp_ref,
    head_ref, emb_ref, flag_ref, shifted_ref, lifted_ref, middle, normed, acc,
):
    step = pl.program_id(0)
    tokens, width = x_ref.shape
    half = woo_ref.shape[0]
    blocks = tokens // HALF

    @pl.when(step == 0)
    def _():
        def body(i):
            rows = pl.ds(pl.multiple_of(i * HALF, HALF), HALF)
            branch = mm(att_ref[rows, :half], woo_ref[...]) + mm(att_ref[rows, half:], wop_ref[...])
            pick = oh_ref[rows, :]
            mid = x_ref[rows, :].astype(F32) + mm(pick, tab_ref[:, 2 * width : 3 * width]) * branch
            middle[rows, :] = mid
            hat, _ = norm_parts(mid)
            scale = mm(pick, tab_ref[:, 3 * width : 4 * width])
            shift = mm(pick, tab_ref[:, 4 * width : 5 * width])
            normed[rows, :] = (hat * scale + shift).astype(BF16)
            acc[rows, :] = jnp.zeros((HALF, width), F32)

        block_loop(blocks, body)

    def body(i):
        rows = pl.ds(pl.multiple_of(i * HALF, HALF), HALF)
        total = acc[rows, :]
        for gu, wd in ((guo_ref, wdo_ref), (gup_ref, wdp_ref)):
            gate = mm(normed[rows, :], gu[0])
            up = mm(normed[rows, :], gu[1])
            hidden = (gate * jax.nn.sigmoid(gate) * up).astype(BF16)
            total = total + mm(hidden, wd[...])
        acc[rows, :] = total

    block_loop(blocks, body)

    @pl.when(step == pl.num_programs(0) - 1)
    def _():
        def body(i):
            rows = pl.ds(pl.multiple_of(i * HALF, HALF), HALF)
            gate = mm(oh_ref[rows, :], tab_ref[:, 5 * width : 6 * width])
            first = middle[rows, :] + gate * acc[rows, :]
            high = first.astype(BF16)
            rest = (first - high.astype(F32)).astype(BF16)
            coords = mm_nt(high, head_ref[...]) + mm_nt(rest, head_ref[...])
            lifted = coords * flag_ref[rows, :]
            lifted_ref[rows, :] = lifted
            high = lifted.astype(BF16)
            rest = (lifted - high.astype(F32)).astype(BF16)
            moved = mm(high, emb_ref[...]) + mm(rest, emb_ref[...])
            shifted_ref[rows, :] = x_ref[rows, :].astype(F32) + moved

        block_loop(blocks, body)


def ffn_specs(att, woo, x, pick, table):
    tokens, width = x.shape
    chunk = FFC
    return [
        whole(*att.shape),
        whole(*woo.shape),
        whole(*woo.shape),
        whole(tokens, width),
        whole(*pick.shape),
        whole(*table.shape),
        pl.BlockSpec((2, width, chunk), lambda j, *_: (0, 0, j)),
        pl.BlockSpec((2, width, chunk), lambda j, *_: (0, 0, j)),
        pl.BlockSpec((chunk, width), lambda j, *_: (j, 0)),
        pl.BlockSpec((chunk, width), lambda j, *_: (j, 0)),
    ]


def ffn_forward(att, woo, wop, x, pick, table, guo, gup, wdo, wdp, head, emb, flags):
    tokens, width = x.shape
    hidden = wdo.shape[0]
    return call(
        ffn_kernel,
        (hidden // FFC,),
        ffn_specs(att, woo, x, pick, table)
        + [whole(*head.shape), whole(*emb.shape), whole(*flags.shape)],
        (whole(tokens, width), whole(tokens, LANES)),
        (
            jax.ShapeDtypeStruct((tokens, width), F32),
            jax.ShapeDtypeStruct((tokens, LANES), F32),
        ),
        [
            pltpu.VMEM((tokens, width), F32),
            pltpu.VMEM((tokens, width), BF16),
            pltpu.VMEM((tokens, width), F32),
        ],
        flops=2 * tokens * width * (6 * hidden + width),
        moved=12 * hidden * width + 6 * tokens * width,
    )(att, woo, wop, x, pick, table, guo, gup, wdo, wdp, head, emb, flags)


def turn_kernel(
    tp_ref, att_ref, woo_ref, wop_ref, x_ref, oh_ref, tab_ref, guo_ref, gup_ref, wdo_ref, wdp_ref,
    gown_ref, gcame_ref, oht_ref,
    outo_ref, outp_ref, gmid_ref, gatt_ref, go_ref, gp_ref, goo_ref, gop_ref, sumo_ref, sump_ref,
    sums_ref, middle, hats, branches, normed, normed_t, gmixed, gmixed_t, mixed, gnormed, hid, dgate, dup,
):
    step = pl.program_id(0)
    tokens, width = x_ref.shape
    half = woo_ref.shape[0]
    blocks = tokens // HALF

    @pl.when(step == 0)
    def _():
        def body(i):
            rows = pl.ds(pl.multiple_of(i * HALF, HALF), HALF)
            branch = mm(att_ref[rows, :half], woo_ref[...]) + mm(att_ref[rows, half:], wop_ref[...])
            branches[rows, :] = branch
            pick = oh_ref[rows, :]
            mid = x_ref[rows, :] + mm(pick, tab_ref[:, 2 * width : 3 * width]) * branch
            middle[rows, :] = mid
            hat, _ = norm_parts(mid)
            scale = mm(pick, tab_ref[:, 3 * width : 4 * width])
            shift = mm(pick, tab_ref[:, 4 * width : 5 * width])
            normed[rows, :] = (hat * scale + shift).astype(BF16)
            gate = mm(pick, tab_ref[:, 5 * width : 6 * width])
            g = put_together(tp_ref[0] == 0, gown_ref[rows, :], gcame_ref[rows, :])
            gmixed[rows, :] = (g.astype(F32) * gate).astype(BF16)
            mixed[rows, :] = jnp.zeros((HALF, width), F32)
            gnormed[rows, :] = jnp.zeros((HALF, width), F32)

        block_loop(blocks, body)
        normed_t[...] = normed[...].T
        gmixed_t[...] = gmixed[...].T

    for gu, wd, out in ((gup_ref, wdp_ref, gp_ref), (guo_ref, wdo_ref, go_ref)):

        def body(i):
            rows = pl.ds(pl.multiple_of(i * BLOCK, BLOCK), BLOCK)
            gate = mm(normed[rows, :], gu[0])
            up = mm(normed[rows, :], gu[1])
            ghid = mm_nt(gmixed[rows, :], wd[...])
            s = jax.nn.sigmoid(gate)
            silu = gate * s
            hidden = (silu * up).astype(BF16)
            hid[rows, :] = hidden
            mixed[rows, :] += mm(hidden, wd[...])
            dg = (ghid * up * (s + silu * (1.0 - s))).astype(BF16)
            du = (ghid * silu).astype(BF16)
            dgate[rows, :] = dg
            dup[rows, :] = du
            gnormed[rows, :] += mm_nt(dg, gu[0]) + mm_nt(du, gu[1])

        block_loop(tokens // BLOCK, body)
        out[0, 0] = mm(normed_t[...], dgate[...]).astype(BF16)
        out[1, 0] = mm(normed_t[...], dup[...]).astype(BF16)
        out[2, 0] = mm(gmixed_t[...], hid[...]).astype(BF16)

    @pl.when(step == pl.num_programs(0) - 1)
    def _():
        first_core = tp_ref[0] == 0
        sums_ref[...] = jnp.zeros(sums_ref.shape, F32)

        def body(i):
            rows = pl.ds(pl.multiple_of(i * HALF, HALF), HALF)
            pick = oh_ref[rows, :]
            turn = oht_ref[i]
            g = put_together(first_core, gown_ref[rows, :], gcame_ref[rows, :]).astype(F32)
            total = mixed[rows, :]
            gate = mm(pick, tab_ref[:, 5 * width : 6 * width])
            mid = middle[rows, :]
            result = (mid + gate * total).astype(BF16)
            low, high = result[:, : width // 2], result[:, width // 2 :]
            outo_ref[rows, :] = jnp.where(first_core, low, high)
            outp_ref[rows, :] = jnp.where(first_core, high, low)
            sums_ref[0] += mm(turn, (g * total).astype(BF16))
            hat, inv_std = norm_parts(mid)
            gn = gnormed[rows, :]
            sums_ref[1] += mm(turn, (gn * hat).astype(BF16))
            sums_ref[2] += mm(turn, gn.astype(BF16))
            scale = mm(pick, tab_ref[:, 3 * width : 4 * width])
            gmid = g + norm_back(gn * scale, hat, inv_std)
            gmid_ref[rows, :] = gmid
            sums_ref[3] += mm(turn, (gmid * branches[rows, :]).astype(BF16))
            gbranch = (gmid * mm(pick, tab_ref[:, 2 * width : 3 * width])).astype(BF16)
            gmixed[rows, :] = gbranch
            gatt_ref[rows, :half] = mm_nt(gbranch, woo_ref[...]).astype(BF16)
            gatt_ref[rows, half:] = mm_nt(gbranch, wop_ref[...]).astype(BF16)

        block_loop(blocks, body)
        gmixed_t[...] = gmixed[...].T
        goo_ref[...] = mm(gmixed_t[...], att_ref[:, :half]).astype(BF16)
        gop_ref[...] = mm(gmixed_t[...], att_ref[:, half:]).astype(BF16)
        low, high = sums_ref[:, :, : width // 2], sums_ref[:, :, width // 2 :]
        sumo_ref[...] = jnp.where(first_core, low, high)
        sump_ref[...] = jnp.where(first_core, high, low)


def ffn_turn(tp, att, woo, wop, x, pick, table, guo, gup, wdo, wdp, g_own, g_came, pick_t):
    tokens, width = x.shape
    half = woo.shape[0]
    hidden = wdo.shape[0]
    grads = jax.ShapeDtypeStruct((3, hidden // FFC, width, FFC), BF16)
    grads_spec = pl.BlockSpec((3, 1, width, FFC), lambda j, *_: (0, j, 0, 0))
    return call(
        turn_kernel,
        (hidden // FFC,),
        ffn_specs(att, woo, x, pick, table) + [whole(tokens, width // 2), whole(tokens, width // 2), whole(*pick_t.shape)],
        (
            whole(tokens, width // 2),
            whole(tokens, width // 2),
            whole(tokens, width),
            whole(tokens, width),
            grads_spec,
            grads_spec,
            whole(width, half),
            whole(width, half),
            whole(4, 16, width // 2),
            whole(4, 16, width // 2),
        ),
        (
            jax.ShapeDtypeStruct((tokens, width // 2), BF16),
            jax.ShapeDtypeStruct((tokens, width // 2), BF16),
            jax.ShapeDtypeStruct((tokens, width), F32),
            jax.ShapeDtypeStruct((tokens, width), BF16),
            grads,
            grads,
            jax.ShapeDtypeStruct((width, half), BF16),
            jax.ShapeDtypeStruct((width, half), BF16),
            jax.ShapeDtypeStruct((4, 16, width // 2), F32),
            jax.ShapeDtypeStruct((4, 16, width // 2), F32),
        ),
        [
            pltpu.VMEM((4, 16, width), F32),
            pltpu.VMEM((tokens, width), F32),
            pltpu.VMEM((8, LANES), F32),
            pltpu.VMEM((tokens, width), F32),
            pltpu.VMEM((tokens, width), BF16),
            pltpu.VMEM((width, tokens), BF16),
            pltpu.VMEM((tokens, width), BF16),
            pltpu.VMEM((width, tokens), BF16),
            pltpu.VMEM((tokens, width), F32),
            pltpu.VMEM((tokens, width), F32),
            pltpu.VMEM((tokens, FFC), BF16),
            pltpu.VMEM((tokens, FFC), BF16),
            pltpu.VMEM((tokens, FFC), BF16),
        ],
        prefetch=1,
        flops=2 * tokens * width * (18 * hidden + 3 * width),
        moved=24 * hidden * width + 12 * tokens * width,
    )(tp, att, woo, wop, x, pick, table, guo, gup, wdo, wdp, g_own, g_came, pick_t)


def attend_back_block(q, segq, gout, logs, keys, keys_t, values, biases, bias_sums, gkeys, gvalues):
    half = LANES // 2
    masks = lane_masks()
    scale = half**-0.5
    scaled = q * jnp.asarray(scale, BF16)
    gqs = []
    for h in range(2):
        query_low = scaled * masks[h]
        query = jnp.concatenate([query_low, segq], axis=1)
        gheads = gout * masks[h]
        chances = [jnp.exp(bias(h, mm_nt(key, query)) - logs[h : h + 1, :]) for key, bias in zip(keys, biases)]
        gchances = [mm_nt(value, gheads) for value in values]
        centre = sum(jnp.sum(p * gp, axis=0, keepdims=True) for p, gp in zip(chances, gchances))
        gq = 0.0
        for b, (p, gp) in enumerate(zip(chances, gchances)):
            gs = p * (gp - centre)
            bias_sums[b](h, gs)
            low = gs.astype(BF16)
            gvalues[b] = gvalues[b] + mm(p.astype(BF16), gheads)
            gkeys[b] = gkeys[b] + mm(low, query_low)
            gq = gq + mm(keys_t[b][h * half : (h + 1) * half, :], low)
        gqs.append(gq * scale)
    return jnp.concatenate(gqs, axis=0).T.astype(BF16)


def diagonal_sums(tile):
    size, wide = tile.shape
    blank = jnp.zeros((SUB, wide), F32)
    groups = [jnp.zeros((SUB, 2 * wide), F32)] * 2
    for i, a in enumerate(range(0, size, SUB)):
        piece = jnp.concatenate([tile[a : a + SUB], blank], axis=1)
        groups[i % 2] = groups[i % 2] + pltpu.roll(piece, size - SUB - a, axis=1)
    total = groups[0] + groups[1]
    rows = lax.broadcasted_iota(jnp.int32, (SUB, 2 * wide), 0)
    moved = sum(pltpu.roll(jnp.where(rows == b, total, 0.0), SUB - 1 - b, axis=1) for b in range(SUB))
    return jnp.sum(moved, axis=0, keepdims=True)


def far_sums(tile, later):
    whole_sum = jnp.sum(jnp.sum(tile, axis=0, keepdims=True), axis=1, keepdims=True)
    edge = tile[:RADIUS, LANES:] if later else tile[HALF - RADIUS :, :LANES]
    sums = diagonal_sums(edge)
    rest = whole_sum - jnp.sum(sums, axis=1, keepdims=True)
    row = jnp.concatenate([sums, jnp.zeros((1, 2 * HALF - sums.shape[1]), F32)], axis=1)
    row = jnp.broadcast_to(row, (8, 2 * HALF))
    if later:
        row = pltpu.roll(row, 2 * HALF - LANES - RADIUS, axis=1)
    lanes = lax.broadcasted_iota(jnp.int32, (1, 2 * HALF), 1)
    return row[:1] + jnp.where(lanes == (0 if later else 2 * HALF - 2), rest, 0.0)


def attend_full_back_kernel(
    q_ref, k_ref, v_ref, g_ref, log_ref, segq_ref, segk_ref, near_ref, far_ref, o_ref, diag_ref, sums
):
    keys, keys_t, values = [], [], []
    for b in range(2):
        rows = pl.ds(b * HALF, HALF)
        key = k_ref[rows, :]
        keys.append(jnp.concatenate([key, segk_ref[rows, :]], axis=1))
        keys_t.append(key.T)
        values.append(v_ref[rows, :])
    gkeys, gvalues = [0.0, 0.0], [0.0, 0.0]
    sums[...] = jnp.zeros(sums.shape, F32)
    for qb in range(2):
        rows = pl.ds(qb * HALF, HALF)
        biases = full_biases(near_ref, far_ref, qb)

        def add(h, gs):
            sums[h] += gs

        def put(h, gs, later):
            row = 3 * h + (0 if later else 2)
            diag_ref[0, row : row + 1, :] = far_sums(gs, later)

        adders = [add, functools.partial(put, later=True)] if qb == 0 else [functools.partial(put, later=False), add]
        o_ref[0, rows, :] = attend_back_block(
            q_ref[rows, :], segq_ref[rows, :], g_ref[rows, :], log_ref[0, 0:2, rows],
            keys, keys_t, values, biases, adders, gkeys, gvalues,
        )
    for b in range(2):
        rows = pl.ds(b * HALF, HALF)
        o_ref[1, rows, :] = gkeys[b].astype(BF16)
        o_ref[2, rows, :] = gvalues[b].astype(BF16)
    for h in range(2):
        diag_ref[0, 3 * h + 1 : 3 * h + 2, :] = diagonal_sums(sums[h])


def attend_half_back_kernel(
    tp_ref, q_ref, k_ref, v_ref, kp_ref, vp_ref, g_ref, log_ref, segq_ref, segk_ref, near_ref, far_ref,
    o_ref, par_ref, diag_ref,
):
    keys, keys_t, values = [], [], []
    for b, (k, v) in enumerate(((k_ref, v_ref), (kp_ref, vp_ref))):
        key = k[...]
        keys.append(jnp.concatenate([key, segk_ref[pl.ds(b * HALF, HALF), :]], axis=1))
        keys_t.append(key.T)
        values.append(v[...])
    first = tp_ref[0] == 0
    biases = half_biases(near_ref, far_ref, first)
    gkeys, gvalues = [0.0, 0.0], [0.0, 0.0]

    def put(h, gs, b):
        sums = jnp.where(first, far_sums(gs, True), far_sums(gs, False)) if b else diagonal_sums(gs)
        diag_ref[0, 2 * h + b : 2 * h + b + 1, :] = sums

    adders = [functools.partial(put, b=b) for b in range(2)]
    o_ref[0] = attend_back_block(
        q_ref[...], segq_ref[...], g_ref[...], log_ref[0, 0:2, :],
        keys, keys_t, values, biases, adders, gkeys, gvalues,
    )
    o_ref[1] = gkeys[0].astype(BF16)
    o_ref[2] = gvalues[0].astype(BF16)
    par_ref[0] = gkeys[1].astype(BF16)
    par_ref[1] = gvalues[1].astype(BF16)


def attend_half_back(tp, qkv, kv_par, g, logs, segq, segk, bias):
    width = qkv.shape[1] // 3
    pairs = width // LANES
    flip = pairs // 2
    return call(
        attend_half_back_kernel,
        (pairs,),
        [
            pl.BlockSpec((HALF, LANES), lambda p, *_: (2, p)),
            pl.BlockSpec((HALF, LANES), lambda p, *_: (2, pairs + p)),
            pl.BlockSpec((HALF, LANES), lambda p, *_: (2, 2 * pairs + p)),
            pl.BlockSpec((HALF, LANES), lambda p, *_: (0, lax.rem(p + flip, pairs))),
            pl.BlockSpec((HALF, LANES), lambda p, *_: (0, pairs + lax.rem(p + flip, pairs))),
            pl.BlockSpec((HALF, LANES), lambda p, *_: (2, p)),
            pl.BlockSpec((1, 8, HALF), lambda p, *_: (p, 0, 2)),
            pl.BlockSpec((HALF, LANES), lambda p, *_: (2, 0)),
            pl.BlockSpec((ROW, LANES), lambda p, *_: (1, 0)),
        ]
        + bias_specs(),
        (
            pl.BlockSpec((3, HALF, LANES), lambda p, *_: (0, 0, p)),
            pl.BlockSpec((2, HALF, LANES), lambda p, *_: (0, 0, p)),
            pl.BlockSpec((1, 8, ROW), lambda p, *_: (p, 0, 0)),
        ),
        (
            jax.ShapeDtypeStruct((3, HALF, width), BF16),
            jax.ShapeDtypeStruct((2, HALF, width), BF16),
            jax.ShapeDtypeStruct((pairs, 8, ROW), F32),
        ),
        prefetch=1,
        flops=10 * HALF * HALF * 256 * 2 * pairs,
        moved=bias[0].size * 4,
    )(tp, qkv, qkv, qkv, kv_par, kv_par, g, logs, segq, segk, *bias)


def attend_full_back(qkv, g, logs, segq, segk, bias):
    width = qkv.shape[1] // 3
    pairs = width // LANES
    return call(
        attend_full_back_kernel,
        (pairs,),
        [
            pl.BlockSpec((ROW, LANES), lambda p: (0, p)),
            pl.BlockSpec((ROW, LANES), lambda p: (0, pairs + p)),
            pl.BlockSpec((ROW, LANES), lambda p: (0, 2 * pairs + p)),
            pl.BlockSpec((ROW, LANES), lambda p: (0, p)),
            pl.BlockSpec((1, 8, ROW), lambda p: (p, 0, 0)),
            pl.BlockSpec((ROW, LANES), lambda p: (0, 0)),
            pl.BlockSpec((ROW, LANES), lambda p: (0, 0)),
        ]
        + bias_specs(),
        (
            pl.BlockSpec((3, ROW, LANES), lambda p: (0, 0, p)),
            pl.BlockSpec((1, 8, ROW), lambda p: (p, 0, 0)),
        ),
        (
            jax.ShapeDtypeStruct((3, ROW, width), BF16),
            jax.ShapeDtypeStruct((pairs, 8, ROW), F32),
        ),
        [pltpu.VMEM((2, HALF, HALF), F32)],
        flops=20 * HALF * HALF * 256 * 2 * pairs,
        moved=bias[0].size * 4,
    )(qkv, qkv, qkv, g, logs, segq, segk, *bias)


def joined_rows(full_ref, half_ref, recv_ref, step, rows_in):
    half = recv_ref.shape[2] // 2
    rows_in[pl.ds(0, ROW), :] = full_ref[0]
    keep = (step > 0).astype(F32).astype(BF16)
    recv = jnp.concatenate([recv_ref[0, :, half:], recv_ref[0, :, :half]], axis=1)
    rows_in[pl.ds(ROW, HALF), :] = half_ref[0] + recv * keep


def qkv_weights_kernel(
    x_ref, oh_ref, tab_ref, full_ref, half_ref, recv_ref, outo_ref, outp_ref, go_ref, gp_ref, normed, normed_t, rows_in
):
    step = pl.program_id(0)
    tokens, width = x_ref.shape
    half = width // 2

    @pl.when(step == 0)
    def _():
        def body(i):
            rows = pl.ds(pl.multiple_of(i * HALF, HALF), HALF)
            hat, _ = norm_parts(x_ref[rows, :])
            pick = oh_ref[rows, :]
            scale = mm(pick, tab_ref[:, :width])
            shift = mm(pick, tab_ref[:, width : 2 * width])
            normed[rows, :] = (hat * scale + shift).astype(BF16)

        block_loop(tokens // HALF, body)
        normed_t[...] = normed[...].T

    joined_rows(full_ref, half_ref, recv_ref, step, rows_in)
    go_ref[0, :, :half] = mm(normed_t[...], rows_in[:, :half]).astype(BF16)
    gp_ref[0, :, :half] = mm(normed_t[...], rows_in[:, half:]).astype(BF16)
    go_ref[0, :, half:] = outo_ref[...]
    gp_ref[0, :, half:] = outp_ref[...]


def row_specs(width):
    return [
        pl.BlockSpec((1, ROW, width), lambda j, *_: (j, 0, 0)),
        pl.BlockSpec((1, HALF, width), lambda j, *_: (j, 0, 0)),
        pl.BlockSpec((1, HALF, width), lambda j, *_: (jnp.maximum(j - 1, 0), 0, 0)),
    ]


def qkv_weights(x, pick, table, full, half_rows, recv, out_own, out_par):
    tokens, width = x.shape
    half = width // 2
    third = half // 3
    spec = pl.BlockSpec((1, width, half + third), lambda j: (j, 0, 0))
    shape = jax.ShapeDtypeStruct((3, width, half + third), BF16)
    out_spec = pl.BlockSpec((width, third), lambda j: (0, j))
    return call(
        qkv_weights_kernel,
        (3,),
        [whole(tokens, width), whole(*pick.shape), whole(*table.shape)] + row_specs(width) + [out_spec, out_spec],
        (spec, spec),
        (shape, shape),
        [
            pltpu.VMEM((tokens, width), BF16),
            pltpu.VMEM((width, tokens), BF16),
            pltpu.VMEM((tokens, width), BF16),
        ],
        flops=2 * tokens * width * 6 * half,
        moved=16 * half * width + 12 * tokens * width,
    )(x, pick, table, full, half_rows, recv, out_own, out_par)


def qkv_back_kernel(
    tp_ref, x_ref, oh_ref, tab_ref, full_ref, half_ref, recv_ref, wo_ref, wp_ref, gmid_ref, lifted_ref, oht_ref,
    gino_ref, ginp_ref, sumo_ref, sump_ref, hats, stds, rows_in, acc, sums,
):
    step = pl.program_id(0)
    tokens, width = x_ref.shape
    half = wo_ref.shape[1]
    blocks = tokens // HALF

    @pl.when(step == 0)
    def _():
        def body(i):
            rows = pl.ds(pl.multiple_of(i * HALF, HALF), HALF)
            hat, inv_std = norm_parts(x_ref[rows, :])
            hats[rows, :] = hat
            stds[rows, :] = inv_std
            acc[rows, :] = jnp.zeros((HALF, width), F32)

        block_loop(blocks, body)

    joined_rows(full_ref, half_ref, recv_ref, step, rows_in)

    def body(i):
        rows = pl.ds(pl.multiple_of(i * HALF, HALF), HALF)
        grad = rows_in[rows, :]
        acc[rows, :] += mm_nt(grad[:, :half], wo_ref[...]) + mm_nt(grad[:, half:], wp_ref[...])

    block_loop(blocks, body)

    @pl.when(step == pl.num_programs(0) - 1)
    def _():
        first_core = tp_ref[0] == 0
        sums[...] = jnp.zeros(sums.shape, F32)

        def body(i):
            rows = pl.ds(pl.multiple_of(i * HALF, HALF), HALF)
            turn = oht_ref[i]
            gn = acc[rows, :]
            hat = hats[rows, :]
            sums[0] += mm(turn, (gn * hat).astype(BF16))
            sums[1] += mm(turn, gn.astype(BF16))
            scale = mm(oh_ref[rows, :], tab_ref[:, :width])
            grad = gmid_ref[rows, :] + norm_back(gn * scale, hat, stds[rows, :])
            low, high = grad[:, : width // 2], grad[:, width // 2 :]
            gino_ref[rows, :] = jnp.where(first_core, low, high)
            ginp_ref[rows, :] = jnp.where(first_core, high, low)
            lifted_t = lifted_ref[rows, :].astype(BF16).T
            sums[2] += mm(lifted_t[:16, :], grad.astype(BF16))

        block_loop(blocks, body)
        low, high = sums[:, :, : width // 2], sums[:, :, width // 2 :]
        sumo_ref[...] = jnp.where(first_core, low, high)
        sump_ref[...] = jnp.where(first_core, high, low)


def qkv_back(tp, x, pick, table, full, half_rows, recv, wo, wp, gmid, lifted, pick_t):
    tokens, width = x.shape
    half = wo.shape[1] // 3
    return call(
        qkv_back_kernel,
        (3,),
        [whole(tokens, width), whole(*pick.shape), whole(*table.shape)]
        + row_specs(width)
        + [
            pl.BlockSpec((width, half), lambda j, *_: (0, j)),
            pl.BlockSpec((width, half), lambda j, *_: (0, j)),
            whole(tokens, width),
            whole(tokens, LANES),
            whole(*pick_t.shape),
        ],
        (
            whole(tokens, width // 2),
            whole(tokens, width // 2),
            whole(3, 16, width // 2),
            whole(3, 16, width // 2),
        ),
        (
            jax.ShapeDtypeStruct((tokens, width // 2), F32),
            jax.ShapeDtypeStruct((tokens, width // 2), F32),
            jax.ShapeDtypeStruct((3, 16, width // 2), F32),
            jax.ShapeDtypeStruct((3, 16, width // 2), F32),
        ),
        [
            pltpu.VMEM((tokens, width), F32),
            pltpu.VMEM((tokens, 1), F32),
            pltpu.VMEM((tokens, width), BF16),
            pltpu.VMEM((tokens, width), F32),
            pltpu.VMEM((3, 16, width), F32),
        ],
        prefetch=1,
        flops=2 * tokens * width * 6 * half,
        moved=12 * half * width + 16 * tokens * width,
    )(tp, x, pick, table, full, half_rows, recv, wo, wp, gmid, lifted, pick_t)


def chain_joins(first_core):
    row = lax.broadcasted_iota(jnp.int32, (16, 16), 0)
    col = lax.broadcasted_iota(jnp.int32, (16, 16), 1)
    lower = ((row == col) & (row < 2 * SEGS)).astype(F32)
    upper = (
        ((row == col) & (row >= SEGS) & (row < 2 * SEGS)) | ((row == col + 2 * SEGS) & (row < 3 * SEGS))
    ).astype(F32)
    return jnp.where(first_core, lower, upper), jnp.where(first_core, upper, lower)


def join_chains(tp_ref, own_ref, came_ref, slope_ref, count, o_ref):
    own_join, came_join = chain_joins(tp_ref[0] == 0)
    cols = own_ref.shape[2]
    for i in range(count):
        both = jnp.dot(own_join, own_ref[i], precision=HIGHEST, preferred_element_type=F32)
        both = both + jnp.dot(came_join, came_ref[i], precision=HIGHEST, preferred_element_type=F32)
        lanes = pl.ds(i * cols, cols)
        o_ref[0:16, lanes] = (both * slope_ref[:, lanes]).astype(BF16)


def early_kernel(tp_ref, own_ref, came_ref, slope_ref, embed_ref, o_ref):
    join_chains(tp_ref, own_ref, came_ref, slope_ref, 4, o_ref)
    o_ref[:, pl.ds(4 * own_ref.shape[2], embed_ref.shape[1])] = embed_ref[...]


def late_kernel(tp_ref, own_ref, came_ref, slope_ref, bins_ref, o_ref):
    cols = own_ref.shape[2]
    join_chains(tp_ref, own_ref, came_ref, slope_ref, 2, o_ref)
    o_ref[:, pl.ds(2 * cols, LANES)] = bins_ref[...].astype(BF16)
    coords = own_ref[2] + came_ref[2]
    parts = [coords[i : i + 1, j : j + LANES] for j in range(0, cols, LANES) for i in range(3)]
    parts.append(jnp.zeros((16 - len(parts), LANES), F32))
    o_ref[:, pl.ds(2 * cols + LANES, LANES)] = jnp.concatenate(parts, axis=0).astype(BF16)


def pack_rows(kernel, tp, own, came, slopes, extra, shape):
    return call(
        kernel,
        (1,),
        [whole(*own.shape), whole(*came.shape), whole(*slopes.shape), whole(*extra.shape)],
        whole(*shape),
        jax.ShapeDtypeStruct(shape, BF16),
        prefetch=1,
        flops=10**6,
        moved=10**5,
    )(tp, own, came, slopes, extra)


def closing_kernel(early_ref, early_came_ref, late_ref, late_came_ref, hat_ref, inv_ref, gain_ref, both_ref, *refs):
    ffn, attn, outs = refs[:2], refs[2:4], refs[4:]
    gu_ref, down_ref, qkv_ref, out_ref = outs[:4]
    w0_ref, b0_ref, w1_ref, w2_ref, b2_ref, w3_ref, b3_ref, w4_ref, w5_ref, b5_ref = outs[4:14]
    table_ref, pgain_ref, proj_ref, coord_ref = outs[14:]

    def total(pair, block):
        return pair[0][0, block].astype(F32) + pair[1][0, block].astype(F32)

    lanes = ffn[0].shape[3]
    chunks = down_ref.shape[1] // lanes
    for block in range(chunks):
        span = pl.ds(block * lanes, lanes)
        gu_ref[:, 0, span] = total(ffn, block)
        gu_ref[:, 1, span] = total(ffn, chunks + block)
        down_ref[:, span] = total(ffn, 2 * chunks + block)
    third = out_ref.shape[1] // 3
    for i in range(3):
        value = total(attn, i)
        qkv_ref[i] = value[:, : 3 * third]
        out_ref[:, i * third : (i + 1) * third] = value[:, 3 * third :]

    cols = coord_ref.shape[1]
    pieces = [(early_ref, late_ref), (early_came_ref, late_came_ref)]
    embed_t = [early[:, 4 * cols :].T for early, _ in pieces]
    weights = [w0_ref, w1_ref, w5_ref, w3_ref, w4_ref, w2_ref]
    biases = [b0_ref, None, b5_ref, b3_ref, None, b2_ref]
    for i, (weight, bias) in enumerate(zip(weights, biases)):
        source, lanes = (1, pl.ds(i * cols, cols)) if i < 2 else (0, pl.ds((i - 2) * cols, cols))
        parts = [piece[source][:, lanes] for piece in pieces]
        weight[...] = sum(mm(embed, part) for embed, part in zip(embed_t, parts))
        if bias is not None:
            bias[...] = sum(jnp.sum(part.astype(F32), axis=0) for part in parts)
    extra = sum(late[:, 2 * cols :].reshape(-1, 16, 2 * LANES).astype(F32).sum(axis=0) for _, late in pieces)
    for i in range(cols // LANES):
        coord_ref[:, pl.ds(i * LANES, LANES)] = extra[3 * i : 3 * i + 3, LANES:]
    bins = extra[:, :LANES]
    hat = hat_ref[...]
    gain = gain_ref[...]
    proj = jnp.dot(bins, hat * gain, precision=HIGHEST, preferred_element_type=F32)
    proj_ref[...] = proj[: proj_ref.shape[0]]
    normed_grad = jnp.dot(bins.T, both_ref[...], precision=HIGHEST, preferred_element_type=F32)
    pgain_ref[...] = jnp.sum(normed_grad * hat, axis=0)
    table_ref[...] = norm_back(normed_grad * gain, hat, inv_ref[...])[: table_ref.shape[0]]


def closing(early, late, hat, inv_std, gain, both, ffn, attn, bins, heads):
    cols = (late[0].shape[1] - 2 * LANES) // 2
    embed = early[0].shape[1] - 4 * cols
    features = hat.shape[1]
    height, lanes = ffn[0].shape[2:]
    weight, bias = (embed, cols), (cols,)
    hidden = lanes * (ffn[0].shape[1] // 3)
    shapes = [(height, 2, hidden), (height, hidden), (3, height, cols), (height, cols)]
    shapes += [weight, bias, weight, weight, bias, weight, bias, weight, weight, bias]
    shapes += [(bins, features), (features,), (heads, features), (3, cols)]
    args = (*early, *late, hat, inv_std, gain, both, *ffn, *attn)
    return call(
        closing_kernel,
        (1,),
        [whole(*a.shape) for a in args],
        tuple(whole(*shape) for shape in shapes),
        tuple(jax.ShapeDtypeStruct(shape, F32) for shape in shapes),
        flops=10**8,
        moved=10**7,
    )(*args)


def halve_kernel(place_ref, *refs, plan, count):
    inputs, outs = refs[:count], refs[count:]
    for stream, (bit, sections) in enumerate(plan):
        sent_ref, kept_ref = outs[2 * stream], outs[2 * stream + 1]
        mine = (place_ref[0] >> bit) & 1
        done = 0
        for first, second, base, chunks, left in sections:
            spot = left.index(bit)
            shift = len(left) - 1
            half = 1 << shift

            def body(n, first=first, second=second, base=base, spot=spot, shift=shift, done=done, mine=mine):
                k = n & ((1 << shift) - 1)
                at = base + ((n >> shift) << (shift + 1)) + ((k >> spot) << (spot + 1)) + (k & ((1 << spot) - 1))
                for which, ref in ((1 - mine, sent_ref), (mine, kept_ref)):
                    block = at + (which << spot)
                    ref[0, done + n] = inputs[first][0, block] + inputs[second][0, block]

            block_loop(chunks * half, body)
            done += chunks * half


def halve(place, streams, bits):
    arrays, specs, plan, shapes = [], [], [], []
    steps = streams[0][0][5]
    if any(len(sections) > 1 or sections[0][5] != steps for sections in streams):
        steps = 1

    def operand(array, index):
        for i, (seen, at) in enumerate(arrays):
            if seen is array and at == index:
                return i
        arrays.append((array, index))
        block = (1, array.shape[1] // steps) + array.shape[2:]
        specs.append(pl.BlockSpec(block, lambda j, *_: (index, j, 0, 0)))
        return len(arrays) - 1

    moved = 0
    for sections, bit in zip(streams, bits):
        entries, blocks = [], 0
        for own, i, came, k, base, chunks, left in sections:
            entries.append((operand(own, i), operand(came, k), base, chunks // steps, left))
            blocks += chunks << (len(left) - 1)
        plan.append((bit, entries))
        shape = (1, blocks) + sections[0][0].shape[2:]
        shapes += [shape, shape]
        moved += 12 * blocks * shape[2] * shape[3]
    outs = call(
        functools.partial(halve_kernel, plan=plan, count=len(arrays)),
        (steps,),
        specs,
        tuple(pl.BlockSpec((1, n // steps, h, c), lambda j, *_: (0, j, 0, 0)) for _, n, h, c in shapes),
        tuple(jax.ShapeDtypeStruct(shape, BF16) for shape in shapes),
        prefetch=1,
        flops=10**6,
        moved=moved,
    )(place, *[array for array, _ in arrays])
    return list(outs[0::2]), list(outs[1::2])


def swap(values):
    return lax.ppermute(values, "tp", [(0, 1), (1, 0)])


def after(values, *others):
    return lax.optimization_barrier((values, *others))[0]


class Cube:
    def __init__(self, rows):
        self.bits = rows.bit_length() - 1
        assert rows == 1 << self.bits
        self.place = lax.axis_index("rows").reshape(1).astype(jnp.int32)
        self.perms = [[(i, i ^ (1 << b)) for i in range(rows)] for b in range(self.bits)]

    def turns(self):
        return [[(i + r) % 3 for i in range(3)] for r in range(3)]

    def gather(self, values, step):
        bit = (list(range(self.bits - 1, 1, -1)) + list(range(min(2, self.bits))))[step]
        came = lax.ppermute(values, "rows", self.perms[bit])
        if step == self.bits - 1:
            return values, came
        return lax.optimization_barrier(jnp.concatenate([values, came], axis=0))


def next_sections(sections, kept, came, bit):
    made, base = [], 0
    for _, _, _, _, _, chunks, left in sections:
        left = [b for b in left if b != bit]
        made.append((kept, 0, came, 0, base, chunks, left))
        base += chunks << len(left)
    return made


def normalize(values):
    centre = jnp.mean(values, axis=-1, keepdims=True)
    shifted = values - centre
    spread = jnp.mean(shifted * shifted, axis=-1, keepdims=True)
    inv_std = lax.rsqrt(spread + EPSILON)
    return shifted * inv_std, inv_std


def three_parts(values):
    high = lax.reduce_precision(values, 8, 7)
    middle = lax.reduce_precision(values - high, 8, 7)
    low = values - high - middle
    return jnp.concatenate([high, middle, low], axis=0).astype(BF16)


def bias_base(heads):
    bins = heads.shape[1]
    low = lambda n: jnp.broadcast_to(heads[:, :1], (heads.shape[0], n))
    top = lambda n: jnp.broadcast_to(heads[:, bins - 1 :], (heads.shape[0], n))
    fill = HALF - RADIUS
    behind = jnp.concatenate([low(fill), heads[:, :RADIUS], low(HALF)], axis=1)
    same = jnp.concatenate([heads[:, RADIUS:], top(fill - 1), low(fill), heads[:, :RADIUS]], axis=1)
    ahead = jnp.concatenate([top(HALF), heads[:, RADIUS:], top(fill - 1)], axis=1)
    return jnp.stack([behind, same, ahead], axis=1)


def bins_of_diagonals():
    places = jnp.arange(ROW, dtype=jnp.int32)[None, :] - (HALF - 1)
    offsets = places + HALF * jnp.arange(-1, 2, dtype=jnp.int32)[:, None]
    bins = jnp.clip(offsets, -RADIUS, RADIUS) + RADIUS
    every = jnp.arange(2 * RADIUS + 1, dtype=jnp.int32)
    return (bins.reshape(-1)[:, None] == every[None, :]).astype(F32)


def per_device(
    layer_input,
    cotangent,
    chain_lengths,
    self_condition_flag,
    time_embedding,
    query_key_value,
    output_projection,
    attention_scale_weight,
    attention_scale_bias,
    attention_shift_weight,
    attention_gate_weight,
    attention_gate_bias,
    transition_scale_weight,
    transition_scale_bias,
    transition_shift_weight,
    transition_gate_weight,
    transition_gate_bias,
    gate_up_projection,
    down_projection,
    pair_table,
    pair_gain,
    pair_projection,
    coordinate_head,
    coordinate_embedding,
    rows,
):
    core = lax.axis_index("tp")
    first_core = core == 0
    tp = core.reshape(1).astype(jnp.int32)
    cols = layer_input.shape[1]
    width = query_key_value.shape[0]
    heads_here = pair_projection.shape[1]
    bins = pair_table.shape[0]
    cube = Cube(rows)

    def side_by_side(own, came, axis):
        return jnp.where(
            first_core, jnp.concatenate([own, came], axis), jnp.concatenate([came, own], axis)
        )

    def scatter_tokens(own, sent):
        came = swap(sent)
        lower = jnp.concatenate([own[:ROW], own[ROW:], came[ROW:], came[:ROW]], axis=0)
        upper = jnp.concatenate([came[:ROW], came[ROW:], own[ROW:], own[:ROW]], axis=0)
        return jnp.where(first_core, lower, upper)

    x_own, x_sent, cot_own, cot_sent = token_halves(tp, layer_input, cotangent)
    x_came = swap(x_sent)
    qkv_own = query_key_value.reshape(width, -1)
    qkv_par = swap(qkv_own)

    mods, early_slopes, late_slopes, embed = modulations(
        time_embedding,
        [
            attention_scale_weight,
            attention_shift_weight,
            attention_gate_weight,
            transition_scale_weight,
            transition_shift_weight,
            transition_gate_weight,
        ],
        [attention_scale_bias, attention_gate_bias, transition_scale_bias, transition_gate_bias],
    )
    table = chain_table(tp, mods, swap(mods))
    mask_q, mask_k, pick, pick_t, flags = masks(tp, chain_lengths, self_condition_flag)

    pair_hat, pair_inv = normalize(pair_table.astype(F32))
    gain = pair_gain.astype(F32)
    pair_normed = pair_hat * gain
    pair_both = jnp.concatenate([pair_projection, swap(pair_projection)], axis=1).astype(F32)
    bias_heads = jnp.transpose(jnp.dot(pair_normed, pair_both, precision=HIGHEST))
    bias_source = jnp.transpose(pair_both)
    bias = bias_tiles(bias_base(bias_heads))

    out_own = output_projection
    out_par = swap(output_projection)
    gu_own = jnp.transpose(gate_up_projection, (1, 0, 2))
    gu_par = swap(gu_own)
    down_own = down_projection
    down_par = swap(down_projection)
    coord = jnp.concatenate([coordinate_head, coordinate_embedding], axis=0)
    coord = side_by_side(coord, swap(coord), 1)
    fill = jnp.zeros((LANES - 3, width), BF16)
    head = jnp.concatenate([coord[:3], fill], axis=0)
    emb = jnp.concatenate([coord[3:], fill], axis=0)
    cot_came = swap(cot_sent)

    def attention(qkv, kv):
        kv_par = swap(kv)
        attended, logs = attend_forward(tp, qkv, kv_par, mask_q, mask_k, bias)
        return qkv, kv_par, attended, logs

    qkv, kv, x = qkv_first(tp, x_own, x_came, pick, table, qkv_own, qkv_par)
    _, _, attended, _ = attention(qkv, kv)
    shifted, lifted = ffn_forward(
        attended, out_own, out_par, x, pick, table, gu_own, gu_par, down_own, down_par, head, emb, flags
    )
    qkv, kv_par, attended, logs = attention(*qkv_forward(shifted, pick, table, qkv_own, qkv_par))
    (
        result_own,
        result_sent,
        grad_middle,
        grad_attended,
        grads_own,
        grads_sent,
        grad_out_own,
        grad_out_sent,
        early_own,
        early_sent,
    ) = ffn_turn(
        tp, attended, out_own, out_par, shifted, pick, table, gu_own, gu_par, down_own, down_par, cot_own, cot_came, pick_t
    )

    early_came = swap(early_sent)

    came_ffn = swap(grads_sent)
    half_grads, far_grads, diag_half = attend_half_back(
        tp, qkv, kv_par, grad_attended, logs, mask_q, mask_k, bias
    )
    came_grads = swap(far_grads)

    turns = cube.turns()
    every = list(range(cube.bits))
    height = width // rows
    slots = lambda values: values.reshape(3, -1, height, values.shape[-1])
    chunks = grads_own.shape[1]
    own_slots, came_slots = slots(grads_own), slots(came_ffn)
    ffn = [[(own_slots, i, came_slots, i, 0, chunks, every)] for i in range(3)]

    def one_round(streams, bits, *others):
        sent, kept = halve(cube.place, streams, bits)
        held = lax.optimization_barrier((*sent, *others))
        came = [lax.ppermute(v, "rows", cube.perms[bit]) for v, bit in zip(held, bits)]
        made = [next_sections(*parts) for parts in zip(streams, kept, came, bits)]
        return made, came, held[len(sent) :]

    early_came, _ = lax.optimization_barrier((early_came, diag_half))
    early = pack_rows(
        early_kernel, tp, early_own, early_came, early_slopes, embed, (16, 4 * cols + embed.shape[1])
    )
    ffn, came, (mask_full, early, _) = one_round(ffn, turns[0], mask_q, early, diag_half)
    full_grads, diag_full = attend_full_back(qkv, grad_attended, logs, mask_full, mask_k, bias)
    early = cube.gather(early, 0)
    ffn, came, (pick_weights, early, _) = one_round(ffn, turns[1], pick, early, diag_full)
    gqkv_own, gqkv_sent = qkv_weights(
        shifted, pick_weights, table, full_grads, half_grads, came_grads, grad_out_own, grad_out_sent
    )
    early = cube.gather(early, 1)
    gqkv_sent, early, *_ = lax.optimization_barrier((gqkv_sent, early, *came))
    own_slots, came_slots = slots(gqkv_own), slots(swap(gqkv_sent))
    streams = [ffn[i] + [(own_slots, i, came_slots, i, 0, 1, every)] for i in range(3)]
    streams, came, (pick_back, early) = one_round(streams, turns[2], pick_weights, early)
    gin_own, gin_sent, late_own, late_sent = qkv_back(
        tp, shifted, pick_back, table, full_grads, half_grads, came_grads, qkv_own, qkv_par, grad_middle, lifted, pick_t
    )
    early = cube.gather(early, 2)
    late_sent, early, *_ = lax.optimization_barrier((late_sent, early, *came))

    diag_half = diag_half[:, :4].reshape(-1, 2, ROW)
    quiet = jnp.zeros_like(diag_half[:, 0])
    diag_far = diag_half[:, 1]
    diag = diag_full[:, :6].reshape(-1, 3, ROW) + jnp.stack(
        [
            jnp.where(first_core, diag_far, quiet),
            diag_half[:, 0],
            jnp.where(first_core, quiet, diag_far),
        ],
        axis=1,
    )
    grad_bins = jnp.dot(diag.reshape(-1, 3 * ROW), bins_of_diagonals(), precision=HIGHEST)
    came_bins = swap(grad_bins)
    grad_bins = grad_bins + jnp.concatenate([came_bins[heads_here:], came_bins[:heads_here]], axis=0)
    bins_fill = jnp.pad(grad_bins, ((0, 16 - 2 * heads_here), (0, LANES - bins)))

    late_came = swap(late_sent)
    late = pack_rows(late_kernel, tp, late_own, late_came, late_slopes, bins_fill, (16, 2 * cols + 2 * LANES))
    ffn = [[stream[0] for stream in streams]]
    attn = [stream[1:] for stream in streams]
    rest = list(range(3, cube.bits))
    waited = []
    for step in range(max(len(rest), 2)):
        now, bits = [], []
        if step < len(rest):
            now, bits = ffn, rest[step : step + 1]
        count = len(now)
        if step < 2:
            attn, came, _ = one_round(attn, turns[step], *waited)
        late = cube.gather(late, step)
        if count:
            ffn, waited, (late,) = one_round(now, bits, late)
    done = max(len(rest), 2)
    attn = [[section for stream in attn for section in stream]]
    for bit in rest:
        attn, came, _ = one_round(attn, [bit])
        if done < cube.bits:
            late = after(late, *waited)
            late = cube.gather(late, done)
            done += 1
    for step in range(done, cube.bits):
        late = cube.gather(late, step)
    for step in range(3, cube.bits):
        early = cube.gather(early, step)
    ffn_last = (ffn[0][0][0], ffn[0][0][2])
    attn_last = (attn[0][0][0], attn[0][0][2])

    layer_output = scatter_tokens(result_own, result_sent)
    input_gradient = scatter_tokens(gin_own, gin_sent)

    bins_pad = ((0, LANES - bins), (0, 0))
    grad_gu, grad_down, grad_qkv, grad_out, *conditioning = closing(
        early,
        late,
        jnp.pad(pair_hat, bins_pad),
        jnp.pad(pair_inv, bins_pad),
        gain[None, :],
        jnp.pad(bias_source, ((0, 16 - 2 * heads_here), (0, 0))),
        ffn_last,
        attn_last,
        bins,
        heads_here,
    )
    *conditioning, grad_table, grad_gain, grad_pair, coord_grad = conditioning
    return (
        layer_output,
        input_gradient,
        jnp.transpose(grad_qkv, (1, 0, 2)),
        grad_out.T,
        *conditioning,
        grad_gu,
        grad_down.T,
        grad_table,
        grad_gain,
        grad_pair.T,
        coord_grad,
    )


def solution(mesh):
    in_specs = (
        P("rows", "tp"),
        P("rows", "tp"),
        P("rows", None),
        P("rows"),
        P("rows", None, None),
        P(None, None, "tp"),
        P("tp", None),
        P(None, "tp"),
        P("tp"),
        P(None, "tp"),
        P(None, "tp"),
        P("tp"),
        P(None, "tp"),
        P("tp"),
        P(None, "tp"),
        P(None, "tp"),
        P("tp"),
        P(None, None, "tp"),
        P("tp", None),
        P(),
        P(),
        P(None, "tp"),
        P(None, "tp"),
        P(None, "tp"),
    )
    out_specs = (
        P("rows", "tp"),
        P("rows", "tp"),
        P("rows", None, "tp"),
        P("tp", "rows"),
        P(None, "tp"),
        P("tp"),
        P(None, "tp"),
        P(None, "tp"),
        P("tp"),
        P(None, "tp"),
        P("tp"),
        P(None, "tp"),
        P(None, "tp"),
        P("tp"),
        P("rows", None, "tp"),
        P("tp", "rows"),
        P(),
        P(),
        P(None, "tp"),
        P(None, "tp"),
    )
    return jax.shard_map(
        functools.partial(per_device, rows=mesh.shape["rows"]),
        mesh=mesh,
        in_specs=in_specs,
        out_specs=out_specs,
        check_vma=False,
    )
```

```python
import functools
import jax
import jax.numpy as jnp
from jax import lax
from jax.experimental import pallas as pl
from jax.experimental.pallas import tpu as pltpu
from jax.sharding import PartitionSpec as P

RADIUS = 32
ROW = 512
HALF = ROW // 2
SEGS = 5
EPSILON = 1e-05
MASKED = -1e30
HIGHEST = lax.Precision.HIGHEST
F32 = jnp.float32
BF16 = jnp.bfloat16
LANES = 128
FFC = 512
BLOCK = 384
SUB = 8
NT = (((1,), (1,)), ((), ()))
VMEM_LIMIT = 60 * 1024 * 1024


def mm(left, right):
    return jnp.dot(left, right, preferred_element_type=F32)


def mm_nt(left, right):
    return lax.dot_general(left, right, NT, preferred_element_type=F32)


def norm_parts(values):
    centre = jnp.mean(values, axis=1, keepdims=True)
    shifted = values - centre
    spread = jnp.mean(shifted * shifted, axis=1, keepdims=True)
    inv_std = lax.rsqrt(spread + EPSILON)
    return shifted * inv_std, inv_std


def norm_back(grad, hat, inv_std):
    first = jnp.mean(grad, axis=1, keepdims=True)
    second = jnp.mean(grad * hat, axis=1, keepdims=True)
    return inv_std * (grad - first - hat * second)


def block_loop(count, body):
    lax.fori_loop(0, count, lambda i, c: (body(i), c)[1], 0)


def call(kernel, grid, in_specs, out_specs, out_shape, scratch=(), prefetch=0, aliases=None, flops=0, moved=0):
    return pl.pallas_call(
        kernel,
        grid_spec=pltpu.PrefetchScalarGridSpec(
            num_scalar_prefetch=prefetch,
            grid=grid,
            in_specs=in_specs,
            out_specs=out_specs,
            scratch_shapes=list(scratch),
        ),
        out_shape=out_shape,
        input_output_aliases=aliases or {},
        compiler_params=pltpu.CompilerParams(
            dimension_semantics=("arbitrary",) * len(grid), vmem_limit_bytes=VMEM_LIMIT
        ),
        cost_estimate=pl.CostEstimate(flops=flops, transcendentals=0, bytes_accessed=moved),
    )


def whole(*shape):
    zeros = (0,) * len(shape)
    return pl.BlockSpec(shape, lambda *_: zeros)


def bias_kernel(base_ref, near_ref, far_ref):
    for h, d, height, start, out in [
        run
        for h in range(base_ref.shape[0])
        for run in (
            (h, 1, HALF, 0, near_ref.at[h]),
            (h, 0, RADIUS, 0, far_ref.at[h, 0]),
            (h, 2, RADIUS, HALF - RADIUS, far_ref.at[h, 1]),
        )
    ]:
        rows = jnp.broadcast_to(base_ref[h, d : d + 1, :], (SUB, 2 * HALF))
        rows = pltpu.roll(rows, 0, axis=1, stride=1, stride_axis=0)
        for a in range(0, height, SUB):
            out[a : a + SUB, :] = pltpu.roll(rows, start + a, axis=1)[:, :HALF]


def bias_tiles(base):
    heads = base.shape[0]
    near, far = (heads, HALF, HALF), (heads, 2, RADIUS, HALF)
    return call(
        bias_kernel,
        (3,),
        [pl.BlockSpec((heads // 3, 3, 2 * HALF), lambda h: (h, 0, 0))],
        (
            pl.BlockSpec((heads // 3,) + near[1:], lambda h: (h, 0, 0)),
            pl.BlockSpec((heads // 3,) + far[1:], lambda h: (h, 0, 0, 0)),
        ),
        (jax.ShapeDtypeStruct(near, F32), jax.ShapeDtypeStruct(far, F32)),
        moved=heads * HALF * HALF * 4,
        flops=10**7,
    )(base)


def bias_specs():
    return [
        pl.BlockSpec((2, HALF, HALF), lambda p, *_: (p, 0, 0)),
        pl.BlockSpec((2, 2, RADIUS, HALF), lambda p, *_: (p, 0, 0, 0)),
    ]


def add_near(near_ref, far_ref, h, scores):
    return scores + near_ref[h]


def add_later(near_ref, far_ref, h, scores):
    edge = far_ref[h, 0]
    return jnp.concatenate([scores[:RADIUS] + edge, scores[RADIUS:] + edge[RADIUS - 1 :, :1]], axis=0)


def add_earlier(near_ref, far_ref, h, scores):
    edge = far_ref[h, 1]
    return jnp.concatenate(
        [scores[: HALF - RADIUS] + edge[:1, HALF - 1 :], scores[HALF - RADIUS :] + edge], axis=0
    )


def add_either(first, near_ref, far_ref, h, scores):
    later, earlier = far_ref[h, 0], far_ref[h, 1]
    rest = jnp.where(first, later[RADIUS - 1 :, :1], earlier[:1, HALF - 1 :])
    return jnp.concatenate(
        [
            scores[:RADIUS] + jnp.where(first, later, rest),
            scores[RADIUS : HALF - RADIUS] + rest,
            scores[HALF - RADIUS :] + jnp.where(first, rest, earlier),
        ],
        axis=0,
    )


def full_biases(near_ref, far_ref, qb):
    kinds = (add_near, add_later) if qb == 0 else (add_earlier, add_near)
    return [functools.partial(kind, near_ref, far_ref) for kind in kinds]


def half_biases(near_ref, far_ref, first):
    return [
        functools.partial(add_near, near_ref, far_ref),
        functools.partial(add_either, first, near_ref, far_ref),
    ]


def mods_kernel(time_ref, *refs):
    weights, biases = refs[:6], {0: refs[6], 2: refs[7], 3: refs[8], 5: refs[9]}
    mods_ref, early_ref, late_ref, embed_ref = refs[10:]
    rows = []
    blank = jnp.zeros((1, time_ref.shape[2]), F32)
    for i in range(time_ref.shape[0]):
        rows += [time_ref[i].astype(F32), blank]
    embed_ref[...] = jnp.concatenate(rows + [blank] * (16 - SEGS * time_ref.shape[0]), axis=0).astype(BF16)
    cols = early_ref.shape[1] // 4
    homes = {0: (late_ref, 0), 1: (late_ref, 1), 5: (early_ref, 0), 3: (early_ref, 1), 4: (early_ref, 2), 2: (early_ref, 3)}
    for i in range(6):
        value = mm(embed_ref[...], weights[i][...])
        slope = jnp.ones_like(value)
        if i in biases:
            value = jax.nn.sigmoid(value + biases[i][...].astype(F32).reshape(1, cols))
            slope = value * (1.0 - value)
        mods_ref[i] = value
        home, place = homes[i]
        home[:, pl.ds(place * cols, cols)] = slope


def modulations(embed, weights, biases):
    cols = weights[0].shape[1]
    args = (embed, *weights, *biases)
    shapes = [(6, 16, cols), (16, 4 * cols), (16, 2 * cols), (16, embed.shape[2])]
    return call(
        mods_kernel,
        (1,),
        [whole(*a.shape) for a in args],
        tuple(whole(*shape) for shape in shapes),
        tuple(jax.ShapeDtypeStruct(shape, dtype) for shape, dtype in zip(shapes, (F32, F32, F32, BF16))),
        flops=10**8,
        moved=2 * 10**6,
    )(*args)


def table_kernel(tp_ref, own_ref, came_ref, o_ref):
    first = tp_ref[0] == 0
    row = lax.broadcasted_iota(jnp.int32, (32, 16), 0)
    col = lax.broadcasted_iota(jnp.int32, (32, 16), 1)
    part = (row >= 2 * SEGS).astype(jnp.int32) + (row >= 4 * SEGS).astype(jnp.int32)
    chain = row - 2 * SEGS * part
    chain = chain + jnp.where((chain < SEGS) & jnp.logical_not(first), 2 * SEGS, 0)
    take = ((col == chain) & (row < 6 * SEGS)).astype(F32)
    rows = lax.broadcasted_iota(jnp.int32, (32, 1), 0)
    width = 2 * own_ref.shape[2]
    for i in range(6):
        own, came = own_ref[i], came_ref[i]
        low, high = jnp.where(first, own, came), jnp.where(first, came, own)
        value = jnp.dot(take, jnp.concatenate([low, high], axis=1), precision=HIGHEST, preferred_element_type=F32)
        top = value.astype(BF16).astype(F32)
        middle = (value - top).astype(BF16).astype(F32)
        parts = jnp.where(rows < 2 * SEGS, top, jnp.where(rows < 4 * SEGS, middle, value - top - middle))
        o_ref[:, pl.ds(i * width, width)] = parts.astype(BF16)


def chain_table(tp, own, came):
    shape = (32, 12 * own.shape[2])
    return call(
        table_kernel,
        (1,),
        [whole(*own.shape), whole(*came.shape)],
        whole(*shape),
        jax.ShapeDtypeStruct(shape, BF16),
        prefetch=1,
        flops=10**7,
        moved=10**6,
    )(tp, own, came)


def masks_kernel(tp_ref, length_ref, flag_ref, q_ref, k_ref, pick_ref, turn_ref, marks_ref):
    core = tp_ref[0]

    def segments(pack, shape, axis, start):
        spot = lax.broadcasted_iota(jnp.int32, shape, axis) + start
        segment = jnp.zeros(shape, jnp.int32)
        end = 0
        for i in range(SEGS - 1):
            end = end + length_ref[pack, i]
            segment = segment + (spot >= end).astype(jnp.int32)
        return segment

    runs = [(2 * core, 0, 0), (2 * core, HALF, 0), (1, HALF * core, SEGS), (1, HALF * (1 - core), SEGS)]
    for i, (pack, start, shift) in enumerate(runs):
        rows = pl.ds(i * HALF, HALF)
        segment = segments(pack, (HALF, LANES), 0, start)
        lanes = lax.broadcasted_iota(jnp.int32, (HALF, LANES), 1)
        k_ref[rows, :] = (segment == lanes).astype(F32).astype(BF16)
        if i == 3:
            break
        q_ref[rows, :] = jnp.where((segment != lanes) & (lanes < SEGS), MASKED, 0.0).astype(BF16)
        chain = (segment + shift)[:, :32]
        lanes = lanes[:, :32]
        spot = lanes - 2 * SEGS * (
            (lanes >= 2 * SEGS).astype(jnp.int32) + (lanes >= 4 * SEGS).astype(jnp.int32)
        )
        pick_ref[rows, :] = ((chain == spot) & (lanes < 6 * SEGS)).astype(F32).astype(BF16)
        marks_ref[rows, :] = jnp.full((HALF, 1), flag_ref[pack].astype(F32))
        across = segments(pack, (16, HALF), 1, start) + shift
        turn_ref[i] = (across == lax.broadcasted_iota(jnp.int32, (16, HALF), 0)).astype(F32).astype(BF16)


def masks(tp, lengths, flags):
    shapes = [(3 * HALF, LANES), (4 * HALF, LANES), (3 * HALF, 32), (3, 16, HALF)]
    return call(
        masks_kernel,
        (1,),
        [],
        tuple(whole(*shape) for shape in shapes) + (whole(3 * HALF, 1),),
        tuple(jax.ShapeDtypeStruct(shape, BF16) for shape in shapes)
        + (jax.ShapeDtypeStruct((3 * HALF, 1), F32),),
        prefetch=3,
        flops=10**6,
        moved=10**6,
    )(tp, lengths, flags)


def halves_kernel(tp_ref, *refs):
    for source, target in zip(refs[:4], refs[4:]):
        target[...] = source[...]


def token_halves(tp, first, second):
    cols = first.shape[1]

    def mine(j, tp_ref):
        return jnp.where(j < 2, 4 * tp_ref[0] + j, 2 + tp_ref[0]), 0

    def others(j, tp_ref):
        return jnp.where(j < 2, 4 * (1 - tp_ref[0]) + j, 3 - tp_ref[0]), 0

    spec = pl.BlockSpec((HALF, cols), lambda j, _: (j, 0))
    shape = jax.ShapeDtypeStruct((3 * HALF, cols), BF16)
    places = [pl.BlockSpec((HALF, cols), place) for place in (mine, others)]
    return call(
        halves_kernel, (3,), places + places, (spec,) * 4, (shape,) * 4, prefetch=1, flops=10, moved=24 * HALF * cols
    )(tp, first, first, second, second)


def put_together(first_core, own, came):
    return jnp.concatenate([jnp.where(first_core, own, came), jnp.where(first_core, came, own)], axis=1)


def qkv_first_kernel(tp_ref, xo_ref, xp_ref, oh_ref, tab_ref, own_ref, par_ref, o_ref, kv_ref, x_ref, normed):
    @pl.when(pl.program_id(0) == 0)
    def _():
        x_ref[...] = put_together(tp_ref[0] == 0, xo_ref[...], xp_ref[...])

    qkv_kernel(x_ref, oh_ref, tab_ref, own_ref, par_ref, o_ref, kv_ref, normed)


def qkv_kernel(x_ref, oh_ref, tab_ref, own_ref, par_ref, o_ref, kv_ref, normed):
    width = x_ref.shape[1]
    half = own_ref.shape[1]

    @pl.when(pl.program_id(0) == 0)
    def _():
        def body(i):
            rows = pl.ds(pl.multiple_of(i * HALF, HALF), HALF)
            hat, _ = norm_parts(x_ref[rows, :].astype(F32))
            pick = oh_ref[rows, :]
            scale = mm(pick, tab_ref[:, :width])
            shift = mm(pick, tab_ref[:, width : 2 * width])
            normed[rows, :] = (hat * scale + shift).astype(BF16)

        block_loop(x_ref.shape[0] // HALF, body)

    o_ref[:, :half] = mm(normed[...], own_ref[...]).astype(BF16)
    o_ref[:, half:] = mm(normed[...], par_ref[...]).astype(BF16)
    kv_ref[...] = o_ref[pl.ds(ROW, HALF), :]


def qkv_outs(tokens, half):
    specs = (
        pl.BlockSpec((tokens, 2 * half), lambda j, *_: (0, j)),
        pl.BlockSpec((HALF, 2 * half), lambda j, *_: (0, jnp.maximum(j - 1, 0))),
    )
    return specs, (jax.ShapeDtypeStruct((tokens, 6 * half), BF16), jax.ShapeDtypeStruct((HALF, 4 * half), BF16))


def qkv_first(tp, x_own, x_came, pick, table, w_own, w_par):
    tokens, cols = x_own.shape
    width = 2 * cols
    half = w_own.shape[1] // 3
    return call(
        qkv_first_kernel,
        (3,),
        [
            whole(tokens, cols),
            whole(tokens, cols),
            whole(*pick.shape),
            whole(*table.shape),
            pl.BlockSpec((width, half), lambda j, *_: (0, j)),
            pl.BlockSpec((width, half), lambda j, *_: (0, j)),
        ],
        (*qkv_outs(tokens, half)[0], whole(tokens, width)),
        (*qkv_outs(tokens, half)[1], jax.ShapeDtypeStruct((tokens, width), BF16)),
        [pltpu.VMEM((tokens, width), BF16)],
        prefetch=1,
        flops=2 * tokens * width * 6 * half,
        moved=tokens * 6 * half * 2 + width * half * 12 + tokens * width * 4,
    )(tp, x_own, x_came, pick, table, w_own, w_par)


def qkv_forward(x, pick, table, w_own, w_par):
    tokens, width = x.shape
    half = w_own.shape[1] // 3
    return call(
        qkv_kernel,
        (3,),
        [
            whole(tokens, width),
            whole(*pick.shape),
            whole(*table.shape),
            pl.BlockSpec((width, half), lambda j: (0, j)),
            pl.BlockSpec((width, half), lambda j: (0, j)),
        ],
        *qkv_outs(tokens, half),
        [pltpu.VMEM((tokens, width), BF16)],
        flops=2 * tokens * width * 6 * half,
        moved=tokens * 6 * half * 2 + width * half * 12 + tokens * width * 4,
    )(x, pick, table, w_own, w_par)


def lane_masks():
    lanes = lax.broadcasted_iota(jnp.int32, (1, LANES), 1)
    first = (lanes < LANES // 2).astype(F32)
    return first.astype(BF16), (1.0 - first).astype(BF16)


def attend_forward_block(q, segq, keys, values_t, biases):
    outs, logs = [], []
    half = LANES // 2
    masks = lane_masks()
    scaled = q * jnp.asarray(half**-0.5, BF16)
    for h in range(2):
        query = jnp.concatenate([scaled * masks[h], segq], axis=1)
        scores = [bias(h, mm_nt(key, query)) for key, bias in zip(keys, biases)]
        tops = [jnp.max(s, axis=0, keepdims=True) for s in scores]
        top = functools.reduce(jnp.maximum, tops)
        weights = [jnp.exp(s - top) for s in scores]
        total = sum(jnp.sum(w, axis=0, keepdims=True) for w in weights)
        mixed = sum(
            mm(vt[h * half : (h + 1) * half, :], w.astype(BF16)) for vt, w in zip(values_t, weights)
        )
        outs.append(mixed / total)
        logs.append(top + jnp.log(total))
    attended = jnp.concatenate(outs, axis=0).T.astype(BF16)
    return attended, jnp.concatenate(logs, axis=0)


def attend_full_kernel(q_ref, k_ref, v_ref, segq_ref, segk_ref, near_ref, far_ref, o_ref, log_ref):
    keys = [
        jnp.concatenate([k_ref[pl.ds(b * HALF, HALF), :], segk_ref[pl.ds(b * HALF, HALF), :]], axis=1)
        for b in range(2)
    ]
    values_t = [v_ref[pl.ds(b * HALF, HALF), :].T for b in range(2)]
    for qb in range(2):
        rows = pl.ds(qb * HALF, HALF)
        biases = full_biases(near_ref, far_ref, qb)
        attended, logs = attend_forward_block(q_ref[rows, :], segq_ref[rows, :], keys, values_t, biases)
        o_ref[rows, :] = attended
        log_ref[0, 0:2, rows] = logs


def attend_half_kernel(
    tp_ref, q_ref, k_ref, v_ref, kp_ref, vp_ref, segq_ref, segk_ref, near_ref, far_ref, oin, login, o_ref, log_ref
):
    keys = [
        jnp.concatenate([k_ref[...], segk_ref[pl.ds(0, HALF), :]], axis=1),
        jnp.concatenate([kp_ref[...], segk_ref[pl.ds(HALF, HALF), :]], axis=1),
    ]
    values_t = [v_ref[...].T, vp_ref[...].T]
    biases = half_biases(near_ref, far_ref, tp_ref[0] == 0)
    attended, logs = attend_forward_block(q_ref[...], segq_ref[...], keys, values_t, biases)
    o_ref[...] = attended
    log_ref[0, 0:2, :] = logs


def attend_forward(tp, qkv, kv_par, segq, segk, bias):
    tokens = qkv.shape[0]
    width = qkv.shape[1] // 3
    pairs = width // LANES
    out_shape = (
        jax.ShapeDtypeStruct((tokens, width), BF16),
        jax.ShapeDtypeStruct((pairs, 8, tokens), F32),
    )
    unit = 4 * HALF * HALF * 256 * 2
    attended, logs = call(
        attend_full_kernel,
        (pairs,),
        [
            pl.BlockSpec((ROW, LANES), lambda p: (0, p)),
            pl.BlockSpec((ROW, LANES), lambda p: (0, pairs + p)),
            pl.BlockSpec((ROW, LANES), lambda p: (0, 2 * pairs + p)),
            pl.BlockSpec((ROW, LANES), lambda p: (0, 0)),
            pl.BlockSpec((ROW, LANES), lambda p: (0, 0)),
        ]
        + bias_specs(),
        (
            pl.BlockSpec((ROW, LANES), lambda p: (0, p)),
            pl.BlockSpec((1, 8, ROW), lambda p: (p, 0, 0)),
        ),
        out_shape,
        flops=unit * 4 * pairs,
        moved=bias[0].size * 4,
    )(qkv, qkv, qkv, segq, segk, *bias)
    flip = pairs // 2
    return call(
        attend_half_kernel,
        (pairs,),
        [
            pl.BlockSpec((HALF, LANES), lambda p, *_: (2, p)),
            pl.BlockSpec((HALF, LANES), lambda p, *_: (2, pairs + p)),
            pl.BlockSpec((HALF, LANES), lambda p, *_: (2, 2 * pairs + p)),
            pl.BlockSpec((HALF, LANES), lambda p, *_: (0, lax.rem(p + flip, pairs))),
            pl.BlockSpec((HALF, LANES), lambda p, *_: (0, pairs + lax.rem(p + flip, pairs))),
            pl.BlockSpec((HALF, LANES), lambda p, *_: (2, 0)),
            pl.BlockSpec((ROW, LANES), lambda p, *_: (1, 0)),
        ]
        + bias_specs()
        + [pl.BlockSpec(memory_space=pl.ANY), pl.BlockSpec(memory_space=pl.ANY)],
        (
            pl.BlockSpec((HALF, LANES), lambda p, *_: (2, p)),
            pl.BlockSpec((1, 8, HALF), lambda p, *_: (p, 0, 2)),
        ),
        out_shape,
        prefetch=1,
        aliases={10: 0, 11: 1},
        flops=unit * 2 * pairs,
        moved=bias[0].size * 4,
    )(tp, qkv, qkv, qkv, kv_par, kv_par, segq, segk, *bias, attended, logs)


def ffn_kernel(
    att_ref, woo_ref, wop_ref, x_ref, oh_ref, tab_ref, guo_ref, gup_ref, wdo_ref, wdp_ref,
    head_ref, emb_ref, flag_ref, shifted_ref, lifted_ref, middle, normed, acc,
):
    step = pl.program_id(0)
    tokens, width = x_ref.shape
    half = woo_ref.shape[0]
    blocks = tokens // HALF

    @pl.when(step == 0)
    def _():
        def body(i):
            rows = pl.ds(pl.multiple_of(i * HALF, HALF), HALF)
            branch = mm(att_ref[rows, :half], woo_ref[...]) + mm(att_ref[rows, half:], wop_ref[...])
            pick = oh_ref[rows, :]
            mid = x_ref[rows, :].astype(F32) + mm(pick, tab_ref[:, 2 * width : 3 * width]) * branch
            middle[rows, :] = mid
            hat, _ = norm_parts(mid)
            scale = mm(pick, tab_ref[:, 3 * width : 4 * width])
            shift = mm(pick, tab_ref[:, 4 * width : 5 * width])
            normed[rows, :] = (hat * scale + shift).astype(BF16)
            acc[rows, :] = jnp.zeros((HALF, width), F32)

        block_loop(blocks, body)

    def body(i):
        rows = pl.ds(pl.multiple_of(i * HALF, HALF), HALF)
        total = acc[rows, :]
        for gu, wd in ((guo_ref, wdo_ref), (gup_ref, wdp_ref)):
            gate = mm(normed[rows, :], gu[0])
            up = mm(normed[rows, :], gu[1])
            hidden = (gate * jax.nn.sigmoid(gate) * up).astype(BF16)
            total = total + mm(hidden, wd[...])
        acc[rows, :] = total

    block_loop(blocks, body)

    @pl.when(step == pl.num_programs(0) - 1)
    def _():
        def body(i):
            rows = pl.ds(pl.multiple_of(i * HALF, HALF), HALF)
            gate = mm(oh_ref[rows, :], tab_ref[:, 5 * width : 6 * width])
            first = middle[rows, :] + gate * acc[rows, :]
            high = first.astype(BF16)
            rest = (first - high.astype(F32)).astype(BF16)
            coords = mm_nt(high, head_ref[...]) + mm_nt(rest, head_ref[...])
            lifted = coords * flag_ref[rows, :]
            lifted_ref[rows, :] = lifted
            high = lifted.astype(BF16)
            rest = (lifted - high.astype(F32)).astype(BF16)
            moved = mm(high, emb_ref[...]) + mm(rest, emb_ref[...])
            shifted_ref[rows, :] = x_ref[rows, :].astype(F32) + moved

        block_loop(blocks, body)


def ffn_specs(att, woo, x, pick, table):
    tokens, width = x.shape
    chunk = FFC
    return [
        whole(*att.shape),
        whole(*woo.shape),
        whole(*woo.shape),
        whole(tokens, width),
        whole(*pick.shape),
        whole(*table.shape),
        pl.BlockSpec((2, width, chunk), lambda j, *_: (0, 0, j)),
        pl.BlockSpec((2, width, chunk), lambda j, *_: (0, 0, j)),
        pl.BlockSpec((chunk, width), lambda j, *_: (j, 0)),
        pl.BlockSpec((chunk, width), lambda j, *_: (j, 0)),
    ]


def ffn_forward(att, woo, wop, x, pick, table, guo, gup, wdo, wdp, head, emb, flags):
    tokens, width = x.shape
    hidden = wdo.shape[0]
    return call(
        ffn_kernel,
        (hidden // FFC,),
        ffn_specs(att, woo, x, pick, table)
        + [whole(*head.shape), whole(*emb.shape), whole(*flags.shape)],
        (whole(tokens, width), whole(tokens, LANES)),
        (
            jax.ShapeDtypeStruct((tokens, width), F32),
            jax.ShapeDtypeStruct((tokens, LANES), F32),
        ),
        [
            pltpu.VMEM((tokens, width), F32),
            pltpu.VMEM((tokens, width), BF16),
            pltpu.VMEM((tokens, width), F32),
        ],
        flops=2 * tokens * width * (6 * hidden + width),
        moved=12 * hidden * width + 6 * tokens * width,
    )(att, woo, wop, x, pick, table, guo, gup, wdo, wdp, head, emb, flags)


def turn_kernel(
    tp_ref, att_ref, woo_ref, wop_ref, x_ref, oh_ref, tab_ref, guo_ref, gup_ref, wdo_ref, wdp_ref,
    gown_ref, gcame_ref, oht_ref,
    outo_ref, outp_ref, gmid_ref, gatt_ref, go_ref, gp_ref, goo_ref, gop_ref, sumo_ref, sump_ref,
    sums_ref, middle, hats, branches, normed, normed_t, gmixed, gmixed_t, mixed, gnormed, hid, dgate, dup,
):
    step = pl.program_id(0)
    tokens, width = x_ref.shape
    half = woo_ref.shape[0]
    blocks = tokens // HALF

    @pl.when(step == 0)
    def _():
        def body(i):
            rows = pl.ds(pl.multiple_of(i * HALF, HALF), HALF)
            branch = mm(att_ref[rows, :half], woo_ref[...]) + mm(att_ref[rows, half:], wop_ref[...])
            branches[rows, :] = branch
            pick = oh_ref[rows, :]
            mid = x_ref[rows, :] + mm(pick, tab_ref[:, 2 * width : 3 * width]) * branch
            middle[rows, :] = mid
            hat, _ = norm_parts(mid)
            scale = mm(pick, tab_ref[:, 3 * width : 4 * width])
            shift = mm(pick, tab_ref[:, 4 * width : 5 * width])
            normed[rows, :] = (hat * scale + shift).astype(BF16)
            gate = mm(pick, tab_ref[:, 5 * width : 6 * width])
            g = put_together(tp_ref[0] == 0, gown_ref[rows, :], gcame_ref[rows, :])
            gmixed[rows, :] = (g.astype(F32) * gate).astype(BF16)
            mixed[rows, :] = jnp.zeros((HALF, width), F32)
            gnormed[rows, :] = jnp.zeros((HALF, width), F32)

        block_loop(blocks, body)
        normed_t[...] = normed[...].T
        gmixed_t[...] = gmixed[...].T

    for gu, wd, out in ((gup_ref, wdp_ref, gp_ref), (guo_ref, wdo_ref, go_ref)):

        def body(i):
            rows = pl.ds(pl.multiple_of(i * BLOCK, BLOCK), BLOCK)
            gate = mm(normed[rows, :], gu[0])
            up = mm(normed[rows, :], gu[1])
            ghid = mm_nt(gmixed[rows, :], wd[...])
            s = jax.nn.sigmoid(gate)
            silu = gate * s
            hidden = (silu * up).astype(BF16)
            hid[rows, :] = hidden
            mixed[rows, :] += mm(hidden, wd[...])
            dg = (ghid * up * (s + silu * (1.0 - s))).astype(BF16)
            du = (ghid * silu).astype(BF16)
            dgate[rows, :] = dg
            dup[rows, :] = du
            gnormed[rows, :] += mm_nt(dg, gu[0]) + mm_nt(du, gu[1])

        block_loop(tokens // BLOCK, body)
        out[0, 0] = mm(normed_t[...], dgate[...]).astype(BF16)
        out[1, 0] = mm(normed_t[...], dup[...]).astype(BF16)
        out[2, 0] = mm(gmixed_t[...], hid[...]).astype(BF16)

    @pl.when(step == pl.num_programs(0) - 1)
    def _():
        first_core = tp_ref[0] == 0
        sums_ref[...] = jnp.zeros(sums_ref.shape, F32)

        def body(i):
            rows = pl.ds(pl.multiple_of(i * HALF, HALF), HALF)
            pick = oh_ref[rows, :]
            turn = oht_ref[i]
            g = put_together(first_core, gown_ref[rows, :], gcame_ref[rows, :]).astype(F32)
            total = mixed[rows, :]
            gate = mm(pick, tab_ref[:, 5 * width : 6 * width])
            mid = middle[rows, :]
            result = (mid + gate * total).astype(BF16)
            low, high = result[:, : width // 2], result[:, width // 2 :]
            outo_ref[rows, :] = jnp.where(first_core, low, high)
            outp_ref[rows, :] = jnp.where(first_core, high, low)
            sums_ref[0] += mm(turn, (g * total).astype(BF16))
            hat, inv_std = norm_parts(mid)
            gn = gnormed[rows, :]
            sums_ref[1] += mm(turn, (gn * hat).astype(BF16))
            sums_ref[2] += mm(turn, gn.astype(BF16))
            scale = mm(pick, tab_ref[:, 3 * width : 4 * width])
            gmid = g + norm_back(gn * scale, hat, inv_std)
            gmid_ref[rows, :] = gmid
            sums_ref[3] += mm(turn, (gmid * branches[rows, :]).astype(BF16))
            gbranch = (gmid * mm(pick, tab_ref[:, 2 * width : 3 * width])).astype(BF16)
            gmixed[rows, :] = gbranch
            gatt_ref[rows, :half] = mm_nt(gbranch, woo_ref[...]).astype(BF16)
            gatt_ref[rows, half:] = mm_nt(gbranch, wop_ref[...]).astype(BF16)

        block_loop(blocks, body)
        gmixed_t[...] = gmixed[...].T
        goo_ref[...] = mm(gmixed_t[...], att_ref[:, :half]).astype(BF16)
        gop_ref[...] = mm(gmixed_t[...], att_ref[:, half:]).astype(BF16)
        low, high = sums_ref[:, :, : width // 2], sums_ref[:, :, width // 2 :]
        sumo_ref[...] = jnp.where(first_core, low, high)
        sump_ref[...] = jnp.where(first_core, high, low)


def ffn_turn(tp, att, woo, wop, x, pick, table, guo, gup, wdo, wdp, g_own, g_came, pick_t):
    tokens, width = x.shape
    half = woo.shape[0]
    hidden = wdo.shape[0]
    grads = jax.ShapeDtypeStruct((3, hidden // FFC, width, FFC), BF16)
    grads_spec = pl.BlockSpec((3, 1, width, FFC), lambda j, *_: (0, j, 0, 0))
    return call(
        turn_kernel,
        (hidden // FFC,),
        ffn_specs(att, woo, x, pick, table) + [whole(tokens, width // 2), whole(tokens, width // 2), whole(*pick_t.shape)],
        (
            whole(tokens, width // 2),
            whole(tokens, width // 2),
            whole(tokens, width),
            whole(tokens, width),
            grads_spec,
            grads_spec,
            whole(width, half),
            whole(width, half),
            whole(4, 16, width // 2),
            whole(4, 16, width // 2),
        ),
        (
            jax.ShapeDtypeStruct((tokens, width // 2), BF16),
            jax.ShapeDtypeStruct((tokens, width // 2), BF16),
            jax.ShapeDtypeStruct((tokens, width), F32),
            jax.ShapeDtypeStruct((tokens, width), BF16),
            grads,
            grads,
            jax.ShapeDtypeStruct((width, half), BF16),
            jax.ShapeDtypeStruct((width, half), BF16),
            jax.ShapeDtypeStruct((4, 16, width // 2), F32),
            jax.ShapeDtypeStruct((4, 16, width // 2), F32),
        ),
        [
            pltpu.VMEM((4, 16, width), F32),
            pltpu.VMEM((tokens, width), F32),
            pltpu.VMEM((8, LANES), F32),
            pltpu.VMEM((tokens, width), F32),
            pltpu.VMEM((tokens, width), BF16),
            pltpu.VMEM((width, tokens), BF16),
            pltpu.VMEM((tokens, width), BF16),
            pltpu.VMEM((width, tokens), BF16),
            pltpu.VMEM((tokens, width), F32),
            pltpu.VMEM((tokens, width), F32),
            pltpu.VMEM((tokens, FFC), BF16),
            pltpu.VMEM((tokens, FFC), BF16),
            pltpu.VMEM((tokens, FFC), BF16),
        ],
        prefetch=1,
        flops=2 * tokens * width * (18 * hidden + 3 * width),
        moved=24 * hidden * width + 12 * tokens * width,
    )(tp, att, woo, wop, x, pick, table, guo, gup, wdo, wdp, g_own, g_came, pick_t)


def attend_back_block(q, segq, gout, logs, keys, keys_t, values, biases, bias_sums, gkeys, gvalues):
    half = LANES // 2
    masks = lane_masks()
    scale = half**-0.5
    scaled = q * jnp.asarray(scale, BF16)
    gqs = []
    for h in range(2):
        query_low = scaled * masks[h]
        query = jnp.concatenate([query_low, segq], axis=1)
        gheads = gout * masks[h]
        chances = [jnp.exp(bias(h, mm_nt(key, query)) - logs[h : h + 1, :]) for key, bias in zip(keys, biases)]
        gchances = [mm_nt(value, gheads) for value in values]
        centre = sum(jnp.sum(p * gp, axis=0, keepdims=True) for p, gp in zip(chances, gchances))
        gq = 0.0
        for b, (p, gp) in enumerate(zip(chances, gchances)):
            gs = p * (gp - centre)
            bias_sums[b](h, gs)
            low = gs.astype(BF16)
            gvalues[b] = gvalues[b] + mm(p.astype(BF16), gheads)
            gkeys[b] = gkeys[b] + mm(low, query_low)
            gq = gq + mm(keys_t[b][h * half : (h + 1) * half, :], low)
        gqs.append(gq * scale)
    return jnp.concatenate(gqs, axis=0).T.astype(BF16)


def diagonal_sums(tile):
    size, wide = tile.shape
    blank = jnp.zeros((SUB, wide), F32)
    groups = [jnp.zeros((SUB, 2 * wide), F32)] * 2
    for i, a in enumerate(range(0, size, SUB)):
        piece = jnp.concatenate([tile[a : a + SUB], blank], axis=1)
        groups[i % 2] = groups[i % 2] + pltpu.roll(piece, size - SUB - a, axis=1)
    total = groups[0] + groups[1]
    rows = lax.broadcasted_iota(jnp.int32, (SUB, 2 * wide), 0)
    moved = sum(pltpu.roll(jnp.where(rows == b, total, 0.0), SUB - 1 - b, axis=1) for b in range(SUB))
    return jnp.sum(moved, axis=0, keepdims=True)


def far_sums(tile, later):
    whole_sum = jnp.sum(jnp.sum(tile, axis=0, keepdims=True), axis=1, keepdims=True)
    edge = tile[:RADIUS, LANES:] if later else tile[HALF - RADIUS :, :LANES]
    sums = diagonal_sums(edge)
    rest = whole_sum - jnp.sum(sums, axis=1, keepdims=True)
    row = jnp.concatenate([sums, jnp.zeros((1, 2 * HALF - sums.shape[1]), F32)], axis=1)
    row = jnp.broadcast_to(row, (8, 2 * HALF))
    if later:
        row = pltpu.roll(row, 2 * HALF - LANES - RADIUS, axis=1)
    lanes = lax.broadcasted_iota(jnp.int32, (1, 2 * HALF), 1)
    return row[:1] + jnp.where(lanes == (0 if later else 2 * HALF - 2), rest, 0.0)


def attend_full_back_kernel(
    q_ref, k_ref, v_ref, g_ref, log_ref, segq_ref, segk_ref, near_ref, far_ref, o_ref, diag_ref, sums
):
    keys, keys_t, values = [], [], []
    for b in range(2):
        rows = pl.ds(b * HALF, HALF)
        key = k_ref[rows, :]
        keys.append(jnp.concatenate([key, segk_ref[rows, :]], axis=1))
        keys_t.append(key.T)
        values.append(v_ref[rows, :])
    gkeys, gvalues = [0.0, 0.0], [0.0, 0.0]
    sums[...] = jnp.zeros(sums.shape, F32)
    for qb in range(2):
        rows = pl.ds(qb * HALF, HALF)
        biases = full_biases(near_ref, far_ref, qb)

        def add(h, gs):
            sums[h] += gs

        def put(h, gs, later):
            row = 3 * h + (0 if later else 2)
            diag_ref[0, row : row + 1, :] = far_sums(gs, later)

        adders = [add, functools.partial(put, later=True)] if qb == 0 else [functools.partial(put, later=False), add]
        o_ref[0, rows, :] = attend_back_block(
            q_ref[rows, :], segq_ref[rows, :], g_ref[rows, :], log_ref[0, 0:2, rows],
            keys, keys_t, values, biases, adders, gkeys, gvalues,
        )
    for b in range(2):
        rows = pl.ds(b * HALF, HALF)
        o_ref[1, rows, :] = gkeys[b].astype(BF16)
        o_ref[2, rows, :] = gvalues[b].astype(BF16)
    for h in range(2):
        diag_ref[0, 3 * h + 1 : 3 * h + 2, :] = diagonal_sums(sums[h])


def attend_half_back_kernel(
    tp_ref, q_ref, k_ref, v_ref, kp_ref, vp_ref, g_ref, log_ref, segq_ref, segk_ref, near_ref, far_ref,
    o_ref, par_ref, diag_ref,
):
    keys, keys_t, values = [], [], []
    for b, (k, v) in enumerate(((k_ref, v_ref), (kp_ref, vp_ref))):
        key = k[...]
        keys.append(jnp.concatenate([key, segk_ref[pl.ds(b * HALF, HALF), :]], axis=1))
        keys_t.append(key.T)
        values.append(v[...])
    first = tp_ref[0] == 0
    biases = half_biases(near_ref, far_ref, first)
    gkeys, gvalues = [0.0, 0.0], [0.0, 0.0]

    def put(h, gs, b):
        sums = jnp.where(first, far_sums(gs, True), far_sums(gs, False)) if b else diagonal_sums(gs)
        diag_ref[0, 2 * h + b : 2 * h + b + 1, :] = sums

    adders = [functools.partial(put, b=b) for b in range(2)]
    o_ref[0] = attend_back_block(
        q_ref[...], segq_ref[...], g_ref[...], log_ref[0, 0:2, :],
        keys, keys_t, values, biases, adders, gkeys, gvalues,
    )
    o_ref[1] = gkeys[0].astype(BF16)
    o_ref[2] = gvalues[0].astype(BF16)
    par_ref[0] = gkeys[1].astype(BF16)
    par_ref[1] = gvalues[1].astype(BF16)


def attend_half_back(tp, qkv, kv_par, g, logs, segq, segk, bias):
    width = qkv.shape[1] // 3
    pairs = width // LANES
    flip = pairs // 2
    return call(
        attend_half_back_kernel,
        (pairs,),
        [
            pl.BlockSpec((HALF, LANES), lambda p, *_: (2, p)),
            pl.BlockSpec((HALF, LANES), lambda p, *_: (2, pairs + p)),
            pl.BlockSpec((HALF, LANES), lambda p, *_: (2, 2 * pairs + p)),
            pl.BlockSpec((HALF, LANES), lambda p, *_: (0, lax.rem(p + flip, pairs))),
            pl.BlockSpec((HALF, LANES), lambda p, *_: (0, pairs + lax.rem(p + flip, pairs))),
            pl.BlockSpec((HALF, LANES), lambda p, *_: (2, p)),
            pl.BlockSpec((1, 8, HALF), lambda p, *_: (p, 0, 2)),
            pl.BlockSpec((HALF, LANES), lambda p, *_: (2, 0)),
            pl.BlockSpec((ROW, LANES), lambda p, *_: (1, 0)),
        ]
        + bias_specs(),
        (
            pl.BlockSpec((3, HALF, LANES), lambda p, *_: (0, 0, p)),
            pl.BlockSpec((2, HALF, LANES), lambda p, *_: (0, 0, p)),
            pl.BlockSpec((1, 8, ROW), lambda p, *_: (p, 0, 0)),
        ),
        (
            jax.ShapeDtypeStruct((3, HALF, width), BF16),
            jax.ShapeDtypeStruct((2, HALF, width), BF16),
            jax.ShapeDtypeStruct((pairs, 8, ROW), F32),
        ),
        prefetch=1,
        flops=10 * HALF * HALF * 256 * 2 * pairs,
        moved=bias[0].size * 4,
    )(tp, qkv, qkv, qkv, kv_par, kv_par, g, logs, segq, segk, *bias)


def attend_full_back(qkv, g, logs, segq, segk, bias):
    width = qkv.shape[1] // 3
    pairs = width // LANES
    return call(
        attend_full_back_kernel,
        (pairs,),
        [
            pl.BlockSpec((ROW, LANES), lambda p: (0, p)),
            pl.BlockSpec((ROW, LANES), lambda p: (0, pairs + p)),
            pl.BlockSpec((ROW, LANES), lambda p: (0, 2 * pairs + p)),
            pl.BlockSpec((ROW, LANES), lambda p: (0, p)),
            pl.BlockSpec((1, 8, ROW), lambda p: (p, 0, 0)),
            pl.BlockSpec((ROW, LANES), lambda p: (0, 0)),
            pl.BlockSpec((ROW, LANES), lambda p: (0, 0)),
        ]
        + bias_specs(),
        (
            pl.BlockSpec((3, ROW, LANES), lambda p: (0, 0, p)),
            pl.BlockSpec((1, 8, ROW), lambda p: (p, 0, 0)),
        ),
        (
            jax.ShapeDtypeStruct((3, ROW, width), BF16),
            jax.ShapeDtypeStruct((pairs, 8, ROW), F32),
        ),
        [pltpu.VMEM((2, HALF, HALF), F32)],
        flops=20 * HALF * HALF * 256 * 2 * pairs,
        moved=bias[0].size * 4,
    )(qkv, qkv, qkv, g, logs, segq, segk, *bias)


def joined_rows(full_ref, half_ref, recv_ref, step, rows_in):
    half = recv_ref.shape[2] // 2
    rows_in[pl.ds(0, ROW), :] = full_ref[0]
    keep = (step > 0).astype(F32).astype(BF16)
    recv = jnp.concatenate([recv_ref[0, :, half:], recv_ref[0, :, :half]], axis=1)
    rows_in[pl.ds(ROW, HALF), :] = half_ref[0] + recv * keep


def qkv_weights_kernel(
    x_ref, oh_ref, tab_ref, full_ref, half_ref, recv_ref, outo_ref, outp_ref, go_ref, gp_ref, normed, normed_t, rows_in
):
    step = pl.program_id(0)
    tokens, width = x_ref.shape
    half = width // 2

    @pl.when(step == 0)
    def _():
        def body(i):
            rows = pl.ds(pl.multiple_of(i * HALF, HALF), HALF)
            hat, _ = norm_parts(x_ref[rows, :])
            pick = oh_ref[rows, :]
            scale = mm(pick, tab_ref[:, :width])
            shift = mm(pick, tab_ref[:, width : 2 * width])
            normed[rows, :] = (hat * scale + shift).astype(BF16)

        block_loop(tokens // HALF, body)
        normed_t[...] = normed[...].T

    joined_rows(full_ref, half_ref, recv_ref, step, rows_in)
    go_ref[0, :, :half] = mm(normed_t[...], rows_in[:, :half]).astype(BF16)
    gp_ref[0, :, :half] = mm(normed_t[...], rows_in[:, half:]).astype(BF16)
    go_ref[0, :, half:] = outo_ref[...]
    gp_ref[0, :, half:] = outp_ref[...]


def row_specs(width):
    return [
        pl.BlockSpec((1, ROW, width), lambda j, *_: (j, 0, 0)),
        pl.BlockSpec((1, HALF, width), lambda j, *_: (j, 0, 0)),
        pl.BlockSpec((1, HALF, width), lambda j, *_: (jnp.maximum(j - 1, 0), 0, 0)),
    ]


def qkv_weights(x, pick, table, full, half_rows, recv, out_own, out_par):
    tokens, width = x.shape
    half = width // 2
    third = half // 3
    spec = pl.BlockSpec((1, width, half + third), lambda j: (j, 0, 0))
    shape = jax.ShapeDtypeStruct((3, width, half + third), BF16)
    out_spec = pl.BlockSpec((width, third), lambda j: (0, j))
    return call(
        qkv_weights_kernel,
        (3,),
        [whole(tokens, width), whole(*pick.shape), whole(*table.shape)] + row_specs(width) + [out_spec, out_spec],
        (spec, spec),
        (shape, shape),
        [
            pltpu.VMEM((tokens, width), BF16),
            pltpu.VMEM((width, tokens), BF16),
            pltpu.VMEM((tokens, width), BF16),
        ],
        flops=2 * tokens * width * 6 * half,
        moved=16 * half * width + 12 * tokens * width,
    )(x, pick, table, full, half_rows, recv, out_own, out_par)


def qkv_back_kernel(
    tp_ref, x_ref, oh_ref, tab_ref, full_ref, half_ref, recv_ref, wo_ref, wp_ref, gmid_ref, lifted_ref, oht_ref,
    gino_ref, ginp_ref, sumo_ref, sump_ref, hats, stds, rows_in, acc, sums,
):
    step = pl.program_id(0)
    tokens, width = x_ref.shape
    half = wo_ref.shape[1]
    blocks = tokens // HALF

    @pl.when(step == 0)
    def _():
        def body(i):
            rows = pl.ds(pl.multiple_of(i * HALF, HALF), HALF)
            hat, inv_std = norm_parts(x_ref[rows, :])
            hats[rows, :] = hat
            stds[rows, :] = inv_std
            acc[rows, :] = jnp.zeros((HALF, width), F32)

        block_loop(blocks, body)

    joined_rows(full_ref, half_ref, recv_ref, step, rows_in)

    def body(i):
        rows = pl.ds(pl.multiple_of(i * HALF, HALF), HALF)
        grad = rows_in[rows, :]
        acc[rows, :] += mm_nt(grad[:, :half], wo_ref[...]) + mm_nt(grad[:, half:], wp_ref[...])

    block_loop(blocks, body)

    @pl.when(step == pl.num_programs(0) - 1)
    def _():
        first_core = tp_ref[0] == 0
        sums[...] = jnp.zeros(sums.shape, F32)

        def body(i):
            rows = pl.ds(pl.multiple_of(i * HALF, HALF), HALF)
            turn = oht_ref[i]
            gn = acc[rows, :]
            hat = hats[rows, :]
            sums[0] += mm(turn, (gn * hat).astype(BF16))
            sums[1] += mm(turn, gn.astype(BF16))
            scale = mm(oh_ref[rows, :], tab_ref[:, :width])
            grad = gmid_ref[rows, :] + norm_back(gn * scale, hat, stds[rows, :])
            low, high = grad[:, : width // 2], grad[:, width // 2 :]
            gino_ref[rows, :] = jnp.where(first_core, low, high)
            ginp_ref[rows, :] = jnp.where(first_core, high, low)
            lifted_t = lifted_ref[rows, :].astype(BF16).T
            sums[2] += mm(lifted_t[:16, :], grad.astype(BF16))

        block_loop(blocks, body)
        low, high = sums[:, :, : width // 2], sums[:, :, width // 2 :]
        sumo_ref[...] = jnp.where(first_core, low, high)
        sump_ref[...] = jnp.where(first_core, high, low)


def qkv_back(tp, x, pick, table, full, half_rows, recv, wo, wp, gmid, lifted, pick_t):
    tokens, width = x.shape
    half = wo.shape[1] // 3
    return call(
        qkv_back_kernel,
        (3,),
        [whole(tokens, width), whole(*pick.shape), whole(*table.shape)]
        + row_specs(width)
        + [
            pl.BlockSpec((width, half), lambda j, *_: (0, j)),
            pl.BlockSpec((width, half), lambda j, *_: (0, j)),
            whole(tokens, width),
            whole(tokens, LANES),
            whole(*pick_t.shape),
        ],
        (
            whole(tokens, width // 2),
            whole(tokens, width // 2),
            whole(3, 16, width // 2),
            whole(3, 16, width // 2),
        ),
        (
            jax.ShapeDtypeStruct((tokens, width // 2), F32),
            jax.ShapeDtypeStruct((tokens, width // 2), F32),
            jax.ShapeDtypeStruct((3, 16, width // 2), F32),
            jax.ShapeDtypeStruct((3, 16, width // 2), F32),
        ),
        [
            pltpu.VMEM((tokens, width), F32),
            pltpu.VMEM((tokens, 1), F32),
            pltpu.VMEM((tokens, width), BF16),
            pltpu.VMEM((tokens, width), F32),
            pltpu.VMEM((3, 16, width), F32),
        ],
        prefetch=1,
        flops=2 * tokens * width * 6 * half,
        moved=12 * half * width + 16 * tokens * width,
    )(tp, x, pick, table, full, half_rows, recv, wo, wp, gmid, lifted, pick_t)


def chain_joins(first_core):
    row = lax.broadcasted_iota(jnp.int32, (16, 16), 0)
    col = lax.broadcasted_iota(jnp.int32, (16, 16), 1)
    lower = ((row == col) & (row < 2 * SEGS)).astype(F32)
    upper = (
        ((row == col) & (row >= SEGS) & (row < 2 * SEGS)) | ((row == col + 2 * SEGS) & (row < 3 * SEGS))
    ).astype(F32)
    return jnp.where(first_core, lower, upper), jnp.where(first_core, upper, lower)


def join_chains(tp_ref, own_ref, came_ref, slope_ref, count, o_ref):
    own_join, came_join = chain_joins(tp_ref[0] == 0)
    cols = own_ref.shape[2]
    for i in range(count):
        both = jnp.dot(own_join, own_ref[i], precision=HIGHEST, preferred_element_type=F32)
        both = both + jnp.dot(came_join, came_ref[i], precision=HIGHEST, preferred_element_type=F32)
        lanes = pl.ds(i * cols, cols)
        o_ref[0:16, lanes] = (both * slope_ref[:, lanes]).astype(BF16)


def early_kernel(tp_ref, own_ref, came_ref, slope_ref, embed_ref, o_ref):
    join_chains(tp_ref, own_ref, came_ref, slope_ref, 4, o_ref)
    o_ref[:, pl.ds(4 * own_ref.shape[2], embed_ref.shape[1])] = embed_ref[...]


def late_kernel(tp_ref, own_ref, came_ref, slope_ref, bins_ref, o_ref):
    cols = own_ref.shape[2]
    join_chains(tp_ref, own_ref, came_ref, slope_ref, 2, o_ref)
    o_ref[:, pl.ds(2 * cols, LANES)] = bins_ref[...].astype(BF16)
    coords = own_ref[2] + came_ref[2]
    parts = [coords[i : i + 1, j : j + LANES] for j in range(0, cols, LANES) for i in range(3)]
    parts.append(jnp.zeros((16 - len(parts), LANES), F32))
    o_ref[:, pl.ds(2 * cols + LANES, LANES)] = jnp.concatenate(parts, axis=0).astype(BF16)


def pack_rows(kernel, tp, own, came, slopes, extra, shape):
    return call(
        kernel,
        (1,),
        [whole(*own.shape), whole(*came.shape), whole(*slopes.shape), whole(*extra.shape)],
        whole(*shape),
        jax.ShapeDtypeStruct(shape, BF16),
        prefetch=1,
        flops=10**6,
        moved=10**5,
    )(tp, own, came, slopes, extra)


def closing_kernel(early_ref, early_came_ref, late_ref, late_came_ref, hat_ref, inv_ref, gain_ref, both_ref, *refs):
    ffn, attn, outs = refs[:2], refs[2:4], refs[4:]
    gu_ref, down_ref, qkv_ref, out_ref = outs[:4]
    w0_ref, b0_ref, w1_ref, w2_ref, b2_ref, w3_ref, b3_ref, w4_ref, w5_ref, b5_ref = outs[4:14]
    table_ref, pgain_ref, proj_ref, coord_ref = outs[14:]

    def total(pair, block):
        return pair[0][0, block].astype(F32) + pair[1][0, block].astype(F32)

    lanes = ffn[0].shape[3]
    chunks = down_ref.shape[1] // lanes
    for block in range(chunks):
        span = pl.ds(block * lanes, lanes)
        gu_ref[:, 0, span] = total(ffn, block)
        gu_ref[:, 1, span] = total(ffn, chunks + block)
        down_ref[:, span] = total(ffn, 2 * chunks + block)
    third = out_ref.shape[1] // 3
    for i in range(3):
        value = total(attn, i)
        qkv_ref[i] = value[:, : 3 * third]
        out_ref[:, i * third : (i + 1) * third] = value[:, 3 * third :]

    cols = coord_ref.shape[1]
    pieces = [(early_ref, late_ref), (early_came_ref, late_came_ref)]
    embed_t = [early[:, 4 * cols :].T for early, _ in pieces]
    weights = [w0_ref, w1_ref, w5_ref, w3_ref, w4_ref, w2_ref]
    biases = [b0_ref, None, b5_ref, b3_ref, None, b2_ref]
    for i, (weight, bias) in enumerate(zip(weights, biases)):
        source, lanes = (1, pl.ds(i * cols, cols)) if i < 2 else (0, pl.ds((i - 2) * cols, cols))
        parts = [piece[source][:, lanes] for piece in pieces]
        weight[...] = sum(mm(embed, part) for embed, part in zip(embed_t, parts))
        if bias is not None:
            bias[...] = sum(jnp.sum(part.astype(F32), axis=0) for part in parts)
    extra = sum(late[:, 2 * cols :].reshape(-1, 16, 2 * LANES).astype(F32).sum(axis=0) for _, late in pieces)
    for i in range(cols // LANES):
        coord_ref[:, pl.ds(i * LANES, LANES)] = extra[3 * i : 3 * i + 3, LANES:]
    bins = extra[:, :LANES]
    hat = hat_ref[...]
    gain = gain_ref[...]
    proj = jnp.dot(bins, hat * gain, precision=HIGHEST, preferred_element_type=F32)
    proj_ref[...] = proj[: proj_ref.shape[0]]
    normed_grad = jnp.dot(bins.T, both_ref[...], precision=HIGHEST, preferred_element_type=F32)
    pgain_ref[...] = jnp.sum(normed_grad * hat, axis=0)
    table_ref[...] = norm_back(normed_grad * gain, hat, inv_ref[...])[: table_ref.shape[0]]


def closing(early, late, hat, inv_std, gain, both, ffn, attn, bins, heads):
    cols = (late[0].shape[1] - 2 * LANES) // 2
    embed = early[0].shape[1] - 4 * cols
    features = hat.shape[1]
    height, lanes = ffn[0].shape[2:]
    weight, bias = (embed, cols), (cols,)
    hidden = lanes * (ffn[0].shape[1] // 3)
    shapes = [(height, 2, hidden), (height, hidden), (3, height, cols), (height, cols)]
    shapes += [weight, bias, weight, weight, bias, weight, bias, weight, weight, bias]
    shapes += [(bins, features), (features,), (heads, features), (3, cols)]
    args = (*early, *late, hat, inv_std, gain, both, *ffn, *attn)
    return call(
        closing_kernel,
        (1,),
        [whole(*a.shape) for a in args],
        tuple(whole(*shape) for shape in shapes),
        tuple(jax.ShapeDtypeStruct(shape, F32) for shape in shapes),
        flops=10**8,
        moved=10**7,
    )(*args)


def halve_kernel(place_ref, *refs, plan, count, keep):
    inputs, outs = refs[:count], refs[count:]
    for (bit, sections), ref in zip(plan, outs):
        mine = (place_ref[0] >> bit) & 1
        which = mine if keep else 1 - mine
        done = 0
        for first, second, base, chunks, left in sections:
            spot = left.index(bit)
            shift = len(left) - 1
            half = 1 << shift

            def body(n, first=first, second=second, base=base, spot=spot, shift=shift, done=done, which=which, ref=ref):
                k = n & ((1 << shift) - 1)
                at = base + ((n >> shift) << (shift + 1)) + ((k >> spot) << (spot + 1)) + (k & ((1 << spot) - 1))
                block = at + (which << spot)
                ref[0, done + n] = inputs[first][0, block] + inputs[second][0, block]

            block_loop(chunks * half, body)
            done += chunks * half


def halve(place, streams, bits, keep):
    arrays, specs, plan, shapes = [], [], [], []
    steps = streams[0][0][5]
    if any(len(sections) > 1 or sections[0][5] != steps for sections in streams):
        steps = 1

    def operand(array, index):
        for i, (seen, at) in enumerate(arrays):
            if seen is array and at == index:
                return i
        arrays.append((array, index))
        block = (1, array.shape[1] // steps) + array.shape[2:]
        specs.append(pl.BlockSpec(block, lambda j, *_: (index, j, 0, 0)))
        return len(arrays) - 1

    moved = 0
    for sections, bit in zip(streams, bits):
        entries, blocks = [], 0
        for own, i, came, k, base, chunks, left in sections:
            entries.append((operand(own, i), operand(came, k), base, chunks // steps, left))
            blocks += chunks << (len(left) - 1)
        plan.append((bit, entries))
        shape = (1, blocks) + sections[0][0].shape[2:]
        shapes.append(shape)
        moved += 6 * blocks * shape[2] * shape[3]
    outs = call(
        functools.partial(halve_kernel, plan=plan, count=len(arrays), keep=keep),
        (steps,),
        specs,
        tuple(pl.BlockSpec((1, n // steps, h, c), lambda j, *_: (0, j, 0, 0)) for _, n, h, c in shapes),
        tuple(jax.ShapeDtypeStruct(shape, BF16) for shape in shapes),
        prefetch=1,
        flops=10**6,
        moved=moved,
    )(place, *[array for array, _ in arrays])
    return list(outs)


def swap(values):
    return lax.ppermute(values, "tp", [(0, 1), (1, 0)])


def after(values, *others):
    return lax.optimization_barrier((values, *others))[0]


class Cube:
    def __init__(self, rows):
        self.bits = rows.bit_length() - 1
        assert rows == 1 << self.bits
        self.place = lax.axis_index("rows").reshape(1).astype(jnp.int32)
        self.perms = [[(i, i ^ (1 << b)) for i in range(rows)] for b in range(self.bits)]

    def turns(self):
        return [[(i + r) % 3 for i in range(3)] for r in range(3)]

    def gather(self, values, step):
        bit = (list(range(self.bits - 1, 1, -1)) + list(range(min(2, self.bits))))[step]
        came = lax.ppermute(values, "rows", self.perms[bit])
        if step == self.bits - 1:
            return values, came
        return lax.optimization_barrier(jnp.concatenate([values, came], axis=0))


def next_sections(sections, kept, came, bit):
    made, base = [], 0
    for _, _, _, _, _, chunks, left in sections:
        left = [b for b in left if b != bit]
        made.append((kept, 0, came, 0, base, chunks, left))
        base += chunks << len(left)
    return made


def normalize(values):
    centre = jnp.mean(values, axis=-1, keepdims=True)
    shifted = values - centre
    spread = jnp.mean(shifted * shifted, axis=-1, keepdims=True)
    inv_std = lax.rsqrt(spread + EPSILON)
    return shifted * inv_std, inv_std


def three_parts(values):
    high = lax.reduce_precision(values, 8, 7)
    middle = lax.reduce_precision(values - high, 8, 7)
    low = values - high - middle
    return jnp.concatenate([high, middle, low], axis=0).astype(BF16)


def bias_base(heads):
    bins = heads.shape[1]
    low = lambda n: jnp.broadcast_to(heads[:, :1], (heads.shape[0], n))
    top = lambda n: jnp.broadcast_to(heads[:, bins - 1 :], (heads.shape[0], n))
    fill = HALF - RADIUS
    behind = jnp.concatenate([low(fill), heads[:, :RADIUS], low(HALF)], axis=1)
    same = jnp.concatenate([heads[:, RADIUS:], top(fill - 1), low(fill), heads[:, :RADIUS]], axis=1)
    ahead = jnp.concatenate([top(HALF), heads[:, RADIUS:], top(fill - 1)], axis=1)
    return jnp.stack([behind, same, ahead], axis=1)


def bins_of_diagonals():
    places = jnp.arange(ROW, dtype=jnp.int32)[None, :] - (HALF - 1)
    offsets = places + HALF * jnp.arange(-1, 2, dtype=jnp.int32)[:, None]
    bins = jnp.clip(offsets, -RADIUS, RADIUS) + RADIUS
    every = jnp.arange(2 * RADIUS + 1, dtype=jnp.int32)
    return (bins.reshape(-1)[:, None] == every[None, :]).astype(F32)


def per_device(
    layer_input,
    cotangent,
    chain_lengths,
    self_condition_flag,
    time_embedding,
    query_key_value,
    output_projection,
    attention_scale_weight,
    attention_scale_bias,
    attention_shift_weight,
    attention_gate_weight,
    attention_gate_bias,
    transition_scale_weight,
    transition_scale_bias,
    transition_shift_weight,
    transition_gate_weight,
    transition_gate_bias,
    gate_up_projection,
    down_projection,
    pair_table,
    pair_gain,
    pair_projection,
    coordinate_head,
    coordinate_embedding,
    rows,
):
    core = lax.axis_index("tp")
    first_core = core == 0
    tp = core.reshape(1).astype(jnp.int32)
    cols = layer_input.shape[1]
    width = query_key_value.shape[0]
    heads_here = pair_projection.shape[1]
    bins = pair_table.shape[0]
    cube = Cube(rows)

    def side_by_side(own, came, axis):
        return jnp.where(
            first_core, jnp.concatenate([own, came], axis), jnp.concatenate([came, own], axis)
        )

    def scatter_tokens(own, sent):
        came = swap(sent)
        lower = jnp.concatenate([own[:ROW], own[ROW:], came[ROW:], came[:ROW]], axis=0)
        upper = jnp.concatenate([came[:ROW], came[ROW:], own[ROW:], own[:ROW]], axis=0)
        return jnp.where(first_core, lower, upper)

    x_own, x_sent, cot_own, cot_sent = token_halves(tp, layer_input, cotangent)
    x_came = swap(x_sent)
    qkv_own = query_key_value.reshape(width, -1)
    qkv_par = swap(qkv_own)

    mods, early_slopes, late_slopes, embed = modulations(
        time_embedding,
        [
            attention_scale_weight,
            attention_shift_weight,
            attention_gate_weight,
            transition_scale_weight,
            transition_shift_weight,
            transition_gate_weight,
        ],
        [attention_scale_bias, attention_gate_bias, transition_scale_bias, transition_gate_bias],
    )
    table = chain_table(tp, mods, swap(mods))
    mask_q, mask_k, pick, pick_t, flags = masks(tp, chain_lengths, self_condition_flag)

    pair_hat, pair_inv = normalize(pair_table.astype(F32))
    gain = pair_gain.astype(F32)
    pair_normed = pair_hat * gain
    pair_both = jnp.concatenate([pair_projection, swap(pair_projection)], axis=1).astype(F32)
    bias_heads = jnp.transpose(jnp.dot(pair_normed, pair_both, precision=HIGHEST))
    bias_source = jnp.transpose(pair_both)
    bias = bias_tiles(bias_base(bias_heads))

    out_own = output_projection
    out_par = swap(output_projection)
    gu_own = jnp.transpose(gate_up_projection, (1, 0, 2))
    gu_par = swap(gu_own)
    down_own = down_projection
    down_par = swap(down_projection)
    coord = jnp.concatenate([coordinate_head, coordinate_embedding], axis=0)
    coord = side_by_side(coord, swap(coord), 1)
    fill = jnp.zeros((LANES - 3, width), BF16)
    head = jnp.concatenate([coord[:3], fill], axis=0)
    emb = jnp.concatenate([coord[3:], fill], axis=0)
    cot_came = swap(cot_sent)

    def attention(qkv, kv):
        kv_par = swap(kv)
        attended, logs = attend_forward(tp, qkv, kv_par, mask_q, mask_k, bias)
        return qkv, kv_par, attended, logs

    qkv, kv, x = qkv_first(tp, x_own, x_came, pick, table, qkv_own, qkv_par)
    _, _, attended, _ = attention(qkv, kv)
    shifted, lifted = ffn_forward(
        attended, out_own, out_par, x, pick, table, gu_own, gu_par, down_own, down_par, head, emb, flags
    )
    qkv, kv_par, attended, logs = attention(*qkv_forward(shifted, pick, table, qkv_own, qkv_par))
    (
        result_own,
        result_sent,
        grad_middle,
        grad_attended,
        grads_own,
        grads_sent,
        grad_out_own,
        grad_out_sent,
        early_own,
        early_sent,
    ) = ffn_turn(
        tp, attended, out_own, out_par, shifted, pick, table, gu_own, gu_par, down_own, down_par, cot_own, cot_came, pick_t
    )

    early_came = swap(early_sent)

    came_ffn = swap(grads_sent)
    half_grads, far_grads, diag_half = attend_half_back(
        tp, qkv, kv_par, grad_attended, logs, mask_q, mask_k, bias
    )
    came_grads = swap(far_grads)

    turns = cube.turns()
    every = list(range(cube.bits))
    height = width // rows
    slots = lambda values: values.reshape(3, -1, height, values.shape[-1])
    chunks = grads_own.shape[1]
    own_slots, came_slots = slots(grads_own), slots(came_ffn)
    ffn = [[(own_slots, i, came_slots, i, 0, chunks, every)] for i in range(3)]

    def one_round(streams, bits, *others):
        sent = halve(cube.place, streams, bits, False)
        *held, place = lax.optimization_barrier((*sent, *others, cube.place))
        came = [lax.ppermute(v, "rows", cube.perms[bit]) for v, bit in zip(held, bits)]
        kept = halve(place, streams, bits, True)
        made = [next_sections(*parts) for parts in zip(streams, kept, came, bits)]
        return made, came, held[len(sent) :]

    ffn, came, (mask_full, early_came, _) = one_round(ffn, turns[0], mask_q, early_came, diag_half)
    early = pack_rows(
        early_kernel, tp, early_own, early_came, early_slopes, embed, (16, 4 * cols + embed.shape[1])
    )
    full_grads, diag_full = attend_full_back(qkv, grad_attended, logs, mask_full, mask_k, bias)
    early = cube.gather(early, 0)
    ffn, came, (pick_weights, early, _) = one_round(ffn, turns[1], pick, early, diag_full)
    gqkv_own, gqkv_sent = qkv_weights(
        shifted, pick_weights, table, full_grads, half_grads, came_grads, grad_out_own, grad_out_sent
    )
    early = cube.gather(early, 1)
    gqkv_sent, early, *_ = lax.optimization_barrier((gqkv_sent, early, *came))
    own_slots, came_slots = slots(gqkv_own), slots(swap(gqkv_sent))
    streams = [ffn[i] + [(own_slots, i, came_slots, i, 0, 1, every)] for i in range(3)]
    streams, came, (pick_back, early) = one_round(streams, turns[2], pick_weights, early)
    gin_own, gin_sent, late_own, late_sent = qkv_back(
        tp, shifted, pick_back, table, full_grads, half_grads, came_grads, qkv_own, qkv_par, grad_middle, lifted, pick_t
    )
    early = cube.gather(early, 2)
    late_sent, early, *_ = lax.optimization_barrier((late_sent, early, *came, *[s[0][0] for s in streams]))

    diag_half = diag_half[:, :4].reshape(-1, 2, ROW)
    quiet = jnp.zeros_like(diag_half[:, 0])
    diag_far = diag_half[:, 1]
    diag = diag_full[:, :6].reshape(-1, 3, ROW) + jnp.stack(
        [
            jnp.where(first_core, diag_far, quiet),
            diag_half[:, 0],
            jnp.where(first_core, quiet, diag_far),
        ],
        axis=1,
    )
    grad_bins = jnp.dot(diag.reshape(-1, 3 * ROW), bins_of_diagonals(), precision=HIGHEST)
    came_bins = swap(grad_bins)
    grad_bins = grad_bins + jnp.concatenate([came_bins[heads_here:], came_bins[:heads_here]], axis=0)
    bins_fill = jnp.pad(grad_bins, ((0, 16 - 2 * heads_here), (0, LANES - bins)))

    late_came = swap(late_sent)
    late = pack_rows(late_kernel, tp, late_own, late_came, late_slopes, bins_fill, (16, 2 * cols + 2 * LANES))
    ffn = [[stream[0] for stream in streams]]
    attn = [stream[1:] for stream in streams]
    rest = list(range(3, cube.bits))
    waited = []
    for step in range(max(len(rest), 2)):
        now, bits = [], []
        if step < len(rest):
            now, bits = ffn, rest[step : step + 1]
        count = len(now)
        if step < 2:
            attn, came, _ = one_round(attn, turns[step], *waited)
        late = cube.gather(late, step)
        if count:
            ffn, waited, (late,) = one_round(now, bits, late)
    done = max(len(rest), 2)
    attn = [[section for stream in attn for section in stream]]
    for bit in rest:
        attn, came, _ = one_round(attn, [bit])
        if done < cube.bits:
            late = after(late, *waited)
            late = cube.gather(late, done)
            done += 1
    for step in range(done, cube.bits):
        late = cube.gather(late, step)
    for step in range(3, cube.bits):
        early = cube.gather(early, step)
    ffn_last = (ffn[0][0][0], ffn[0][0][2])
    attn_last = (attn[0][0][0], attn[0][0][2])

    layer_output = scatter_tokens(result_own, result_sent)
    input_gradient = scatter_tokens(gin_own, gin_sent)

    bins_pad = ((0, LANES - bins), (0, 0))
    grad_gu, grad_down, grad_qkv, grad_out, *conditioning = closing(
        early,
        late,
        jnp.pad(pair_hat, bins_pad),
        jnp.pad(pair_inv, bins_pad),
        gain[None, :],
        jnp.pad(bias_source, ((0, 16 - 2 * heads_here), (0, 0))),
        ffn_last,
        attn_last,
        bins,
        heads_here,
    )
    *conditioning, grad_table, grad_gain, grad_pair, coord_grad = conditioning
    return (
        layer_output,
        input_gradient,
        jnp.transpose(grad_qkv, (1, 0, 2)),
        grad_out.T,
        *conditioning,
        grad_gu,
        grad_down.T,
        grad_table,
        grad_gain,
        grad_pair.T,
        coord_grad,
    )


def solution(mesh):
    in_specs = (
        P("rows", "tp"),
        P("rows", "tp"),
        P("rows", None),
        P("rows"),
        P("rows", None, None),
        P(None, None, "tp"),
        P("tp", None),
        P(None, "tp"),
        P("tp"),
        P(None, "tp"),
        P(None, "tp"),
        P("tp"),
        P(None, "tp"),
        P("tp"),
        P(None, "tp"),
        P(None, "tp"),
        P("tp"),
        P(None, None, "tp"),
        P("tp", None),
        P(),
        P(),
        P(None, "tp"),
        P(None, "tp"),
        P(None, "tp"),
    )
    out_specs = (
        P("rows", "tp"),
        P("rows", "tp"),
        P("rows", None, "tp"),
        P("tp", "rows"),
        P(None, "tp"),
        P("tp"),
        P(None, "tp"),
        P(None, "tp"),
        P("tp"),
        P(None, "tp"),
        P("tp"),
        P(None, "tp"),
        P(None, "tp"),
        P("tp"),
        P("rows", None, "tp"),
        P("tp", "rows"),
        P(),
        P(),
        P(None, "tp"),
        P(None, "tp"),
    )
    return jax.shard_map(
        functools.partial(per_device, rows=mesh.shape["rows"]),
        mesh=mesh,
        in_specs=in_specs,
        out_specs=out_specs,
        check_vma=False,
    )
```

```python
import functools
import jax
import jax.numpy as jnp
from jax import lax
from jax.experimental import pallas as pl
from jax.experimental.pallas import tpu as pltpu
from jax.sharding import PartitionSpec as P

RADIUS = 32
ROW = 512
HALF = ROW // 2
SEGS = 5
EPSILON = 1e-05
MASKED = -1e30
HIGHEST = lax.Precision.HIGHEST
F32 = jnp.float32
BF16 = jnp.bfloat16
LANES = 128
FFC = 512
BLOCK = 384
SUB = 8
NT = (((1,), (1,)), ((), ()))
VMEM_LIMIT = 60 * 1024 * 1024


def mm(left, right):
    return jnp.dot(left, right, preferred_element_type=F32)


def mm_nt(left, right):
    return lax.dot_general(left, right, NT, preferred_element_type=F32)


def norm_parts(values):
    centre = jnp.mean(values, axis=1, keepdims=True)
    shifted = values - centre
    spread = jnp.mean(shifted * shifted, axis=1, keepdims=True)
    inv_std = lax.rsqrt(spread + EPSILON)
    return shifted * inv_std, inv_std


def norm_back(grad, hat, inv_std):
    first = jnp.mean(grad, axis=1, keepdims=True)
    second = jnp.mean(grad * hat, axis=1, keepdims=True)
    return inv_std * (grad - first - hat * second)


def block_loop(count, body):
    lax.fori_loop(0, count, lambda i, c: (body(i), c)[1], 0)


def call(kernel, grid, in_specs, out_specs, out_shape, scratch=(), prefetch=0, aliases=None, flops=0, moved=0):
    return pl.pallas_call(
        kernel,
        grid_spec=pltpu.PrefetchScalarGridSpec(
            num_scalar_prefetch=prefetch,
            grid=grid,
            in_specs=in_specs,
            out_specs=out_specs,
            scratch_shapes=list(scratch),
        ),
        out_shape=out_shape,
        input_output_aliases=aliases or {},
        compiler_params=pltpu.CompilerParams(
            dimension_semantics=("arbitrary",) * len(grid), vmem_limit_bytes=VMEM_LIMIT
        ),
        cost_estimate=pl.CostEstimate(flops=flops, transcendentals=0, bytes_accessed=moved),
    )


def whole(*shape):
    zeros = (0,) * len(shape)
    return pl.BlockSpec(shape, lambda *_: zeros)


def bias_kernel(base_ref, near_ref, far_ref):
    for h, d, height, start, out in [
        run
        for h in range(base_ref.shape[0])
        for run in (
            (h, 1, HALF, 0, near_ref.at[h]),
            (h, 0, RADIUS, 0, far_ref.at[h, 0]),
            (h, 2, RADIUS, HALF - RADIUS, far_ref.at[h, 1]),
        )
    ]:
        rows = jnp.broadcast_to(base_ref[h, d : d + 1, :], (SUB, 2 * HALF))
        rows = pltpu.roll(rows, 0, axis=1, stride=1, stride_axis=0)
        for a in range(0, height, SUB):
            out[a : a + SUB, :] = pltpu.roll(rows, start + a, axis=1)[:, :HALF]


def bias_tiles(base):
    heads = base.shape[0]
    near, far = (heads, HALF, HALF), (heads, 2, RADIUS, HALF)
    return call(
        bias_kernel,
        (3,),
        [pl.BlockSpec((heads // 3, 3, 2 * HALF), lambda h: (h, 0, 0))],
        (
            pl.BlockSpec((heads // 3,) + near[1:], lambda h: (h, 0, 0)),
            pl.BlockSpec((heads // 3,) + far[1:], lambda h: (h, 0, 0, 0)),
        ),
        (jax.ShapeDtypeStruct(near, F32), jax.ShapeDtypeStruct(far, F32)),
        moved=heads * HALF * HALF * 4,
        flops=10**7,
    )(base)


def bias_specs():
    return [
        pl.BlockSpec((2, HALF, HALF), lambda p, *_: (p, 0, 0)),
        pl.BlockSpec((2, 2, RADIUS, HALF), lambda p, *_: (p, 0, 0, 0)),
    ]


def add_near(near_ref, far_ref, h, scores):
    return scores + near_ref[h]


def add_later(near_ref, far_ref, h, scores):
    edge = far_ref[h, 0]
    return jnp.concatenate([scores[:RADIUS] + edge, scores[RADIUS:] + edge[RADIUS - 1 :, :1]], axis=0)


def add_earlier(near_ref, far_ref, h, scores):
    edge = far_ref[h, 1]
    return jnp.concatenate(
        [scores[: HALF - RADIUS] + edge[:1, HALF - 1 :], scores[HALF - RADIUS :] + edge], axis=0
    )


def add_either(first, near_ref, far_ref, h, scores):
    later, earlier = far_ref[h, 0], far_ref[h, 1]
    rest = jnp.where(first, later[RADIUS - 1 :, :1], earlier[:1, HALF - 1 :])
    return jnp.concatenate(
        [
            scores[:RADIUS] + jnp.where(first, later, rest),
            scores[RADIUS : HALF - RADIUS] + rest,
            scores[HALF - RADIUS :] + jnp.where(first, rest, earlier),
        ],
        axis=0,
    )


def full_biases(near_ref, far_ref, qb):
    kinds = (add_near, add_later) if qb == 0 else (add_earlier, add_near)
    return [functools.partial(kind, near_ref, far_ref) for kind in kinds]


def half_biases(near_ref, far_ref, first):
    return [
        functools.partial(add_near, near_ref, far_ref),
        functools.partial(add_either, first, near_ref, far_ref),
    ]


def mods_kernel(time_ref, *refs):
    weights, biases = refs[:6], {0: refs[6], 2: refs[7], 3: refs[8], 5: refs[9]}
    mods_ref, early_ref, late_ref, embed_ref = refs[10:]
    rows = []
    blank = jnp.zeros((1, time_ref.shape[2]), F32)
    for i in range(time_ref.shape[0]):
        rows += [time_ref[i].astype(F32), blank]
    embed_ref[...] = jnp.concatenate(rows + [blank] * (16 - SEGS * time_ref.shape[0]), axis=0).astype(BF16)
    cols = early_ref.shape[1] // 4
    homes = {0: (late_ref, 0), 1: (late_ref, 1), 5: (early_ref, 0), 3: (early_ref, 1), 4: (early_ref, 2), 2: (early_ref, 3)}
    for i in range(6):
        value = mm(embed_ref[...], weights[i][...])
        slope = jnp.ones_like(value)
        if i in biases:
            value = jax.nn.sigmoid(value + biases[i][...].astype(F32).reshape(1, cols))
            slope = value * (1.0 - value)
        mods_ref[i] = value
        home, place = homes[i]
        home[:, pl.ds(place * cols, cols)] = slope


def modulations(embed, weights, biases):
    cols = weights[0].shape[1]
    args = (embed, *weights, *biases)
    shapes = [(6, 16, cols), (16, 4 * cols), (16, 2 * cols), (16, embed.shape[2])]
    return call(
        mods_kernel,
        (1,),
        [whole(*a.shape) for a in args],
        tuple(whole(*shape) for shape in shapes),
        tuple(jax.ShapeDtypeStruct(shape, dtype) for shape, dtype in zip(shapes, (F32, F32, F32, BF16))),
        flops=10**8,
        moved=2 * 10**6,
    )(*args)


def table_kernel(tp_ref, own_ref, came_ref, o_ref):
    first = tp_ref[0] == 0
    row = lax.broadcasted_iota(jnp.int32, (32, 16), 0)
    col = lax.broadcasted_iota(jnp.int32, (32, 16), 1)
    part = (row >= 2 * SEGS).astype(jnp.int32) + (row >= 4 * SEGS).astype(jnp.int32)
    chain = row - 2 * SEGS * part
    chain = chain + jnp.where((chain < SEGS) & jnp.logical_not(first), 2 * SEGS, 0)
    take = ((col == chain) & (row < 6 * SEGS)).astype(F32)
    rows = lax.broadcasted_iota(jnp.int32, (32, 1), 0)
    width = 2 * own_ref.shape[2]
    for i in range(6):
        own, came = own_ref[i], came_ref[i]
        low, high = jnp.where(first, own, came), jnp.where(first, came, own)
        value = jnp.dot(take, jnp.concatenate([low, high], axis=1), precision=HIGHEST, preferred_element_type=F32)
        top = value.astype(BF16).astype(F32)
        middle = (value - top).astype(BF16).astype(F32)
        parts = jnp.where(rows < 2 * SEGS, top, jnp.where(rows < 4 * SEGS, middle, value - top - middle))
        o_ref[:, pl.ds(i * width, width)] = parts.astype(BF16)


def chain_table(tp, own, came):
    shape = (32, 12 * own.shape[2])
    return call(
        table_kernel,
        (1,),
        [whole(*own.shape), whole(*came.shape)],
        whole(*shape),
        jax.ShapeDtypeStruct(shape, BF16),
        prefetch=1,
        flops=10**7,
        moved=10**6,
    )(tp, own, came)


def masks_kernel(tp_ref, length_ref, flag_ref, q_ref, k_ref, pick_ref, turn_ref, marks_ref):
    core = tp_ref[0]

    def segments(pack, shape, axis, start):
        spot = lax.broadcasted_iota(jnp.int32, shape, axis) + start
        segment = jnp.zeros(shape, jnp.int32)
        end = 0
        for i in range(SEGS - 1):
            end = end + length_ref[pack, i]
            segment = segment + (spot >= end).astype(jnp.int32)
        return segment

    runs = [(2 * core, 0, 0), (2 * core, HALF, 0), (1, HALF * core, SEGS), (1, HALF * (1 - core), SEGS)]
    for i, (pack, start, shift) in enumerate(runs):
        rows = pl.ds(i * HALF, HALF)
        segment = segments(pack, (HALF, LANES), 0, start)
        lanes = lax.broadcasted_iota(jnp.int32, (HALF, LANES), 1)
        k_ref[rows, :] = (segment == lanes).astype(F32).astype(BF16)
        if i == 3:
            break
        q_ref[rows, :] = jnp.where((segment != lanes) & (lanes < SEGS), MASKED, 0.0).astype(BF16)
        chain = (segment + shift)[:, :32]
        lanes = lanes[:, :32]
        spot = lanes - 2 * SEGS * (
            (lanes >= 2 * SEGS).astype(jnp.int32) + (lanes >= 4 * SEGS).astype(jnp.int32)
        )
        pick_ref[rows, :] = ((chain == spot) & (lanes < 6 * SEGS)).astype(F32).astype(BF16)
        marks_ref[rows, :] = jnp.full((HALF, 1), flag_ref[pack].astype(F32))
        across = segments(pack, (16, HALF), 1, start) + shift
        turn_ref[i] = (across == lax.broadcasted_iota(jnp.int32, (16, HALF), 0)).astype(F32).astype(BF16)


def masks(tp, lengths, flags):
    shapes = [(3 * HALF, LANES), (4 * HALF, LANES), (3 * HALF, 32), (3, 16, HALF)]
    return call(
        masks_kernel,
        (1,),
        [],
        tuple(whole(*shape) for shape in shapes) + (whole(3 * HALF, 1),),
        tuple(jax.ShapeDtypeStruct(shape, BF16) for shape in shapes)
        + (jax.ShapeDtypeStruct((3 * HALF, 1), F32),),
        prefetch=3,
        flops=10**6,
        moved=10**6,
    )(tp, lengths, flags)


def halves_kernel(tp_ref, *refs):
    for source, target in zip(refs[:4], refs[4:]):
        target[...] = source[...]


def token_halves(tp, first, second):
    cols = first.shape[1]

    def mine(j, tp_ref):
        return jnp.where(j < 2, 4 * tp_ref[0] + j, 2 + tp_ref[0]), 0

    def others(j, tp_ref):
        return jnp.where(j < 2, 4 * (1 - tp_ref[0]) + j, 3 - tp_ref[0]), 0

    spec = pl.BlockSpec((HALF, cols), lambda j, _: (j, 0))
    shape = jax.ShapeDtypeStruct((3 * HALF, cols), BF16)
    places = [pl.BlockSpec((HALF, cols), place) for place in (mine, others)]
    return call(
        halves_kernel, (3,), places + places, (spec,) * 4, (shape,) * 4, prefetch=1, flops=10, moved=24 * HALF * cols
    )(tp, first, first, second, second)


def put_together(first_core, own, came):
    return jnp.concatenate([jnp.where(first_core, own, came), jnp.where(first_core, came, own)], axis=1)


def qkv_first_kernel(tp_ref, xo_ref, xp_ref, oh_ref, tab_ref, own_ref, par_ref, o_ref, kv_ref, x_ref, normed):
    @pl.when(pl.program_id(0) == 0)
    def _():
        x_ref[...] = put_together(tp_ref[0] == 0, xo_ref[...], xp_ref[...])

    qkv_kernel(x_ref, oh_ref, tab_ref, own_ref, par_ref, o_ref, kv_ref, normed)


def qkv_kernel(x_ref, oh_ref, tab_ref, own_ref, par_ref, o_ref, kv_ref, normed):
    width = x_ref.shape[1]
    half = own_ref.shape[1]

    @pl.when(pl.program_id(0) == 0)
    def _():
        def body(i):
            rows = pl.ds(pl.multiple_of(i * HALF, HALF), HALF)
            hat, _ = norm_parts(x_ref[rows, :].astype(F32))
            pick = oh_ref[rows, :]
            scale = mm(pick, tab_ref[:, :width])
            shift = mm(pick, tab_ref[:, width : 2 * width])
            normed[rows, :] = (hat * scale + shift).astype(BF16)

        block_loop(x_ref.shape[0] // HALF, body)

    o_ref[:, :half] = mm(normed[...], own_ref[...]).astype(BF16)
    o_ref[:, half:] = mm(normed[...], par_ref[...]).astype(BF16)
    kv_ref[...] = o_ref[pl.ds(ROW, HALF), :]


def qkv_outs(tokens, half):
    specs = (
        pl.BlockSpec((tokens, 2 * half), lambda j, *_: (0, j)),
        pl.BlockSpec((HALF, 2 * half), lambda j, *_: (0, jnp.maximum(j - 1, 0))),
    )
    return specs, (jax.ShapeDtypeStruct((tokens, 6 * half), BF16), jax.ShapeDtypeStruct((HALF, 4 * half), BF16))


def qkv_first(tp, x_own, x_came, pick, table, w_own, w_par):
    tokens, cols = x_own.shape
    width = 2 * cols
    half = w_own.shape[1] // 3
    return call(
        qkv_first_kernel,
        (3,),
        [
            whole(tokens, cols),
            whole(tokens, cols),
            whole(*pick.shape),
            whole(*table.shape),
            pl.BlockSpec((width, half), lambda j, *_: (0, j)),
            pl.BlockSpec((width, half), lambda j, *_: (0, j)),
        ],
        (*qkv_outs(tokens, half)[0], whole(tokens, width)),
        (*qkv_outs(tokens, half)[1], jax.ShapeDtypeStruct((tokens, width), BF16)),
        [pltpu.VMEM((tokens, width), BF16)],
        prefetch=1,
        flops=2 * tokens * width * 6 * half,
        moved=tokens * 6 * half * 2 + width * half * 12 + tokens * width * 4,
    )(tp, x_own, x_came, pick, table, w_own, w_par)


def qkv_forward(x, pick, table, w_own, w_par):
    tokens, width = x.shape
    half = w_own.shape[1] // 3
    return call(
        qkv_kernel,
        (3,),
        [
            whole(tokens, width),
            whole(*pick.shape),
            whole(*table.shape),
            pl.BlockSpec((width, half), lambda j: (0, j)),
            pl.BlockSpec((width, half), lambda j: (0, j)),
        ],
        *qkv_outs(tokens, half),
        [pltpu.VMEM((tokens, width), BF16)],
        flops=2 * tokens * width * 6 * half,
        moved=tokens * 6 * half * 2 + width * half * 12 + tokens * width * 4,
    )(x, pick, table, w_own, w_par)


def lane_masks():
    lanes = lax.broadcasted_iota(jnp.int32, (1, LANES), 1)
    first = (lanes < LANES // 2).astype(F32)
    return first.astype(BF16), (1.0 - first).astype(BF16)


def attend_forward_block(q, segq, keys, values_t, biases):
    outs, logs = [], []
    half = LANES // 2
    masks = lane_masks()
    scaled = q * jnp.asarray(half**-0.5, BF16)
    for h in range(2):
        query = jnp.concatenate([scaled * masks[h], segq], axis=1)
        scores = [bias(h, mm_nt(key, query)) for key, bias in zip(keys, biases)]
        tops = [jnp.max(s, axis=0, keepdims=True) for s in scores]
        top = functools.reduce(jnp.maximum, tops)
        weights = [jnp.exp(s - top) for s in scores]
        total = sum(jnp.sum(w, axis=0, keepdims=True) for w in weights)
        mixed = sum(
            mm(vt[h * half : (h + 1) * half, :], w.astype(BF16)) for vt, w in zip(values_t, weights)
        )
        outs.append(mixed / total)
        logs.append(top + jnp.log(total))
    attended = jnp.concatenate(outs, axis=0).T.astype(BF16)
    return attended, jnp.concatenate(logs, axis=0)


def attend_full_kernel(q_ref, k_ref, v_ref, segq_ref, segk_ref, near_ref, far_ref, o_ref, log_ref):
    keys = [
        jnp.concatenate([k_ref[pl.ds(b * HALF, HALF), :], segk_ref[pl.ds(b * HALF, HALF), :]], axis=1)
        for b in range(2)
    ]
    values_t = [v_ref[pl.ds(b * HALF, HALF), :].T for b in range(2)]
    for qb in range(2):
        rows = pl.ds(qb * HALF, HALF)
        biases = full_biases(near_ref, far_ref, qb)
        attended, logs = attend_forward_block(q_ref[rows, :], segq_ref[rows, :], keys, values_t, biases)
        o_ref[rows, :] = attended
        log_ref[0, 0:2, rows] = logs


def attend_half_kernel(
    tp_ref, q_ref, k_ref, v_ref, kp_ref, vp_ref, segq_ref, segk_ref, near_ref, far_ref, oin, login, o_ref, log_ref
):
    keys = [
        jnp.concatenate([k_ref[...], segk_ref[pl.ds(0, HALF), :]], axis=1),
        jnp.concatenate([kp_ref[...], segk_ref[pl.ds(HALF, HALF), :]], axis=1),
    ]
    values_t = [v_ref[...].T, vp_ref[...].T]
    biases = half_biases(near_ref, far_ref, tp_ref[0] == 0)
    attended, logs = attend_forward_block(q_ref[...], segq_ref[...], keys, values_t, biases)
    o_ref[...] = attended
    log_ref[0, 0:2, :] = logs


def attend_forward(tp, qkv, kv_par, segq, segk, bias):
    tokens = qkv.shape[0]
    width = qkv.shape[1] // 3
    pairs = width // LANES
    out_shape = (
        jax.ShapeDtypeStruct((tokens, width), BF16),
        jax.ShapeDtypeStruct((pairs, 8, tokens), F32),
    )
    unit = 4 * HALF * HALF * 256 * 2
    attended, logs = call(
        attend_full_kernel,
        (pairs,),
        [
            pl.BlockSpec((ROW, LANES), lambda p: (0, p)),
            pl.BlockSpec((ROW, LANES), lambda p: (0, pairs + p)),
            pl.BlockSpec((ROW, LANES), lambda p: (0, 2 * pairs + p)),
            pl.BlockSpec((ROW, LANES), lambda p: (0, 0)),
            pl.BlockSpec((ROW, LANES), lambda p: (0, 0)),
        ]
        + bias_specs(),
        (
            pl.BlockSpec((ROW, LANES), lambda p: (0, p)),
            pl.BlockSpec((1, 8, ROW), lambda p: (p, 0, 0)),
        ),
        out_shape,
        flops=unit * 4 * pairs,
        moved=bias[0].size * 4,
    )(qkv, qkv, qkv, segq, segk, *bias)
    flip = pairs // 2
    return call(
        attend_half_kernel,
        (pairs,),
        [
            pl.BlockSpec((HALF, LANES), lambda p, *_: (2, p)),
            pl.BlockSpec((HALF, LANES), lambda p, *_: (2, pairs + p)),
            pl.BlockSpec((HALF, LANES), lambda p, *_: (2, 2 * pairs + p)),
            pl.BlockSpec((HALF, LANES), lambda p, *_: (0, lax.rem(p + flip, pairs))),
            pl.BlockSpec((HALF, LANES), lambda p, *_: (0, pairs + lax.rem(p + flip, pairs))),
            pl.BlockSpec((HALF, LANES), lambda p, *_: (2, 0)),
            pl.BlockSpec((ROW, LANES), lambda p, *_: (1, 0)),
        ]
        + bias_specs()
        + [pl.BlockSpec(memory_space=pl.ANY), pl.BlockSpec(memory_space=pl.ANY)],
        (
            pl.BlockSpec((HALF, LANES), lambda p, *_: (2, p)),
            pl.BlockSpec((1, 8, HALF), lambda p, *_: (p, 0, 2)),
        ),
        out_shape,
        prefetch=1,
        aliases={10: 0, 11: 1},
        flops=unit * 2 * pairs,
        moved=bias[0].size * 4,
    )(tp, qkv, qkv, qkv, kv_par, kv_par, segq, segk, *bias, attended, logs)


def ffn_kernel(
    att_ref, woo_ref, wop_ref, x_ref, oh_ref, tab_ref, guo_ref, gup_ref, wdo_ref, wdp_ref,
    head_ref, emb_ref, flag_ref, shifted_ref, lifted_ref, middle, normed, acc,
):
    step = pl.program_id(0)
    tokens, width = x_ref.shape
    half = woo_ref.shape[0]
    blocks = tokens // HALF

    @pl.when(step == 0)
    def _():
        def body(i):
            rows = pl.ds(pl.multiple_of(i * HALF, HALF), HALF)
            branch = mm(att_ref[rows, :half], woo_ref[...]) + mm(att_ref[rows, half:], wop_ref[...])
            pick = oh_ref[rows, :]
            mid = x_ref[rows, :].astype(F32) + mm(pick, tab_ref[:, 2 * width : 3 * width]) * branch
            middle[rows, :] = mid
            hat, _ = norm_parts(mid)
            scale = mm(pick, tab_ref[:, 3 * width : 4 * width])
            shift = mm(pick, tab_ref[:, 4 * width : 5 * width])
            normed[rows, :] = (hat * scale + shift).astype(BF16)
            acc[rows, :] = jnp.zeros((HALF, width), F32)

        block_loop(blocks, body)

    def body(i):
        rows = pl.ds(pl.multiple_of(i * HALF, HALF), HALF)
        total = acc[rows, :]
        for gu, wd in ((guo_ref, wdo_ref), (gup_ref, wdp_ref)):
            gate = mm(normed[rows, :], gu[0])
            up = mm(normed[rows, :], gu[1])
            hidden = (gate * jax.nn.sigmoid(gate) * up).astype(BF16)
            total = total + mm(hidden, wd[...])
        acc[rows, :] = total

    block_loop(blocks, body)

    @pl.when(step == pl.num_programs(0) - 1)
    def _():
        def body(i):
            rows = pl.ds(pl.multiple_of(i * HALF, HALF), HALF)
            gate = mm(oh_ref[rows, :], tab_ref[:, 5 * width : 6 * width])
            first = middle[rows, :] + gate * acc[rows, :]
            high = first.astype(BF16)
            rest = (first - high.astype(F32)).astype(BF16)
            coords = mm_nt(high, head_ref[...]) + mm_nt(rest, head_ref[...])
            lifted = coords * flag_ref[rows, :]
            lifted_ref[rows, :] = lifted
            high = lifted.astype(BF16)
            rest = (lifted - high.astype(F32)).astype(BF16)
            moved = mm(high, emb_ref[...]) + mm(rest, emb_ref[...])
            shifted_ref[rows, :] = x_ref[rows, :].astype(F32) + moved

        block_loop(blocks, body)


def ffn_specs(att, woo, x, pick, table):
    tokens, width = x.shape
    chunk = FFC
    return [
        whole(*att.shape),
        whole(*woo.shape),
        whole(*woo.shape),
        whole(tokens, width),
        whole(*pick.shape),
        whole(*table.shape),
        pl.BlockSpec((2, width, chunk), lambda j, *_: (0, 0, j)),
        pl.BlockSpec((2, width, chunk), lambda j, *_: (0, 0, j)),
        pl.BlockSpec((chunk, width), lambda j, *_: (j, 0)),
        pl.BlockSpec((chunk, width), lambda j, *_: (j, 0)),
    ]


def ffn_forward(att, woo, wop, x, pick, table, guo, gup, wdo, wdp, head, emb, flags):
    tokens, width = x.shape
    hidden = wdo.shape[0]
    return call(
        ffn_kernel,
        (hidden // FFC,),
        ffn_specs(att, woo, x, pick, table)
        + [whole(*head.shape), whole(*emb.shape), whole(*flags.shape)],
        (whole(tokens, width), whole(tokens, LANES)),
        (
            jax.ShapeDtypeStruct((tokens, width), F32),
            jax.ShapeDtypeStruct((tokens, LANES), F32),
        ),
        [
            pltpu.VMEM((tokens, width), F32),
            pltpu.VMEM((tokens, width), BF16),
            pltpu.VMEM((tokens, width), F32),
        ],
        flops=2 * tokens * width * (6 * hidden + width),
        moved=12 * hidden * width + 6 * tokens * width,
    )(att, woo, wop, x, pick, table, guo, gup, wdo, wdp, head, emb, flags)


def turn_kernel(
    tp_ref, att_ref, woo_ref, wop_ref, x_ref, oh_ref, tab_ref, guo_ref, gup_ref, wdo_ref, wdp_ref,
    gown_ref, gcame_ref, oht_ref,
    outo_ref, outp_ref, gmid_ref, gatt_ref, go_ref, gp_ref, goo_ref, gop_ref, sumo_ref, sump_ref,
    sums_ref, middle, hats, branches, normed, normed_t, gmixed, gmixed_t, mixed, gnormed, hid, dgate, dup,
):
    step = pl.program_id(0)
    tokens, width = x_ref.shape
    half = woo_ref.shape[0]
    blocks = tokens // HALF

    @pl.when(step == 0)
    def _():
        def body(i):
            rows = pl.ds(pl.multiple_of(i * HALF, HALF), HALF)
            branch = mm(att_ref[rows, :half], woo_ref[...]) + mm(att_ref[rows, half:], wop_ref[...])
            branches[rows, :] = branch
            pick = oh_ref[rows, :]
            mid = x_ref[rows, :] + mm(pick, tab_ref[:, 2 * width : 3 * width]) * branch
            middle[rows, :] = mid
            hat, _ = norm_parts(mid)
            scale = mm(pick, tab_ref[:, 3 * width : 4 * width])
            shift = mm(pick, tab_ref[:, 4 * width : 5 * width])
            normed[rows, :] = (hat * scale + shift).astype(BF16)
            gate = mm(pick, tab_ref[:, 5 * width : 6 * width])
            g = put_together(tp_ref[0] == 0, gown_ref[rows, :], gcame_ref[rows, :])
            gmixed[rows, :] = (g.astype(F32) * gate).astype(BF16)
            mixed[rows, :] = jnp.zeros((HALF, width), F32)
            gnormed[rows, :] = jnp.zeros((HALF, width), F32)

        block_loop(blocks, body)
        normed_t[...] = normed[...].T
        gmixed_t[...] = gmixed[...].T

    for gu, wd, out in ((gup_ref, wdp_ref, gp_ref), (guo_ref, wdo_ref, go_ref)):

        def body(i):
            rows = pl.ds(pl.multiple_of(i * BLOCK, BLOCK), BLOCK)
            gate = mm(normed[rows, :], gu[0])
            up = mm(normed[rows, :], gu[1])
            ghid = mm_nt(gmixed[rows, :], wd[...])
            s = jax.nn.sigmoid(gate)
            silu = gate * s
            hidden = (silu * up).astype(BF16)
            hid[rows, :] = hidden
            mixed[rows, :] += mm(hidden, wd[...])
            dg = (ghid * up * (s + silu * (1.0 - s))).astype(BF16)
            du = (ghid * silu).astype(BF16)
            dgate[rows, :] = dg
            dup[rows, :] = du
            gnormed[rows, :] += mm_nt(dg, gu[0]) + mm_nt(du, gu[1])

        block_loop(tokens // BLOCK, body)
        out[0, 0] = mm(normed_t[...], dgate[...]).astype(BF16)
        out[1, 0] = mm(normed_t[...], dup[...]).astype(BF16)
        out[2, 0] = mm(gmixed_t[...], hid[...]).astype(BF16)

    @pl.when(step == pl.num_programs(0) - 1)
    def _():
        first_core = tp_ref[0] == 0
        sums_ref[...] = jnp.zeros(sums_ref.shape, F32)

        def body(i):
            rows = pl.ds(pl.multiple_of(i * HALF, HALF), HALF)
            pick = oh_ref[rows, :]
            turn = oht_ref[i]
            g = put_together(first_core, gown_ref[rows, :], gcame_ref[rows, :]).astype(F32)
            total = mixed[rows, :]
            gate = mm(pick, tab_ref[:, 5 * width : 6 * width])
            mid = middle[rows, :]
            result = (mid + gate * total).astype(BF16)
            low, high = result[:, : width // 2], result[:, width // 2 :]
            outo_ref[rows, :] = jnp.where(first_core, low, high)
            outp_ref[rows, :] = jnp.where(first_core, high, low)
            sums_ref[0] += mm(turn, (g * total).astype(BF16))
            hat, inv_std = norm_parts(mid)
            gn = gnormed[rows, :]
            sums_ref[1] += mm(turn, (gn * hat).astype(BF16))
            sums_ref[2] += mm(turn, gn.astype(BF16))
            scale = mm(pick, tab_ref[:, 3 * width : 4 * width])
            gmid = g + norm_back(gn * scale, hat, inv_std)
            gmid_ref[rows, :] = gmid
            sums_ref[3] += mm(turn, (gmid * branches[rows, :]).astype(BF16))
            gbranch = (gmid * mm(pick, tab_ref[:, 2 * width : 3 * width])).astype(BF16)
            gmixed[rows, :] = gbranch
            gatt_ref[rows, :half] = mm_nt(gbranch, woo_ref[...]).astype(BF16)
            gatt_ref[rows, half:] = mm_nt(gbranch, wop_ref[...]).astype(BF16)

        block_loop(blocks, body)
        gmixed_t[...] = gmixed[...].T
        goo_ref[...] = mm(gmixed_t[...], att_ref[:, :half]).astype(BF16)
        gop_ref[...] = mm(gmixed_t[...], att_ref[:, half:]).astype(BF16)
        low, high = sums_ref[:, :, : width // 2], sums_ref[:, :, width // 2 :]
        sumo_ref[...] = jnp.where(first_core, low, high)
        sump_ref[...] = jnp.where(first_core, high, low)


def ffn_turn(tp, att, woo, wop, x, pick, table, guo, gup, wdo, wdp, g_own, g_came, pick_t):
    tokens, width = x.shape
    half = woo.shape[0]
    hidden = wdo.shape[0]
    grads = jax.ShapeDtypeStruct((3, hidden // FFC, width, FFC), BF16)
    grads_spec = pl.BlockSpec((3, 1, width, FFC), lambda j, *_: (0, j, 0, 0))
    return call(
        turn_kernel,
        (hidden // FFC,),
        ffn_specs(att, woo, x, pick, table) + [whole(tokens, width // 2), whole(tokens, width // 2), whole(*pick_t.shape)],
        (
            whole(tokens, width // 2),
            whole(tokens, width // 2),
            whole(tokens, width),
            whole(tokens, width),
            grads_spec,
            grads_spec,
            whole(width, half),
            whole(width, half),
            whole(4, 16, width // 2),
            whole(4, 16, width // 2),
        ),
        (
            jax.ShapeDtypeStruct((tokens, width // 2), BF16),
            jax.ShapeDtypeStruct((tokens, width // 2), BF16),
            jax.ShapeDtypeStruct((tokens, width), F32),
            jax.ShapeDtypeStruct((tokens, width), BF16),
            grads,
            grads,
            jax.ShapeDtypeStruct((width, half), BF16),
            jax.ShapeDtypeStruct((width, half), BF16),
            jax.ShapeDtypeStruct((4, 16, width // 2), F32),
            jax.ShapeDtypeStruct((4, 16, width // 2), F32),
        ),
        [
            pltpu.VMEM((4, 16, width), F32),
            pltpu.VMEM((tokens, width), F32),
            pltpu.VMEM((8, LANES), F32),
            pltpu.VMEM((tokens, width), F32),
            pltpu.VMEM((tokens, width), BF16),
            pltpu.VMEM((width, tokens), BF16),
            pltpu.VMEM((tokens, width), BF16),
            pltpu.VMEM((width, tokens), BF16),
            pltpu.VMEM((tokens, width), F32),
            pltpu.VMEM((tokens, width), F32),
            pltpu.VMEM((tokens, FFC), BF16),
            pltpu.VMEM((tokens, FFC), BF16),
            pltpu.VMEM((tokens, FFC), BF16),
        ],
        prefetch=1,
        flops=2 * tokens * width * (18 * hidden + 3 * width),
        moved=24 * hidden * width + 12 * tokens * width,
    )(tp, att, woo, wop, x, pick, table, guo, gup, wdo, wdp, g_own, g_came, pick_t)


def attend_back_block(q, segq, gout, logs, keys, keys_t, values, biases, bias_sums, gkeys, gvalues):
    half = LANES // 2
    masks = lane_masks()
    scale = half**-0.5
    scaled = q * jnp.asarray(scale, BF16)
    gqs = []
    for h in range(2):
        query_low = scaled * masks[h]
        query = jnp.concatenate([query_low, segq], axis=1)
        gheads = gout * masks[h]
        chances = [jnp.exp(bias(h, mm_nt(key, query)) - logs[h : h + 1, :]) for key, bias in zip(keys, biases)]
        gchances = [mm_nt(value, gheads) for value in values]
        centre = sum(jnp.sum(p * gp, axis=0, keepdims=True) for p, gp in zip(chances, gchances))
        gq = 0.0
        for b, (p, gp) in enumerate(zip(chances, gchances)):
            gs = p * (gp - centre)
            bias_sums[b](h, gs)
            low = gs.astype(BF16)
            gvalues[b] = gvalues[b] + mm(p.astype(BF16), gheads)
            gkeys[b] = gkeys[b] + mm(low, query_low)
            gq = gq + mm(keys_t[b][h * half : (h + 1) * half, :], low)
        gqs.append(gq * scale)
    return jnp.concatenate(gqs, axis=0).T.astype(BF16)


def diagonal_sums(tile):
    size, wide = tile.shape
    blank = jnp.zeros((SUB, wide), F32)
    groups = [jnp.zeros((SUB, 2 * wide), F32)] * 2
    for i, a in enumerate(range(0, size, SUB)):
        piece = jnp.concatenate([tile[a : a + SUB], blank], axis=1)
        groups[i % 2] = groups[i % 2] + pltpu.roll(piece, size - SUB - a, axis=1)
    total = groups[0] + groups[1]
    rows = lax.broadcasted_iota(jnp.int32, (SUB, 2 * wide), 0)
    moved = sum(pltpu.roll(jnp.where(rows == b, total, 0.0), SUB - 1 - b, axis=1) for b in range(SUB))
    return jnp.sum(moved, axis=0, keepdims=True)


def far_sums(tile, later):
    whole_sum = jnp.sum(jnp.sum(tile, axis=0, keepdims=True), axis=1, keepdims=True)
    edge = tile[:RADIUS, LANES:] if later else tile[HALF - RADIUS :, :LANES]
    sums = diagonal_sums(edge)
    rest = whole_sum - jnp.sum(sums, axis=1, keepdims=True)
    row = jnp.concatenate([sums, jnp.zeros((1, 2 * HALF - sums.shape[1]), F32)], axis=1)
    row = jnp.broadcast_to(row, (8, 2 * HALF))
    if later:
        row = pltpu.roll(row, 2 * HALF - LANES - RADIUS, axis=1)
    lanes = lax.broadcasted_iota(jnp.int32, (1, 2 * HALF), 1)
    return row[:1] + jnp.where(lanes == (0 if later else 2 * HALF - 2), rest, 0.0)


def attend_full_back_kernel(
    q_ref, k_ref, v_ref, g_ref, log_ref, segq_ref, segk_ref, near_ref, far_ref, o_ref, diag_ref, sums
):
    keys, keys_t, values = [], [], []
    for b in range(2):
        rows = pl.ds(b * HALF, HALF)
        key = k_ref[rows, :]
        keys.append(jnp.concatenate([key, segk_ref[rows, :]], axis=1))
        keys_t.append(key.T)
        values.append(v_ref[rows, :])
    gkeys, gvalues = [0.0, 0.0], [0.0, 0.0]
    sums[...] = jnp.zeros(sums.shape, F32)
    for qb in range(2):
        rows = pl.ds(qb * HALF, HALF)
        biases = full_biases(near_ref, far_ref, qb)

        def add(h, gs):
            sums[h] += gs

        def put(h, gs, later):
            row = 3 * h + (0 if later else 2)
            diag_ref[0, row : row + 1, :] = far_sums(gs, later)

        adders = [add, functools.partial(put, later=True)] if qb == 0 else [functools.partial(put, later=False), add]
        o_ref[0, rows, :] = attend_back_block(
            q_ref[rows, :], segq_ref[rows, :], g_ref[rows, :], log_ref[0, 0:2, rows],
            keys, keys_t, values, biases, adders, gkeys, gvalues,
        )
    for b in range(2):
        rows = pl.ds(b * HALF, HALF)
        o_ref[1, rows, :] = gkeys[b].astype(BF16)
        o_ref[2, rows, :] = gvalues[b].astype(BF16)
    for h in range(2):
        diag_ref[0, 3 * h + 1 : 3 * h + 2, :] = diagonal_sums(sums[h])


def attend_half_back_kernel(
    tp_ref, q_ref, k_ref, v_ref, kp_ref, vp_ref, g_ref, log_ref, segq_ref, segk_ref, near_ref, far_ref,
    o_ref, par_ref, diag_ref,
):
    keys, keys_t, values = [], [], []
    for b, (k, v) in enumerate(((k_ref, v_ref), (kp_ref, vp_ref))):
        key = k[...]
        keys.append(jnp.concatenate([key, segk_ref[pl.ds(b * HALF, HALF), :]], axis=1))
        keys_t.append(key.T)
        values.append(v[...])
    first = tp_ref[0] == 0
    biases = half_biases(near_ref, far_ref, first)
    gkeys, gvalues = [0.0, 0.0], [0.0, 0.0]

    def put(h, gs, b):
        sums = jnp.where(first, far_sums(gs, True), far_sums(gs, False)) if b else diagonal_sums(gs)
        diag_ref[0, 2 * h + b : 2 * h + b + 1, :] = sums

    adders = [functools.partial(put, b=b) for b in range(2)]
    o_ref[0] = attend_back_block(
        q_ref[...], segq_ref[...], g_ref[...], log_ref[0, 0:2, :],
        keys, keys_t, values, biases, adders, gkeys, gvalues,
    )
    o_ref[1] = gkeys[0].astype(BF16)
    o_ref[2] = gvalues[0].astype(BF16)
    par_ref[0] = gkeys[1].astype(BF16)
    par_ref[1] = gvalues[1].astype(BF16)


def attend_half_back(tp, qkv, kv_par, g, logs, segq, segk, bias):
    width = qkv.shape[1] // 3
    pairs = width // LANES
    flip = pairs // 2
    return call(
        attend_half_back_kernel,
        (pairs,),
        [
            pl.BlockSpec((HALF, LANES), lambda p, *_: (2, p)),
            pl.BlockSpec((HALF, LANES), lambda p, *_: (2, pairs + p)),
            pl.BlockSpec((HALF, LANES), lambda p, *_: (2, 2 * pairs + p)),
            pl.BlockSpec((HALF, LANES), lambda p, *_: (0, lax.rem(p + flip, pairs))),
            pl.BlockSpec((HALF, LANES), lambda p, *_: (0, pairs + lax.rem(p + flip, pairs))),
            pl.BlockSpec((HALF, LANES), lambda p, *_: (2, p)),
            pl.BlockSpec((1, 8, HALF), lambda p, *_: (p, 0, 2)),
            pl.BlockSpec((HALF, LANES), lambda p, *_: (2, 0)),
            pl.BlockSpec((ROW, LANES), lambda p, *_: (1, 0)),
        ]
        + bias_specs(),
        (
            pl.BlockSpec((3, HALF, LANES), lambda p, *_: (0, 0, p)),
            pl.BlockSpec((2, HALF, LANES), lambda p, *_: (0, 0, p)),
            pl.BlockSpec((1, 8, ROW), lambda p, *_: (p, 0, 0)),
        ),
        (
            jax.ShapeDtypeStruct((3, HALF, width), BF16),
            jax.ShapeDtypeStruct((2, HALF, width), BF16),
            jax.ShapeDtypeStruct((pairs, 8, ROW), F32),
        ),
        prefetch=1,
        flops=10 * HALF * HALF * 256 * 2 * pairs,
        moved=bias[0].size * 4,
    )(tp, qkv, qkv, qkv, kv_par, kv_par, g, logs, segq, segk, *bias)


def attend_full_back(qkv, g, logs, segq, segk, bias):
    width = qkv.shape[1] // 3
    pairs = width // LANES
    return call(
        attend_full_back_kernel,
        (pairs,),
        [
            pl.BlockSpec((ROW, LANES), lambda p: (0, p)),
            pl.BlockSpec((ROW, LANES), lambda p: (0, pairs + p)),
            pl.BlockSpec((ROW, LANES), lambda p: (0, 2 * pairs + p)),
            pl.BlockSpec((ROW, LANES), lambda p: (0, p)),
            pl.BlockSpec((1, 8, ROW), lambda p: (p, 0, 0)),
            pl.BlockSpec((ROW, LANES), lambda p: (0, 0)),
            pl.BlockSpec((ROW, LANES), lambda p: (0, 0)),
        ]
        + bias_specs(),
        (
            pl.BlockSpec((3, ROW, LANES), lambda p: (0, 0, p)),
            pl.BlockSpec((1, 8, ROW), lambda p: (p, 0, 0)),
        ),
        (
            jax.ShapeDtypeStruct((3, ROW, width), BF16),
            jax.ShapeDtypeStruct((pairs, 8, ROW), F32),
        ),
        [pltpu.VMEM((2, HALF, HALF), F32)],
        flops=20 * HALF * HALF * 256 * 2 * pairs,
        moved=bias[0].size * 4,
    )(qkv, qkv, qkv, g, logs, segq, segk, *bias)


def joined_rows(full_ref, half_ref, recv_ref, step, rows_in):
    half = recv_ref.shape[2] // 2
    rows_in[pl.ds(0, ROW), :] = full_ref[0]
    keep = (step > 0).astype(F32).astype(BF16)
    recv = jnp.concatenate([recv_ref[0, :, half:], recv_ref[0, :, :half]], axis=1)
    rows_in[pl.ds(ROW, HALF), :] = half_ref[0] + recv * keep


def qkv_weights_kernel(
    x_ref, oh_ref, tab_ref, full_ref, half_ref, recv_ref, outo_ref, outp_ref, go_ref, gp_ref, normed, normed_t, rows_in
):
    step = pl.program_id(0)
    tokens, width = x_ref.shape
    half = width // 2

    @pl.when(step == 0)
    def _():
        def body(i):
            rows = pl.ds(pl.multiple_of(i * HALF, HALF), HALF)
            hat, _ = norm_parts(x_ref[rows, :])
            pick = oh_ref[rows, :]
            scale = mm(pick, tab_ref[:, :width])
            shift = mm(pick, tab_ref[:, width : 2 * width])
            normed[rows, :] = (hat * scale + shift).astype(BF16)

        block_loop(tokens // HALF, body)
        normed_t[...] = normed[...].T

    joined_rows(full_ref, half_ref, recv_ref, step, rows_in)
    go_ref[0, :, :half] = mm(normed_t[...], rows_in[:, :half]).astype(BF16)
    gp_ref[0, :, :half] = mm(normed_t[...], rows_in[:, half:]).astype(BF16)
    go_ref[0, :, half:] = outo_ref[...]
    gp_ref[0, :, half:] = outp_ref[...]


def row_specs(width):
    return [
        pl.BlockSpec((1, ROW, width), lambda j, *_: (j, 0, 0)),
        pl.BlockSpec((1, HALF, width), lambda j, *_: (j, 0, 0)),
        pl.BlockSpec((1, HALF, width), lambda j, *_: (jnp.maximum(j - 1, 0), 0, 0)),
    ]


def qkv_weights(x, pick, table, full, half_rows, recv, out_own, out_par):
    tokens, width = x.shape
    half = width // 2
    third = half // 3
    spec = pl.BlockSpec((1, width, half + third), lambda j: (j, 0, 0))
    shape = jax.ShapeDtypeStruct((3, width, half + third), BF16)
    out_spec = pl.BlockSpec((width, third), lambda j: (0, j))
    return call(
        qkv_weights_kernel,
        (3,),
        [whole(tokens, width), whole(*pick.shape), whole(*table.shape)] + row_specs(width) + [out_spec, out_spec],
        (spec, spec),
        (shape, shape),
        [
            pltpu.VMEM((tokens, width), BF16),
            pltpu.VMEM((width, tokens), BF16),
            pltpu.VMEM((tokens, width), BF16),
        ],
        flops=2 * tokens * width * 6 * half,
        moved=16 * half * width + 12 * tokens * width,
    )(x, pick, table, full, half_rows, recv, out_own, out_par)


def qkv_back_kernel(
    tp_ref, x_ref, oh_ref, tab_ref, full_ref, half_ref, recv_ref, wo_ref, wp_ref, gmid_ref, lifted_ref, oht_ref,
    gino_ref, ginp_ref, sumo_ref, sump_ref, hats, stds, rows_in, acc, sums,
):
    step = pl.program_id(0)
    tokens, width = x_ref.shape
    half = wo_ref.shape[1]
    blocks = tokens // HALF

    @pl.when(step == 0)
    def _():
        def body(i):
            rows = pl.ds(pl.multiple_of(i * HALF, HALF), HALF)
            hat, inv_std = norm_parts(x_ref[rows, :])
            hats[rows, :] = hat
            stds[rows, :] = inv_std
            acc[rows, :] = jnp.zeros((HALF, width), F32)

        block_loop(blocks, body)

    joined_rows(full_ref, half_ref, recv_ref, step, rows_in)

    def body(i):
        rows = pl.ds(pl.multiple_of(i * HALF, HALF), HALF)
        grad = rows_in[rows, :]
        acc[rows, :] += mm_nt(grad[:, :half], wo_ref[...]) + mm_nt(grad[:, half:], wp_ref[...])

    block_loop(blocks, body)

    @pl.when(step == pl.num_programs(0) - 1)
    def _():
        first_core = tp_ref[0] == 0
        sums[...] = jnp.zeros(sums.shape, F32)

        def body(i):
            rows = pl.ds(pl.multiple_of(i * HALF, HALF), HALF)
            turn = oht_ref[i]
            gn = acc[rows, :]
            hat = hats[rows, :]
            sums[0] += mm(turn, (gn * hat).astype(BF16))
            sums[1] += mm(turn, gn.astype(BF16))
            scale = mm(oh_ref[rows, :], tab_ref[:, :width])
            grad = gmid_ref[rows, :] + norm_back(gn * scale, hat, stds[rows, :])
            low, high = grad[:, : width // 2], grad[:, width // 2 :]
            gino_ref[rows, :] = jnp.where(first_core, low, high)
            ginp_ref[rows, :] = jnp.where(first_core, high, low)
            lifted_t = lifted_ref[rows, :].astype(BF16).T
            sums[2] += mm(lifted_t[:16, :], grad.astype(BF16))

        block_loop(blocks, body)
        low, high = sums[:, :, : width // 2], sums[:, :, width // 2 :]
        sumo_ref[...] = jnp.where(first_core, low, high)
        sump_ref[...] = jnp.where(first_core, high, low)


def qkv_back(tp, x, pick, table, full, half_rows, recv, wo, wp, gmid, lifted, pick_t):
    tokens, width = x.shape
    half = wo.shape[1] // 3
    return call(
        qkv_back_kernel,
        (3,),
        [whole(tokens, width), whole(*pick.shape), whole(*table.shape)]
        + row_specs(width)
        + [
            pl.BlockSpec((width, half), lambda j, *_: (0, j)),
            pl.BlockSpec((width, half), lambda j, *_: (0, j)),
            whole(tokens, width),
            whole(tokens, LANES),
            whole(*pick_t.shape),
        ],
        (
            whole(tokens, width // 2),
            whole(tokens, width // 2),
            whole(3, 16, width // 2),
            whole(3, 16, width // 2),
        ),
        (
            jax.ShapeDtypeStruct((tokens, width // 2), F32),
            jax.ShapeDtypeStruct((tokens, width // 2), F32),
            jax.ShapeDtypeStruct((3, 16, width // 2), F32),
            jax.ShapeDtypeStruct((3, 16, width // 2), F32),
        ),
        [
            pltpu.VMEM((tokens, width), F32),
            pltpu.VMEM((tokens, 1), F32),
            pltpu.VMEM((tokens, width), BF16),
            pltpu.VMEM((tokens, width), F32),
            pltpu.VMEM((3, 16, width), F32),
        ],
        prefetch=1,
        flops=2 * tokens * width * 6 * half,
        moved=12 * half * width + 16 * tokens * width,
    )(tp, x, pick, table, full, half_rows, recv, wo, wp, gmid, lifted, pick_t)


def chain_joins(first_core):
    row = lax.broadcasted_iota(jnp.int32, (16, 16), 0)
    col = lax.broadcasted_iota(jnp.int32, (16, 16), 1)
    lower = ((row == col) & (row < 2 * SEGS)).astype(F32)
    upper = (
        ((row == col) & (row >= SEGS) & (row < 2 * SEGS)) | ((row == col + 2 * SEGS) & (row < 3 * SEGS))
    ).astype(F32)
    return jnp.where(first_core, lower, upper), jnp.where(first_core, upper, lower)


def join_chains(tp_ref, own_ref, came_ref, slope_ref, count, o_ref):
    own_join, came_join = chain_joins(tp_ref[0] == 0)
    cols = own_ref.shape[2]
    for i in range(count):
        both = jnp.dot(own_join, own_ref[i], precision=HIGHEST, preferred_element_type=F32)
        both = both + jnp.dot(came_join, came_ref[i], precision=HIGHEST, preferred_element_type=F32)
        lanes = pl.ds(i * cols, cols)
        o_ref[0:16, lanes] = (both * slope_ref[:, lanes]).astype(BF16)


def early_kernel(tp_ref, own_ref, came_ref, slope_ref, embed_ref, o_ref):
    join_chains(tp_ref, own_ref, came_ref, slope_ref, 4, o_ref)
    o_ref[:, pl.ds(4 * own_ref.shape[2], embed_ref.shape[1])] = embed_ref[...]


def late_kernel(tp_ref, own_ref, came_ref, slope_ref, bins_ref, o_ref):
    cols = own_ref.shape[2]
    join_chains(tp_ref, own_ref, came_ref, slope_ref, 2, o_ref)
    o_ref[:, pl.ds(2 * cols, LANES)] = bins_ref[...].astype(BF16)
    coords = own_ref[2] + came_ref[2]
    parts = [coords[i : i + 1, j : j + LANES] for j in range(0, cols, LANES) for i in range(3)]
    parts.append(jnp.zeros((16 - len(parts), LANES), F32))
    o_ref[:, pl.ds(2 * cols + LANES, LANES)] = jnp.concatenate(parts, axis=0).astype(BF16)


def pack_rows(kernel, tp, own, came, slopes, extra, shape):
    return call(
        kernel,
        (1,),
        [whole(*own.shape), whole(*came.shape), whole(*slopes.shape), whole(*extra.shape)],
        whole(*shape),
        jax.ShapeDtypeStruct(shape, BF16),
        prefetch=1,
        flops=10**6,
        moved=10**5,
    )(tp, own, came, slopes, extra)


def closing_kernel(early_ref, early_came_ref, late_ref, late_came_ref, hat_ref, inv_ref, gain_ref, both_ref, *refs):
    ffn, attn, outs = refs[:2], refs[2:4], refs[4:]
    gu_ref, down_ref, qkv_ref, out_ref = outs[:4]
    w0_ref, b0_ref, w1_ref, w2_ref, b2_ref, w3_ref, b3_ref, w4_ref, w5_ref, b5_ref = outs[4:14]
    table_ref, pgain_ref, proj_ref, coord_ref = outs[14:]

    def total(pair, block):
        return pair[0][0, block].astype(F32) + pair[1][0, block].astype(F32)

    lanes = ffn[0].shape[3]
    chunks = down_ref.shape[1] // lanes
    for block in range(chunks):
        span = pl.ds(block * lanes, lanes)
        gu_ref[:, 0, span] = total(ffn, block)
        gu_ref[:, 1, span] = total(ffn, chunks + block)
        down_ref[:, span] = total(ffn, 2 * chunks + block)
    third = out_ref.shape[1] // 3
    for i in range(3):
        value = total(attn, i)
        qkv_ref[i] = value[:, : 3 * third]
        out_ref[:, i * third : (i + 1) * third] = value[:, 3 * third :]

    cols = coord_ref.shape[1]
    pieces = [(early_ref, late_ref), (early_came_ref, late_came_ref)]
    embed_t = [early[:, 4 * cols :].T for early, _ in pieces]
    weights = [w0_ref, w1_ref, w5_ref, w3_ref, w4_ref, w2_ref]
    biases = [b0_ref, None, b5_ref, b3_ref, None, b2_ref]
    for i, (weight, bias) in enumerate(zip(weights, biases)):
        source, lanes = (1, pl.ds(i * cols, cols)) if i < 2 else (0, pl.ds((i - 2) * cols, cols))
        parts = [piece[source][:, lanes] for piece in pieces]
        weight[...] = sum(mm(embed, part) for embed, part in zip(embed_t, parts))
        if bias is not None:
            bias[...] = sum(jnp.sum(part.astype(F32), axis=0) for part in parts)
    extra = sum(late[:, 2 * cols :].reshape(-1, 16, 2 * LANES).astype(F32).sum(axis=0) for _, late in pieces)
    for i in range(cols // LANES):
        coord_ref[:, pl.ds(i * LANES, LANES)] = extra[3 * i : 3 * i + 3, LANES:]
    bins = extra[:, :LANES]
    hat = hat_ref[...]
    gain = gain_ref[...]
    proj = jnp.dot(bins, hat * gain, precision=HIGHEST, preferred_element_type=F32)
    proj_ref[...] = proj[: proj_ref.shape[0]]
    normed_grad = jnp.dot(bins.T, both_ref[...], precision=HIGHEST, preferred_element_type=F32)
    pgain_ref[...] = jnp.sum(normed_grad * hat, axis=0)
    table_ref[...] = norm_back(normed_grad * gain, hat, inv_ref[...])[: table_ref.shape[0]]


def closing(early, late, hat, inv_std, gain, both, ffn, attn, bins, heads):
    cols = (late[0].shape[1] - 2 * LANES) // 2
    embed = early[0].shape[1] - 4 * cols
    features = hat.shape[1]
    height, lanes = ffn[0].shape[2:]
    weight, bias = (embed, cols), (cols,)
    hidden = lanes * (ffn[0].shape[1] // 3)
    shapes = [(height, 2, hidden), (height, hidden), (3, height, cols), (height, cols)]
    shapes += [weight, bias, weight, weight, bias, weight, bias, weight, weight, bias]
    shapes += [(bins, features), (features,), (heads, features), (3, cols)]
    args = (*early, *late, hat, inv_std, gain, both, *ffn, *attn)
    return call(
        closing_kernel,
        (1,),
        [whole(*a.shape) for a in args],
        tuple(whole(*shape) for shape in shapes),
        tuple(jax.ShapeDtypeStruct(shape, F32) for shape in shapes),
        flops=10**8,
        moved=10**7,
    )(*args)


def halve_kernel(place_ref, *refs, plan, count):
    inputs, outs = refs[:count], refs[count:]
    for stream, (bit, sections) in enumerate(plan):
        sent_ref, kept_ref = outs[2 * stream], outs[2 * stream + 1]
        mine = (place_ref[0] >> bit) & 1
        done = 0
        for first, second, base, chunks, left in sections:
            spot = left.index(bit)
            shift = len(left) - 1
            half = 1 << shift

            def body(n, first=first, second=second, base=base, spot=spot, shift=shift, done=done, mine=mine):
                k = n & ((1 << shift) - 1)
                at = base + ((n >> shift) << (shift + 1)) + ((k >> spot) << (spot + 1)) + (k & ((1 << spot) - 1))
                for which, ref in ((1 - mine, sent_ref), (mine, kept_ref)):
                    block = at + (which << spot)
                    ref[0, done + n] = inputs[first][0, block] + inputs[second][0, block]

            block_loop(chunks * half, body)
            done += chunks * half


def half_kernel(place_ref, *refs, plan, count):
    inputs, outs = refs[:count], refs[count:]
    for sections, ref in zip(plan, outs):
        done = 0
        for first in sections:
            _, chunks, high, _, low, _, _ = inputs[first].shape
            shift = high.bit_length() - 1

            def body(n, first=first, shift=shift, low=low, done=done, ref=ref):
                at = (0, n >> shift, n & ((1 << shift) - 1), 0)
                ref[0, pl.ds(done + n * low, low)] = inputs[first][at] + inputs[first + 1][at]

            block_loop(chunks * high, body)
            done += chunks * high * low


def half_of(place, streams, bits, keep):
    arrays, specs, plan, shapes = [], [], [], []
    steps = streams[0][0][5]
    if any(len(sections) > 1 or sections[0][5] != steps for sections in streams):
        steps = 1
    moved = 0
    for sections, bit in zip(streams, bits):
        entries, blocks = [], 0
        for own, i, came, k, _, chunks, left in sections:
            low = 1 << left.index(bit)
            high = (1 << (len(left) - 1)) // low
            entries.append(len(arrays))
            for array, index in ((own, i), (came, k)):
                arrays.append(array.reshape((-1, chunks, high, 2, low) + array.shape[2:]))

                def at(j, place_ref, index=index, bit=bit):
                    mine = (place_ref[0] >> bit) & 1
                    return index, j, 0, mine if keep else 1 - mine, 0, 0, 0

                specs.append(pl.BlockSpec((1, chunks // steps, high, 1, low) + array.shape[2:], at))
            blocks += chunks * high * low
        plan.append(entries)
        shape = (1, blocks) + sections[0][0].shape[2:]
        shapes.append(shape)
        moved += 6 * blocks * shape[2] * shape[3]
    return call(
        functools.partial(half_kernel, plan=plan, count=len(arrays)),
        (steps,),
        specs,
        tuple(pl.BlockSpec((1, n // steps, h, c), lambda j, *_: (0, j, 0, 0)) for _, n, h, c in shapes),
        tuple(jax.ShapeDtypeStruct(shape, BF16) for shape in shapes),
        prefetch=1,
        flops=10**6,
        moved=moved,
    )(place, *arrays)


def halve(place, streams, bits):
    arrays, specs, plan, shapes = [], [], [], []
    steps = streams[0][0][5]
    if any(len(sections) > 1 or sections[0][5] != steps for sections in streams):
        steps = 1

    def operand(array, index):
        for i, (seen, at) in enumerate(arrays):
            if seen is array and at == index:
                return i
        arrays.append((array, index))
        block = (1, array.shape[1] // steps) + array.shape[2:]
        specs.append(pl.BlockSpec(block, lambda j, *_: (index, j, 0, 0)))
        return len(arrays) - 1

    moved = 0
    for sections, bit in zip(streams, bits):
        entries, blocks = [], 0
        for own, i, came, k, base, chunks, left in sections:
            entries.append((operand(own, i), operand(came, k), base, chunks // steps, left))
            blocks += chunks << (len(left) - 1)
        plan.append((bit, entries))
        shape = (1, blocks) + sections[0][0].shape[2:]
        shapes += [shape, shape]
        moved += 12 * blocks * shape[2] * shape[3]
    outs = call(
        functools.partial(halve_kernel, plan=plan, count=len(arrays)),
        (steps,),
        specs,
        tuple(pl.BlockSpec((1, n // steps, h, c), lambda j, *_: (0, j, 0, 0)) for _, n, h, c in shapes),
        tuple(jax.ShapeDtypeStruct(shape, BF16) for shape in shapes),
        prefetch=1,
        flops=10**6,
        moved=moved,
    )(place, *[array for array, _ in arrays])
    return list(outs[0::2]), list(outs[1::2])


def swap(values):
    return lax.ppermute(values, "tp", [(0, 1), (1, 0)])


def after(values, *others):
    return lax.optimization_barrier((values, *others))[0]


class Cube:
    def __init__(self, rows):
        self.bits = rows.bit_length() - 1
        assert rows == 1 << self.bits
        self.place = lax.axis_index("rows").reshape(1).astype(jnp.int32)
        self.perms = [[(i, i ^ (1 << b)) for i in range(rows)] for b in range(self.bits)]

    def turns(self):
        return [[(i + r) % 3 for i in range(3)] for r in range(3)]

    def gather(self, values, step):
        bit = (list(range(self.bits - 1, 1, -1)) + list(range(min(2, self.bits))))[step]
        came = lax.ppermute(values, "rows", self.perms[bit])
        if step == self.bits - 1:
            return values, came
        return lax.optimization_barrier(jnp.concatenate([values, came], axis=0))


def next_sections(sections, kept, came, bit):
    made, base = [], 0
    for _, _, _, _, _, chunks, left in sections:
        left = [b for b in left if b != bit]
        made.append((kept, 0, came, 0, base, chunks, left))
        base += chunks << len(left)
    return made


def normalize(values):
    centre = jnp.mean(values, axis=-1, keepdims=True)
    shifted = values - centre
    spread = jnp.mean(shifted * shifted, axis=-1, keepdims=True)
    inv_std = lax.rsqrt(spread + EPSILON)
    return shifted * inv_std, inv_std


def three_parts(values):
    high = lax.reduce_precision(values, 8, 7)
    middle = lax.reduce_precision(values - high, 8, 7)
    low = values - high - middle
    return jnp.concatenate([high, middle, low], axis=0).astype(BF16)


def bias_base(heads):
    bins = heads.shape[1]
    low = lambda n: jnp.broadcast_to(heads[:, :1], (heads.shape[0], n))
    top = lambda n: jnp.broadcast_to(heads[:, bins - 1 :], (heads.shape[0], n))
    fill = HALF - RADIUS
    behind = jnp.concatenate([low(fill), heads[:, :RADIUS], low(HALF)], axis=1)
    same = jnp.concatenate([heads[:, RADIUS:], top(fill - 1), low(fill), heads[:, :RADIUS]], axis=1)
    ahead = jnp.concatenate([top(HALF), heads[:, RADIUS:], top(fill - 1)], axis=1)
    return jnp.stack([behind, same, ahead], axis=1)


def bins_of_diagonals():
    places = jnp.arange(ROW, dtype=jnp.int32)[None, :] - (HALF - 1)
    offsets = places + HALF * jnp.arange(-1, 2, dtype=jnp.int32)[:, None]
    bins = jnp.clip(offsets, -RADIUS, RADIUS) + RADIUS
    every = jnp.arange(2 * RADIUS + 1, dtype=jnp.int32)
    return (bins.reshape(-1)[:, None] == every[None, :]).astype(F32)


def per_device(
    layer_input,
    cotangent,
    chain_lengths,
    self_condition_flag,
    time_embedding,
    query_key_value,
    output_projection,
    attention_scale_weight,
    attention_scale_bias,
    attention_shift_weight,
    attention_gate_weight,
    attention_gate_bias,
    transition_scale_weight,
    transition_scale_bias,
    transition_shift_weight,
    transition_gate_weight,
    transition_gate_bias,
    gate_up_projection,
    down_projection,
    pair_table,
    pair_gain,
    pair_projection,
    coordinate_head,
    coordinate_embedding,
    rows,
):
    core = lax.axis_index("tp")
    first_core = core == 0
    tp = core.reshape(1).astype(jnp.int32)
    cols = layer_input.shape[1]
    width = query_key_value.shape[0]
    heads_here = pair_projection.shape[1]
    bins = pair_table.shape[0]
    cube = Cube(rows)

    def side_by_side(own, came, axis):
        return jnp.where(
            first_core, jnp.concatenate([own, came], axis), jnp.concatenate([came, own], axis)
        )

    def scatter_tokens(own, sent):
        came = swap(sent)
        lower = jnp.concatenate([own[:ROW], own[ROW:], came[ROW:], came[:ROW]], axis=0)
        upper = jnp.concatenate([came[:ROW], came[ROW:], own[ROW:], own[:ROW]], axis=0)
        return jnp.where(first_core, lower, upper)

    x_own, x_sent, cot_own, cot_sent = token_halves(tp, layer_input, cotangent)
    x_came = swap(x_sent)
    qkv_own = query_key_value.reshape(width, -1)
    qkv_par = swap(qkv_own)

    mods, early_slopes, late_slopes, embed = modulations(
        time_embedding,
        [
            attention_scale_weight,
            attention_shift_weight,
            attention_gate_weight,
            transition_scale_weight,
            transition_shift_weight,
            transition_gate_weight,
        ],
        [attention_scale_bias, attention_gate_bias, transition_scale_bias, transition_gate_bias],
    )
    table = chain_table(tp, mods, swap(mods))
    mask_q, mask_k, pick, pick_t, flags = masks(tp, chain_lengths, self_condition_flag)

    pair_hat, pair_inv = normalize(pair_table.astype(F32))
    gain = pair_gain.astype(F32)
    pair_normed = pair_hat * gain
    pair_both = jnp.concatenate([pair_projection, swap(pair_projection)], axis=1).astype(F32)
    bias_heads = jnp.transpose(jnp.dot(pair_normed, pair_both, precision=HIGHEST))
    bias_source = jnp.transpose(pair_both)
    bias = bias_tiles(bias_base(bias_heads))

    out_own = output_projection
    out_par = swap(output_projection)
    gu_own = jnp.transpose(gate_up_projection, (1, 0, 2))
    gu_par = swap(gu_own)
    down_own = down_projection
    down_par = swap(down_projection)
    coord = jnp.concatenate([coordinate_head, coordinate_embedding], axis=0)
    coord = side_by_side(coord, swap(coord), 1)
    fill = jnp.zeros((LANES - 3, width), BF16)
    head = jnp.concatenate([coord[:3], fill], axis=0)
    emb = jnp.concatenate([coord[3:], fill], axis=0)
    cot_came = swap(cot_sent)

    def attention(qkv, kv):
        kv_par = swap(kv)
        attended, logs = attend_forward(tp, qkv, kv_par, mask_q, mask_k, bias)
        return qkv, kv_par, attended, logs

    qkv, kv, x = qkv_first(tp, x_own, x_came, pick, table, qkv_own, qkv_par)
    _, _, attended, _ = attention(qkv, kv)
    shifted, lifted = ffn_forward(
        attended, out_own, out_par, x, pick, table, gu_own, gu_par, down_own, down_par, head, emb, flags
    )
    qkv, kv_par, attended, logs = attention(*qkv_forward(shifted, pick, table, qkv_own, qkv_par))
    (
        result_own,
        result_sent,
        grad_middle,
        grad_attended,
        grads_own,
        grads_sent,
        grad_out_own,
        grad_out_sent,
        early_own,
        early_sent,
    ) = ffn_turn(
        tp, attended, out_own, out_par, shifted, pick, table, gu_own, gu_par, down_own, down_par, cot_own, cot_came, pick_t
    )

    early_came = swap(early_sent)

    came_ffn = swap(grads_sent)
    half_grads, far_grads, diag_half = attend_half_back(
        tp, qkv, kv_par, grad_attended, logs, mask_q, mask_k, bias
    )
    came_grads = swap(far_grads)

    turns = cube.turns()
    every = list(range(cube.bits))
    height = width // rows
    slots = lambda values: values.reshape(3, -1, height, values.shape[-1])
    chunks = grads_own.shape[1]
    own_slots, came_slots = slots(grads_own), slots(came_ffn)
    ffn = [[(own_slots, i, came_slots, i, 0, chunks, every)] for i in range(3)]

    def one_round(streams, bits, *others, whole_arrays=False):
        if whole_arrays:
            sent = half_of(cube.place, streams, bits, False)
            *held, place = lax.optimization_barrier((*sent, *others, cube.place))
            kept = half_of(place, streams, bits, True)
        else:
            sent, kept = halve(cube.place, streams, bits)
            held = lax.optimization_barrier((*sent, *others))
        came = [lax.ppermute(v, "rows", cube.perms[bit]) for v, bit in zip(held, bits)]
        made = [next_sections(*parts) for parts in zip(streams, kept, came, bits)]
        return made, came, held[len(sent) :]

    ffn, came, (mask_full, early_came, _) = one_round(
        ffn, turns[0], mask_q, early_came, diag_half, whole_arrays=True
    )
    early = pack_rows(
        early_kernel, tp, early_own, early_came, early_slopes, embed, (16, 4 * cols + embed.shape[1])
    )
    full_grads, diag_full = attend_full_back(qkv, grad_attended, logs, mask_full, mask_k, bias)
    early = cube.gather(early, 0)
    ffn, came, (pick_weights, early, _) = one_round(ffn, turns[1], pick, early, diag_full, whole_arrays=True)
    gqkv_own, gqkv_sent = qkv_weights(
        shifted, pick_weights, table, full_grads, half_grads, came_grads, grad_out_own, grad_out_sent
    )
    early = cube.gather(early, 1)
    gqkv_sent, early, *_ = lax.optimization_barrier((gqkv_sent, early, *came, *[f[0][0] for f in ffn]))
    own_slots, came_slots = slots(gqkv_own), slots(swap(gqkv_sent))
    streams = [ffn[i] + [(own_slots, i, came_slots, i, 0, 1, every)] for i in range(3)]
    streams, came, (pick_back, early) = one_round(streams, turns[2], pick_weights, early, whole_arrays=True)
    gin_own, gin_sent, late_own, late_sent = qkv_back(
        tp, shifted, pick_back, table, full_grads, half_grads, came_grads, qkv_own, qkv_par, grad_middle, lifted, pick_t
    )
    early = cube.gather(early, 2)
    late_sent, early, *_ = lax.optimization_barrier((late_sent, early, *came, *[f[0][0] for f in streams]))

    diag_half = diag_half[:, :4].reshape(-1, 2, ROW)
    quiet = jnp.zeros_like(diag_half[:, 0])
    diag_far = diag_half[:, 1]
    diag = diag_full[:, :6].reshape(-1, 3, ROW) + jnp.stack(
        [
            jnp.where(first_core, diag_far, quiet),
            diag_half[:, 0],
            jnp.where(first_core, quiet, diag_far),
        ],
        axis=1,
    )
    grad_bins = jnp.dot(diag.reshape(-1, 3 * ROW), bins_of_diagonals(), precision=HIGHEST)
    came_bins = swap(grad_bins)
    grad_bins = grad_bins + jnp.concatenate([came_bins[heads_here:], came_bins[:heads_here]], axis=0)
    bins_fill = jnp.pad(grad_bins, ((0, 16 - 2 * heads_here), (0, LANES - bins)))

    late_came = swap(late_sent)
    late = pack_rows(late_kernel, tp, late_own, late_came, late_slopes, bins_fill, (16, 2 * cols + 2 * LANES))
    ffn = [[stream[0] for stream in streams]]
    attn = [stream[1:] for stream in streams]
    rest = list(range(3, cube.bits))
    waited = []
    for step in range(max(len(rest), 2)):
        now, bits = [], []
        if step < len(rest):
            now, bits = ffn, rest[step : step + 1]
        count = len(now)
        if step < 2:
            attn, came, _ = one_round(attn, turns[step], *waited)
        late = cube.gather(late, step)
        if count:
            ffn, waited, (late,) = one_round(now, bits, late)
    done = max(len(rest), 2)
    attn = [[section for stream in attn for section in stream]]
    for bit in rest:
        attn, came, _ = one_round(attn, [bit])
        if done < cube.bits:
            late = after(late, *waited)
            late = cube.gather(late, done)
            done += 1
    for step in range(done, cube.bits):
        late = cube.gather(late, step)
    for step in range(3, cube.bits):
        early = cube.gather(early, step)
    ffn_last = (ffn[0][0][0], ffn[0][0][2])
    attn_last = (attn[0][0][0], attn[0][0][2])

    layer_output = scatter_tokens(result_own, result_sent)
    input_gradient = scatter_tokens(gin_own, gin_sent)

    bins_pad = ((0, LANES - bins), (0, 0))
    grad_gu, grad_down, grad_qkv, grad_out, *conditioning = closing(
        early,
        late,
        jnp.pad(pair_hat, bins_pad),
        jnp.pad(pair_inv, bins_pad),
        gain[None, :],
        jnp.pad(bias_source, ((0, 16 - 2 * heads_here), (0, 0))),
        ffn_last,
        attn_last,
        bins,
        heads_here,
    )
    *conditioning, grad_table, grad_gain, grad_pair, coord_grad = conditioning
    return (
        layer_output,
        input_gradient,
        jnp.transpose(grad_qkv, (1, 0, 2)),
        grad_out.T,
        *conditioning,
        grad_gu,
        grad_down.T,
        grad_table,
        grad_gain,
        grad_pair.T,
        coord_grad,
    )


def solution(mesh):
    in_specs = (
        P("rows", "tp"),
        P("rows", "tp"),
        P("rows", None),
        P("rows"),
        P("rows", None, None),
        P(None, None, "tp"),
        P("tp", None),
        P(None, "tp"),
        P("tp"),
        P(None, "tp"),
        P(None, "tp"),
        P("tp"),
        P(None, "tp"),
        P("tp"),
        P(None, "tp"),
        P(None, "tp"),
        P("tp"),
        P(None, None, "tp"),
        P("tp", None),
        P(),
        P(),
        P(None, "tp"),
        P(None, "tp"),
        P(None, "tp"),
    )
    out_specs = (
        P("rows", "tp"),
        P("rows", "tp"),
        P("rows", None, "tp"),
        P("tp", "rows"),
        P(None, "tp"),
        P("tp"),
        P(None, "tp"),
        P(None, "tp"),
        P("tp"),
        P(None, "tp"),
        P("tp"),
        P(None, "tp"),
        P(None, "tp"),
        P("tp"),
        P("rows", None, "tp"),
        P("tp", "rows"),
        P(),
        P(),
        P(None, "tp"),
        P(None, "tp"),
    )
    return jax.shard_map(
        functools.partial(per_device, rows=mesh.shape["rows"]),
        mesh=mesh,
        in_specs=in_specs,
        out_specs=out_specs,
        check_vma=False,
    )
```

```python
import functools
import jax
import jax.numpy as jnp
from jax import lax
from jax.experimental import pallas as pl
from jax.experimental.pallas import tpu as pltpu
from jax.sharding import PartitionSpec as P

RADIUS = 32
ROW = 512
HALF = ROW // 2
SEGS = 5
EPSILON = 1e-05
MASKED = -1e30
HIGHEST = lax.Precision.HIGHEST
F32 = jnp.float32
BF16 = jnp.bfloat16
LANES = 128
FFC = 512
BLOCK = 384
SUB = 8
NT = (((1,), (1,)), ((), ()))
VMEM_LIMIT = 60 * 1024 * 1024


def mm(left, right):
    return jnp.dot(left, right, preferred_element_type=F32)


def mm_nt(left, right):
    return lax.dot_general(left, right, NT, preferred_element_type=F32)


def norm_parts(values):
    centre = jnp.mean(values, axis=1, keepdims=True)
    shifted = values - centre
    spread = jnp.mean(shifted * shifted, axis=1, keepdims=True)
    inv_std = lax.rsqrt(spread + EPSILON)
    return shifted * inv_std, inv_std


def norm_back(grad, hat, inv_std):
    first = jnp.mean(grad, axis=1, keepdims=True)
    second = jnp.mean(grad * hat, axis=1, keepdims=True)
    return inv_std * (grad - first - hat * second)


def block_loop(count, body):
    lax.fori_loop(0, count, lambda i, c: (body(i), c)[1], 0)


def call(kernel, grid, in_specs, out_specs, out_shape, scratch=(), prefetch=0, aliases=None, flops=0, moved=0):
    return pl.pallas_call(
        kernel,
        grid_spec=pltpu.PrefetchScalarGridSpec(
            num_scalar_prefetch=prefetch,
            grid=grid,
            in_specs=in_specs,
            out_specs=out_specs,
            scratch_shapes=list(scratch),
        ),
        out_shape=out_shape,
        input_output_aliases=aliases or {},
        compiler_params=pltpu.CompilerParams(
            dimension_semantics=("arbitrary",) * len(grid), vmem_limit_bytes=VMEM_LIMIT
        ),
        cost_estimate=pl.CostEstimate(flops=flops, transcendentals=0, bytes_accessed=moved),
    )


def whole(*shape):
    zeros = (0,) * len(shape)
    return pl.BlockSpec(shape, lambda *_: zeros)


def bias_kernel(base_ref, near_ref, far_ref):
    for h, d, height, start, out in [
        run
        for h in range(base_ref.shape[0])
        for run in (
            (h, 1, HALF, 0, near_ref.at[h]),
            (h, 0, RADIUS, 0, far_ref.at[h, 0]),
            (h, 2, RADIUS, HALF - RADIUS, far_ref.at[h, 1]),
        )
    ]:
        rows = jnp.broadcast_to(base_ref[h, d : d + 1, :], (SUB, 2 * HALF))
        rows = pltpu.roll(rows, 0, axis=1, stride=1, stride_axis=0)
        for a in range(0, height, SUB):
            out[a : a + SUB, :] = pltpu.roll(rows, start + a, axis=1)[:, :HALF]


def bias_tiles(base):
    heads = base.shape[0]
    near, far = (heads, HALF, HALF), (heads, 2, RADIUS, HALF)
    return call(
        bias_kernel,
        (3,),
        [pl.BlockSpec((heads // 3, 3, 2 * HALF), lambda h: (h, 0, 0))],
        (
            pl.BlockSpec((heads // 3,) + near[1:], lambda h: (h, 0, 0)),
            pl.BlockSpec((heads // 3,) + far[1:], lambda h: (h, 0, 0, 0)),
        ),
        (jax.ShapeDtypeStruct(near, F32), jax.ShapeDtypeStruct(far, F32)),
        moved=heads * HALF * HALF * 4,
        flops=10**7,
    )(base)


def bias_specs():
    return [
        pl.BlockSpec((2, HALF, HALF), lambda p, *_: (p, 0, 0)),
        pl.BlockSpec((2, 2, RADIUS, HALF), lambda p, *_: (p, 0, 0, 0)),
    ]


def add_near(near_ref, far_ref, h, scores):
    return scores + near_ref[h]


def add_later(near_ref, far_ref, h, scores):
    edge = far_ref[h, 0]
    return jnp.concatenate([scores[:RADIUS] + edge, scores[RADIUS:] + edge[RADIUS - 1 :, :1]], axis=0)


def add_earlier(near_ref, far_ref, h, scores):
    edge = far_ref[h, 1]
    return jnp.concatenate(
        [scores[: HALF - RADIUS] + edge[:1, HALF - 1 :], scores[HALF - RADIUS :] + edge], axis=0
    )


def add_either(first, near_ref, far_ref, h, scores):
    later, earlier = far_ref[h, 0], far_ref[h, 1]
    rest = jnp.where(first, later[RADIUS - 1 :, :1], earlier[:1, HALF - 1 :])
    return jnp.concatenate(
        [
            scores[:RADIUS] + jnp.where(first, later, rest),
            scores[RADIUS : HALF - RADIUS] + rest,
            scores[HALF - RADIUS :] + jnp.where(first, rest, earlier),
        ],
        axis=0,
    )


def full_biases(near_ref, far_ref, qb):
    kinds = (add_near, add_later) if qb == 0 else (add_earlier, add_near)
    return [functools.partial(kind, near_ref, far_ref) for kind in kinds]


def half_biases(near_ref, far_ref, first):
    return [
        functools.partial(add_near, near_ref, far_ref),
        functools.partial(add_either, first, near_ref, far_ref),
    ]


def mods_kernel(time_ref, *refs):
    weights, biases = refs[:6], {0: refs[6], 2: refs[7], 3: refs[8], 5: refs[9]}
    mods_ref, early_ref, late_ref, embed_ref = refs[10:]
    rows = []
    blank = jnp.zeros((1, time_ref.shape[2]), F32)
    for i in range(time_ref.shape[0]):
        rows += [time_ref[i].astype(F32), blank]
    embed_ref[...] = jnp.concatenate(rows + [blank] * (16 - SEGS * time_ref.shape[0]), axis=0).astype(BF16)
    cols = early_ref.shape[1] // 4
    homes = {0: (late_ref, 0), 1: (late_ref, 1), 5: (early_ref, 0), 3: (early_ref, 1), 4: (early_ref, 2), 2: (early_ref, 3)}
    for i in range(6):
        value = mm(embed_ref[...], weights[i][...])
        slope = jnp.ones_like(value)
        if i in biases:
            value = jax.nn.sigmoid(value + biases[i][...].astype(F32).reshape(1, cols))
            slope = value * (1.0 - value)
        mods_ref[i] = value
        home, place = homes[i]
        home[:, pl.ds(place * cols, cols)] = slope


def modulations(embed, weights, biases):
    cols = weights[0].shape[1]
    args = (embed, *weights, *biases)
    shapes = [(6, 16, cols), (16, 4 * cols), (16, 2 * cols), (16, embed.shape[2])]
    return call(
        mods_kernel,
        (1,),
        [whole(*a.shape) for a in args],
        tuple(whole(*shape) for shape in shapes),
        tuple(jax.ShapeDtypeStruct(shape, dtype) for shape, dtype in zip(shapes, (F32, F32, F32, BF16))),
        flops=10**8,
        moved=2 * 10**6,
    )(*args)


def table_kernel(tp_ref, own_ref, came_ref, o_ref):
    first = tp_ref[0] == 0
    row = lax.broadcasted_iota(jnp.int32, (32, 16), 0)
    col = lax.broadcasted_iota(jnp.int32, (32, 16), 1)
    part = (row >= 2 * SEGS).astype(jnp.int32) + (row >= 4 * SEGS).astype(jnp.int32)
    chain = row - 2 * SEGS * part
    chain = chain + jnp.where((chain < SEGS) & jnp.logical_not(first), 2 * SEGS, 0)
    take = ((col == chain) & (row < 6 * SEGS)).astype(F32)
    rows = lax.broadcasted_iota(jnp.int32, (32, 1), 0)
    width = 2 * own_ref.shape[2]
    for i in range(6):
        own, came = own_ref[i], came_ref[i]
        low, high = jnp.where(first, own, came), jnp.where(first, came, own)
        value = jnp.dot(take, jnp.concatenate([low, high], axis=1), precision=HIGHEST, preferred_element_type=F32)
        top = value.astype(BF16).astype(F32)
        middle = (value - top).astype(BF16).astype(F32)
        parts = jnp.where(rows < 2 * SEGS, top, jnp.where(rows < 4 * SEGS, middle, value - top - middle))
        o_ref[:, pl.ds(i * width, width)] = parts.astype(BF16)


def chain_table(tp, own, came):
    shape = (32, 12 * own.shape[2])
    return call(
        table_kernel,
        (1,),
        [whole(*own.shape), whole(*came.shape)],
        whole(*shape),
        jax.ShapeDtypeStruct(shape, BF16),
        prefetch=1,
        flops=10**7,
        moved=10**6,
    )(tp, own, came)


def masks_kernel(tp_ref, length_ref, flag_ref, q_ref, k_ref, pick_ref, turn_ref, marks_ref):
    core = tp_ref[0]

    def segments(pack, shape, axis, start):
        spot = lax.broadcasted_iota(jnp.int32, shape, axis) + start
        segment = jnp.zeros(shape, jnp.int32)
        end = 0
        for i in range(SEGS - 1):
            end = end + length_ref[pack, i]
            segment = segment + (spot >= end).astype(jnp.int32)
        return segment

    runs = [(2 * core, 0, 0), (2 * core, HALF, 0), (1, HALF * core, SEGS), (1, HALF * (1 - core), SEGS)]
    for i, (pack, start, shift) in enumerate(runs):
        rows = pl.ds(i * HALF, HALF)
        segment = segments(pack, (HALF, LANES), 0, start)
        lanes = lax.broadcasted_iota(jnp.int32, (HALF, LANES), 1)
        k_ref[rows, :] = (segment == lanes).astype(F32).astype(BF16)
        if i == 3:
            break
        q_ref[rows, :] = jnp.where((segment != lanes) & (lanes < SEGS), MASKED, 0.0).astype(BF16)
        chain = (segment + shift)[:, :32]
        lanes = lanes[:, :32]
        spot = lanes - 2 * SEGS * (
            (lanes >= 2 * SEGS).astype(jnp.int32) + (lanes >= 4 * SEGS).astype(jnp.int32)
        )
        pick_ref[rows, :] = ((chain == spot) & (lanes < 6 * SEGS)).astype(F32).astype(BF16)
        marks_ref[rows, :] = jnp.full((HALF, 1), flag_ref[pack].astype(F32))
        across = segments(pack, (16, HALF), 1, start) + shift
        turn_ref[i] = (across == lax.broadcasted_iota(jnp.int32, (16, HALF), 0)).astype(F32).astype(BF16)


def masks(tp, lengths, flags):
    shapes = [(3 * HALF, LANES), (4 * HALF, LANES), (3 * HALF, 32), (3, 16, HALF)]
    return call(
        masks_kernel,
        (1,),
        [],
        tuple(whole(*shape) for shape in shapes) + (whole(3 * HALF, 1),),
        tuple(jax.ShapeDtypeStruct(shape, BF16) for shape in shapes)
        + (jax.ShapeDtypeStruct((3 * HALF, 1), F32),),
        prefetch=3,
        flops=10**6,
        moved=10**6,
    )(tp, lengths, flags)


def halves_kernel(tp_ref, *refs):
    for source, target in zip(refs[:4], refs[4:]):
        target[...] = source[...]


def token_halves(tp, first, second):
    cols = first.shape[1]

    def mine(j, tp_ref):
        return jnp.where(j < 2, 4 * tp_ref[0] + j, 2 + tp_ref[0]), 0

    def others(j, tp_ref):
        return jnp.where(j < 2, 4 * (1 - tp_ref[0]) + j, 3 - tp_ref[0]), 0

    spec = pl.BlockSpec((HALF, cols), lambda j, _: (j, 0))
    shape = jax.ShapeDtypeStruct((3 * HALF, cols), BF16)
    places = [pl.BlockSpec((HALF, cols), place) for place in (mine, others)]
    return call(
        halves_kernel, (3,), places + places, (spec,) * 4, (shape,) * 4, prefetch=1, flops=10, moved=24 * HALF * cols
    )(tp, first, first, second, second)


def put_together(first_core, own, came):
    return jnp.concatenate([jnp.where(first_core, own, came), jnp.where(first_core, came, own)], axis=1)


def qkv_first_kernel(tp_ref, xo_ref, xp_ref, oh_ref, tab_ref, own_ref, par_ref, o_ref, kv_ref, x_ref, normed):
    @pl.when(pl.program_id(0) == 0)
    def _():
        x_ref[...] = put_together(tp_ref[0] == 0, xo_ref[...], xp_ref[...])

    qkv_kernel(x_ref, oh_ref, tab_ref, own_ref, par_ref, o_ref, kv_ref, normed)


def qkv_kernel(x_ref, oh_ref, tab_ref, own_ref, par_ref, o_ref, kv_ref, normed):
    width = x_ref.shape[1]
    half = own_ref.shape[1]

    @pl.when(pl.program_id(0) == 0)
    def _():
        def body(i):
            rows = pl.ds(pl.multiple_of(i * HALF, HALF), HALF)
            hat, _ = norm_parts(x_ref[rows, :].astype(F32))
            pick = oh_ref[rows, :]
            scale = mm(pick, tab_ref[:, :width])
            shift = mm(pick, tab_ref[:, width : 2 * width])
            normed[rows, :] = (hat * scale + shift).astype(BF16)

        block_loop(x_ref.shape[0] // HALF, body)

    o_ref[:, :half] = mm(normed[...], own_ref[...]).astype(BF16)
    o_ref[:, half:] = mm(normed[...], par_ref[...]).astype(BF16)
    kv_ref[...] = o_ref[pl.ds(ROW, HALF), :]


def qkv_outs(tokens, half):
    specs = (
        pl.BlockSpec((tokens, 2 * half), lambda j, *_: (0, j)),
        pl.BlockSpec((HALF, 2 * half), lambda j, *_: (0, jnp.maximum(j - 1, 0))),
    )
    return specs, (jax.ShapeDtypeStruct((tokens, 6 * half), BF16), jax.ShapeDtypeStruct((HALF, 4 * half), BF16))


def qkv_first(tp, x_own, x_came, pick, table, w_own, w_par):
    tokens, cols = x_own.shape
    width = 2 * cols
    half = w_own.shape[1] // 3
    return call(
        qkv_first_kernel,
        (3,),
        [
            whole(tokens, cols),
            whole(tokens, cols),
            whole(*pick.shape),
            whole(*table.shape),
            pl.BlockSpec((width, half), lambda j, *_: (0, j)),
            pl.BlockSpec((width, half), lambda j, *_: (0, j)),
        ],
        (*qkv_outs(tokens, half)[0], whole(tokens, width)),
        (*qkv_outs(tokens, half)[1], jax.ShapeDtypeStruct((tokens, width), BF16)),
        [pltpu.VMEM((tokens, width), BF16)],
        prefetch=1,
        flops=2 * tokens * width * 6 * half,
        moved=tokens * 6 * half * 2 + width * half * 12 + tokens * width * 4,
    )(tp, x_own, x_came, pick, table, w_own, w_par)


def qkv_forward(x, pick, table, w_own, w_par):
    tokens, width = x.shape
    half = w_own.shape[1] // 3
    return call(
        qkv_kernel,
        (3,),
        [
            whole(tokens, width),
            whole(*pick.shape),
            whole(*table.shape),
            pl.BlockSpec((width, half), lambda j: (0, j)),
            pl.BlockSpec((width, half), lambda j: (0, j)),
        ],
        *qkv_outs(tokens, half),
        [pltpu.VMEM((tokens, width), BF16)],
        flops=2 * tokens * width * 6 * half,
        moved=tokens * 6 * half * 2 + width * half * 12 + tokens * width * 4,
    )(x, pick, table, w_own, w_par)


def lane_masks():
    lanes = lax.broadcasted_iota(jnp.int32, (1, LANES), 1)
    first = (lanes < LANES // 2).astype(F32)
    return first.astype(BF16), (1.0 - first).astype(BF16)


def attend_forward_block(q, segq, keys, values_t, biases):
    outs, logs = [], []
    half = LANES // 2
    masks = lane_masks()
    scaled = q * jnp.asarray(half**-0.5, BF16)
    for h in range(2):
        query = jnp.concatenate([scaled * masks[h], segq], axis=1)
        scores = [bias(h, mm_nt(key, query)) for key, bias in zip(keys, biases)]
        tops = [jnp.max(s, axis=0, keepdims=True) for s in scores]
        top = functools.reduce(jnp.maximum, tops)
        weights = [jnp.exp(s - top) for s in scores]
        total = sum(jnp.sum(w, axis=0, keepdims=True) for w in weights)
        mixed = sum(
            mm(vt[h * half : (h + 1) * half, :], w.astype(BF16)) for vt, w in zip(values_t, weights)
        )
        outs.append(mixed / total)
        logs.append(top + jnp.log(total))
    attended = jnp.concatenate(outs, axis=0).T.astype(BF16)
    return attended, jnp.concatenate(logs, axis=0)


def attend_full_kernel(q_ref, k_ref, v_ref, segq_ref, segk_ref, near_ref, far_ref, o_ref, log_ref):
    keys = [
        jnp.concatenate([k_ref[pl.ds(b * HALF, HALF), :], segk_ref[pl.ds(b * HALF, HALF), :]], axis=1)
        for b in range(2)
    ]
    values_t = [v_ref[pl.ds(b * HALF, HALF), :].T for b in range(2)]
    for qb in range(2):
        rows = pl.ds(qb * HALF, HALF)
        biases = full_biases(near_ref, far_ref, qb)
        attended, logs = attend_forward_block(q_ref[rows, :], segq_ref[rows, :], keys, values_t, biases)
        o_ref[rows, :] = attended
        log_ref[0, 0:2, rows] = logs


def attend_half_kernel(
    tp_ref, q_ref, k_ref, v_ref, kp_ref, vp_ref, segq_ref, segk_ref, near_ref, far_ref, oin, login, o_ref, log_ref
):
    keys = [
        jnp.concatenate([k_ref[...], segk_ref[pl.ds(0, HALF), :]], axis=1),
        jnp.concatenate([kp_ref[...], segk_ref[pl.ds(HALF, HALF), :]], axis=1),
    ]
    values_t = [v_ref[...].T, vp_ref[...].T]
    biases = half_biases(near_ref, far_ref, tp_ref[0] == 0)
    attended, logs = attend_forward_block(q_ref[...], segq_ref[...], keys, values_t, biases)
    o_ref[...] = attended
    log_ref[0, 0:2, :] = logs


def attend_forward(tp, qkv, kv_par, segq, segk, bias):
    tokens = qkv.shape[0]
    width = qkv.shape[1] // 3
    pairs = width // LANES
    out_shape = (
        jax.ShapeDtypeStruct((tokens, width), BF16),
        jax.ShapeDtypeStruct((pairs, 8, tokens), F32),
    )
    unit = 4 * HALF * HALF * 256 * 2
    attended, logs = call(
        attend_full_kernel,
        (pairs,),
        [
            pl.BlockSpec((ROW, LANES), lambda p: (0, p)),
            pl.BlockSpec((ROW, LANES), lambda p: (0, pairs + p)),
            pl.BlockSpec((ROW, LANES), lambda p: (0, 2 * pairs + p)),
            pl.BlockSpec((ROW, LANES), lambda p: (0, 0)),
            pl.BlockSpec((ROW, LANES), lambda p: (0, 0)),
        ]
        + bias_specs(),
        (
            pl.BlockSpec((ROW, LANES), lambda p: (0, p)),
            pl.BlockSpec((1, 8, ROW), lambda p: (p, 0, 0)),
        ),
        out_shape,
        flops=unit * 4 * pairs,
        moved=bias[0].size * 4,
    )(qkv, qkv, qkv, segq, segk, *bias)
    flip = pairs // 2
    return call(
        attend_half_kernel,
        (pairs,),
        [
            pl.BlockSpec((HALF, LANES), lambda p, *_: (2, p)),
            pl.BlockSpec((HALF, LANES), lambda p, *_: (2, pairs + p)),
            pl.BlockSpec((HALF, LANES), lambda p, *_: (2, 2 * pairs + p)),
            pl.BlockSpec((HALF, LANES), lambda p, *_: (0, lax.rem(p + flip, pairs))),
            pl.BlockSpec((HALF, LANES), lambda p, *_: (0, pairs + lax.rem(p + flip, pairs))),
            pl.BlockSpec((HALF, LANES), lambda p, *_: (2, 0)),
            pl.BlockSpec((ROW, LANES), lambda p, *_: (1, 0)),
        ]
        + bias_specs()
        + [pl.BlockSpec(memory_space=pl.ANY), pl.BlockSpec(memory_space=pl.ANY)],
        (
            pl.BlockSpec((HALF, LANES), lambda p, *_: (2, p)),
            pl.BlockSpec((1, 8, HALF), lambda p, *_: (p, 0, 2)),
        ),
        out_shape,
        prefetch=1,
        aliases={10: 0, 11: 1},
        flops=unit * 2 * pairs,
        moved=bias[0].size * 4,
    )(tp, qkv, qkv, qkv, kv_par, kv_par, segq, segk, *bias, attended, logs)


def ffn_kernel(
    att_ref, woo_ref, wop_ref, x_ref, oh_ref, tab_ref, guo_ref, gup_ref, wdo_ref, wdp_ref,
    head_ref, emb_ref, flag_ref, shifted_ref, lifted_ref, middle, normed, acc,
):
    step = pl.program_id(0)
    tokens, width = x_ref.shape
    half = woo_ref.shape[0]
    blocks = tokens // HALF

    @pl.when(step == 0)
    def _():
        def body(i):
            rows = pl.ds(pl.multiple_of(i * HALF, HALF), HALF)
            branch = mm(att_ref[rows, :half], woo_ref[...]) + mm(att_ref[rows, half:], wop_ref[...])
            pick = oh_ref[rows, :]
            mid = x_ref[rows, :].astype(F32) + mm(pick, tab_ref[:, 2 * width : 3 * width]) * branch
            middle[rows, :] = mid
            hat, _ = norm_parts(mid)
            scale = mm(pick, tab_ref[:, 3 * width : 4 * width])
            shift = mm(pick, tab_ref[:, 4 * width : 5 * width])
            normed[rows, :] = (hat * scale + shift).astype(BF16)
            acc[rows, :] = jnp.zeros((HALF, width), F32)

        block_loop(blocks, body)

    def body(i):
        rows = pl.ds(pl.multiple_of(i * HALF, HALF), HALF)
        total = acc[rows, :]
        for gu, wd in ((guo_ref, wdo_ref), (gup_ref, wdp_ref)):
            gate = mm(normed[rows, :], gu[0])
            up = mm(normed[rows, :], gu[1])
            hidden = (gate * jax.nn.sigmoid(gate) * up).astype(BF16)
            total = total + mm(hidden, wd[...])
        acc[rows, :] = total

    block_loop(blocks, body)

    @pl.when(step == pl.num_programs(0) - 1)
    def _():
        def body(i):
            rows = pl.ds(pl.multiple_of(i * HALF, HALF), HALF)
            gate = mm(oh_ref[rows, :], tab_ref[:, 5 * width : 6 * width])
            first = middle[rows, :] + gate * acc[rows, :]
            high = first.astype(BF16)
            rest = (first - high.astype(F32)).astype(BF16)
            coords = mm_nt(high, head_ref[...]) + mm_nt(rest, head_ref[...])
            lifted = coords * flag_ref[rows, :]
            lifted_ref[rows, :] = lifted
            high = lifted.astype(BF16)
            rest = (lifted - high.astype(F32)).astype(BF16)
            moved = mm(high, emb_ref[...]) + mm(rest, emb_ref[...])
            shifted_ref[rows, :] = x_ref[rows, :].astype(F32) + moved

        block_loop(blocks, body)


def ffn_specs(att, woo, x, pick, table):
    tokens, width = x.shape
    chunk = FFC
    return [
        whole(*att.shape),
        whole(*woo.shape),
        whole(*woo.shape),
        whole(tokens, width),
        whole(*pick.shape),
        whole(*table.shape),
        pl.BlockSpec((2, width, chunk), lambda j, *_: (0, 0, j)),
        pl.BlockSpec((2, width, chunk), lambda j, *_: (0, 0, j)),
        pl.BlockSpec((chunk, width), lambda j, *_: (j, 0)),
        pl.BlockSpec((chunk, width), lambda j, *_: (j, 0)),
    ]


def ffn_forward(att, woo, wop, x, pick, table, guo, gup, wdo, wdp, head, emb, flags):
    tokens, width = x.shape
    hidden = wdo.shape[0]
    return call(
        ffn_kernel,
        (hidden // FFC,),
        ffn_specs(att, woo, x, pick, table)
        + [whole(*head.shape), whole(*emb.shape), whole(*flags.shape)],
        (whole(tokens, width), whole(tokens, LANES)),
        (
            jax.ShapeDtypeStruct((tokens, width), F32),
            jax.ShapeDtypeStruct((tokens, LANES), F32),
        ),
        [
            pltpu.VMEM((tokens, width), F32),
            pltpu.VMEM((tokens, width), BF16),
            pltpu.VMEM((tokens, width), F32),
        ],
        flops=2 * tokens * width * (6 * hidden + width),
        moved=12 * hidden * width + 6 * tokens * width,
    )(att, woo, wop, x, pick, table, guo, gup, wdo, wdp, head, emb, flags)


def turn_kernel(
    tp_ref, att_ref, woo_ref, wop_ref, x_ref, oh_ref, tab_ref, guo_ref, gup_ref, wdo_ref, wdp_ref,
    gown_ref, gcame_ref, oht_ref,
    outo_ref, outp_ref, gmid_ref, gatt_ref, go_ref, gp_ref, goo_ref, gop_ref, sumo_ref, sump_ref,
    sums_ref, middle, hats, branches, normed, normed_t, gmixed, gmixed_t, mixed, gnormed, hid, dgate, dup,
):
    step = pl.program_id(0)
    tokens, width = x_ref.shape
    half = woo_ref.shape[0]
    blocks = tokens // HALF

    @pl.when(step == 0)
    def _():
        def body(i):
            rows = pl.ds(pl.multiple_of(i * HALF, HALF), HALF)
            branch = mm(att_ref[rows, :half], woo_ref[...]) + mm(att_ref[rows, half:], wop_ref[...])
            branches[rows, :] = branch
            pick = oh_ref[rows, :]
            mid = x_ref[rows, :] + mm(pick, tab_ref[:, 2 * width : 3 * width]) * branch
            middle[rows, :] = mid
            hat, _ = norm_parts(mid)
            scale = mm(pick, tab_ref[:, 3 * width : 4 * width])
            shift = mm(pick, tab_ref[:, 4 * width : 5 * width])
            normed[rows, :] = (hat * scale + shift).astype(BF16)
            gate = mm(pick, tab_ref[:, 5 * width : 6 * width])
            g = put_together(tp_ref[0] == 0, gown_ref[rows, :], gcame_ref[rows, :])
            gmixed[rows, :] = (g.astype(F32) * gate).astype(BF16)
            mixed[rows, :] = jnp.zeros((HALF, width), F32)
            gnormed[rows, :] = jnp.zeros((HALF, width), F32)

        block_loop(blocks, body)
        normed_t[...] = normed[...].T
        gmixed_t[...] = gmixed[...].T

    for gu, wd, out in ((gup_ref, wdp_ref, gp_ref), (guo_ref, wdo_ref, go_ref)):

        def body(i):
            rows = pl.ds(pl.multiple_of(i * BLOCK, BLOCK), BLOCK)
            gate = mm(normed[rows, :], gu[0])
            up = mm(normed[rows, :], gu[1])
            ghid = mm_nt(gmixed[rows, :], wd[...])
            s = jax.nn.sigmoid(gate)
            silu = gate * s
            hidden = (silu * up).astype(BF16)
            hid[rows, :] = hidden
            mixed[rows, :] += mm(hidden, wd[...])
            dg = (ghid * up * (s + silu * (1.0 - s))).astype(BF16)
            du = (ghid * silu).astype(BF16)
            dgate[rows, :] = dg
            dup[rows, :] = du
            gnormed[rows, :] += mm_nt(dg, gu[0]) + mm_nt(du, gu[1])

        block_loop(tokens // BLOCK, body)
        out[0, 0] = mm(normed_t[...], dgate[...]).astype(BF16)
        out[1, 0] = mm(normed_t[...], dup[...]).astype(BF16)
        out[2, 0] = mm(gmixed_t[...], hid[...]).astype(BF16)

    @pl.when(step == pl.num_programs(0) - 1)
    def _():
        first_core = tp_ref[0] == 0
        sums_ref[...] = jnp.zeros(sums_ref.shape, F32)

        def body(i):
            rows = pl.ds(pl.multiple_of(i * HALF, HALF), HALF)
            pick = oh_ref[rows, :]
            turn = oht_ref[i]
            g = put_together(first_core, gown_ref[rows, :], gcame_ref[rows, :]).astype(F32)
            total = mixed[rows, :]
            gate = mm(pick, tab_ref[:, 5 * width : 6 * width])
            mid = middle[rows, :]
            result = (mid + gate * total).astype(BF16)
            low, high = result[:, : width // 2], result[:, width // 2 :]
            outo_ref[rows, :] = jnp.where(first_core, low, high)
            outp_ref[rows, :] = jnp.where(first_core, high, low)
            sums_ref[0] += mm(turn, (g * total).astype(BF16))
            hat, inv_std = norm_parts(mid)
            gn = gnormed[rows, :]
            sums_ref[1] += mm(turn, (gn * hat).astype(BF16))
            sums_ref[2] += mm(turn, gn.astype(BF16))
            scale = mm(pick, tab_ref[:, 3 * width : 4 * width])
            gmid = g + norm_back(gn * scale, hat, inv_std)
            gmid_ref[rows, :] = gmid
            sums_ref[3] += mm(turn, (gmid * branches[rows, :]).astype(BF16))
            gbranch = (gmid * mm(pick, tab_ref[:, 2 * width : 3 * width])).astype(BF16)
            gmixed[rows, :] = gbranch
            gatt_ref[rows, :half] = mm_nt(gbranch, woo_ref[...]).astype(BF16)
            gatt_ref[rows, half:] = mm_nt(gbranch, wop_ref[...]).astype(BF16)

        block_loop(blocks, body)
        gmixed_t[...] = gmixed[...].T
        goo_ref[...] = mm(gmixed_t[...], att_ref[:, :half]).astype(BF16)
        gop_ref[...] = mm(gmixed_t[...], att_ref[:, half:]).astype(BF16)
        low, high = sums_ref[:, :, : width // 2], sums_ref[:, :, width // 2 :]
        sumo_ref[...] = jnp.where(first_core, low, high)
        sump_ref[...] = jnp.where(first_core, high, low)


def ffn_turn(tp, att, woo, wop, x, pick, table, guo, gup, wdo, wdp, g_own, g_came, pick_t):
    tokens, width = x.shape
    half = woo.shape[0]
    hidden = wdo.shape[0]
    grads = jax.ShapeDtypeStruct((3, hidden // FFC, width, FFC), BF16)
    grads_spec = pl.BlockSpec((3, 1, width, FFC), lambda j, *_: (0, j, 0, 0))
    return call(
        turn_kernel,
        (hidden // FFC,),
        ffn_specs(att, woo, x, pick, table) + [whole(tokens, width // 2), whole(tokens, width // 2), whole(*pick_t.shape)],
        (
            whole(tokens, width // 2),
            whole(tokens, width // 2),
            whole(tokens, width),
            whole(tokens, width),
            grads_spec,
            grads_spec,
            whole(width, half),
            whole(width, half),
            whole(4, 16, width // 2),
            whole(4, 16, width // 2),
        ),
        (
            jax.ShapeDtypeStruct((tokens, width // 2), BF16),
            jax.ShapeDtypeStruct((tokens, width // 2), BF16),
            jax.ShapeDtypeStruct((tokens, width), F32),
            jax.ShapeDtypeStruct((tokens, width), BF16),
            grads,
            grads,
            jax.ShapeDtypeStruct((width, half), BF16),
            jax.ShapeDtypeStruct((width, half), BF16),
            jax.ShapeDtypeStruct((4, 16, width // 2), F32),
            jax.ShapeDtypeStruct((4, 16, width // 2), F32),
        ),
        [
            pltpu.VMEM((4, 16, width), F32),
            pltpu.VMEM((tokens, width), F32),
            pltpu.VMEM((8, LANES), F32),
            pltpu.VMEM((tokens, width), F32),
            pltpu.VMEM((tokens, width), BF16),
            pltpu.VMEM((width, tokens), BF16),
            pltpu.VMEM((tokens, width), BF16),
            pltpu.VMEM((width, tokens), BF16),
            pltpu.VMEM((tokens, width), F32),
            pltpu.VMEM((tokens, width), F32),
            pltpu.VMEM((tokens, FFC), BF16),
            pltpu.VMEM((tokens, FFC), BF16),
            pltpu.VMEM((tokens, FFC), BF16),
        ],
        prefetch=1,
        flops=2 * tokens * width * (18 * hidden + 3 * width),
        moved=24 * hidden * width + 12 * tokens * width,
    )(tp, att, woo, wop, x, pick, table, guo, gup, wdo, wdp, g_own, g_came, pick_t)


def attend_back_block(q, segq, gout, logs, keys, keys_t, values, biases, bias_sums, gkeys, gvalues):
    half = LANES // 2
    masks = lane_masks()
    scale = half**-0.5
    scaled = q * jnp.asarray(scale, BF16)
    gqs = []
    for h in range(2):
        query_low = scaled * masks[h]
        query = jnp.concatenate([query_low, segq], axis=1)
        gheads = gout * masks[h]
        chances = [jnp.exp(bias(h, mm_nt(key, query)) - logs[h : h + 1, :]) for key, bias in zip(keys, biases)]
        gchances = [mm_nt(value, gheads) for value in values]
        centre = sum(jnp.sum(p * gp, axis=0, keepdims=True) for p, gp in zip(chances, gchances))
        gq = 0.0
        for b, (p, gp) in enumerate(zip(chances, gchances)):
            gs = p * (gp - centre)
            bias_sums[b](h, gs)
            low = gs.astype(BF16)
            gvalues[b] = gvalues[b] + mm(p.astype(BF16), gheads)
            gkeys[b] = gkeys[b] + mm(low, query_low)
            gq = gq + mm(keys_t[b][h * half : (h + 1) * half, :], low)
        gqs.append(gq * scale)
    return jnp.concatenate(gqs, axis=0).T.astype(BF16)


def diagonal_sums(tile):
    size, wide = tile.shape
    blank = jnp.zeros((SUB, wide), F32)
    groups = [jnp.zeros((SUB, 2 * wide), F32)] * 2
    for i, a in enumerate(range(0, size, SUB)):
        piece = jnp.concatenate([tile[a : a + SUB], blank], axis=1)
        groups[i % 2] = groups[i % 2] + pltpu.roll(piece, size - SUB - a, axis=1)
    total = groups[0] + groups[1]
    rows = lax.broadcasted_iota(jnp.int32, (SUB, 2 * wide), 0)
    moved = sum(pltpu.roll(jnp.where(rows == b, total, 0.0), SUB - 1 - b, axis=1) for b in range(SUB))
    return jnp.sum(moved, axis=0, keepdims=True)


def far_sums(tile, later):
    whole_sum = jnp.sum(jnp.sum(tile, axis=0, keepdims=True), axis=1, keepdims=True)
    edge = tile[:RADIUS, LANES:] if later else tile[HALF - RADIUS :, :LANES]
    sums = diagonal_sums(edge)
    rest = whole_sum - jnp.sum(sums, axis=1, keepdims=True)
    row = jnp.concatenate([sums, jnp.zeros((1, 2 * HALF - sums.shape[1]), F32)], axis=1)
    row = jnp.broadcast_to(row, (8, 2 * HALF))
    if later:
        row = pltpu.roll(row, 2 * HALF - LANES - RADIUS, axis=1)
    lanes = lax.broadcasted_iota(jnp.int32, (1, 2 * HALF), 1)
    return row[:1] + jnp.where(lanes == (0 if later else 2 * HALF - 2), rest, 0.0)


def attend_full_back_kernel(
    q_ref, k_ref, v_ref, g_ref, log_ref, segq_ref, segk_ref, near_ref, far_ref, o_ref, diag_ref, sums
):
    keys, keys_t, values = [], [], []
    for b in range(2):
        rows = pl.ds(b * HALF, HALF)
        key = k_ref[rows, :]
        keys.append(jnp.concatenate([key, segk_ref[rows, :]], axis=1))
        keys_t.append(key.T)
        values.append(v_ref[rows, :])
    gkeys, gvalues = [0.0, 0.0], [0.0, 0.0]
    sums[...] = jnp.zeros(sums.shape, F32)
    for qb in range(2):
        rows = pl.ds(qb * HALF, HALF)
        biases = full_biases(near_ref, far_ref, qb)

        def add(h, gs):
            sums[h] += gs

        def put(h, gs, later):
            row = 3 * h + (0 if later else 2)
            diag_ref[0, row : row + 1, :] = far_sums(gs, later)

        adders = [add, functools.partial(put, later=True)] if qb == 0 else [functools.partial(put, later=False), add]
        o_ref[0, rows, :] = attend_back_block(
            q_ref[rows, :], segq_ref[rows, :], g_ref[rows, :], log_ref[0, 0:2, rows],
            keys, keys_t, values, biases, adders, gkeys, gvalues,
        )
    for b in range(2):
        rows = pl.ds(b * HALF, HALF)
        o_ref[1, rows, :] = gkeys[b].astype(BF16)
        o_ref[2, rows, :] = gvalues[b].astype(BF16)
    for h in range(2):
        diag_ref[0, 3 * h + 1 : 3 * h + 2, :] = diagonal_sums(sums[h])


def attend_half_back_kernel(
    tp_ref, q_ref, k_ref, v_ref, kp_ref, vp_ref, g_ref, log_ref, segq_ref, segk_ref, near_ref, far_ref,
    o_ref, par_ref, diag_ref,
):
    keys, keys_t, values = [], [], []
    for b, (k, v) in enumerate(((k_ref, v_ref), (kp_ref, vp_ref))):
        key = k[...]
        keys.append(jnp.concatenate([key, segk_ref[pl.ds(b * HALF, HALF), :]], axis=1))
        keys_t.append(key.T)
        values.append(v[...])
    first = tp_ref[0] == 0
    biases = half_biases(near_ref, far_ref, first)
    gkeys, gvalues = [0.0, 0.0], [0.0, 0.0]

    def put(h, gs, b):
        sums = jnp.where(first, far_sums(gs, True), far_sums(gs, False)) if b else diagonal_sums(gs)
        diag_ref[0, 2 * h + b : 2 * h + b + 1, :] = sums

    adders = [functools.partial(put, b=b) for b in range(2)]
    o_ref[0] = attend_back_block(
        q_ref[...], segq_ref[...], g_ref[...], log_ref[0, 0:2, :],
        keys, keys_t, values, biases, adders, gkeys, gvalues,
    )
    o_ref[1] = gkeys[0].astype(BF16)
    o_ref[2] = gvalues[0].astype(BF16)
    par_ref[0] = gkeys[1].astype(BF16)
    par_ref[1] = gvalues[1].astype(BF16)


def attend_half_back(tp, qkv, kv_par, g, logs, segq, segk, bias):
    width = qkv.shape[1] // 3
    pairs = width // LANES
    flip = pairs // 2
    return call(
        attend_half_back_kernel,
        (pairs,),
        [
            pl.BlockSpec((HALF, LANES), lambda p, *_: (2, p)),
            pl.BlockSpec((HALF, LANES), lambda p, *_: (2, pairs + p)),
            pl.BlockSpec((HALF, LANES), lambda p, *_: (2, 2 * pairs + p)),
            pl.BlockSpec((HALF, LANES), lambda p, *_: (0, lax.rem(p + flip, pairs))),
            pl.BlockSpec((HALF, LANES), lambda p, *_: (0, pairs + lax.rem(p + flip, pairs))),
            pl.BlockSpec((HALF, LANES), lambda p, *_: (2, p)),
            pl.BlockSpec((1, 8, HALF), lambda p, *_: (p, 0, 2)),
            pl.BlockSpec((HALF, LANES), lambda p, *_: (2, 0)),
            pl.BlockSpec((ROW, LANES), lambda p, *_: (1, 0)),
        ]
        + bias_specs(),
        (
            pl.BlockSpec((3, HALF, LANES), lambda p, *_: (0, 0, p)),
            pl.BlockSpec((2, HALF, LANES), lambda p, *_: (0, 0, p)),
            pl.BlockSpec((1, 8, ROW), lambda p, *_: (p, 0, 0)),
        ),
        (
            jax.ShapeDtypeStruct((3, HALF, width), BF16),
            jax.ShapeDtypeStruct((2, HALF, width), BF16),
            jax.ShapeDtypeStruct((pairs, 8, ROW), F32),
        ),
        prefetch=1,
        flops=10 * HALF * HALF * 256 * 2 * pairs,
        moved=bias[0].size * 4,
    )(tp, qkv, qkv, qkv, kv_par, kv_par, g, logs, segq, segk, *bias)


def attend_full_back(qkv, g, logs, segq, segk, bias):
    width = qkv.shape[1] // 3
    pairs = width // LANES
    return call(
        attend_full_back_kernel,
        (pairs,),
        [
            pl.BlockSpec((ROW, LANES), lambda p: (0, p)),
            pl.BlockSpec((ROW, LANES), lambda p: (0, pairs + p)),
            pl.BlockSpec((ROW, LANES), lambda p: (0, 2 * pairs + p)),
            pl.BlockSpec((ROW, LANES), lambda p: (0, p)),
            pl.BlockSpec((1, 8, ROW), lambda p: (p, 0, 0)),
            pl.BlockSpec((ROW, LANES), lambda p: (0, 0)),
            pl.BlockSpec((ROW, LANES), lambda p: (0, 0)),
        ]
        + bias_specs(),
        (
            pl.BlockSpec((3, ROW, LANES), lambda p: (0, 0, p)),
            pl.BlockSpec((1, 8, ROW), lambda p: (p, 0, 0)),
        ),
        (
            jax.ShapeDtypeStruct((3, ROW, width), BF16),
            jax.ShapeDtypeStruct((pairs, 8, ROW), F32),
        ),
        [pltpu.VMEM((2, HALF, HALF), F32)],
        flops=20 * HALF * HALF * 256 * 2 * pairs,
        moved=bias[0].size * 4,
    )(qkv, qkv, qkv, g, logs, segq, segk, *bias)


def joined_rows(full_ref, half_ref, recv_ref, step, rows_in):
    half = recv_ref.shape[2] // 2
    rows_in[pl.ds(0, ROW), :] = full_ref[0]
    keep = (step > 0).astype(F32).astype(BF16)
    recv = jnp.concatenate([recv_ref[0, :, half:], recv_ref[0, :, :half]], axis=1)
    rows_in[pl.ds(ROW, HALF), :] = half_ref[0] + recv * keep


def qkv_weights_kernel(
    x_ref, oh_ref, tab_ref, full_ref, half_ref, recv_ref, outo_ref, outp_ref, go_ref, gp_ref, normed, normed_t, rows_in
):
    step = pl.program_id(0)
    tokens, width = x_ref.shape
    half = width // 2

    @pl.when(step == 0)
    def _():
        def body(i):
            rows = pl.ds(pl.multiple_of(i * HALF, HALF), HALF)
            hat, _ = norm_parts(x_ref[rows, :])
            pick = oh_ref[rows, :]
            scale = mm(pick, tab_ref[:, :width])
            shift = mm(pick, tab_ref[:, width : 2 * width])
            normed[rows, :] = (hat * scale + shift).astype(BF16)

        block_loop(tokens // HALF, body)
        normed_t[...] = normed[...].T

    joined_rows(full_ref, half_ref, recv_ref, step, rows_in)
    go_ref[0, :, :half] = mm(normed_t[...], rows_in[:, :half]).astype(BF16)
    gp_ref[0, :, :half] = mm(normed_t[...], rows_in[:, half:]).astype(BF16)
    go_ref[0, :, half:] = outo_ref[...]
    gp_ref[0, :, half:] = outp_ref[...]


def row_specs(width):
    return [
        pl.BlockSpec((1, ROW, width), lambda j, *_: (j, 0, 0)),
        pl.BlockSpec((1, HALF, width), lambda j, *_: (j, 0, 0)),
        pl.BlockSpec((1, HALF, width), lambda j, *_: (jnp.maximum(j - 1, 0), 0, 0)),
    ]


def qkv_weights(x, pick, table, full, half_rows, recv, out_own, out_par):
    tokens, width = x.shape
    half = width // 2
    third = half // 3
    spec = pl.BlockSpec((1, width, half + third), lambda j: (j, 0, 0))
    shape = jax.ShapeDtypeStruct((3, width, half + third), BF16)
    out_spec = pl.BlockSpec((width, third), lambda j: (0, j))
    return call(
        qkv_weights_kernel,
        (3,),
        [whole(tokens, width), whole(*pick.shape), whole(*table.shape)] + row_specs(width) + [out_spec, out_spec],
        (spec, spec),
        (shape, shape),
        [
            pltpu.VMEM((tokens, width), BF16),
            pltpu.VMEM((width, tokens), BF16),
            pltpu.VMEM((tokens, width), BF16),
        ],
        flops=2 * tokens * width * 6 * half,
        moved=16 * half * width + 12 * tokens * width,
    )(x, pick, table, full, half_rows, recv, out_own, out_par)


def qkv_back_kernel(
    tp_ref, x_ref, oh_ref, tab_ref, full_ref, half_ref, recv_ref, wo_ref, wp_ref, gmid_ref, lifted_ref, oht_ref,
    gino_ref, ginp_ref, sumo_ref, sump_ref, hats, stds, rows_in, acc, sums,
):
    step = pl.program_id(0)
    tokens, width = x_ref.shape
    half = wo_ref.shape[1]
    blocks = tokens // HALF

    @pl.when(step == 0)
    def _():
        def body(i):
            rows = pl.ds(pl.multiple_of(i * HALF, HALF), HALF)
            hat, inv_std = norm_parts(x_ref[rows, :])
            hats[rows, :] = hat
            stds[rows, :] = inv_std
            acc[rows, :] = jnp.zeros((HALF, width), F32)

        block_loop(blocks, body)

    joined_rows(full_ref, half_ref, recv_ref, step, rows_in)

    def body(i):
        rows = pl.ds(pl.multiple_of(i * HALF, HALF), HALF)
        grad = rows_in[rows, :]
        acc[rows, :] += mm_nt(grad[:, :half], wo_ref[...]) + mm_nt(grad[:, half:], wp_ref[...])

    block_loop(blocks, body)

    @pl.when(step == pl.num_programs(0) - 1)
    def _():
        first_core = tp_ref[0] == 0
        sums[...] = jnp.zeros(sums.shape, F32)

        def body(i):
            rows = pl.ds(pl.multiple_of(i * HALF, HALF), HALF)
            turn = oht_ref[i]
            gn = acc[rows, :]
            hat = hats[rows, :]
            sums[0] += mm(turn, (gn * hat).astype(BF16))
            sums[1] += mm(turn, gn.astype(BF16))
            scale = mm(oh_ref[rows, :], tab_ref[:, :width])
            grad = gmid_ref[rows, :] + norm_back(gn * scale, hat, stds[rows, :])
            low, high = grad[:, : width // 2], grad[:, width // 2 :]
            gino_ref[rows, :] = jnp.where(first_core, low, high)
            ginp_ref[rows, :] = jnp.where(first_core, high, low)
            lifted_t = lifted_ref[rows, :].astype(BF16).T
            sums[2] += mm(lifted_t[:16, :], grad.astype(BF16))

        block_loop(blocks, body)
        low, high = sums[:, :, : width // 2], sums[:, :, width // 2 :]
        sumo_ref[...] = jnp.where(first_core, low, high)
        sump_ref[...] = jnp.where(first_core, high, low)


def qkv_back(tp, x, pick, table, full, half_rows, recv, wo, wp, gmid, lifted, pick_t):
    tokens, width = x.shape
    half = wo.shape[1] // 3
    return call(
        qkv_back_kernel,
        (3,),
        [whole(tokens, width), whole(*pick.shape), whole(*table.shape)]
        + row_specs(width)
        + [
            pl.BlockSpec((width, half), lambda j, *_: (0, j)),
            pl.BlockSpec((width, half), lambda j, *_: (0, j)),
            whole(tokens, width),
            whole(tokens, LANES),
            whole(*pick_t.shape),
        ],
        (
            whole(tokens, width // 2),
            whole(tokens, width // 2),
            whole(3, 16, width // 2),
            whole(3, 16, width // 2),
        ),
        (
            jax.ShapeDtypeStruct((tokens, width // 2), F32),
            jax.ShapeDtypeStruct((tokens, width // 2), F32),
            jax.ShapeDtypeStruct((3, 16, width // 2), F32),
            jax.ShapeDtypeStruct((3, 16, width // 2), F32),
        ),
        [
            pltpu.VMEM((tokens, width), F32),
            pltpu.VMEM((tokens, 1), F32),
            pltpu.VMEM((tokens, width), BF16),
            pltpu.VMEM((tokens, width), F32),
            pltpu.VMEM((3, 16, width), F32),
        ],
        prefetch=1,
        flops=2 * tokens * width * 6 * half,
        moved=12 * half * width + 16 * tokens * width,
    )(tp, x, pick, table, full, half_rows, recv, wo, wp, gmid, lifted, pick_t)


def chain_joins(first_core):
    row = lax.broadcasted_iota(jnp.int32, (16, 16), 0)
    col = lax.broadcasted_iota(jnp.int32, (16, 16), 1)
    lower = ((row == col) & (row < 2 * SEGS)).astype(F32)
    upper = (
        ((row == col) & (row >= SEGS) & (row < 2 * SEGS)) | ((row == col + 2 * SEGS) & (row < 3 * SEGS))
    ).astype(F32)
    return jnp.where(first_core, lower, upper), jnp.where(first_core, upper, lower)


def join_chains(tp_ref, own_ref, came_ref, slope_ref, count, o_ref):
    own_join, came_join = chain_joins(tp_ref[0] == 0)
    cols = own_ref.shape[2]
    for i in range(count):
        both = jnp.dot(own_join, own_ref[i], precision=HIGHEST, preferred_element_type=F32)
        both = both + jnp.dot(came_join, came_ref[i], precision=HIGHEST, preferred_element_type=F32)
        lanes = pl.ds(i * cols, cols)
        o_ref[0:16, lanes] = (both * slope_ref[:, lanes]).astype(BF16)


def early_kernel(tp_ref, own_ref, came_ref, slope_ref, embed_ref, o_ref):
    join_chains(tp_ref, own_ref, came_ref, slope_ref, 4, o_ref)
    o_ref[:, pl.ds(4 * own_ref.shape[2], embed_ref.shape[1])] = embed_ref[...]


def late_kernel(tp_ref, own_ref, came_ref, slope_ref, bins_ref, o_ref):
    cols = own_ref.shape[2]
    join_chains(tp_ref, own_ref, came_ref, slope_ref, 2, o_ref)
    o_ref[:, pl.ds(2 * cols, LANES)] = bins_ref[...].astype(BF16)
    coords = own_ref[2] + came_ref[2]
    parts = [coords[i : i + 1, j : j + LANES] for j in range(0, cols, LANES) for i in range(3)]
    parts.append(jnp.zeros((16 - len(parts), LANES), F32))
    o_ref[:, pl.ds(2 * cols + LANES, LANES)] = jnp.concatenate(parts, axis=0).astype(BF16)


def pack_rows(kernel, tp, own, came, slopes, extra, shape):
    return call(
        kernel,
        (1,),
        [whole(*own.shape), whole(*came.shape), whole(*slopes.shape), whole(*extra.shape)],
        whole(*shape),
        jax.ShapeDtypeStruct(shape, BF16),
        prefetch=1,
        flops=10**6,
        moved=10**5,
    )(tp, own, came, slopes, extra)


def closing_kernel(early_ref, early_came_ref, late_ref, late_came_ref, hat_ref, inv_ref, gain_ref, both_ref, *refs):
    ffn, attn, outs = refs[:2], refs[2:4], refs[4:]
    gu_ref, down_ref, qkv_ref, out_ref = outs[:4]
    w0_ref, b0_ref, w1_ref, w2_ref, b2_ref, w3_ref, b3_ref, w4_ref, w5_ref, b5_ref = outs[4:14]
    table_ref, pgain_ref, proj_ref, coord_ref = outs[14:]

    def total(pair, block):
        return pair[0][0, block].astype(F32) + pair[1][0, block].astype(F32)

    lanes = ffn[0].shape[3]
    chunks = down_ref.shape[1] // lanes
    for block in range(chunks):
        span = pl.ds(block * lanes, lanes)
        gu_ref[:, 0, span] = total(ffn, block)
        gu_ref[:, 1, span] = total(ffn, chunks + block)
        down_ref[:, span] = total(ffn, 2 * chunks + block)
    third = out_ref.shape[1] // 3
    for i in range(3):
        value = total(attn, i)
        qkv_ref[i] = value[:, : 3 * third]
        out_ref[:, i * third : (i + 1) * third] = value[:, 3 * third :]

    cols = coord_ref.shape[1]
    pieces = [(early_ref, late_ref), (early_came_ref, late_came_ref)]
    embed_t = [early[:, 4 * cols :].T for early, _ in pieces]
    weights = [w0_ref, w1_ref, w5_ref, w3_ref, w4_ref, w2_ref]
    biases = [b0_ref, None, b5_ref, b3_ref, None, b2_ref]
    for i, (weight, bias) in enumerate(zip(weights, biases)):
        source, lanes = (1, pl.ds(i * cols, cols)) if i < 2 else (0, pl.ds((i - 2) * cols, cols))
        parts = [piece[source][:, lanes] for piece in pieces]
        weight[...] = sum(mm(embed, part) for embed, part in zip(embed_t, parts))
        if bias is not None:
            bias[...] = sum(jnp.sum(part.astype(F32), axis=0) for part in parts)
    extra = sum(late[:, 2 * cols :].reshape(-1, 16, 2 * LANES).astype(F32).sum(axis=0) for _, late in pieces)
    for i in range(cols // LANES):
        coord_ref[:, pl.ds(i * LANES, LANES)] = extra[3 * i : 3 * i + 3, LANES:]
    bins = extra[:, :LANES]
    hat = hat_ref[...]
    gain = gain_ref[...]
    proj = jnp.dot(bins, hat * gain, precision=HIGHEST, preferred_element_type=F32)
    proj_ref[...] = proj[: proj_ref.shape[0]]
    normed_grad = jnp.dot(bins.T, both_ref[...], precision=HIGHEST, preferred_element_type=F32)
    pgain_ref[...] = jnp.sum(normed_grad * hat, axis=0)
    table_ref[...] = norm_back(normed_grad * gain, hat, inv_ref[...])[: table_ref.shape[0]]


def closing(early, late, hat, inv_std, gain, both, ffn, attn, bins, heads):
    cols = (late[0].shape[1] - 2 * LANES) // 2
    embed = early[0].shape[1] - 4 * cols
    features = hat.shape[1]
    height, lanes = ffn[0].shape[2:]
    weight, bias = (embed, cols), (cols,)
    hidden = lanes * (ffn[0].shape[1] // 3)
    shapes = [(height, 2, hidden), (height, hidden), (3, height, cols), (height, cols)]
    shapes += [weight, bias, weight, weight, bias, weight, bias, weight, weight, bias]
    shapes += [(bins, features), (features,), (heads, features), (3, cols)]
    args = (*early, *late, hat, inv_std, gain, both, *ffn, *attn)
    return call(
        closing_kernel,
        (1,),
        [whole(*a.shape) for a in args],
        tuple(whole(*shape) for shape in shapes),
        tuple(jax.ShapeDtypeStruct(shape, F32) for shape in shapes),
        flops=10**8,
        moved=10**7,
    )(*args)


def halve_kernel(place_ref, *refs, plan, count):
    inputs, outs = refs[:count], refs[count:]
    for stream, (bit, sections) in enumerate(plan):
        sent_ref, kept_ref = outs[2 * stream], outs[2 * stream + 1]
        mine = (place_ref[0] >> bit) & 1
        done = 0
        for first, second, base, chunks, left in sections:
            spot = left.index(bit)
            shift = len(left) - 1
            half = 1 << shift

            def body(n, first=first, second=second, base=base, spot=spot, shift=shift, done=done, mine=mine):
                k = n & ((1 << shift) - 1)
                at = base + ((n >> shift) << (shift + 1)) + ((k >> spot) << (spot + 1)) + (k & ((1 << spot) - 1))
                for which, ref in ((1 - mine, sent_ref), (mine, kept_ref)):
                    block = at + (which << spot)
                    ref[0, done + n] = inputs[first][0, block] + inputs[second][0, block]

            block_loop(chunks * half, body)
            done += chunks * half


def bins_kernel(tp_ref, full_ref, half_ref, o_ref):
    first = tp_ref[0] == 0
    lane = lax.broadcasted_iota(jnp.int32, (ROW, LANES), 0)
    column = lax.broadcasted_iota(jnp.int32, (ROW, LANES), 1)
    heads = [(p, h) for p in range(full_ref.shape[0]) for h in range(2)]
    blank = jnp.zeros((o_ref.shape[0] - len(heads), ROW), F32)
    total = jnp.zeros(o_ref.shape, F32)
    for d in range(3):
        rows = []
        for p, h in heads:
            row = 2 * h + (d != 1)
            extra = half_ref[p, row : row + 1, :]
            if d != 1:
                extra = jnp.where(first if d == 0 else jnp.logical_not(first), extra, 0.0)
            rows.append(full_ref[p, 3 * h + d : 3 * h + d + 1, :] + extra)
        bins = jnp.clip(lane - (HALF - 1) + HALF * (d - 1), -RADIUS, RADIUS) + RADIUS
        total = total + jnp.dot(
            jnp.concatenate(rows + [blank], axis=0),
            (bins == column).astype(F32),
            precision=HIGHEST,
            preferred_element_type=F32,
        )
    o_ref[...] = total


def bin_sums(tp, full, half):
    return call(
        bins_kernel,
        (1,),
        [whole(*full.shape), whole(*half.shape)],
        whole(16, LANES),
        jax.ShapeDtypeStruct((16, LANES), F32),
        prefetch=1,
        flops=10**7,
        moved=4 * 10**5,
    )(tp, full, half)


def half_kernel(place_ref, *refs, plan, count):
    inputs, outs = refs[:count], refs[count:]
    for sections, ref in zip(plan, outs):
        done = 0
        for first in sections:
            _, chunks, high, _, low, _, _ = inputs[first].shape
            shift = high.bit_length() - 1

            def body(n, first=first, shift=shift, low=low, done=done, ref=ref):
                at = (0, n >> shift, n & ((1 << shift) - 1), 0)
                ref[0, pl.ds(done + n * low, low)] = inputs[first][at] + inputs[first + 1][at]

            block_loop(chunks * high, body)
            done += chunks * high * low


def half_of(place, streams, bits, keep):
    arrays, specs, plan, shapes = [], [], [], []
    steps = streams[0][0][5]
    if any(len(sections) > 1 or sections[0][5] != steps for sections in streams):
        steps = 1
    moved = 0
    for sections, bit in zip(streams, bits):
        entries, blocks = [], 0
        for own, i, came, k, _, chunks, left in sections:
            low = 1 << left.index(bit)
            high = (1 << (len(left) - 1)) // low
            entries.append(len(arrays))
            for array, index in ((own, i), (came, k)):
                arrays.append(array.reshape((-1, chunks, high, 2, low) + array.shape[2:]))

                def at(j, place_ref, index=index, bit=bit):
                    mine = (place_ref[0] >> bit) & 1
                    return index, j, 0, mine if keep else 1 - mine, 0, 0, 0

                specs.append(pl.BlockSpec((1, chunks // steps, high, 1, low) + array.shape[2:], at))
            blocks += chunks * high * low
        plan.append(entries)
        shape = (1, blocks) + sections[0][0].shape[2:]
        shapes.append(shape)
        moved += 6 * blocks * shape[2] * shape[3]
    return call(
        functools.partial(half_kernel, plan=plan, count=len(arrays)),
        (steps,),
        specs,
        tuple(pl.BlockSpec((1, n // steps, h, c), lambda j, *_: (0, j, 0, 0)) for _, n, h, c in shapes),
        tuple(jax.ShapeDtypeStruct(shape, BF16) for shape in shapes),
        prefetch=1,
        flops=10**6,
        moved=moved,
    )(place, *arrays)


def halve(place, streams, bits):
    arrays, specs, plan, shapes = [], [], [], []
    steps = streams[0][0][5]
    if any(len(sections) > 1 or sections[0][5] != steps for sections in streams):
        steps = 1

    def operand(array, index):
        for i, (seen, at) in enumerate(arrays):
            if seen is array and at == index:
                return i
        arrays.append((array, index))
        block = (1, array.shape[1] // steps) + array.shape[2:]
        specs.append(pl.BlockSpec(block, lambda j, *_: (index, j, 0, 0)))
        return len(arrays) - 1

    moved = 0
    for sections, bit in zip(streams, bits):
        entries, blocks = [], 0
        for own, i, came, k, base, chunks, left in sections:
            entries.append((operand(own, i), operand(came, k), base, chunks // steps, left))
            blocks += chunks << (len(left) - 1)
        plan.append((bit, entries))
        shape = (1, blocks) + sections[0][0].shape[2:]
        shapes += [shape, shape]
        moved += 12 * blocks * shape[2] * shape[3]
    outs = call(
        functools.partial(halve_kernel, plan=plan, count=len(arrays)),
        (steps,),
        specs,
        tuple(pl.BlockSpec((1, n // steps, h, c), lambda j, *_: (0, j, 0, 0)) for _, n, h, c in shapes),
        tuple(jax.ShapeDtypeStruct(shape, BF16) for shape in shapes),
        prefetch=1,
        flops=10**6,
        moved=moved,
    )(place, *[array for array, _ in arrays])
    return list(outs[0::2]), list(outs[1::2])


def swap(values):
    return lax.ppermute(values, "tp", [(0, 1), (1, 0)])


def after(values, *others):
    return lax.optimization_barrier((values, *others))[0]


class Cube:
    def __init__(self, rows):
        self.bits = rows.bit_length() - 1
        assert rows == 1 << self.bits
        self.place = lax.axis_index("rows").reshape(1).astype(jnp.int32)
        self.perms = [[(i, i ^ (1 << b)) for i in range(rows)] for b in range(self.bits)]

    def turns(self):
        return [[(i + r) % 3 for i in range(3)] for r in range(3)]

    def gather(self, values, step):
        bit = (list(range(self.bits - 1, 1, -1)) + list(range(min(2, self.bits))))[step]
        came = lax.ppermute(values, "rows", self.perms[bit])
        if step == self.bits - 1:
            return values, came
        return lax.optimization_barrier(jnp.concatenate([values, came], axis=0))


def next_sections(sections, kept, came, bit):
    made, base = [], 0
    for _, _, _, _, _, chunks, left in sections:
        left = [b for b in left if b != bit]
        made.append((kept, 0, came, 0, base, chunks, left))
        base += chunks << len(left)
    return made


def normalize(values):
    centre = jnp.mean(values, axis=-1, keepdims=True)
    shifted = values - centre
    spread = jnp.mean(shifted * shifted, axis=-1, keepdims=True)
    inv_std = lax.rsqrt(spread + EPSILON)
    return shifted * inv_std, inv_std


def three_parts(values):
    high = lax.reduce_precision(values, 8, 7)
    middle = lax.reduce_precision(values - high, 8, 7)
    low = values - high - middle
    return jnp.concatenate([high, middle, low], axis=0).astype(BF16)


def bias_base(heads):
    bins = heads.shape[1]
    low = lambda n: jnp.broadcast_to(heads[:, :1], (heads.shape[0], n))
    top = lambda n: jnp.broadcast_to(heads[:, bins - 1 :], (heads.shape[0], n))
    fill = HALF - RADIUS
    behind = jnp.concatenate([low(fill), heads[:, :RADIUS], low(HALF)], axis=1)
    same = jnp.concatenate([heads[:, RADIUS:], top(fill - 1), low(fill), heads[:, :RADIUS]], axis=1)
    ahead = jnp.concatenate([top(HALF), heads[:, RADIUS:], top(fill - 1)], axis=1)
    return jnp.stack([behind, same, ahead], axis=1)


def per_device(
    layer_input,
    cotangent,
    chain_lengths,
    self_condition_flag,
    time_embedding,
    query_key_value,
    output_projection,
    attention_scale_weight,
    attention_scale_bias,
    attention_shift_weight,
    attention_gate_weight,
    attention_gate_bias,
    transition_scale_weight,
    transition_scale_bias,
    transition_shift_weight,
    transition_gate_weight,
    transition_gate_bias,
    gate_up_projection,
    down_projection,
    pair_table,
    pair_gain,
    pair_projection,
    coordinate_head,
    coordinate_embedding,
    rows,
):
    core = lax.axis_index("tp")
    first_core = core == 0
    tp = core.reshape(1).astype(jnp.int32)
    cols = layer_input.shape[1]
    width = query_key_value.shape[0]
    heads_here = pair_projection.shape[1]
    bins = pair_table.shape[0]
    cube = Cube(rows)

    def side_by_side(own, came, axis):
        return jnp.where(
            first_core, jnp.concatenate([own, came], axis), jnp.concatenate([came, own], axis)
        )

    def scatter_tokens(own, sent):
        came = swap(sent)
        lower = jnp.concatenate([own[:ROW], own[ROW:], came[ROW:], came[:ROW]], axis=0)
        upper = jnp.concatenate([came[:ROW], came[ROW:], own[ROW:], own[:ROW]], axis=0)
        return jnp.where(first_core, lower, upper)

    x_own, x_sent, cot_own, cot_sent = token_halves(tp, layer_input, cotangent)
    x_came = swap(x_sent)
    qkv_own = query_key_value.reshape(width, -1)
    qkv_par = swap(qkv_own)

    mods, early_slopes, late_slopes, embed = modulations(
        time_embedding,
        [
            attention_scale_weight,
            attention_shift_weight,
            attention_gate_weight,
            transition_scale_weight,
            transition_shift_weight,
            transition_gate_weight,
        ],
        [attention_scale_bias, attention_gate_bias, transition_scale_bias, transition_gate_bias],
    )
    table = chain_table(tp, mods, swap(mods))
    mask_q, mask_k, pick, pick_t, flags = masks(tp, chain_lengths, self_condition_flag)

    pair_hat, pair_inv = normalize(pair_table.astype(F32))
    gain = pair_gain.astype(F32)
    pair_normed = pair_hat * gain
    pair_both = jnp.concatenate([pair_projection, swap(pair_projection)], axis=1).astype(F32)
    bias_heads = jnp.transpose(jnp.dot(pair_normed, pair_both, precision=HIGHEST))
    bias_source = jnp.transpose(pair_both)
    bias = bias_tiles(bias_base(bias_heads))

    out_own = output_projection
    out_par = swap(output_projection)
    gu_own = jnp.transpose(gate_up_projection, (1, 0, 2))
    gu_par = swap(gu_own)
    down_own = down_projection
    down_par = swap(down_projection)
    coord = jnp.concatenate([coordinate_head, coordinate_embedding], axis=0)
    coord = side_by_side(coord, swap(coord), 1)
    fill = jnp.zeros((LANES - 3, width), BF16)
    head = jnp.concatenate([coord[:3], fill], axis=0)
    emb = jnp.concatenate([coord[3:], fill], axis=0)
    cot_came = swap(cot_sent)

    def attention(qkv, kv):
        kv_par = swap(kv)
        attended, logs = attend_forward(tp, qkv, kv_par, mask_q, mask_k, bias)
        return qkv, kv_par, attended, logs

    qkv, kv, x = qkv_first(tp, x_own, x_came, pick, table, qkv_own, qkv_par)
    _, _, attended, _ = attention(qkv, kv)
    shifted, lifted = ffn_forward(
        attended, out_own, out_par, x, pick, table, gu_own, gu_par, down_own, down_par, head, emb, flags
    )
    qkv, kv_par, attended, logs = attention(*qkv_forward(shifted, pick, table, qkv_own, qkv_par))
    (
        result_own,
        result_sent,
        grad_middle,
        grad_attended,
        grads_own,
        grads_sent,
        grad_out_own,
        grad_out_sent,
        early_own,
        early_sent,
    ) = ffn_turn(
        tp, attended, out_own, out_par, shifted, pick, table, gu_own, gu_par, down_own, down_par, cot_own, cot_came, pick_t
    )

    early_came = swap(early_sent)

    came_ffn = swap(grads_sent)
    half_grads, far_grads, diag_half = attend_half_back(
        tp, qkv, kv_par, grad_attended, logs, mask_q, mask_k, bias
    )
    came_grads = swap(far_grads)

    turns = cube.turns()
    every = list(range(cube.bits))
    height = width // rows
    slots = lambda values: values.reshape(3, -1, height, values.shape[-1])
    chunks = grads_own.shape[1]
    own_slots, came_slots = slots(grads_own), slots(came_ffn)
    ffn = [[(own_slots, i, came_slots, i, 0, chunks, every)] for i in range(3)]

    def one_round(streams, bits, *others, whole_arrays=False):
        if whole_arrays:
            sent = half_of(cube.place, streams, bits, False)
            *held, place = lax.optimization_barrier((*sent, *others, cube.place))
            kept = half_of(place, streams, bits, True)
        else:
            sent, kept = halve(cube.place, streams, bits)
            held = lax.optimization_barrier((*sent, *others))
        came = [lax.ppermute(v, "rows", cube.perms[bit]) for v, bit in zip(held, bits)]
        made = [next_sections(*parts) for parts in zip(streams, kept, came, bits)]
        return made, came, held[len(sent) :]

    ffn, came, (mask_full, early_came, _) = one_round(
        ffn, turns[0], mask_q, early_came, diag_half, whole_arrays=True
    )
    early = pack_rows(
        early_kernel, tp, early_own, early_came, early_slopes, embed, (16, 4 * cols + embed.shape[1])
    )
    full_grads, diag_full = attend_full_back(qkv, grad_attended, logs, mask_full, mask_k, bias)
    early = cube.gather(early, 0)
    ffn, came, (pick_weights, early, _) = one_round(ffn, turns[1], pick, early, diag_full, whole_arrays=True)
    gqkv_own, gqkv_sent = qkv_weights(
        shifted, pick_weights, table, full_grads, half_grads, came_grads, grad_out_own, grad_out_sent
    )
    early = cube.gather(early, 1)
    gqkv_sent, early, *_ = lax.optimization_barrier((gqkv_sent, early, *came, *[f[0][0] for f in ffn]))
    own_slots, came_slots = slots(gqkv_own), slots(swap(gqkv_sent))
    streams = [ffn[i] + [(own_slots, i, came_slots, i, 0, 1, every)] for i in range(3)]
    streams, came, (pick_back, early) = one_round(streams, turns[2], pick_weights, early, whole_arrays=True)
    gin_own, gin_sent, late_own, late_sent = qkv_back(
        tp, shifted, pick_back, table, full_grads, half_grads, came_grads, qkv_own, qkv_par, grad_middle, lifted, pick_t
    )
    early = cube.gather(early, 2)
    late_sent, early, *_ = lax.optimization_barrier((late_sent, early, *came, *[f[0][0] for f in streams]))

    grad_bins = bin_sums(tp, diag_full, diag_half)
    came_bins = swap(grad_bins)
    came_bins = jnp.concatenate(
        [came_bins[heads_here : 2 * heads_here], came_bins[:heads_here], came_bins[2 * heads_here :]], axis=0
    )
    bins_fill = grad_bins + came_bins

    late_came = swap(late_sent)
    late = pack_rows(late_kernel, tp, late_own, late_came, late_slopes, bins_fill, (16, 2 * cols + 2 * LANES))
    ffn = [[stream[0] for stream in streams]]
    attn = [stream[1:] for stream in streams]
    rest = list(range(3, cube.bits))
    waited = []
    for step in range(max(len(rest), 2)):
        now, bits = [], []
        if step < len(rest):
            now, bits = ffn, rest[step : step + 1]
        count = len(now)
        if step < 2:
            attn, came, _ = one_round(attn, turns[step], *waited)
        late = cube.gather(late, step)
        if count:
            ffn, waited, (late,) = one_round(now, bits, late)
    done = max(len(rest), 2)
    attn = [[section for stream in attn for section in stream]]
    for bit in rest:
        attn, came, _ = one_round(attn, [bit])
        if done < cube.bits:
            late = after(late, *waited)
            late = cube.gather(late, done)
            done += 1
    for step in range(done, cube.bits):
        late = cube.gather(late, step)
    for step in range(3, cube.bits):
        early = cube.gather(early, step)
    ffn_last = (ffn[0][0][0], ffn[0][0][2])
    attn_last = (attn[0][0][0], attn[0][0][2])

    layer_output = scatter_tokens(result_own, result_sent)
    input_gradient = scatter_tokens(gin_own, gin_sent)

    bins_pad = ((0, LANES - bins), (0, 0))
    grad_gu, grad_down, grad_qkv, grad_out, *conditioning = closing(
        early,
        late,
        jnp.pad(pair_hat, bins_pad),
        jnp.pad(pair_inv, bins_pad),
        gain[None, :],
        jnp.pad(bias_source, ((0, 16 - 2 * heads_here), (0, 0))),
        ffn_last,
        attn_last,
        bins,
        heads_here,
    )
    *conditioning, grad_table, grad_gain, grad_pair, coord_grad = conditioning
    return (
        layer_output,
        input_gradient,
        jnp.transpose(grad_qkv, (1, 0, 2)),
        grad_out.T,
        *conditioning,
        grad_gu,
        grad_down.T,
        grad_table,
        grad_gain,
        grad_pair.T,
        coord_grad,
    )


def solution(mesh):
    in_specs = (
        P("rows", "tp"),
        P("rows", "tp"),
        P("rows", None),
        P("rows"),
        P("rows", None, None),
        P(None, None, "tp"),
        P("tp", None),
        P(None, "tp"),
        P("tp"),
        P(None, "tp"),
        P(None, "tp"),
        P("tp"),
        P(None, "tp"),
        P("tp"),
        P(None, "tp"),
        P(None, "tp"),
        P("tp"),
        P(None, None, "tp"),
        P("tp", None),
        P(),
        P(),
        P(None, "tp"),
        P(None, "tp"),
        P(None, "tp"),
    )
    out_specs = (
        P("rows", "tp"),
        P("rows", "tp"),
        P("rows", None, "tp"),
        P("tp", "rows"),
        P(None, "tp"),
        P("tp"),
        P(None, "tp"),
        P(None, "tp"),
        P("tp"),
        P(None, "tp"),
        P("tp"),
        P(None, "tp"),
        P(None, "tp"),
        P("tp"),
        P("rows", None, "tp"),
        P("tp", "rows"),
        P(),
        P(),
        P(None, "tp"),
        P(None, "tp"),
    )
    return jax.shard_map(
        functools.partial(per_device, rows=mesh.shape["rows"]),
        mesh=mesh,
        in_specs=in_specs,
        out_specs=out_specs,
        check_vma=False,
    )
```
